32 devices in a mesh: seq: 16 (over z, y, x), head: 2 (over core).
Axes of the slice: x: 2, y: 2, z: 4, core: 2. Of those that a mesh axis runs over, the one named last changes fastest.
Arguments:
- tokens: bfloat16 [16384, 768], P(('seq', 'head')), may hold values from -6 to 6
- documents: int32 [16384], replicated, may hold values from 0 to 15, never falling along the last dimension, each value on 1 to 4096 neighbouring positions
- offsets: int32 [5, 16], P(None, 'head'), may hold values from 0 to 15, as said below
- in_proj: bfloat16 [3, 768, 768], P(None, None, 'head'), may hold values from -0.21875 to 0.21875
- out_proj: bfloat16 [768, 768], P('head'), may hold values from -4 to 4
- up_proj: bfloat16 [768, 3072], P(None, 'head'), may hold values from -0.21875 to 0.21875
- down_proj: bfloat16 [3072, 768], P('head'), may hold values from -0.109375 to 0.109375
- first_gain: float32 [768], replicated, may hold values from 0.25 to 1.75
- first_shift: float32 [768], replicated, may hold values from -3 to 3
- second_gain: float32 [768], replicated, may hold values from 0.25 to 1.75
- second_shift: float32 [768], replicated, may hold values from -3 to 3
- cotangent: bfloat16 [16384, 768], P(('seq', 'head')), may hold values from -6 to 6
Outputs:
- block_out: bfloat16 [16384, 768], P(('seq', 'head'))
- grad_tokens: float32 [16384, 768], P(('seq', 'head'))
- grad_in_proj: float32 [3, 768, 768], P(None, None, 'head')
- grad_out_proj: float32 [768, 768], P('head')
- grad_up_proj: float32 [768, 3072], P(None, 'head')
- grad_down_proj: float32 [3072, 768], P('head')
- grad_first_gain: float32 [768], replicated
- grad_first_shift: float32 [768], replicated
- grad_second_gain: float32 [768], replicated
- grad_second_shift: float32 [768], replicated
The draws below stay inside these ranges and needn't reach their ends.
Inputs may be any that keep to these rules, and one draw needn't show every extreme that they name: `documents`: slide numbers of the packed tiles never fall; each slide covers 1 to 4096 tiles, one exactly 4096. offsets[b, h] lies in 0 to 2^b - 1; in every branch b some head has offset 2^b - 1.
All inputs are finite; a program needn't handle non-finite values.
Results may differ from the reference program's by a relative error of at most 0.015.
Values may be sent and summed in bfloat16 or wider, within the bound.
A program may use at most 256 MiB of HBM per device.

```python
import math
import jax
import jax.numpy as jnp
import numpy as np
from jax import lax

D = 768
H = 16
E = 48
F = 3072
BRANCHES = 5
SEG0 = 1024
TOKENS = 16384
DOCS = 16
DOC_MOST = 4096


def draw_offsets(key, part):
    rows_out = []
    head_ids = jnp.arange(H, dtype=jnp.int32)
    for branch in range(BRANCHES):
        drawn = jax.random.randint(jax.random.fold_in(key, 101 + branch), (H,), 0, 2 ** branch).astype(jnp.int32)
        top_head = jax.random.randint(jax.random.fold_in(key, 211 + branch), (), 0, H).astype(jnp.int32)
        rows_out.append(jnp.where(head_ids == top_head, jnp.int32(2 ** branch - 1), drawn))
    return jnp.stack(rows_out).astype(jnp.int32)


def levels(stream_key, shape, cuts, smallest, largest):
    factor_of = 1.0
    for axis_at, shards_of in cuts:
        steps = jax.random.uniform(jax.random.fold_in(jax.random.fold_in(stream_key, 6), axis_at), (shards_of,), jnp.float32, smallest / len(cuts), largest / len(cuts))
        factor_of = factor_of * jnp.repeat(jnp.exp(steps), shape[axis_at] // shards_of).reshape((-1,) + (1,) * (len(shape) - 1 - axis_at))
    return factor_of


def split_up(count, total, most, lean):
    weights = [(1 << 20) // math.isqrt(rank ** lean) + 1 for rank in range(2, count + 1)]
    spare, given = total - most - (count - 1), [1] * (count - 1)
    while spare > 0:
        movable = [i for i in range(count - 1) if given[i] < most]
        pool, left = sum([weights[i] for i in movable]), spare
        for i in movable:
            addition = min(most - given[i], max(1, left * weights[i] // pool), spare)
            given[i] = given[i] + addition
            spare = spare - addition
    return np.array([most] + given)


def uneven(key, count, total, most, skew):
    if count == 2:
        one = jax.random.randint(key, (), max(1, total - most), min(most, total - 1) + 1)
        return jnp.stack([one, total - one])
    tallies = jnp.asarray(split_up(count, total, most, skew), jnp.int32)
    twos = (count - 1) // 2
    giver, sink = tallies[1:1 + 2 * twos:2], tallies[2:2 + 2 * twos:2]
    slack = jnp.minimum(giver - 1, most - sink)
    moved = jax.random.randint(jax.random.fold_in(key, 1), (twos,), 0, 1 << 20) % (slack + 1)
    tallies = tallies.at[1:1 + 2 * twos:2].set(giver - moved).at[2:2 + 2 * twos:2].set(sink + moved)
    return tallies[jax.random.permutation(jax.random.fold_in(key, 2), count)]


def noise(key, extent, scale, bound, split=(), held_as=jnp.bfloat16):
    entries = scale * jax.random.normal(key, extent, jnp.float32)
    if split:
        entries = entries * levels(key, extent, split, -0.22, 0.18)
    return jnp.clip(entries, -bound, bound).astype(held_as)


def setup_inputs(seed: int = 0) -> dict:
    key_of = jax.random.split(jax.random.key(seed), 13)
    return {
        "tokens": noise(key_of[0], (TOKENS, D), 1.0, 6.0, ((0, 32),)),
        "documents": jnp.searchsorted(jnp.cumsum(uneven(key_of[1], DOCS, TOKENS, DOC_MOST, 2)), jnp.arange(TOKENS), side="right").astype(jnp.int32),
        "offsets": draw_offsets(jax.random.fold_in(key_of[12], 71), 0),
        "in_proj": noise(key_of[3], (3, D, H * E), D ** -0.5, 0.21875, ((2, 2),)),
        "out_proj": noise(key_of[4], (H * E, D), 2 ** -0.5, 4.0, ((0, 2),)),
        "up_proj": noise(key_of[5], (D, F), D ** -0.5, 0.21875, ((1, 2),)),
        "down_proj": noise(key_of[6], (F, D), F ** -0.5, 0.109375, ((0, 2),)),
        "first_gain": jnp.clip(1.0 + 0.15 * jax.random.normal(key_of[7], (D,), jnp.float32), 0.25, 1.75),
        "first_shift": noise(key_of[8], (D,), 0.5, 3.0, (), jnp.float32),
        "second_gain": jnp.clip(1.0 + 0.15 * jax.random.normal(key_of[9], (D,), jnp.float32), 0.25, 1.75),
        "second_shift": noise(key_of[10], (D,), 0.5, 3.0, (), jnp.float32),
        "cotangent": noise(key_of[11], (TOKENS, D), 1.0, 6.0, ((0, 32),)),
    }


@jax.custom_vjp
def low(v):
    return lax.optimization_barrier(v.astype(jnp.bfloat16)).astype(jnp.float32)

@jax.custom_vjp
def low_back(v):
    return v

def low_keep(v):
    return (low(v), None)

def low_pass(kept, grad):
    return (grad,)

def back_keep(v):
    return (v, None)

def back_low(kept, grad):
    return (low(grad),)
low.defvjp(low_keep, low_pass)
low_back.defvjp(back_keep, back_low)
EPS = 1e-05
NEG = -1e+30
HIGHEST = lax.Precision.HIGHEST

def norm_rows(values, gain, shift):
    centre = lax.optimization_barrier(jnp.mean(values, axis=-1, keepdims=True))
    centred = values - centre
    spread = lax.optimization_barrier(jnp.mean(centred * centred, axis=-1, keepdims=True))
    return centred * lax.rsqrt(spread + EPS) * gain + shift

def pick_rows(values, stride, chosen_at):
    dims_in = values.shape
    blocked = values.reshape((dims_in[0] // stride, stride) + dims_in[1:])
    pick_index = chosen_at.reshape((1, 1, dims_in[1]) + (1,) * (len(dims_in) - 2))
    pick_index = jnp.broadcast_to(pick_index, (blocked.shape[0], 1) + dims_in[1:])
    return jnp.take_along_axis(blocked, pick_index, axis=1)[:, 0]

def place_rows(values, stride, chosen_at, filler):
    dims_in = values.shape
    slot_ids = jnp.arange(stride, dtype=jnp.int32).reshape((1, stride, 1) + (1,) * (len(dims_in) - 2))
    chosen = slot_ids == chosen_at.reshape((1, 1, dims_in[1]) + (1,) * (len(dims_in) - 2))
    spread = jnp.where(chosen, values[:, None], filler)
    return spread.reshape((dims_in[0] * stride,) + dims_in[1:])

def segment_attend(items):
    q_blk, k_blk, v_blk, q_docs, k_docs = items
    scores = low_back(jnp.einsum('qhe,khe->hqk', q_blk, k_blk, precision=HIGHEST))
    same_doc = q_docs.T[:, :, None] == k_docs.T[:, None, :]
    scores = jnp.where(same_doc, scores, NEG)
    row_top = lax.optimization_barrier(jnp.max(scores, axis=-1, keepdims=True))
    row_sum = lax.optimization_barrier(jnp.sum(jnp.exp(scores - row_top), axis=-1, keepdims=True))
    log_sum = row_top + jnp.log(row_sum)
    prob_rows = low(jnp.exp(scores - log_sum))
    result = low_back(jnp.einsum('hqk,khe->qhe', prob_rows, v_blk, precision=HIGHEST))
    return (result, log_sum[..., 0].T)

def layer(x_rows, in_proj, out_proj, up_proj, down_proj, first_gain, first_shift, second_gain, second_shift, documents, offsets):
    normed_one = low(norm_rows(x_rows, first_gain, first_shift))
    projected = jnp.einsum('td,jdc->jtc', normed_one, in_proj, precision=HIGHEST)
    queries = low(low_back(projected[0]) * E ** (-0.5)).reshape(TOKENS, H, E)
    keys = low(low_back(projected[1])).reshape(TOKENS, H, E)
    values = low(low_back(projected[2])).reshape(TOKENS, H, E)
    head_docs = jnp.broadcast_to(documents[:, None], (TOKENS, H))
    out_list = []
    lse_list = []
    for branch in range(BRANCHES):
        stride = 2 ** branch
        seg_span = SEG0 * stride
        n_segs = TOKENS // seg_span
        chosen_at = offsets[branch]
        q_sel = pick_rows(queries, stride, chosen_at).reshape(n_segs, SEG0, H, E)
        k_sel = pick_rows(keys, stride, chosen_at).reshape(n_segs, SEG0, H, E)
        v_sel = pick_rows(values, stride, chosen_at).reshape(n_segs, SEG0, H, E)
        d_sel = pick_rows(head_docs, stride, chosen_at).reshape(n_segs, SEG0, H)
        out_sel, lse_sel = lax.map(jax.checkpoint(segment_attend), (q_sel, k_sel, v_sel, d_sel, d_sel))
        out_list.append(place_rows(out_sel.reshape(TOKENS // stride, H, E), stride, chosen_at, 0.0))
        lse_list.append(place_rows(lse_sel.reshape(TOKENS // stride, H), stride, chosen_at, NEG))
    lse_stack = jnp.stack(lse_list)
    lse_top = lax.optimization_barrier(jnp.max(lse_stack, axis=0))
    lse_all = lse_top + jnp.log(lax.optimization_barrier(jnp.sum(jnp.exp(lse_stack - lse_top), axis=0)))
    mix_weights = jnp.exp(lse_stack - lse_all)
    merged = mix_weights[0][..., None] * out_list[0]
    for branch in range(1, BRANCHES):
        merged = merged + mix_weights[branch][..., None] * out_list[branch]
    mixed = low(merged.reshape(TOKENS, H * E))
    attn_rows = low_back(jnp.dot(mixed, out_proj, precision=HIGHEST))
    hidden_one = x_rows + attn_rows
    normed_two = low(norm_rows(hidden_one, second_gain, second_shift))
    pre_act = low_back(jnp.dot(normed_two, up_proj, precision=HIGHEST))
    hidden = low(jax.nn.gelu(pre_act, approximate=False))
    return hidden_one + low_back(jnp.dot(hidden, down_proj, precision=HIGHEST))

def reference(tokens, documents, offsets, in_proj, out_proj, up_proj, down_proj, first_gain, first_shift, second_gain, second_shift, cotangent):

    def forward(x_rows, w_qkv, w_out, w_up, w_down, gain_one, shift_one, gain_two, shift_two):
        return layer(x_rows, w_qkv, w_out, w_up, w_down, gain_one, shift_one, gain_two, shift_two, documents, offsets)
    primals = (tokens.astype(jnp.float32), in_proj.astype(jnp.float32), out_proj.astype(jnp.float32), up_proj.astype(jnp.float32), down_proj.astype(jnp.float32), first_gain.astype(jnp.float32), first_shift.astype(jnp.float32), second_gain.astype(jnp.float32), second_shift.astype(jnp.float32))
    result, pullback = jax.vjp(forward, *primals)
    grads = pullback(cotangent.astype(jnp.float32))
    return (result.astype(jnp.bfloat16), grads[0], grads[1], grads[2], grads[3], grads[4], grads[5], grads[6], grads[7], grads[8])
```

```python
import math
from functools import partial

import jax
import jax.numpy as jnp
from jax import lax
from jax.experimental import pallas as pl
from jax.experimental.pallas import tpu as pltpu
from jax.sharding import PartitionSpec as P

E = 48
BRANCHES = 5
SEG0 = 1024
SLOTS = 16
BIT_ROWS = 16
DOC_BITS = 6
ROWS_IN = 3 * E + BIT_ROWS
ROWS_OUT = E + BIT_ROWS
EPS = 1e-05
FAR = 1e30
LOG2E = math.log2(math.e)
LN2 = math.log(2.0)
BF = jnp.bfloat16
F32 = jnp.float32
VMEM_LIMIT = 48 * 2**20


def params(**more):
    return pltpu.CompilerParams(vmem_limit_bytes=VMEM_LIMIT, **more)


def norm_rows(values, gain, shift):
    centre = jnp.mean(values, axis=-1, keepdims=True)
    centred = values - centre
    spread = jnp.mean(centred * centred, axis=-1, keepdims=True)
    return centred * lax.rsqrt(spread + EPS) * gain + shift


def reversed_bits(value, count):
    out = jnp.zeros_like(value)
    for bit in range(count):
        out = out * 2 + value // 2**bit % 2
    return out


def bit_reversed(value, count):
    return int(format(value, f"0{count}b")[::-1], 2)


def branch_shape(branch, heads):
    stride = 2**branch
    return (stride, SEG0 // stride, max(1, heads // stride), max(1, stride // heads))


def pieces_of(value):
    high = value.astype(BF).astype(F32)
    rest = value - high
    middle = rest.astype(BF).astype(F32)
    return high, middle, (rest - middle).astype(BF).astype(F32)


def row_block(placed, columns):
    ids = lax.broadcasted_iota(jnp.int32, (BIT_ROWS, columns), 0)
    block = jnp.zeros((BIT_ROWS, columns), F32)
    for row, value in placed.items():
        block = jnp.where(ids == row, value, block)
    return block


def lane_block(ref, lead, rows, start, count):
    if count >= 128:
        return ref[lead + (rows, pl.ds(pl.multiple_of(start * count, 128), count))]
    per = 128 // count
    wide = ref[lead + (rows, pl.ds(pl.multiple_of(start // per * 128, 128), 128))].astype(F32)
    out = wide[:, :count]
    for part in range(1, per):
        out = jnp.where(start % per == part, wide[:, part * count : (part + 1) * count], out)
    return out.astype(ref.dtype)


def pack_kernel(heads, starts, proj, bits, own, *sends):
    head = pl.program_id(0)
    for j in range(3):
        own[0, 0, j * E : (j + 1) * E, :] = proj[j]
    own[0, 0, 3 * E :, :] = bits[...]
    for branch in range(1, BRANCHES):
        send = sends[branch - 1]
        count = send.shape[-1]
        block = lane_block(own, (0, 0), slice(None), starts[branch, head], count)
        for copy in range(send.shape[0]):
            send[copy, 0] = block


def pack_heads(heads, starts, proj, bits):
    span = proj.shape[-1]
    outs = [jax.ShapeDtypeStruct((1, heads, ROWS_IN, span), BF)]
    specs = [pl.BlockSpec((1, 1, ROWS_IN, span), lambda h, s: (0, h, 0, 0))]
    for branch in range(1, BRANCHES):
        stride, count, per, split = branch_shape(branch, heads)
        outs.append(jax.ShapeDtypeStruct((stride, per, ROWS_IN, count), BF))
        specs.append(
            pl.BlockSpec((split, 1, ROWS_IN, count), lambda h, s, per=per: (h // per, h % per, 0, 0))
        )
    return pl.pallas_call(
        partial(pack_kernel, heads),
        grid_spec=pltpu.PrefetchScalarGridSpec(
            num_scalar_prefetch=1,
            grid=(heads,),
            in_specs=[
                pl.BlockSpec((3, E, span), lambda h, s: (0, h, 0)),
                pl.BlockSpec((BIT_ROWS, span), lambda h, s: (0, 0)),
            ],
            out_specs=specs,
        ),
        out_shape=outs,
        compiler_params=params(),
        name="pack_heads",
    )(starts, proj, bits)


def joined(ref, low, high):
    if ref.shape[0] == 1:
        return ref[0, 0, low:high, :]
    return jnp.concatenate([ref[m, 0, low:high, :] for m in range(ref.shape[0])], axis=1)


def split_out(ref, rows, value, column, count):
    width = ref.shape[-1]
    if ref.shape[0] == 1:
        ref[0, 0, rows, pl.ds(column, count)] = value
        return
    size = min(width, count)
    for start in range(column, column + count, size):
        lanes = slice(start % width, start % width + size)
        ref[start // width, 0, rows, lanes] = value[:, start - column : start - column + size]


def query_side(part, x, queries, split):
    bits = joined(x, 3 * E, ROWS_IN)
    if split == 1:
        return joined(x, 0, E), bits, bits
    lanes = pl.ds(pl.multiple_of(part[0] * queries, 128), queries)
    return x[0, 0, 0:E, lanes], x[0, 0, 3 * E : ROWS_IN, lanes], bits


def forward_kernel(queries, split, tile, part, x, out, q_aug):
    q, q_bits, bits = query_side(part, x, queries, split)
    q_aug[0:E, :] = q
    q_aug[E:, :] = (q_bits.astype(F32) * -FAR).astype(BF)
    k_bits = (1.0 - bits.astype(F32)).astype(BF)
    k_rows = jnp.concatenate([joined(x, E, 2 * E), k_bits], axis=0).T
    v_aug = jnp.concatenate([joined(x, 2 * E, 3 * E), jnp.ones_like(bits)], axis=0)
    base = 0
    if split > 1:
        base = pl.multiple_of(part[0] * queries, 128)
        out[0, 0, 0:E, :] = jnp.zeros((E, out.shape[-1]), BF)
        out[0, 0, E:, :] = row_block({0: -FAR}, out.shape[-1]).astype(BF)
    for step in range(queries // tile):
        column = step * tile
        s = jnp.dot(k_rows, q_aug[:, column : column + tile], preferred_element_type=F32)
        top = jnp.max(s, axis=0, keepdims=True)
        p = jnp.exp2(s - top).astype(BF)
        o = jnp.dot(v_aug, p, preferred_element_type=F32)
        total = o[E : E + 1]
        lse = top + jnp.log2(total)
        high, middle, low = pieces_of(lse)
        split_out(out, slice(0, E), (o[:E] * (1.0 / total)).astype(BF), base + column, tile)
        block = row_block({0: high, 1: middle, 2: low}, tile).astype(BF)
        split_out(out, slice(E, None), block, base + column, tile)


def backward_kernel(queries, split, tile, part, x, g, out, q_aug, g_aug, gk, gv):
    q, q_bits, bits = query_side(part, x, queries, split)
    if split == 1:
        g_aug[...] = joined(g, 0, ROWS_OUT)
    else:
        g_aug[...] = g[0, 0, :, pl.ds(pl.multiple_of(part[0] * queries, 128), queries)]
    extra = g_aug[E:, :].astype(F32)
    ids = lax.broadcasted_iota(jnp.int32, extra.shape, 0)
    q_aug[0:E, :] = q
    q_aug[E:, :] = jnp.where(ids >= 12, extra, q_bits.astype(F32) * -FAR).astype(BF)
    k_bits = (1.0 - bits.astype(F32)).astype(BF)
    k_aug = jnp.concatenate([joined(x, E, 2 * E), k_bits], axis=0)
    k_rows = k_aug.T
    v_ids = lax.broadcasted_iota(jnp.int32, bits.shape, 0)
    v_bits = jnp.where(v_ids < 3, 1.0, 0.0).astype(BF)
    v_rows = jnp.concatenate([joined(x, 2 * E, 3 * E), v_bits], axis=0).T
    q_rows = jnp.concatenate([q, jnp.zeros((BIT_ROWS, queries), BF)], axis=0).T
    g_rows = g_aug[...].T
    base = 0
    if split > 1:
        base = pl.multiple_of(part[0] * queries, 128)
        out[0, 0, 0:E, :] = jnp.zeros((E, out.shape[-1]), BF)
    for step in range(queries // tile):
        column = step * tile
        span = slice(column, column + tile)
        p = jnp.exp2(jnp.dot(k_rows, q_aug[:, span], preferred_element_type=F32))
        gs = p * jnp.dot(v_rows, g_aug[:, span], preferred_element_type=F32)
        p, gs = p.astype(BF), gs.astype(BF)
        gq = jnp.dot(k_aug, gs, preferred_element_type=F32)[:E]
        split_out(out, slice(0, E), gq.astype(BF), base + column, tile)
        new_k = jnp.dot(gs, q_rows[span], preferred_element_type=F32)
        new_v = jnp.dot(p, g_rows[span], preferred_element_type=F32)
        if step == 0:
            gk[...] = new_k
            gv[...] = new_v
        else:
            gk[...] += new_k
            gv[...] += new_v
    width = out.shape[-1]
    k_cols = (gk[...].T[:E] * LN2).astype(BF)
    v_cols = gv[...].T[:E].astype(BF)
    split_out(out, slice(E, 2 * E), k_cols, 0, k_cols.shape[1])
    split_out(out, slice(2 * E, 3 * E), v_cols, 0, k_cols.shape[1])


def unit_spec(array):
    members, _, rows, width = array.shape
    return pl.BlockSpec((members, 1, rows, width), lambda u, p: (0, u, 0, 0))


def unit_cost(units, keys, queries, dots):
    return pl.CostEstimate(
        flops=dots * 2 * units * keys * queries * 256,
        transcendentals=units * keys * queries,
        bytes_accessed=units * keys * 1000,
    )


def attend_forward(part, x, split):
    members, units, _, width = x.shape
    keys = members * width
    queries = keys // split
    out = jax.ShapeDtypeStruct((members, units, ROWS_OUT, width), BF)
    return pl.pallas_call(
        partial(forward_kernel, queries, split, min(256, queries)),
        grid_spec=pltpu.PrefetchScalarGridSpec(
            num_scalar_prefetch=1,
            grid=(units,),
            in_specs=[unit_spec(x)],
            out_specs=unit_spec(out),
            scratch_shapes=[pltpu.VMEM((ROWS_OUT, queries), BF)],
        ),
        out_shape=out,
        compiler_params=params(),
        cost_estimate=unit_cost(units, keys, queries, 2),
        name="attend_forward",
    )(part, x)


def attend_backward(part, x, g, split):
    members, units, _, width = x.shape
    keys = members * width
    queries = keys // split
    out = jax.ShapeDtypeStruct((members, units, 3 * E, width), BF)
    return pl.pallas_call(
        partial(backward_kernel, queries, split, min(256, queries)),
        grid_spec=pltpu.PrefetchScalarGridSpec(
            num_scalar_prefetch=1,
            grid=(units,),
            in_specs=[unit_spec(x), unit_spec(g)],
            out_specs=unit_spec(out),
            scratch_shapes=[
                pltpu.VMEM((ROWS_OUT, queries), BF),
                pltpu.VMEM((ROWS_OUT, queries), BF),
                pltpu.VMEM((keys, ROWS_OUT), F32),
                pltpu.VMEM((keys, ROWS_OUT), F32),
            ],
        ),
        out_shape=out,
        compiler_params=params(),
        cost_estimate=unit_cost(units, keys, queries, 5),
        name="attend_backward",
    )(part, x, g)


def spread_lanes(value, start, count):
    if count >= 128:
        return value, None
    per = 128 // count
    lanes = lax.broadcasted_iota(jnp.int32, (1, 128), 1)
    return jnp.concatenate([value] * per, axis=1), lanes // count == start % per


def aligned(start, count):
    if count >= 128:
        return pl.ds(pl.multiple_of(start * count, 128), count)
    return pl.ds(pl.multiple_of(start // (128 // count) * 128, 128), 128)


def merge_kernel(heads, starts, first, *refs):
    seconds, (mixed, merged, lse) = refs[: BRANCHES - 1], refs[BRANCHES - 1 :]
    head = pl.program_id(0)
    extra = first[0, 0, E:, :].astype(F32)
    merged[0] = first[0, 0, :E, :].astype(F32)
    lse[0] = extra[0:1] + extra[1:2] + extra[2:3]
    for branch in range(1, BRANCHES):
        got = seconds[branch - 1]
        count = got.shape[-1]
        start = starts[branch, head]
        lanes = aligned(start, count)
        for copy in range(got.shape[0]):
            value, mask = spread_lanes(got[copy, 0].astype(F32), start, count)
            new_lse = value[E : E + 1] + value[E + 1 : E + 2] + value[E + 2 : E + 3]
            if mask is not None:
                new_lse = jnp.where(mask, new_lse, -FAR)
            old_lse = lse[0, :, lanes]
            top = jnp.maximum(old_lse, new_lse)
            both = top + jnp.log2(jnp.exp2(old_lse - top) + jnp.exp2(new_lse - top))
            old_w = jnp.exp2(old_lse - both)
            new_w = jnp.exp2(new_lse - both)
            merged[0, :, lanes] = merged[0, :, lanes] * old_w + value[:E] * new_w
            lse[0, :, lanes] = both
    mixed[...] = merged[0].astype(BF)


def merge_heads(heads, starts, first, seconds):
    span = first.shape[-1]
    specs = [pl.BlockSpec((1, 1, ROWS_OUT, span), lambda h, s: (0, h, 0, 0))]
    for branch in range(1, BRANCHES):
        stride, count, per, split = branch_shape(branch, heads)
        specs.append(
            pl.BlockSpec((split, 1, ROWS_OUT, count), lambda h, s, per=per: (h // per, h % per, 0, 0))
        )
    return pl.pallas_call(
        partial(merge_kernel, heads),
        grid_spec=pltpu.PrefetchScalarGridSpec(
            num_scalar_prefetch=1,
            grid=(heads,),
            in_specs=specs,
            out_specs=[
                pl.BlockSpec((E, span), lambda h, s: (h, 0)),
                pl.BlockSpec((1, E, span), lambda h, s: (h, 0, 0)),
                pl.BlockSpec((1, 1, span), lambda h, s: (h, 0, 0)),
            ],
        ),
        out_shape=[
            jax.ShapeDtypeStruct((heads * E, span), BF),
            jax.ShapeDtypeStruct((heads, E, span), F32),
            jax.ShapeDtypeStruct((heads, 1, span), F32),
        ],
        compiler_params=params(),
        name="merge_heads",
    )(starts, first, *seconds)


def spread_kernel(heads, starts, grad, merged, lse, own, *sends):
    head = pl.program_id(0)
    low = grad[...].astype(BF)
    dots = jnp.sum(low.astype(F32) * merged[0], axis=0, keepdims=True)
    own[0, 0, :E, :] = low
    d = pieces_of(-dots)
    m = pieces_of(-lse[0])
    placed = {0: d[0], 1: d[1], 2: d[2], 12: m[0], 13: m[1], 14: m[2]}
    own[0, 0, E:, :] = row_block(placed, grad.shape[-1]).astype(BF)
    for branch in range(1, BRANCHES):
        send = sends[branch - 1]
        count = send.shape[-1]
        block = lane_block(own, (0, 0), slice(None), starts[branch, head], count)
        for copy in range(send.shape[0]):
            send[copy, 0] = block


def spread_heads(heads, starts, grad, merged, lse):
    span = grad.shape[-1]
    outs = [jax.ShapeDtypeStruct((1, heads, ROWS_OUT, span), BF)]
    specs = [pl.BlockSpec((1, 1, ROWS_OUT, span), lambda h, s: (0, h, 0, 0))]
    for branch in range(1, BRANCHES):
        stride, count, per, split = branch_shape(branch, heads)
        outs.append(jax.ShapeDtypeStruct((stride, per, ROWS_OUT, count), BF))
        specs.append(
            pl.BlockSpec((split, 1, ROWS_OUT, count), lambda h, s, per=per: (h // per, h % per, 0, 0))
        )
    return pl.pallas_call(
        partial(spread_kernel, heads),
        grid_spec=pltpu.PrefetchScalarGridSpec(
            num_scalar_prefetch=1,
            grid=(heads,),
            in_specs=[
                pl.BlockSpec((E, span), lambda h, s: (h, 0)),
                pl.BlockSpec((1, E, span), lambda h, s: (h, 0, 0)),
                pl.BlockSpec((1, 1, span), lambda h, s: (h, 0, 0)),
            ],
            out_specs=specs,
        ),
        out_shape=outs,
        compiler_params=params(),
        name="spread_heads",
    )(starts, grad, merged, lse)


def gather_kernel(heads, starts, first, *refs):
    seconds, (out, total) = refs[: BRANCHES - 1], refs[BRANCHES - 1 :]
    head = pl.program_id(0)
    total[...] = first[0, 0].astype(F32)
    for branch in range(1, BRANCHES):
        got = seconds[branch - 1]
        count = got.shape[-1]
        start = starts[branch, head]
        lanes = aligned(start, count)
        value = got[0, 0].astype(F32)
        for copy in range(1, got.shape[0]):
            value += got[copy, 0].astype(F32)
        value, mask = spread_lanes(value, start, count)
        if mask is not None:
            value = jnp.where(mask, value, 0.0)
        total[:, lanes] += value
    out[0] = (total[0:E, :] * E ** (-0.5)).astype(BF)
    out[1] = total[E : 2 * E, :].astype(BF)
    out[2] = total[2 * E :, :].astype(BF)


def gather_heads(heads, starts, first, seconds):
    span = first.shape[-1]
    specs = [pl.BlockSpec((1, 1, 3 * E, span), lambda h, s: (0, h, 0, 0))]
    for branch in range(1, BRANCHES):
        stride, count, per, split = branch_shape(branch, heads)
        specs.append(
            pl.BlockSpec((split, 1, 3 * E, count), lambda h, s, per=per: (h // per, h % per, 0, 0))
        )
    return pl.pallas_call(
        partial(gather_kernel, heads),
        grid_spec=pltpu.PrefetchScalarGridSpec(
            num_scalar_prefetch=1,
            grid=(heads,),
            in_specs=specs,
            out_specs=pl.BlockSpec((3, E, span), lambda h, s: (0, h, 0)),
            scratch_shapes=[pltpu.VMEM((3 * E, span), F32)],
        ),
        out_shape=jax.ShapeDtypeStruct((3, heads * E, span), BF),
        compiler_params=params(),
        name="gather_heads",
    )(starts, first, *seconds)


def exchange(value, branch):
    size = lax.axis_size("seq")
    stride = 2**branch
    groups = None
    if stride != size:
        groups = [[g * stride + i for i in range(stride)] for g in range(size // stride)]
    return lax.all_to_all(value, "seq", 0, 0, axis_index_groups=groups, tiled=True)


def to_unit(value, whole):
    if not whole:
        return value
    members, units, rows, width = value.shape
    return value.transpose(1, 2, 0, 3).reshape(1, units, rows, members * width)


def from_unit(value, members, whole):
    if not whole:
        return value
    _, units, rows, width = value.shape
    return value.reshape(units, rows, members, width // members).transpose(2, 0, 1, 3)


def rolled(value, step):
    size = lax.axis_size("head")
    return lax.ppermute(value, "head", [(s, (s + step) % size) for s in range(size)])


def all_rows(own):
    size = lax.axis_size("head")
    me = lax.axis_index("head")
    got = [own] + [rolled(own, step) for step in range(1, size)]
    if size == 2:
        return [jnp.where(me == 0, got[0], got[1]), jnp.where(me == 0, got[1], got[0])]
    stacked = jnp.stack(got)
    return [stacked[(me - place) % size] for place in range(size)]


def sum_rows(parts):
    size = lax.axis_size("head")
    me = lax.axis_index("head")
    total = lax.dynamic_index_in_dim(parts, me, 0, keepdims=False).astype(F32)
    for step in range(1, size):
        sent = lax.dynamic_index_in_dim(parts, (me + step) % size, 0, keepdims=False)
        total = total + rolled(sent, step).astype(F32)
    return total


def sum_seq(value):
    size = lax.axis_size("seq")
    got = lax.all_to_all(value.astype(BF), "seq", 0, 0, tiled=True)
    mine = got.reshape((size, value.shape[0] // size) + value.shape[1:]).astype(F32).sum(0)
    full = jnp.broadcast_to(mine.astype(BF)[None], (size,) + mine.shape)
    return lax.all_to_all(full, "seq", 0, 0, tiled=True).reshape(value.shape).astype(F32)


def local(
    tokens,
    documents,
    offsets,
    in_proj,
    out_proj,
    up_proj,
    down_proj,
    first_gain,
    first_shift,
    second_gain,
    second_shift,
    cotangent,
):
    head_count = lax.axis_size("head")
    seq_id = lax.axis_index("seq")
    row_count, width = tokens.shape
    seq_len = row_count * head_count
    heads = offsets.shape[1]
    per_slot = row_count // SLOTS
    gelu_exact = partial(jax.nn.gelu, approximate=False)

    ids = lax.broadcasted_iota(jnp.int32, (row_count, row_count), 0)
    slot = reversed_bits(ids // per_slot, 4)
    source = ids % per_slot * SLOTS + slot
    order = (source == lax.broadcasted_iota(jnp.int32, (row_count, row_count), 1)).astype(BF)

    def sorted_rows(values):
        return jnp.dot(order, values, preferred_element_type=F32)

    def shard_rows(own):
        parts = [part.reshape(SLOTS, per_slot, -1) for part in all_rows(own)]
        return jnp.stack(parts, axis=1).reshape(seq_len, -1)

    def device_parts(values):
        split = values.reshape(SLOTS, head_count, per_slot, -1)
        return jnp.moveaxis(split, 1, 0).reshape(head_count, row_count, -1)

    x_rows = sorted_rows(tokens)
    cot_low = sorted_rows(cotangent).astype(BF)
    normed_one = norm_rows(x_rows, first_gain, first_shift)
    gathered_one = shard_rows(normed_one.astype(BF))
    cot_all = shard_rows(cot_low)

    my_docs = lax.dynamic_slice_in_dim(documents, seq_id * seq_len, seq_len)
    my_docs = my_docs.reshape(head_count, per_slot, 2, 2, 2, 2).transpose(5, 4, 3, 2, 0, 1).reshape(seq_len)
    bit_ids = jnp.arange(BIT_ROWS, dtype=jnp.int32)[:, None]
    doc_bit = my_docs[None, :] // 2 ** (bit_ids % DOC_BITS) % 2
    bits = jnp.where(bit_ids < DOC_BITS, doc_bit, jnp.where(bit_ids < 2 * DOC_BITS, 1 - doc_bit, 0))
    bits = bits.astype(BF)
    starts = jnp.stack([reversed_bits(offsets[b], b) for b in range(BRANCHES)])

    scales = jnp.array([E ** (-0.5) * LOG2E, 1.0, 1.0], F32)[:, None, None]
    projected = jnp.einsum("td,jdc->jct", gathered_one, in_proj, preferred_element_type=F32)
    projected = (projected * scales).astype(BF)
    own, *sends = pack_heads(heads, starts, projected, bits)

    shapes = [branch_shape(b, heads) for b in range(BRANCHES)]
    whole = [s[3] > 1 or s[1] < 128 for s in shapes]
    places = [(seq_id % s[0] % s[3]).astype(jnp.int32).reshape(1) for s in shapes]

    received = [None] + [exchange(sends[b - 1], b) for b in range(1, BRANCHES)]
    first_out = attend_forward(places[0], own, 1)
    units = [own]
    outs = []
    for b in range(1, BRANCHES):
        unit = to_unit(received[b], whole[b])
        units.append(unit)
        result = attend_forward(places[b], unit, shapes[b][3])
        outs.append(exchange(from_unit(result, shapes[b][0], whole[b]), b))
    mixed, merged, lse = merge_heads(heads, starts, first_out, outs)

    attn_part = jnp.einsum("ct,cd->td", mixed, out_proj, preferred_element_type=F32).astype(BF)
    hidden_one = x_rows + sum_rows(device_parts(attn_part))
    normed_two = norm_rows(hidden_one, second_gain, second_shift)
    gathered_two = shard_rows(normed_two.astype(BF))
    pre_act = jnp.dot(gathered_two, up_proj, preferred_element_type=F32)
    hidden, gelu_pull = jax.vjp(gelu_exact, pre_act)
    hidden = hidden.astype(BF)
    down_part = jnp.dot(hidden, down_proj, preferred_element_type=F32).astype(BF)
    block_rows = hidden_one + sum_rows(device_parts(down_part))
    block_out = jnp.dot(order.T, block_rows.astype(BF), preferred_element_type=F32).astype(BF)

    grad_down = jnp.einsum("tf,td->fd", hidden, cot_all, preferred_element_type=F32).astype(BF)
    grad_act = jnp.einsum("td,fd->tf", cot_all, down_proj, preferred_element_type=F32)
    grad_pre = gelu_pull(grad_act)[0].astype(BF)
    grad_up = jnp.einsum("td,tf->df", gathered_two, grad_pre, preferred_element_type=F32).astype(BF)
    norm_part = jnp.einsum("tf,df->td", grad_pre, up_proj, preferred_element_type=F32).astype(BF)
    grad_normed_two = sum_rows(device_parts(norm_part))
    pull_two = jax.vjp(norm_rows, hidden_one, second_gain, second_shift)[1]
    grad_ln_two, grad_gain_two, grad_shift_two = pull_two(grad_normed_two)
    grad_hidden_one = cot_low.astype(F32) + grad_ln_two
    grad_attn = shard_rows(grad_hidden_one.astype(BF))
    grad_out = jnp.einsum("ct,td->cd", mixed, grad_attn, preferred_element_type=F32).astype(BF)
    grad_merged = jnp.einsum("td,cd->ct", grad_attn, out_proj, preferred_element_type=F32)

    own_g, *sends_g = spread_heads(heads, starts, grad_merged, merged, lse)
    received_g = [None] + [exchange(sends_g[b - 1], b) for b in range(1, BRANCHES)]
    first_grad = attend_backward(places[0], own, own_g, 1)
    grads = []
    for b in range(1, BRANCHES):
        unit_g = to_unit(received_g[b], whole[b])
        result = attend_backward(places[b], units[b], unit_g, shapes[b][3])
        grads.append(exchange(from_unit(result, shapes[b][0], whole[b]), b))
    grad_qkv = gather_heads(heads, starts, first_grad, grads)

    grad_in = jnp.einsum("td,jct->jdc", gathered_one, grad_qkv, preferred_element_type=F32)
    one_part = jnp.einsum("jct,jdc->td", grad_qkv, in_proj, preferred_element_type=F32).astype(BF)
    grad_normed_one = sum_rows(device_parts(one_part))
    pull_one = jax.vjp(norm_rows, x_rows, first_gain, first_shift)[1]
    grad_ln_one, grad_gain_one, grad_shift_one = pull_one(grad_normed_one)
    grad_tokens = jnp.dot(
        order.T.astype(F32),
        grad_hidden_one + grad_ln_one,
        precision=lax.Precision.HIGHEST,
        preferred_element_type=F32,
    )

    middle = lax.psum((grad_out, grad_up, grad_down), "seq")
    flat_in = grad_in.reshape(3 * width, heads * E)
    grad_in = sum_seq(flat_in).reshape(3, width, heads * E)
    gains = jnp.stack([grad_gain_one, grad_shift_one, grad_gain_two, grad_shift_two])
    gains = lax.psum(gains, ("seq", "head"))
    return (
        block_out,
        grad_tokens,
        grad_in,
        middle[0].astype(F32),
        middle[1].astype(F32),
        middle[2].astype(F32),
        gains[0],
        gains[1],
        gains[2],
        gains[3],
    )


def solution(mesh):
    placed = (
        P(("seq", "head"), None),
        P(),
        P(None, "head"),
        P(None, None, "head"),
        P("head", None),
        P(None, "head"),
        P("head", None),
        P(),
        P(),
        P(),
        P(),
        P(("seq", "head"), None),
    )
    return jax.shard_map(
        local,
        mesh=mesh,
        in_specs=placed,
        out_specs=(
            P(("seq", "head"), None),
            P(("seq", "head"), None),
            P(None, None, "head"),
            P("head", None),
            P(None, "head"),
            P("head", None),
            P(),
            P(),
            P(),
            P(),
        ),
        check_vma=False,
    )
```

```python
import math
from functools import partial

import jax
import jax.numpy as jnp
from jax import lax
from jax.experimental import pallas as pl
from jax.experimental.pallas import tpu as pltpu
from jax.sharding import PartitionSpec as P

E = 48
BRANCHES = 5
SEG0 = 1024
SLOTS = 16
BIT_ROWS = 16
DOC_BITS = 6
ROWS_IN = 3 * E + BIT_ROWS
ROWS_OUT = E + BIT_ROWS
EPS = 1e-05
FAR = 1e30
LOG2E = math.log2(math.e)
LN2 = math.log(2.0)
BF = jnp.bfloat16
F32 = jnp.float32
VMEM_LIMIT = 48 * 2**20


def params(**more):
    return pltpu.CompilerParams(vmem_limit_bytes=VMEM_LIMIT, **more)


def norm_rows(values, gain, shift):
    centre = jnp.mean(values, axis=-1, keepdims=True)
    centred = values - centre
    spread = jnp.mean(centred * centred, axis=-1, keepdims=True)
    return centred * lax.rsqrt(spread + EPS) * gain + shift


def reversed_bits(value, count):
    out = jnp.zeros_like(value)
    for bit in range(count):
        out = out * 2 + value // 2**bit % 2
    return out


def bit_reversed(value, count):
    return int(format(value, f"0{count}b")[::-1], 2)


def branch_shape(branch, heads):
    stride = 2**branch
    return (stride, SEG0 // stride, max(1, heads // stride), max(1, stride // heads))


def pieces_of(value):
    high = value.astype(BF).astype(F32)
    rest = value - high
    middle = rest.astype(BF).astype(F32)
    return high, middle, (rest - middle).astype(BF).astype(F32)


def row_block(placed, columns):
    ids = lax.broadcasted_iota(jnp.int32, (BIT_ROWS, columns), 0)
    block = jnp.zeros((BIT_ROWS, columns), F32)
    for row, value in placed.items():
        block = jnp.where(ids == row, value, block)
    return block


def lane_block(ref, rows, start, count):
    return ref[0, 0, rows, aligned(start, count)]


def aligned(start, count):
    if count >= 128:
        return pl.ds(pl.multiple_of(start * count, 128), count)
    return pl.ds(pl.multiple_of(start // (128 // count) * 128, 128), 128)


def moved_part(block, count, source, target):
    per = 128 // count
    lanes = lax.broadcasted_iota(jnp.int32, (1, 128), 1)
    out = block
    for shift in range(1, per):
        turned = jnp.concatenate([block[:, -shift * count :], block[:, : -shift * count]], axis=1)
        out = jnp.where((target - source) % per == shift, turned, out)
    return jnp.where(lanes // count == target, out, 0.0)


def pack_kernel(heads, starts, place, proj, bits, own, *sends):
    head = pl.program_id(0)
    for j in range(3):
        own[0, 0, j * E : (j + 1) * E, :] = proj[j]
    own[0, 0, 3 * E :, :] = bits[...]
    send_blocks(heads, head, starts, place, own, sends)


def send_blocks(heads, head, starts, place, own, sends):
    for branch in range(1, BRANCHES):
        count = branch_shape(branch, heads)[1]
        send = sends[branch - 1]
        start = starts[branch, head]
        block = lane_block(own, slice(None), start, count)
        if count < 128:
            per = 128 // count
            block = moved_part(block.astype(F32), count, start % per, place[0] % per).astype(BF)
        for copy in range(send.shape[0]):
            send[copy, 0] = block


def send_shapes(heads, rows):
    outs, specs = [], []
    for branch in range(1, BRANCHES):
        stride, count, per, split = branch_shape(branch, heads)
        count = max(count, 128)
        outs.append(jax.ShapeDtypeStruct((stride, per, rows, count), BF))
        specs.append(
            pl.BlockSpec((split, 1, rows, count), lambda h, s, t, per=per: (h // per, h % per, 0, 0))
        )
    return outs, specs


def pack_heads(heads, starts, place, proj, bits):
    span = proj.shape[-1]
    sends, send_specs = send_shapes(heads, ROWS_IN)
    return pl.pallas_call(
        partial(pack_kernel, heads),
        grid_spec=pltpu.PrefetchScalarGridSpec(
            num_scalar_prefetch=2,
            grid=(heads,),
            in_specs=[
                pl.BlockSpec((3, E, span), lambda h, s, t: (0, h, 0)),
                pl.BlockSpec((BIT_ROWS, span), lambda h, s, t: (0, 0)),
            ],
            out_specs=[pl.BlockSpec((1, 1, ROWS_IN, span), lambda h, s, t: (0, h, 0, 0))] + send_specs,
        ),
        out_shape=[jax.ShapeDtypeStruct((1, heads, ROWS_IN, span), BF)] + sends,
        compiler_params=params(),
        name="pack_heads",
    )(starts, place, proj, bits)


def load_unit(ref, unit, count, x):
    if ref.shape[0] == 1:
        x[...] = ref[0, unit]
        return
    width = ref.shape[-1]
    per = width // count
    for block in range(ref.shape[0] // per):
        value = ref[block * per, unit]
        for other in range(1, per):
            value = value + ref[block * per + other, unit]
        x[:, block * width : (block + 1) * width] = value


def store_unit(ref, unit, rows, value, column, count):
    width = ref.shape[-1]
    size = min(width, count)
    for start in range(column, column + count, size):
        lanes = slice(start % width, start % width + size)
        ref[start // width, unit, rows, lanes] = value[:, start - column : start - column + size]


def forward_unit(x, q_aug, base, queries, tile, put):
    if isinstance(base, int):
        lanes = slice(base, base + queries)
    else:
        lanes = pl.ds(pl.multiple_of(base, 128), queries)
    q_aug[0:E, :queries] = x[0:E, lanes]
    q_aug[E:, :queries] = (x[3 * E :, lanes].astype(F32) * -FAR).astype(BF)
    bits = x[3 * E :, :].astype(F32)
    k_rows = jnp.concatenate([x[E : 2 * E, :], (1.0 - bits).astype(BF)], axis=0).T
    v_aug = jnp.concatenate([x[2 * E : 3 * E, :], jnp.ones(bits.shape, BF)], axis=0)
    for step in range(queries // tile):
        column = step * tile
        s = jnp.dot(k_rows, q_aug[:, column : column + tile], preferred_element_type=F32)
        top = jnp.max(s, axis=0, keepdims=True)
        p = jnp.exp2(s - top).astype(BF)
        o = jnp.dot(v_aug, p, preferred_element_type=F32)
        total = o[E : E + 1]
        high, middle, low = pieces_of(top + jnp.log2(total))
        block = row_block({0: high, 1: middle, 2: low}, tile)
        put(column, jnp.concatenate([o[:E] * (1.0 / total), block], axis=0).astype(BF))


def group_place(branch):
    stride = 2**branch
    me = lax.axis_index("seq")
    return me // stride * stride, me % stride


def meet_group():
    base, place = group_place(BRANCHES - 1)
    size = 2 ** (BRANCHES - 1)
    barrier = pltpu.get_barrier_semaphore()

    @pl.loop(1, size)
    def _(step):
        pl.semaphore_signal(
            barrier,
            inc=1,
            device_id={"seq": base + (place + step) % size},
            device_id_type=pl.DeviceIdType.MESH,
        )

    pl.semaphore_wait(barrier, size - 1)


def group_copies(branch, source, target, source_block, send_sems, recv_sems, local_sem):
    stride = 2**branch
    base, place = group_place(branch)
    first = stride - branch - 2
    copies = [
        pltpu.make_async_copy(source.at[source_block(place)], target.at[place], local_sem.at[branch - 1])
    ]
    for step in range(1, stride):
        member = (place + step) % stride
        copies.append(
            pltpu.make_async_remote_copy(
                src_ref=source.at[source_block(member)],
                dst_ref=target.at[place],
                send_sem=send_sems.at[first + step],
                recv_sem=recv_sems.at[first + step],
                device_id={"seq": base + member},
                device_id_type=pl.DeviceIdType.MESH,
            )
        )
    return copies


def exchange_forward_kernel(heads, own, *refs):
    count = BRANCHES - 1
    sends, refs = refs[:count], refs[count:]
    first, refs = refs[0], refs[1:]
    gots, refs = refs[:count], refs[count:]
    backs, refs = refs[:count], refs[count:]
    outs, refs = refs[:count], refs[count:]
    x, q_aug, in_send, in_recv, in_local, out_send, out_recv, out_local = refs
    tile = 256
    meet_group()
    coming = {}
    for branch in range(1, BRANCHES):
        coming[branch] = group_copies(
            branch, sends[branch - 1], gots[branch - 1], lambda m: m, in_send, in_recv, in_local
        )
        for copy in coming[branch]:
            copy.start()

    @pl.loop(0, heads)
    def _(head):
        x[...] = own[0, head]

        def put(column, value):
            first[0, head, :, column : column + tile] = value

        forward_unit(x, q_aug, 0, SEG0, tile, put)

    leaving = []
    for branch in range(1, BRANCHES):
        stride, lanes, units, split = branch_shape(branch, heads)
        got, out = gots[branch - 1], outs[branch - 1]
        for copy in coming[branch]:
            copy.wait()
        queries = SEG0 // split
        base = 0 if split == 1 else lax.axis_index("seq") % split * queries

        @pl.loop(0, units)
        def _(unit):
            load_unit(got, unit, lanes, x)
            if split == 1:

                def put(column, value):
                    store_unit(out, unit, slice(None), value, column, value.shape[1])

            else:
                empty = row_block({0: -FAR}, 128)
                empty = jnp.concatenate([jnp.zeros((E, 128), F32), empty], axis=0).astype(BF)
                for block in range(SEG0 // 128):
                    store_unit(out, unit, slice(None), empty, block * 128, 128)

                def put(column, value):
                    width = out.shape[-1]
                    for start in range(0, value.shape[1], width):
                        block = (base + column + start) // width
                        out[block, unit] = value[:, start : start + width]

            forward_unit(x, q_aug, base, queries, min(tile, queries), put)

        per = out.shape[-1] // lanes
        copies = group_copies(
            branch, out, backs[branch - 1], lambda m: m // per, out_send, out_recv, out_local
        )
        for copy in copies:
            copy.start()
        leaving += copies
    for copy in leaving:
        copy.wait()


def exchange_scratch():
    copies = 2**BRANCHES - 2 - BRANCHES + 1
    one = [
        pltpu.SemaphoreType.DMA((copies,)),
        pltpu.SemaphoreType.DMA((copies,)),
        pltpu.SemaphoreType.DMA((BRANCHES - 1,)),
    ]
    return one + one


def unit_cost(units, dots):
    return pl.CostEstimate(
        flops=dots * 2 * units * SEG0 * SEG0 * 256,
        transcendentals=units * SEG0 * SEG0,
        bytes_accessed=units * SEG0 * 1000,
    )


def vmem_specs(count):
    return [pl.BlockSpec(memory_space=pltpu.VMEM)] * count


def out_blocks(heads, rows):
    shapes = []
    for branch in range(1, BRANCHES):
        stride, count, units, split = branch_shape(branch, heads)
        width = max(count, 128)
        shapes.append((SEG0 // width, units, rows, width))
    return shapes


def exchange_forward(heads, own, sends):
    backs = send_shapes(heads, ROWS_OUT)[0]
    gots = send_shapes(heads, ROWS_IN)[0]
    first = jax.ShapeDtypeStruct((1, heads, ROWS_OUT, SEG0), BF)
    results = pl.pallas_call(
        partial(exchange_forward_kernel, heads),
        in_specs=vmem_specs(1 + len(sends)),
        out_specs=vmem_specs(1 + len(gots) + len(backs)),
        out_shape=[first] + gots + backs,
        scratch_shapes=[pltpu.VMEM(shape, BF) for shape in out_blocks(heads, ROWS_OUT)]
        + [pltpu.VMEM((ROWS_IN, SEG0), BF), pltpu.VMEM((ROWS_OUT, SEG0), BF)]
        + exchange_scratch(),
        compiler_params=params(collective_id=0, has_side_effects=True),
        cost_estimate=unit_cost(2 * heads, 2),
        name="exchange_forward",
    )(own, *sends)
    return results[0], results[1 : 1 + len(gots)], results[1 + len(gots) :]


def backward_unit(x, g, q_aug, gk, gv, base, queries, tile, put):
    if isinstance(base, int):
        lanes = slice(base, base + queries)
    else:
        lanes = pl.ds(pl.multiple_of(base, 128), queries)
    extra = g[E:, lanes].astype(F32)
    ids = lax.broadcasted_iota(jnp.int32, extra.shape, 0)
    q = x[0:E, lanes]
    q_aug[0:E, :queries] = q
    q_aug[E:, :queries] = jnp.where(ids >= 12, extra, x[3 * E :, lanes].astype(F32) * -FAR).astype(BF)
    bits = x[3 * E :, :].astype(F32)
    k_aug = jnp.concatenate([x[E : 2 * E, :], (1.0 - bits).astype(BF)], axis=0)
    k_rows = k_aug.T
    v_ids = lax.broadcasted_iota(jnp.int32, bits.shape, 0)
    v_bits = jnp.where(v_ids < 3, 1.0, 0.0).astype(BF)
    v_rows = jnp.concatenate([x[2 * E : 3 * E, :], v_bits], axis=0).T
    q_rows = jnp.concatenate([q, jnp.zeros((BIT_ROWS, queries), BF)], axis=0).T
    g_all = g[:, lanes]
    g_rows = g_all.T
    for step in range(queries // tile):
        column = step * tile
        span = slice(column, column + tile)
        p = jnp.exp2(jnp.dot(k_rows, q_aug[:, span], preferred_element_type=F32))
        gs = p * jnp.dot(v_rows, g_all[:, span], preferred_element_type=F32)
        p, gs = p.astype(BF), gs.astype(BF)
        put(column, jnp.dot(k_aug, gs, preferred_element_type=F32)[:E].astype(BF))
        new_k = jnp.dot(gs, q_rows[span], preferred_element_type=F32)
        new_v = jnp.dot(p, g_rows[span], preferred_element_type=F32)
        if step == 0:
            gk[...] = new_k
            gv[...] = new_v
        else:
            gk[...] += new_k
            gv[...] += new_v
    return (gk[...].T[:E] * LN2).astype(BF), gv[...].T[:E].astype(BF)


def exchange_backward_kernel(heads, own, own_g, *refs):
    count = BRANCHES - 1
    units_in, refs = refs[:count], refs[count:]
    sends, refs = refs[:count], refs[count:]
    first, refs = refs[0], refs[1:]
    backs, refs = refs[:count], refs[count:]
    gots, refs = refs[:count], refs[count:]
    outs, refs = refs[:count], refs[count:]
    x, g, q_aug, gk, gv, in_send, in_recv, in_local, out_send, out_recv, out_local = refs
    tile = 256
    meet_group()
    coming = {}
    for branch in range(1, BRANCHES):
        coming[branch] = group_copies(
            branch, sends[branch - 1], gots[branch - 1], lambda m: m, in_send, in_recv, in_local
        )
        for copy in coming[branch]:
            copy.start()

    def own_heads(low, high):
        @pl.loop(low, high)
        def _(head):
            x[...] = own[0, head]
            g[...] = own_g[0, head]

            def put(column, value):
                first[0, head, :E, column : column + tile] = value

            k_cols, v_cols = backward_unit(x, g, q_aug, gk, gv, 0, SEG0, tile, put)
            first[0, head, E : 2 * E, :] = k_cols
            first[0, head, 2 * E :, :] = v_cols

    own_heads(0, heads // 2)
    leaving = []
    for branch in range(1, BRANCHES):
        stride, lanes, units, split = branch_shape(branch, heads)
        got, out, unit_in = gots[branch - 1], outs[branch - 1], units_in[branch - 1]
        for copy in coming[branch]:
            copy.wait()
        queries = SEG0 // split
        base = 0 if split == 1 else lax.axis_index("seq") % split * queries

        @pl.loop(0, units)
        def _(unit):
            load_unit(unit_in, unit, lanes, x)
            load_unit(got, unit, lanes, g)
            if split == 1:

                def put(column, value):
                    store_unit(out, unit, slice(0, E), value, column, value.shape[1])

            else:
                empty = jnp.zeros((E, 128), BF)
                for block in range(SEG0 // 128):
                    store_unit(out, unit, slice(0, E), empty, block * 128, 128)

                def put(column, value):
                    width = out.shape[-1]
                    for start in range(0, value.shape[1], width):
                        block = (base + column + start) // width
                        out[block, unit, :E, :] = value[:, start : start + width]

            k_cols, v_cols = backward_unit(x, g, q_aug, gk, gv, base, queries, min(tile, queries), put)
            store_unit(out, unit, slice(E, 2 * E), k_cols, 0, SEG0)
            store_unit(out, unit, slice(2 * E, 3 * E), v_cols, 0, SEG0)

        per = out.shape[-1] // lanes
        copies = group_copies(
            branch, out, backs[branch - 1], lambda m: m // per, out_send, out_recv, out_local
        )
        for copy in copies:
            copy.start()
        leaving += copies
    own_heads(heads // 2, heads)
    for copy in leaving:
        copy.wait()


def exchange_backward(heads, own, own_g, units, sends):
    backs = send_shapes(heads, 3 * E)[0]
    first = jax.ShapeDtypeStruct((1, heads, 3 * E, SEG0), BF)
    results = pl.pallas_call(
        partial(exchange_backward_kernel, heads),
        in_specs=vmem_specs(2 + len(units) + len(sends)),
        out_specs=vmem_specs(1 + len(backs)),
        out_shape=[first] + backs,
        scratch_shapes=[pltpu.VMEM(shape.shape, BF) for shape in send_shapes(heads, ROWS_OUT)[0]]
        + [pltpu.VMEM(shape, BF) for shape in out_blocks(heads, 3 * E)]
        + [
            pltpu.VMEM((ROWS_IN, SEG0), BF),
            pltpu.VMEM((ROWS_OUT, SEG0), BF),
            pltpu.VMEM((ROWS_OUT, SEG0), BF),
            pltpu.VMEM((SEG0, ROWS_OUT), F32),
            pltpu.VMEM((SEG0, ROWS_OUT), F32),
        ]
        + exchange_scratch(),
        compiler_params=params(collective_id=1, has_side_effects=True),
        cost_estimate=unit_cost(2 * heads, 5),
        name="exchange_backward",
    )(own, own_g, *units, *sends)
    return results[0], results[1:]


def placed_part(value, count, start, place):
    if count >= 128:
        return value, None
    per = 128 // count
    lanes = lax.broadcasted_iota(jnp.int32, (1, 128), 1)
    return moved_part(value, count, place % per, start % per), lanes // count == start % per


def merge_kernel(heads, starts, place, first, *refs):
    seconds, (mixed, merged, lse) = refs[: BRANCHES - 1], refs[BRANCHES - 1 :]
    head = pl.program_id(0)
    extra = first[0, 0, E:, :].astype(F32)
    merged[0] = first[0, 0, :E, :].astype(F32)
    lse[0] = extra[0:1] + extra[1:2] + extra[2:3]
    for branch in range(1, BRANCHES):
        got = seconds[branch - 1]
        count = branch_shape(branch, heads)[1]
        start = starts[branch, head]
        lanes = aligned(start, count)
        for copy in range(got.shape[0]):
            value, mask = placed_part(got[copy, 0].astype(F32), count, start, place[0])
            new_lse = value[E : E + 1] + value[E + 1 : E + 2] + value[E + 2 : E + 3]
            if mask is not None:
                new_lse = jnp.where(mask, new_lse, -FAR)
            old_lse = lse[0, :, lanes]
            top = jnp.maximum(old_lse, new_lse)
            both = top + jnp.log2(jnp.exp2(old_lse - top) + jnp.exp2(new_lse - top))
            old_w = jnp.exp2(old_lse - both)
            new_w = jnp.exp2(new_lse - both)
            merged[0, :, lanes] = merged[0, :, lanes] * old_w + value[:E] * new_w
            lse[0, :, lanes] = both
    mixed[...] = merged[0].astype(BF)


def merge_heads(heads, starts, place, first, seconds):
    span = first.shape[-1]
    return pl.pallas_call(
        partial(merge_kernel, heads),
        grid_spec=pltpu.PrefetchScalarGridSpec(
            num_scalar_prefetch=2,
            grid=(heads,),
            in_specs=[pl.BlockSpec((1, 1, ROWS_OUT, span), lambda h, s, t: (0, h, 0, 0))]
            + send_shapes(heads, ROWS_OUT)[1],
            out_specs=[
                pl.BlockSpec((E, span), lambda h, s, t: (h, 0)),
                pl.BlockSpec((1, E, span), lambda h, s, t: (h, 0, 0)),
                pl.BlockSpec((1, 1, span), lambda h, s, t: (h, 0, 0)),
            ],
        ),
        out_shape=[
            jax.ShapeDtypeStruct((heads * E, span), BF),
            jax.ShapeDtypeStruct((heads, E, span), F32),
            jax.ShapeDtypeStruct((heads, 1, span), F32),
        ],
        compiler_params=params(),
        name="merge_heads",
    )(starts, place, first, *seconds)


def spread_kernel(heads, starts, place, grad, merged, lse, own, *sends):
    head = pl.program_id(0)
    low = grad[...].astype(BF)
    dots = jnp.sum(low.astype(F32) * merged[0], axis=0, keepdims=True)
    own[0, 0, :E, :] = low
    d = pieces_of(-dots)
    m = pieces_of(-lse[0])
    placed = {0: d[0], 1: d[1], 2: d[2], 12: m[0], 13: m[1], 14: m[2]}
    own[0, 0, E:, :] = row_block(placed, grad.shape[-1]).astype(BF)
    send_blocks(heads, head, starts, place, own, sends)


def spread_heads(heads, starts, place, grad, merged, lse):
    span = grad.shape[-1]
    sends, send_specs = send_shapes(heads, ROWS_OUT)
    return pl.pallas_call(
        partial(spread_kernel, heads),
        grid_spec=pltpu.PrefetchScalarGridSpec(
            num_scalar_prefetch=2,
            grid=(heads,),
            in_specs=[
                pl.BlockSpec((E, span), lambda h, s, t: (h, 0)),
                pl.BlockSpec((1, E, span), lambda h, s, t: (h, 0, 0)),
                pl.BlockSpec((1, 1, span), lambda h, s, t: (h, 0, 0)),
            ],
            out_specs=[pl.BlockSpec((1, 1, ROWS_OUT, span), lambda h, s, t: (0, h, 0, 0))] + send_specs,
        ),
        out_shape=[jax.ShapeDtypeStruct((1, heads, ROWS_OUT, span), BF)] + sends,
        compiler_params=params(),
        name="spread_heads",
    )(starts, place, grad, merged, lse)


def gather_kernel(heads, starts, place, first, *refs):
    seconds, (out, total) = refs[: BRANCHES - 1], refs[BRANCHES - 1 :]
    head = pl.program_id(0)
    total[...] = first[0, 0].astype(F32)
    for branch in range(1, BRANCHES):
        got = seconds[branch - 1]
        count = branch_shape(branch, heads)[1]
        start = starts[branch, head]
        lanes = aligned(start, count)
        value = got[0, 0].astype(F32)
        for copy in range(1, got.shape[0]):
            value += got[copy, 0].astype(F32)
        value = placed_part(value, count, start, place[0])[0]
        total[:, lanes] += value
    out[0] = (total[0:E, :] * E ** (-0.5)).astype(BF)
    out[1] = total[E : 2 * E, :].astype(BF)
    out[2] = total[2 * E :, :].astype(BF)


def gather_heads(heads, starts, place, first, seconds):
    span = first.shape[-1]
    return pl.pallas_call(
        partial(gather_kernel, heads),
        grid_spec=pltpu.PrefetchScalarGridSpec(
            num_scalar_prefetch=2,
            grid=(heads,),
            in_specs=[pl.BlockSpec((1, 1, 3 * E, span), lambda h, s, t: (0, h, 0, 0))]
            + send_shapes(heads, 3 * E)[1],
            out_specs=pl.BlockSpec((3, E, span), lambda h, s, t: (0, h, 0)),
            scratch_shapes=[pltpu.VMEM((3 * E, span), F32)],
        ),
        out_shape=jax.ShapeDtypeStruct((3, heads * E, span), BF),
        compiler_params=params(),
        name="gather_heads",
    )(starts, place, first, *seconds)


def rolled(value, step):
    size = lax.axis_size("head")
    return lax.ppermute(value, "head", [(s, (s + step) % size) for s in range(size)])


def all_rows(own):
    size = lax.axis_size("head")
    me = lax.axis_index("head")
    got = [own] + [rolled(own, step) for step in range(1, size)]
    if size == 2:
        return [jnp.where(me == 0, got[0], got[1]), jnp.where(me == 0, got[1], got[0])]
    stacked = jnp.stack(got)
    return [stacked[(me - place) % size] for place in range(size)]


def sum_rows(parts):
    size = lax.axis_size("head")
    me = lax.axis_index("head")
    total = lax.dynamic_index_in_dim(parts, me, 0, keepdims=False).astype(F32)
    for step in range(1, size):
        sent = lax.dynamic_index_in_dim(parts, (me + step) % size, 0, keepdims=False)
        total = total + rolled(sent, step).astype(F32)
    return total


def sum_seq(value):
    size = lax.axis_size("seq")
    got = lax.all_to_all(value.astype(BF), "seq", 0, 0, tiled=True)
    mine = got.reshape((size, value.shape[0] // size) + value.shape[1:]).astype(F32).sum(0)
    full = jnp.broadcast_to(mine.astype(BF)[None], (size,) + mine.shape)
    return lax.all_to_all(full, "seq", 0, 0, tiled=True).reshape(value.shape).astype(F32)


def local(
    tokens,
    documents,
    offsets,
    in_proj,
    out_proj,
    up_proj,
    down_proj,
    first_gain,
    first_shift,
    second_gain,
    second_shift,
    cotangent,
):
    head_count = lax.axis_size("head")
    seq_id = lax.axis_index("seq")
    row_count, width = tokens.shape
    seq_len = row_count * head_count
    heads = offsets.shape[1]
    per_slot = row_count // SLOTS
    gelu_exact = partial(jax.nn.gelu, approximate=False)

    ids = lax.broadcasted_iota(jnp.int32, (row_count, row_count), 0)
    slot = reversed_bits(ids // per_slot, 4)
    source = ids % per_slot * SLOTS + slot
    order = (source == lax.broadcasted_iota(jnp.int32, (row_count, row_count), 1)).astype(BF)

    def sorted_rows(values):
        return jnp.dot(order, values, preferred_element_type=F32)

    def shard_rows(own):
        parts = [part.reshape(SLOTS, per_slot, -1) for part in all_rows(own)]
        return jnp.stack(parts, axis=1).reshape(seq_len, -1)

    def device_parts(values):
        split = values.reshape(SLOTS, head_count, per_slot, -1)
        return jnp.moveaxis(split, 1, 0).reshape(head_count, row_count, -1)

    x_rows = sorted_rows(tokens)
    cot_low = sorted_rows(cotangent).astype(BF)
    normed_one = norm_rows(x_rows, first_gain, first_shift)
    gathered_one = shard_rows(normed_one.astype(BF))
    cot_all = shard_rows(cot_low)

    my_docs = lax.dynamic_slice_in_dim(documents, seq_id * seq_len, seq_len)
    my_docs = my_docs.reshape(head_count, per_slot, 2, 2, 2, 2).transpose(5, 4, 3, 2, 0, 1).reshape(seq_len)
    bit_ids = jnp.arange(BIT_ROWS, dtype=jnp.int32)[:, None]
    doc_bit = my_docs[None, :] // 2 ** (bit_ids % DOC_BITS) % 2
    bits = jnp.where(bit_ids < DOC_BITS, doc_bit, jnp.where(bit_ids < 2 * DOC_BITS, 1 - doc_bit, 0))
    bits = bits.astype(BF)
    starts = jnp.stack([reversed_bits(offsets[b], b) for b in range(BRANCHES)])

    scales = jnp.array([E ** (-0.5) * LOG2E, 1.0, 1.0], F32)[:, None, None]
    projected = jnp.einsum("td,jdc->jct", gathered_one, in_proj, preferred_element_type=F32)
    projected = (projected * scales).astype(BF)
    place = seq_id.astype(jnp.int32).reshape(1)
    own, *sends = pack_heads(heads, starts, place, projected, bits)
    first_out, units, outs = exchange_forward(heads, own, sends)
    mixed, merged, lse = merge_heads(heads, starts, place, first_out, outs)

    attn_part = jnp.einsum("ct,cd->td", mixed, out_proj, preferred_element_type=F32).astype(BF)
    hidden_one = x_rows + sum_rows(device_parts(attn_part))
    normed_two = norm_rows(hidden_one, second_gain, second_shift)
    gathered_two = shard_rows(normed_two.astype(BF))
    pre_act = jnp.dot(gathered_two, up_proj, preferred_element_type=F32)
    hidden, gelu_pull = jax.vjp(gelu_exact, pre_act)
    hidden = hidden.astype(BF)
    down_part = jnp.dot(hidden, down_proj, preferred_element_type=F32).astype(BF)
    block_rows = hidden_one + sum_rows(device_parts(down_part))
    block_out = jnp.dot(order.T, block_rows.astype(BF), preferred_element_type=F32).astype(BF)

    grad_down = jnp.einsum("tf,td->fd", hidden, cot_all, preferred_element_type=F32).astype(BF)
    grad_act = jnp.einsum("td,fd->tf", cot_all, down_proj, preferred_element_type=F32)
    grad_pre = gelu_pull(grad_act)[0].astype(BF)
    grad_up = jnp.einsum("td,tf->df", gathered_two, grad_pre, preferred_element_type=F32).astype(BF)
    norm_part = jnp.einsum("tf,df->td", grad_pre, up_proj, preferred_element_type=F32).astype(BF)
    grad_normed_two = sum_rows(device_parts(norm_part))
    pull_two = jax.vjp(norm_rows, hidden_one, second_gain, second_shift)[1]
    grad_ln_two, grad_gain_two, grad_shift_two = pull_two(grad_normed_two)
    grad_hidden_one = cot_low.astype(F32) + grad_ln_two
    grad_attn = shard_rows(grad_hidden_one.astype(BF))
    grad_out = jnp.einsum("ct,td->cd", mixed, grad_attn, preferred_element_type=F32).astype(BF)
    grad_merged = jnp.einsum("td,cd->ct", grad_attn, out_proj, preferred_element_type=F32)

    own_g, *sends_g = spread_heads(heads, starts, place, grad_merged, merged, lse)
    first_grad, grads = exchange_backward(heads, own, own_g, units, sends_g)
    grad_qkv = gather_heads(heads, starts, place, first_grad, grads)

    grad_in = jnp.einsum("td,jct->jdc", gathered_one, grad_qkv, preferred_element_type=F32)
    one_part = jnp.einsum("jct,jdc->td", grad_qkv, in_proj, preferred_element_type=F32).astype(BF)
    grad_normed_one = sum_rows(device_parts(one_part))
    pull_one = jax.vjp(norm_rows, x_rows, first_gain, first_shift)[1]
    grad_ln_one, grad_gain_one, grad_shift_one = pull_one(grad_normed_one)
    grad_tokens = jnp.dot(
        order.T.astype(F32),
        grad_hidden_one + grad_ln_one,
        precision=lax.Precision.HIGHEST,
        preferred_element_type=F32,
    )

    middle = lax.psum((grad_out, grad_up, grad_down), "seq")
    flat_in = grad_in.reshape(3 * width, heads * E)
    grad_in = sum_seq(flat_in).reshape(3, width, heads * E)
    gains = jnp.stack([grad_gain_one, grad_shift_one, grad_gain_two, grad_shift_two])
    gains = lax.psum(gains, ("seq", "head"))
    return (
        block_out,
        grad_tokens,
        grad_in,
        middle[0].astype(F32),
        middle[1].astype(F32),
        middle[2].astype(F32),
        gains[0],
        gains[1],
        gains[2],
        gains[3],
    )


def solution(mesh):
    placed = (
        P(("seq", "head"), None),
        P(),
        P(None, "head"),
        P(None, None, "head"),
        P("head", None),
        P(None, "head"),
        P("head", None),
        P(),
        P(),
        P(),
        P(),
        P(("seq", "head"), None),
    )
    return jax.shard_map(
        local,
        mesh=mesh,
        in_specs=placed,
        out_specs=(
            P(("seq", "head"), None),
            P(("seq", "head"), None),
            P(None, None, "head"),
            P("head", None),
            P(None, "head"),
            P("head", None),
            P(),
            P(),
            P(),
            P(),
        ),
        check_vma=False,
    )
```

```python
import math
from functools import partial

import jax
import jax.numpy as jnp
from jax import lax
from jax.experimental import pallas as pl
from jax.experimental.pallas import tpu as pltpu
from jax.sharding import PartitionSpec as P

E = 48
BRANCHES = 5
SEG0 = 1024
SLOTS = 16
BIT_ROWS = 16
DOC_BITS = 6
ROWS_IN = 3 * E + BIT_ROWS
ROWS_OUT = E + BIT_ROWS
EPS = 1e-05
FAR = 1e30
LOG2E = math.log2(math.e)
LN2 = math.log(2.0)
BF = jnp.bfloat16
F32 = jnp.float32
VMEM_LIMIT = 48 * 2**20


def params(**more):
    return pltpu.CompilerParams(vmem_limit_bytes=VMEM_LIMIT, **more)


def norm_rows(values, gain, shift):
    centre = jnp.mean(values, axis=-1, keepdims=True)
    centred = values - centre
    spread = jnp.mean(centred * centred, axis=-1, keepdims=True)
    return centred * lax.rsqrt(spread + EPS) * gain + shift


def reversed_bits(value, count):
    out = jnp.zeros_like(value)
    for bit in range(count):
        out = out * 2 + value // 2**bit % 2
    return out


def bit_reversed(value, count):
    return int(format(value, f"0{count}b")[::-1], 2)


def branch_shape(branch, heads):
    stride = 2**branch
    return (stride, SEG0 // stride, max(1, heads // stride), max(1, stride // heads))


def pieces_of(value):
    high = value.astype(BF).astype(F32)
    rest = value - high
    middle = rest.astype(BF).astype(F32)
    return high, middle, (rest - middle).astype(BF).astype(F32)


def row_block(placed, columns):
    ids = lax.broadcasted_iota(jnp.int32, (BIT_ROWS, columns), 0)
    block = jnp.zeros((BIT_ROWS, columns), F32)
    for row, value in placed.items():
        block = jnp.where(ids == row, value, block)
    return block


def lane_block(ref, rows, start, count):
    return ref[0, 0, rows, aligned(start, count)]


def aligned(start, count):
    if count >= 128:
        return pl.ds(pl.multiple_of(start * count, 128), count)
    return pl.ds(pl.multiple_of(start // (128 // count) * 128, 128), 128)


def moved_part(block, count, source, target):
    per = 128 // count
    lanes = lax.broadcasted_iota(jnp.int32, (1, 128), 1)
    out = block
    for shift in range(1, per):
        turned = jnp.concatenate([block[:, -shift * count :], block[:, : -shift * count]], axis=1)
        out = jnp.where((target - source) % per == shift, turned, out)
    return jnp.where(lanes // count == target, out, 0.0)


def pack_kernel(heads, starts, place, proj, bits, own, *sends):
    head = pl.program_id(0)
    for j in range(3):
        own[0, 0, j * E : (j + 1) * E, :] = proj[j]
    own[0, 0, 3 * E :, :] = bits[...]
    send_blocks(heads, head, starts, place, own, sends)


def send_blocks(heads, head, starts, place, own, sends):
    for branch in range(1, BRANCHES):
        count = branch_shape(branch, heads)[1]
        send = sends[branch - 1]
        start = starts[branch, head]
        block = lane_block(own, slice(None), start, count)
        if count < 128:
            per = 128 // count
            block = moved_part(block.astype(F32), count, start % per, place[0] % per).astype(BF)
        for copy in range(send.shape[0]):
            send[copy, 0] = block


def send_shapes(heads, rows):
    outs, specs = [], []
    for branch in range(1, BRANCHES):
        stride, count, per, split = branch_shape(branch, heads)
        count = max(count, 128)
        outs.append(jax.ShapeDtypeStruct((stride, per, rows, count), BF))
        specs.append(
            pl.BlockSpec((split, 1, rows, count), lambda h, s, t, per=per: (h // per, h % per, 0, 0))
        )
    return outs, specs


def pack_heads(heads, starts, place, proj, bits):
    span = proj.shape[-1]
    sends, send_specs = send_shapes(heads, ROWS_IN)
    return pl.pallas_call(
        partial(pack_kernel, heads),
        grid_spec=pltpu.PrefetchScalarGridSpec(
            num_scalar_prefetch=2,
            grid=(heads,),
            in_specs=[
                pl.BlockSpec((3, E, span), lambda h, s, t: (0, h, 0)),
                pl.BlockSpec((BIT_ROWS, span), lambda h, s, t: (0, 0)),
            ],
            out_specs=[pl.BlockSpec((1, 1, ROWS_IN, span), lambda h, s, t: (0, h, 0, 0))] + send_specs,
        ),
        out_shape=[jax.ShapeDtypeStruct((1, heads, ROWS_IN, span), BF)] + sends,
        compiler_params=params(),
        name="pack_heads",
    )(starts, place, proj, bits)


def load_unit(ref, unit, count, x):
    if ref.shape[0] == 1:
        x[...] = ref[0, unit]
        return
    width = ref.shape[-1]
    per = width // count
    for block in range(ref.shape[0] // per):
        value = ref[block * per, unit]
        for other in range(1, per):
            value = value + ref[block * per + other, unit]
        x[:, block * width : (block + 1) * width] = value


def store_unit(ref, unit, rows, value, column, count):
    width = ref.shape[-1]
    size = min(width, count)
    for start in range(column, column + count, size):
        lanes = slice(start % width, start % width + size)
        ref[start // width, unit, rows, lanes] = value[:, start - column : start - column + size]


def forward_unit(x, q_aug, base, queries, tile, put):
    if isinstance(base, int):
        lanes = slice(base, base + queries)
    else:
        lanes = pl.ds(pl.multiple_of(base, 128), queries)
    q_aug[0:E, :queries] = x[0:E, lanes]
    q_aug[E:, :queries] = (x[3 * E :, lanes].astype(F32) * -FAR).astype(BF)
    bits = x[3 * E :, :].astype(F32)
    k_rows = jnp.concatenate([x[E : 2 * E, :], (1.0 - bits).astype(BF)], axis=0).T
    v_aug = jnp.concatenate([x[2 * E : 3 * E, :], jnp.ones(bits.shape, BF)], axis=0)
    for step in range(queries // tile):
        column = step * tile
        s = jnp.dot(k_rows, q_aug[:, column : column + tile], preferred_element_type=F32)
        top = jnp.max(s, axis=0, keepdims=True)
        p = jnp.exp2(s - top).astype(BF)
        o = jnp.dot(v_aug, p, preferred_element_type=F32)
        total = o[E : E + 1]
        high, middle, low = pieces_of(top + jnp.log2(total))
        block = row_block({0: high, 1: middle, 2: low}, tile)
        put(column, jnp.concatenate([o[:E] * (1.0 / total), block], axis=0).astype(BF))


def group_place(branch):
    stride = 2**branch
    me = lax.axis_index("seq")
    return me // stride * stride, me % stride


def meet_axis():
    size = lax.axis_size("seq")
    me = lax.axis_index("seq")
    barrier = pltpu.get_barrier_semaphore()

    @pl.loop(1, size)
    def _(step):
        pl.semaphore_signal(
            barrier, inc=1, device_id={"seq": (me + step) % size}, device_id_type=pl.DeviceIdType.MESH
        )

    pl.semaphore_wait(barrier, size - 1)


class Reduction:
    STEPS = 7

    def __init__(self, order, parts, total, half, quarter, others, send, recv):
        self.parts, self.total = parts, total
        self.half, self.quarter, self.others = half, quarter, others
        self.send, self.recv = send, recv
        me = lax.axis_index("seq")
        self.rest = lax.axis_size("seq") // 4
        self.me = me
        bits = (me % 2, me // 2 % 2)
        self.bits = [bits[bit] for bit in order]
        self.partners = [me + (1 - 2 * bits[bit]) * 2**bit for bit in order]
        self.place = me // 4
        self.flying = []

    def copy(self, source, target, device, sem):
        made = pltpu.make_async_remote_copy(
            src_ref=source,
            dst_ref=target,
            send_sem=self.send.at[sem],
            recv_sem=self.recv.at[sem],
            device_id={"seq": device},
            device_id_type=pl.DeviceIdType.MESH,
        )
        made.start()

        def wait():
            made.wait()

        self.flying.append(wait)

    def land(self):
        for wait in self.flying:
            wait()
        self.flying = []

    def others_of(self):
        for step in range(1, self.rest):
            place = (self.place + step) % self.rest
            yield step, place, place * 4 + self.me % 4

    def step(self, number):
        one, two = self.bits
        rest = self.rest
        if number == 0:
            self.copy(self.parts.at[1 - one], self.half, self.partners[0], 0)
            return
        self.land()
        if number == 1:

            @pl.loop(0, 2 * rest)
            def _(i):
                j, z = i // rest, i % rest
                mine = self.parts[one, j, z].astype(F32)
                self.half[j, z] = (mine + self.half[j, z].astype(F32)).astype(BF)

            self.copy(self.half.at[1 - two], self.quarter, self.partners[1], 1)
        elif number == 2:

            @pl.loop(0, rest)
            def _(z):
                mine = self.half[two, z].astype(F32)
                self.quarter[z] = (mine + self.quarter[z].astype(F32)).astype(BF)

            for step, place, device in self.others_of():
                self.copy(self.quarter.at[place], self.others.at[step - 1], device, 1 + step)
        elif number == 3:
            mine = self.quarter[self.place].astype(F32)
            for step in range(1, rest):
                mine = mine + self.others[step - 1].astype(F32)
            self.total[one, two, self.place] = mine.astype(BF)
            block = self.total.at[one, two, self.place]
            for step, place, device in self.others_of():
                self.copy(block, block, device, rest + step)
        elif number == 4:
            block = self.total.at[one, two]
            self.copy(block, block, self.partners[1], 2 * rest)
        elif number == 5:
            block = self.total.at[one]
            self.copy(block, block, self.partners[0], 2 * rest + 1)

    @staticmethod
    def scratch(size, rows, columns):
        rest = size // 4
        count = 2 * rest + 2
        return [
            pltpu.VMEM((2, rest, rows, columns), BF),
            pltpu.VMEM((rest, rows, columns), BF),
            pltpu.VMEM((rest - 1, rows, columns), BF),
            pltpu.SemaphoreType.DMA((count,)),
            pltpu.SemaphoreType.DMA((count,)),
        ]


def reduction_parts(value, size):
    rows, columns = value.shape
    return value.reshape(2, 2, size // 4, rows // size, columns)


def reduction_whole(value):
    return value.reshape(-1, value.shape[-1])


def make_reductions(orders, parts, totals, scratch):
    out = []
    for order, one, total in zip(orders, parts, totals):
        out.append(Reduction(order, one, total, *scratch[:5]))
        scratch = scratch[5:]
    return out


def group_copies(branch, source, target, source_block, send_sems, recv_sems, local_sem):
    stride = 2**branch
    base, place = group_place(branch)
    first = stride - branch - 2
    copies = [
        pltpu.make_async_copy(source.at[source_block(place)], target.at[place], local_sem.at[branch - 1])
    ]
    for step in range(1, stride):
        member = (place + step) % stride
        copies.append(
            pltpu.make_async_remote_copy(
                src_ref=source.at[source_block(member)],
                dst_ref=target.at[place],
                send_sem=send_sems.at[first + step],
                recv_sem=recv_sems.at[first + step],
                device_id={"seq": base + member},
                device_id_type=pl.DeviceIdType.MESH,
            )
        )
    return copies


def exchange_forward_kernel(heads, own, *refs):
    count = BRANCHES - 1
    sends, refs = refs[:count], refs[count:]
    first, refs = refs[0], refs[1:]
    gots, refs = refs[:count], refs[count:]
    backs, refs = refs[:count], refs[count:]
    outs, refs = refs[:count], refs[count:]
    x, q_aug, in_send, in_recv, in_local, out_send, out_recv, out_local = refs
    tile = 256
    meet_axis()
    coming = {}
    for branch in range(1, BRANCHES):
        coming[branch] = group_copies(
            branch, sends[branch - 1], gots[branch - 1], lambda m: m, in_send, in_recv, in_local
        )
        for copy in coming[branch]:
            copy.start()

    @pl.loop(0, heads)
    def _(head):
        x[...] = own[0, head]

        def put(column, value):
            first[0, head, :, column : column + tile] = value

        forward_unit(x, q_aug, 0, SEG0, tile, put)

    leaving = []
    for branch in range(1, BRANCHES):
        stride, lanes, units, split = branch_shape(branch, heads)
        got, out = gots[branch - 1], outs[branch - 1]
        for copy in coming[branch]:
            copy.wait()
        queries = SEG0 // split
        base = 0 if split == 1 else lax.axis_index("seq") % split * queries

        @pl.loop(0, units)
        def _(unit):
            load_unit(got, unit, lanes, x)
            if split == 1:

                def put(column, value):
                    store_unit(out, unit, slice(None), value, column, value.shape[1])

            else:
                empty = row_block({0: -FAR}, 128)
                empty = jnp.concatenate([jnp.zeros((E, 128), F32), empty], axis=0).astype(BF)
                for block in range(SEG0 // 128):
                    store_unit(out, unit, slice(None), empty, block * 128, 128)

                def put(column, value):
                    width = out.shape[-1]
                    for start in range(0, value.shape[1], width):
                        block = (base + column + start) // width
                        out[block, unit] = value[:, start : start + width]

            forward_unit(x, q_aug, base, queries, min(tile, queries), put)

        per = out.shape[-1] // lanes
        copies = group_copies(
            branch, out, backs[branch - 1], lambda m: m // per, out_send, out_recv, out_local
        )
        for copy in copies:
            copy.start()
        leaving += copies
    for copy in leaving:
        copy.wait()


def exchange_scratch():
    copies = 2**BRANCHES - 2 - BRANCHES + 1
    one = [
        pltpu.SemaphoreType.DMA((copies,)),
        pltpu.SemaphoreType.DMA((copies,)),
        pltpu.SemaphoreType.DMA((BRANCHES - 1,)),
    ]
    return one + one


def unit_cost(units, dots):
    return pl.CostEstimate(
        flops=dots * 2 * units * SEG0 * SEG0 * 256,
        transcendentals=units * SEG0 * SEG0,
        bytes_accessed=units * SEG0 * 1000,
    )


def vmem_specs(count):
    return [pl.BlockSpec(memory_space=pltpu.VMEM)] * count


def out_blocks(heads, rows):
    shapes = []
    for branch in range(1, BRANCHES):
        stride, count, units, split = branch_shape(branch, heads)
        width = max(count, 128)
        shapes.append((SEG0 // width, units, rows, width))
    return shapes


def exchange_forward(heads, own, sends):
    backs = send_shapes(heads, ROWS_OUT)[0]
    gots = send_shapes(heads, ROWS_IN)[0]
    first = jax.ShapeDtypeStruct((1, heads, ROWS_OUT, SEG0), BF)
    results = pl.pallas_call(
        partial(exchange_forward_kernel, heads),
        in_specs=vmem_specs(1 + len(sends)),
        out_specs=vmem_specs(1 + len(gots) + len(backs)),
        out_shape=[first] + gots + backs,
        scratch_shapes=[pltpu.VMEM(shape, BF) for shape in out_blocks(heads, ROWS_OUT)]
        + [pltpu.VMEM((ROWS_IN, SEG0), BF), pltpu.VMEM((ROWS_OUT, SEG0), BF)]
        + exchange_scratch(),
        compiler_params=params(collective_id=0, has_side_effects=True),
        cost_estimate=unit_cost(2 * heads, 2),
        name="exchange_forward",
    )(own, *sends)
    return results[0], results[1 : 1 + len(gots)], results[1 + len(gots) :]


def backward_unit(x, g, q_aug, gk, gv, base, queries, tile, put):
    if isinstance(base, int):
        lanes = slice(base, base + queries)
    else:
        lanes = pl.ds(pl.multiple_of(base, 128), queries)
    extra = g[E:, lanes].astype(F32)
    ids = lax.broadcasted_iota(jnp.int32, extra.shape, 0)
    q = x[0:E, lanes]
    q_aug[0:E, :queries] = q
    q_aug[E:, :queries] = jnp.where(ids >= 12, extra, x[3 * E :, lanes].astype(F32) * -FAR).astype(BF)
    bits = x[3 * E :, :].astype(F32)
    k_aug = jnp.concatenate([x[E : 2 * E, :], (1.0 - bits).astype(BF)], axis=0)
    k_rows = k_aug.T
    v_ids = lax.broadcasted_iota(jnp.int32, bits.shape, 0)
    v_bits = jnp.where(v_ids < 3, 1.0, 0.0).astype(BF)
    v_rows = jnp.concatenate([x[2 * E : 3 * E, :], v_bits], axis=0).T
    q_rows = jnp.concatenate([q, jnp.zeros((BIT_ROWS, queries), BF)], axis=0).T
    g_all = g[:, lanes]
    g_rows = g_all.T
    for step in range(queries // tile):
        column = step * tile
        span = slice(column, column + tile)
        p = jnp.exp2(jnp.dot(k_rows, q_aug[:, span], preferred_element_type=F32))
        gs = p * jnp.dot(v_rows, g_all[:, span], preferred_element_type=F32)
        p, gs = p.astype(BF), gs.astype(BF)
        put(column, jnp.dot(k_aug, gs, preferred_element_type=F32)[:E].astype(BF))
        new_k = jnp.dot(gs, q_rows[span], preferred_element_type=F32)
        new_v = jnp.dot(p, g_rows[span], preferred_element_type=F32)
        if step == 0:
            gk[...] = new_k
            gv[...] = new_v
        else:
            gk[...] += new_k
            gv[...] += new_v
    return (gk[...].T[:E] * LN2).astype(BF), gv[...].T[:E].astype(BF)


def reduction_plan(streams, blocks):
    early = {
        0: [(s, 0) for s in range(streams)],
        6: [(1, 1)],
        7: [(0, 1)],
        9: [(1, 2), (0, 2)],
        10: [(3, 1)],
        11: [(2, 1), (4, 1), (1, 3), (0, 3)],
        13: [(3, 2), (1, 4), (0, 4)],
        14: [(2, 2), (4, 2)],
        15: [(3, 3), (1, 5), (0, 5)],
        16: [(2, 3), (4, 3)],
    }
    done = {s: 0 for s in range(streams)}
    plan = {}
    for block, events in early.items():
        for stream, step in events:
            if stream < streams:
                plan.setdefault(block * blocks // 16, []).append((stream, step))
                done[stream] = step + 1
    last = []
    for step in range(Reduction.STEPS):
        last += [(s, step) for s in (1, 0, 3, 2, 4) if s < streams and step >= done[s]]
    return plan, last


def stream_orders(count):
    return [((0, 1), (1, 0))[s % 2] for s in range(count)]


def exchange_backward_kernel(heads, streams, own, own_g, *refs):
    count = BRANCHES - 1
    units_in, refs = refs[:count], refs[count:]
    sends, refs = refs[:count], refs[count:]
    parts, refs = refs[:streams], refs[streams:]
    first, refs = refs[0], refs[1:]
    backs, refs = refs[:count], refs[count:]
    totals, refs = refs[:streams], refs[streams:]
    gots, refs = refs[:count], refs[count:]
    outs, refs = refs[:count], refs[count:]
    x, g, q_aug, gk, gv, in_send, in_recv, in_local, out_send, out_recv, out_local = refs[:11]
    reductions = make_reductions(stream_orders(streams), parts, totals, refs[11:])
    shapes = [branch_shape(b, heads) for b in range(BRANCHES)]
    blocks = heads + sum(shape[2] for shape in shapes[1:])
    plan, last = reduction_plan(streams, blocks)
    tile = 256
    meet_axis()
    coming = {}
    for branch in range(1, BRANCHES):
        coming[branch] = group_copies(
            branch, sends[branch - 1], gots[branch - 1], lambda m: m, in_send, in_recv, in_local
        )
        for copy in coming[branch]:
            copy.start()

    def events(block):
        for stream, step in plan.get(block, []):
            reductions[stream].step(step)

    def run_blocks(done, low, high, body):
        size = high - low
        marks = [i for i in range(1, size) if plan.get(done + i)]
        edges = [0] + marks + [size]
        for at, to in zip(edges, edges[1:]):
            events(done + at)
            if to - at == 1:
                body(low + at)
            else:
                pl.loop(low + at, low + to)(body)
        return done + size

    def own_head(head):
        x[...] = own[0, head]
        g[...] = own_g[0, head]

        def put(column, value):
            first[0, head, :E, column : column + tile] = value

        k_cols, v_cols = backward_unit(x, g, q_aug, gk, gv, 0, SEG0, tile, put)
        first[0, head, E : 2 * E, :] = k_cols
        first[0, head, 2 * E :, :] = v_cols

    done = run_blocks(0, 0, heads // 2, own_head)
    leaving = []
    for branch in range(1, BRANCHES):
        stride, lanes, units, split = shapes[branch]
        got, out, unit_in = gots[branch - 1], outs[branch - 1], units_in[branch - 1]
        for copy in coming[branch]:
            copy.wait()
        queries = SEG0 // split
        base = 0 if split == 1 else lax.axis_index("seq") % split * queries

        def other_head(unit):
            load_unit(unit_in, unit, lanes, x)
            load_unit(got, unit, lanes, g)
            if split == 1:

                def put(column, value):
                    store_unit(out, unit, slice(0, E), value, column, value.shape[1])

            else:
                empty = jnp.zeros((E, 128), BF)
                for block in range(SEG0 // 128):
                    store_unit(out, unit, slice(0, E), empty, block * 128, 128)

                def put(column, value):
                    width = out.shape[-1]
                    for start in range(0, value.shape[1], width):
                        block = (base + column + start) // width
                        out[block, unit, :E, :] = value[:, start : start + width]

            k_cols, v_cols = backward_unit(x, g, q_aug, gk, gv, base, queries, min(tile, queries), put)
            store_unit(out, unit, slice(E, 2 * E), k_cols, 0, SEG0)
            store_unit(out, unit, slice(2 * E, 3 * E), v_cols, 0, SEG0)

        done = run_blocks(done, 0, units, other_head)
        per = out.shape[-1] // lanes
        copies = group_copies(
            branch, out, backs[branch - 1], lambda m: m // per, out_send, out_recv, out_local
        )
        for copy in copies:
            copy.start()
        leaving += copies
    done = run_blocks(done, heads // 2, heads, own_head)
    events(done)
    for copy in leaving:
        copy.wait()
    for stream, step in last:
        reductions[stream].step(step)


def exchange_backward(heads, own, own_g, units, sends, terms):
    size = lax.axis_size("seq")
    backs = send_shapes(heads, 3 * E)[0]
    first = jax.ShapeDtypeStruct((1, heads, 3 * E, SEG0), BF)
    parts = [reduction_parts(term, size) for term in terms]
    scratch = []
    for part in parts:
        scratch += Reduction.scratch(size, *part.shape[-2:])
    results = pl.pallas_call(
        partial(exchange_backward_kernel, heads, len(parts)),
        in_specs=vmem_specs(2 + len(units) + len(sends) + len(parts)),
        out_specs=vmem_specs(1 + len(backs) + len(parts)),
        out_shape=[first] + backs + [jax.ShapeDtypeStruct(part.shape, BF) for part in parts],
        scratch_shapes=[pltpu.VMEM(shape.shape, BF) for shape in send_shapes(heads, ROWS_OUT)[0]]
        + [pltpu.VMEM(shape, BF) for shape in out_blocks(heads, 3 * E)]
        + [
            pltpu.VMEM((ROWS_IN, SEG0), BF),
            pltpu.VMEM((ROWS_OUT, SEG0), BF),
            pltpu.VMEM((ROWS_OUT, SEG0), BF),
            pltpu.VMEM((SEG0, ROWS_OUT), F32),
            pltpu.VMEM((SEG0, ROWS_OUT), F32),
        ]
        + exchange_scratch()
        + scratch,
        compiler_params=params(collective_id=1, has_side_effects=True),
        cost_estimate=unit_cost(2 * heads, 5),
        name="exchange_backward",
    )(own, own_g, *units, *sends, *parts)
    sums = [reduction_whole(total) for total in results[1 + len(backs) :]]
    return results[0], results[1 : 1 + len(backs)], sums


def last_sums_kernel(streams, gains, *refs):
    parts, refs = refs[:streams], refs[streams:]
    gains_out, refs = refs[0], refs[1:]
    totals, refs = refs[:streams], refs[streams:]
    one, two, others, send, recv = refs[:5]
    reductions = make_reductions(stream_orders(streams), parts, totals, refs[5:])
    me = lax.axis_index("seq")
    rest = lax.axis_size("seq") // 4
    place = me // 4

    def copy(source, target, device, sem):
        return pltpu.make_async_remote_copy(
            src_ref=source,
            dst_ref=target,
            send_sem=send.at[sem],
            recv_sem=recv.at[sem],
            device_id={"seq": device},
            device_id_type=pl.DeviceIdType.MESH,
        )

    meet_axis()
    for reduction in reductions:
        reduction.step(0)
    swap = copy(gains, one, me + 1 - 2 * (me % 2), 0)
    swap.start()
    swap.wait()
    one[...] += gains[...]
    for reduction in reductions:
        reduction.step(1)
    swap = copy(one, two, me + 2 - 4 * (me // 2 % 2), 1)
    swap.start()
    swap.wait()
    two[...] += one[...]
    for reduction in reductions:
        reduction.step(2)
    others[place] = two[...]
    swaps = []
    for step in range(1, rest):
        device = (place + step) % rest * 4 + me % 4
        swaps.append(copy(two, others.at[place], device, 1 + step))
        swaps[-1].start()
    for swap in swaps:
        swap.wait()
    total = others[0]
    for z in range(1, rest):
        total = total + others[z]
    gains_out[...] = total
    for number in range(3, Reduction.STEPS):
        for reduction in reductions:
            reduction.step(number)


def last_sums(gains, terms):
    size = lax.axis_size("seq")
    parts = [reduction_parts(term, size) for term in terms]
    scratch = []
    for part in parts:
        scratch += Reduction.scratch(size, *part.shape[-2:])
    results = pl.pallas_call(
        partial(last_sums_kernel, len(parts)),
        in_specs=vmem_specs(1 + len(parts)),
        out_specs=vmem_specs(1 + len(parts)),
        out_shape=[jax.ShapeDtypeStruct(gains.shape, F32)]
        + [jax.ShapeDtypeStruct(part.shape, BF) for part in parts],
        scratch_shapes=[
            pltpu.VMEM(gains.shape, F32),
            pltpu.VMEM(gains.shape, F32),
            pltpu.VMEM((size // 4,) + gains.shape, F32),
            pltpu.SemaphoreType.DMA((size // 4 + 1,)),
            pltpu.SemaphoreType.DMA((size // 4 + 1,)),
        ]
        + scratch,
        compiler_params=params(collective_id=2, has_side_effects=True),
        name="last_sums",
    )(gains, *parts)
    return results[0], [reduction_whole(total) for total in results[1:]]


def placed_part(value, count, start, place):
    if count >= 128:
        return value, None
    per = 128 // count
    lanes = lax.broadcasted_iota(jnp.int32, (1, 128), 1)
    return moved_part(value, count, place % per, start % per), lanes // count == start % per


def merge_kernel(heads, starts, place, first, *refs):
    seconds, (mixed, merged, lse) = refs[: BRANCHES - 1], refs[BRANCHES - 1 :]
    head = pl.program_id(0)
    extra = first[0, 0, E:, :].astype(F32)
    merged[0] = first[0, 0, :E, :].astype(F32)
    lse[0] = extra[0:1] + extra[1:2] + extra[2:3]
    for branch in range(1, BRANCHES):
        got = seconds[branch - 1]
        count = branch_shape(branch, heads)[1]
        start = starts[branch, head]
        lanes = aligned(start, count)
        for copy in range(got.shape[0]):
            value, mask = placed_part(got[copy, 0].astype(F32), count, start, place[0])
            new_lse = value[E : E + 1] + value[E + 1 : E + 2] + value[E + 2 : E + 3]
            if mask is not None:
                new_lse = jnp.where(mask, new_lse, -FAR)
            old_lse = lse[0, :, lanes]
            top = jnp.maximum(old_lse, new_lse)
            both = top + jnp.log2(jnp.exp2(old_lse - top) + jnp.exp2(new_lse - top))
            old_w = jnp.exp2(old_lse - both)
            new_w = jnp.exp2(new_lse - both)
            merged[0, :, lanes] = merged[0, :, lanes] * old_w + value[:E] * new_w
            lse[0, :, lanes] = both
    mixed[...] = merged[0].astype(BF)


def merge_heads(heads, starts, place, first, seconds):
    span = first.shape[-1]
    return pl.pallas_call(
        partial(merge_kernel, heads),
        grid_spec=pltpu.PrefetchScalarGridSpec(
            num_scalar_prefetch=2,
            grid=(heads,),
            in_specs=[pl.BlockSpec((1, 1, ROWS_OUT, span), lambda h, s, t: (0, h, 0, 0))]
            + send_shapes(heads, ROWS_OUT)[1],
            out_specs=[
                pl.BlockSpec((E, span), lambda h, s, t: (h, 0)),
                pl.BlockSpec((1, E, span), lambda h, s, t: (h, 0, 0)),
                pl.BlockSpec((1, 1, span), lambda h, s, t: (h, 0, 0)),
            ],
        ),
        out_shape=[
            jax.ShapeDtypeStruct((heads * E, span), BF),
            jax.ShapeDtypeStruct((heads, E, span), F32),
            jax.ShapeDtypeStruct((heads, 1, span), F32),
        ],
        compiler_params=params(),
        name="merge_heads",
    )(starts, place, first, *seconds)


def spread_kernel(heads, starts, place, grad, merged, lse, own, *sends):
    head = pl.program_id(0)
    low = grad[...].astype(BF)
    dots = jnp.sum(low.astype(F32) * merged[0], axis=0, keepdims=True)
    own[0, 0, :E, :] = low
    d = pieces_of(-dots)
    m = pieces_of(-lse[0])
    placed = {0: d[0], 1: d[1], 2: d[2], 12: m[0], 13: m[1], 14: m[2]}
    own[0, 0, E:, :] = row_block(placed, grad.shape[-1]).astype(BF)
    send_blocks(heads, head, starts, place, own, sends)


def spread_heads(heads, starts, place, grad, merged, lse):
    span = grad.shape[-1]
    sends, send_specs = send_shapes(heads, ROWS_OUT)
    return pl.pallas_call(
        partial(spread_kernel, heads),
        grid_spec=pltpu.PrefetchScalarGridSpec(
            num_scalar_prefetch=2,
            grid=(heads,),
            in_specs=[
                pl.BlockSpec((E, span), lambda h, s, t: (h, 0)),
                pl.BlockSpec((1, E, span), lambda h, s, t: (h, 0, 0)),
                pl.BlockSpec((1, 1, span), lambda h, s, t: (h, 0, 0)),
            ],
            out_specs=[pl.BlockSpec((1, 1, ROWS_OUT, span), lambda h, s, t: (0, h, 0, 0))] + send_specs,
        ),
        out_shape=[jax.ShapeDtypeStruct((1, heads, ROWS_OUT, span), BF)] + sends,
        compiler_params=params(),
        name="spread_heads",
    )(starts, place, grad, merged, lse)


def gather_kernel(heads, starts, place, first, *refs):
    seconds, (out, total) = refs[: BRANCHES - 1], refs[BRANCHES - 1 :]
    head = pl.program_id(0)
    total[...] = first[0, 0].astype(F32)
    for branch in range(1, BRANCHES):
        got = seconds[branch - 1]
        count = branch_shape(branch, heads)[1]
        start = starts[branch, head]
        lanes = aligned(start, count)
        value = got[0, 0].astype(F32)
        for copy in range(1, got.shape[0]):
            value += got[copy, 0].astype(F32)
        value = placed_part(value, count, start, place[0])[0]
        total[:, lanes] += value
    out[0] = (total[0:E, :] * E ** (-0.5)).astype(BF)
    out[1] = total[E : 2 * E, :].astype(BF)
    out[2] = total[2 * E :, :].astype(BF)


def gather_heads(heads, starts, place, first, seconds):
    span = first.shape[-1]
    return pl.pallas_call(
        partial(gather_kernel, heads),
        grid_spec=pltpu.PrefetchScalarGridSpec(
            num_scalar_prefetch=2,
            grid=(heads,),
            in_specs=[pl.BlockSpec((1, 1, 3 * E, span), lambda h, s, t: (0, h, 0, 0))]
            + send_shapes(heads, 3 * E)[1],
            out_specs=pl.BlockSpec((3, E, span), lambda h, s, t: (0, h, 0)),
            scratch_shapes=[pltpu.VMEM((3 * E, span), F32)],
        ),
        out_shape=jax.ShapeDtypeStruct((3, heads * E, span), BF),
        compiler_params=params(),
        name="gather_heads",
    )(starts, place, first, *seconds)


def rolled(value, step):
    size = lax.axis_size("head")
    return lax.ppermute(value, "head", [(s, (s + step) % size) for s in range(size)])


def all_rows(own):
    size = lax.axis_size("head")
    me = lax.axis_index("head")
    got = [own] + [rolled(own, step) for step in range(1, size)]
    if size == 2:
        return [jnp.where(me == 0, got[0], got[1]), jnp.where(me == 0, got[1], got[0])]
    stacked = jnp.stack(got)
    return [stacked[(me - place) % size] for place in range(size)]


def sum_rows(parts):
    size = lax.axis_size("head")
    me = lax.axis_index("head")
    total = lax.dynamic_index_in_dim(parts, me, 0, keepdims=False).astype(F32)
    for step in range(1, size):
        sent = lax.dynamic_index_in_dim(parts, (me + step) % size, 0, keepdims=False)
        total = total + rolled(sent, step).astype(F32)
    return total


def local(
    tokens,
    documents,
    offsets,
    in_proj,
    out_proj,
    up_proj,
    down_proj,
    first_gain,
    first_shift,
    second_gain,
    second_shift,
    cotangent,
):
    head_count = lax.axis_size("head")
    seq_id = lax.axis_index("seq")
    row_count, width = tokens.shape
    seq_len = row_count * head_count
    heads = offsets.shape[1]
    per_slot = row_count // SLOTS
    gelu_exact = partial(jax.nn.gelu, approximate=False)

    ids = lax.broadcasted_iota(jnp.int32, (row_count, row_count), 0)
    slot = reversed_bits(ids // per_slot, 4)
    source = ids % per_slot * SLOTS + slot
    order = (source == lax.broadcasted_iota(jnp.int32, (row_count, row_count), 1)).astype(BF)

    def sorted_rows(values):
        return jnp.dot(order, values, preferred_element_type=F32)

    def shard_rows(own):
        parts = [part.reshape(SLOTS, per_slot, -1) for part in all_rows(own)]
        return jnp.stack(parts, axis=1).reshape(seq_len, -1)

    def device_parts(values):
        split = values.reshape(SLOTS, head_count, per_slot, -1)
        return jnp.moveaxis(split, 1, 0).reshape(head_count, row_count, -1)

    x_rows = sorted_rows(tokens)
    cot_low = sorted_rows(cotangent).astype(BF)
    normed_one = norm_rows(x_rows, first_gain, first_shift)
    gathered_one = shard_rows(normed_one.astype(BF))
    cot_all = shard_rows(cot_low)

    my_docs = lax.dynamic_slice_in_dim(documents, seq_id * seq_len, seq_len)
    my_docs = my_docs.reshape(head_count, per_slot, 2, 2, 2, 2).transpose(5, 4, 3, 2, 0, 1).reshape(seq_len)
    bit_ids = jnp.arange(BIT_ROWS, dtype=jnp.int32)[:, None]
    doc_bit = my_docs[None, :] // 2 ** (bit_ids % DOC_BITS) % 2
    bits = jnp.where(bit_ids < DOC_BITS, doc_bit, jnp.where(bit_ids < 2 * DOC_BITS, 1 - doc_bit, 0))
    bits = bits.astype(BF)
    starts = jnp.stack([reversed_bits(offsets[b], b) for b in range(BRANCHES)])

    scales = jnp.array([E ** (-0.5) * LOG2E, 1.0, 1.0], F32)[:, None, None]
    projected = jnp.einsum("td,jdc->jct", gathered_one, in_proj, preferred_element_type=F32)
    projected = (projected * scales).astype(BF)
    place = seq_id.astype(jnp.int32).reshape(1)
    own, *sends = pack_heads(heads, starts, place, projected, bits)
    first_out, units, outs = exchange_forward(heads, own, sends)
    mixed, merged, lse = merge_heads(heads, starts, place, first_out, outs)

    attn_part = jnp.einsum("ct,cd->td", mixed, out_proj, preferred_element_type=F32).astype(BF)
    hidden_one = x_rows + sum_rows(device_parts(attn_part))
    normed_two = norm_rows(hidden_one, second_gain, second_shift)
    gathered_two = shard_rows(normed_two.astype(BF))
    pre_act = jnp.dot(gathered_two, up_proj, preferred_element_type=F32)
    hidden, gelu_pull = jax.vjp(gelu_exact, pre_act)
    hidden = hidden.astype(BF)
    down_part = jnp.dot(hidden, down_proj, preferred_element_type=F32).astype(BF)
    block_rows = hidden_one + sum_rows(device_parts(down_part))
    block_out = jnp.dot(order.T, block_rows.astype(BF), preferred_element_type=F32).astype(BF)

    chunks = max(1, up_proj.shape[1] // width)

    def columns(values):
        return jnp.split(values, chunks, axis=1)

    grad_down = [
        jnp.einsum("tf,td->fd", part, cot_all, preferred_element_type=F32).astype(BF) for part in columns(hidden)
    ]
    grad_act = jnp.einsum("td,fd->tf", cot_all, down_proj, preferred_element_type=F32)
    grad_pre = gelu_pull(grad_act)[0].astype(BF)
    grad_up = [
        jnp.einsum("td,tf->df", gathered_two, part, preferred_element_type=F32).astype(BF)
        for part in columns(grad_pre)
    ]
    norm_part = jnp.einsum("tf,df->td", grad_pre, up_proj, preferred_element_type=F32).astype(BF)
    grad_normed_two = sum_rows(device_parts(norm_part))
    pull_two = jax.vjp(norm_rows, hidden_one, second_gain, second_shift)[1]
    grad_ln_two, grad_gain_two, grad_shift_two = pull_two(grad_normed_two)
    grad_hidden_one = cot_low.astype(F32) + grad_ln_two
    grad_attn = shard_rows(grad_hidden_one.astype(BF))
    grad_out = jnp.einsum("ct,td->cd", mixed, grad_attn, preferred_element_type=F32).astype(BF)
    grad_merged = jnp.einsum("td,cd->ct", grad_attn, out_proj, preferred_element_type=F32)

    own_g, *sends_g = spread_heads(heads, starts, place, grad_merged, merged, lse)
    terms = [term for pair in zip(grad_up, grad_down) for term in pair] + [grad_out]
    first_grad, grads, sums = exchange_backward(heads, own, own_g, units, sends_g, terms)
    grad_qkv = gather_heads(heads, starts, place, first_grad, grads)

    grad_in = jnp.einsum("td,jct->jdc", gathered_one, grad_qkv, preferred_element_type=F32)
    one_part = jnp.einsum("jct,jdc->td", grad_qkv, in_proj, preferred_element_type=F32).astype(BF)
    grad_normed_one = sum_rows(device_parts(one_part))
    pull_one = jax.vjp(norm_rows, x_rows, first_gain, first_shift)[1]
    grad_ln_one, grad_gain_one, grad_shift_one = pull_one(grad_normed_one)
    grad_tokens = jnp.dot(
        order.T.astype(F32),
        grad_hidden_one + grad_ln_one,
        precision=lax.Precision.HIGHEST,
        preferred_element_type=F32,
    )

    gains = jnp.stack([grad_gain_one, grad_shift_one, grad_gain_two, grad_shift_two])
    gains = jnp.concatenate([gains, jnp.zeros_like(gains)])
    gains = sum(all_rows(gains))
    gains, grad_in = last_sums(gains, [grad_in[j].astype(BF) for j in range(3)])
    return (
        block_out,
        grad_tokens,
        jnp.stack(grad_in).astype(F32),
        sums[-1].astype(F32),
        jnp.concatenate(sums[:-1:2], axis=1).astype(F32),
        jnp.concatenate(sums[1:-1:2], axis=0).astype(F32),
        gains[0],
        gains[1],
        gains[2],
        gains[3],
    )


def solution(mesh):
    placed = (
        P(("seq", "head"), None),
        P(),
        P(None, "head"),
        P(None, None, "head"),
        P("head", None),
        P(None, "head"),
        P("head", None),
        P(),
        P(),
        P(),
        P(),
        P(("seq", "head"), None),
    )
    return jax.shard_map(
        local,
        mesh=mesh,
        in_specs=placed,
        out_specs=(
            P(("seq", "head"), None),
            P(("seq", "head"), None),
            P(None, None, "head"),
            P("head", None),
            P(None, "head"),
            P("head", None),
            P(),
            P(),
            P(),
            P(),
        ),
        check_vma=False,
    )
```

```python
import math
from functools import partial

import jax
import jax.numpy as jnp
from jax import lax
from jax.experimental import pallas as pl
from jax.experimental.pallas import tpu as pltpu
from jax.sharding import PartitionSpec as P

E = 48
BRANCHES = 5
SEG0 = 1024
SLOTS = 16
BIT_ROWS = 16
DOC_BITS = 6
ROWS_IN = 3 * E + BIT_ROWS
ROWS_OUT = E + BIT_ROWS
EPS = 1e-05
FAR = 1e30
LOG2E = math.log2(math.e)
LN2 = math.log(2.0)
BF = jnp.bfloat16
F32 = jnp.float32
VMEM_LIMIT = 48 * 2**20


def params(**more):
    return pltpu.CompilerParams(vmem_limit_bytes=VMEM_LIMIT, **more)


def norm_rows(values, gain, shift):
    centre = jnp.mean(values, axis=-1, keepdims=True)
    centred = values - centre
    spread = jnp.mean(centred * centred, axis=-1, keepdims=True)
    return centred * lax.rsqrt(spread + EPS) * gain + shift


def reversed_bits(value, count):
    out = jnp.zeros_like(value)
    for bit in range(count):
        out = out * 2 + value // 2**bit % 2
    return out


def bit_reversed(value, count):
    return int(format(value, f"0{count}b")[::-1], 2)


def branch_shape(branch, heads):
    stride = 2**branch
    return (stride, SEG0 // stride, max(1, heads // stride), max(1, stride // heads))


def pieces_of(value):
    high = value.astype(BF).astype(F32)
    rest = value - high
    middle = rest.astype(BF).astype(F32)
    return high, middle, (rest - middle).astype(BF).astype(F32)


def row_block(placed, columns):
    ids = lax.broadcasted_iota(jnp.int32, (BIT_ROWS, columns), 0)
    block = jnp.zeros((BIT_ROWS, columns), F32)
    for row, value in placed.items():
        block = jnp.where(ids == row, value, block)
    return block


def lane_block(ref, rows, start, count):
    return ref[0, 0, rows, aligned(start, count)]


def aligned(start, count):
    if count >= 128:
        return pl.ds(pl.multiple_of(start * count, 128), count)
    return pl.ds(pl.multiple_of(start // (128 // count) * 128, 128), 128)


def moved_part(block, count, source, target):
    per = 128 // count
    lanes = lax.broadcasted_iota(jnp.int32, (1, 128), 1)
    out = block
    for shift in range(1, per):
        turned = jnp.concatenate([block[:, -shift * count :], block[:, : -shift * count]], axis=1)
        out = jnp.where((target - source) % per == shift, turned, out)
    return jnp.where(lanes // count == target, out, 0.0)


def pack_kernel(heads, starts, place, proj, bits, own, *sends):
    head = pl.program_id(0)
    for j in range(3):
        own[0, 0, j * E : (j + 1) * E, :] = proj[j]
    own[0, 0, 3 * E :, :] = bits[...]
    send_blocks(heads, head, starts, place, own, sends)


def send_blocks(heads, head, starts, place, own, sends):
    for branch in range(1, BRANCHES):
        count = branch_shape(branch, heads)[1]
        send = sends[branch - 1]
        start = starts[branch, head]
        block = lane_block(own, slice(None), start, count)
        if count < 128:
            per = 128 // count
            block = moved_part(block.astype(F32), count, start % per, place[0] % per).astype(BF)
        for copy in range(send.shape[0]):
            send[copy, 0] = block


def send_shapes(heads, rows):
    outs, specs = [], []
    for branch in range(1, BRANCHES):
        stride, count, per, split = branch_shape(branch, heads)
        count = max(count, 128)
        outs.append(jax.ShapeDtypeStruct((stride, per, rows, count), BF))
        specs.append(
            pl.BlockSpec((split, 1, rows, count), lambda h, s, t, per=per: (h // per, h % per, 0, 0))
        )
    return outs, specs


def pack_heads(heads, starts, place, proj, bits):
    span = proj.shape[-1]
    sends, send_specs = send_shapes(heads, ROWS_IN)
    return pl.pallas_call(
        partial(pack_kernel, heads),
        grid_spec=pltpu.PrefetchScalarGridSpec(
            num_scalar_prefetch=2,
            grid=(heads,),
            in_specs=[
                pl.BlockSpec((3, E, span), lambda h, s, t: (0, h, 0)),
                pl.BlockSpec((BIT_ROWS, span), lambda h, s, t: (0, 0)),
            ],
            out_specs=[pl.BlockSpec((1, 1, ROWS_IN, span), lambda h, s, t: (0, h, 0, 0))] + send_specs,
        ),
        out_shape=[jax.ShapeDtypeStruct((1, heads, ROWS_IN, span), BF)] + sends,
        compiler_params=params(),
        name="pack_heads",
    )(starts, place, proj, bits)


def load_unit(ref, unit, count, x):
    if ref.shape[0] == 1:
        x[...] = ref[0, unit]
        return
    width = ref.shape[-1]
    per = width // count
    for block in range(ref.shape[0] // per):
        value = ref[block * per, unit]
        for other in range(1, per):
            value = value + ref[block * per + other, unit]
        x[:, block * width : (block + 1) * width] = value


def store_unit(ref, unit, rows, value, column, count):
    width = ref.shape[-1]
    size = min(width, count)
    for start in range(column, column + count, size):
        lanes = slice(start % width, start % width + size)
        ref[start // width, unit, rows, lanes] = value[:, start - column : start - column + size]


def forward_unit(x, q_aug, base, queries, tile, put):
    if isinstance(base, int):
        lanes = slice(base, base + queries)
    else:
        lanes = pl.ds(pl.multiple_of(base, 128), queries)
    q_aug[0:E, :queries] = x[0:E, lanes]
    q_aug[E:, :queries] = (x[3 * E :, lanes].astype(F32) * -FAR).astype(BF)
    bits = x[3 * E :, :].astype(F32)
    k_rows = jnp.concatenate([x[E : 2 * E, :], (1.0 - bits).astype(BF)], axis=0).T
    v_aug = jnp.concatenate([x[2 * E : 3 * E, :], jnp.ones(bits.shape, BF)], axis=0)
    for step in range(queries // tile):
        column = step * tile
        s = jnp.dot(k_rows, q_aug[:, column : column + tile], preferred_element_type=F32)
        top = jnp.max(s, axis=0, keepdims=True)
        p = jnp.exp2(s - top).astype(BF)
        o = jnp.dot(v_aug, p, preferred_element_type=F32)
        total = o[E : E + 1]
        high, middle, low = pieces_of(top + jnp.log2(total))
        block = row_block({0: high, 1: middle, 2: low}, tile)
        put(column, jnp.concatenate([o[:E] * (1.0 / total), block], axis=0).astype(BF))


def group_place(branch):
    stride = 2**branch
    me = lax.axis_index("seq")
    return me // stride * stride, me % stride


def meet(*axes):
    barrier = pltpu.get_barrier_semaphore()
    count = 0
    for axis in axes:
        size = lax.axis_size(axis)
        me = lax.axis_index(axis)

        @pl.loop(1, size)
        def _(step):
            pl.semaphore_signal(
                barrier, inc=1, device_id={axis: (me + step) % size}, device_id_type=pl.DeviceIdType.MESH
            )

        count += size - 1
    pl.semaphore_wait(barrier, count)


class Reduction:
    STEPS = 7

    def __init__(self, order, total, half, quarter, others, send, recv):
        self.total = total
        self.half, self.quarter, self.others = half, quarter, others
        self.send, self.recv = send, recv
        me = lax.axis_index("seq")
        self.rest = lax.axis_size("seq") // 4
        self.me = me
        bits = (me % 2, me // 2 % 2)
        self.bits = [bits[bit] for bit in order]
        self.partners = [me + (1 - 2 * bits[bit]) * 2**bit for bit in order]
        self.place = me // 4

    def copy(self, source, target, device, sem):
        return pltpu.make_async_remote_copy(
            src_ref=source,
            dst_ref=target,
            send_sem=self.send.at[sem],
            recv_sem=self.recv.at[sem],
            device_id={"seq": device},
            device_id_type=pl.DeviceIdType.MESH,
        )

    def copies(self, number):
        one, two = self.bits
        rest = self.rest
        others = []
        for step in range(1, rest):
            place = (self.place + step) % rest
            others.append((step, place, place * 4 + self.me % 4))
        if number == 0:
            return [self.copy(self.total.at[1 - one], self.half, self.partners[0], 0)]
        if number == 1:
            return [self.copy(self.half.at[1 - two], self.quarter, self.partners[1], 1)]
        if number == 2:
            return [
                self.copy(self.quarter.at[place], self.others.at[step - 1], device, 1 + step)
                for step, place, device in others
            ]
        if number == 3:
            block = self.total.at[one, two, self.place]
            return [self.copy(block, block, device, rest + step) for step, place, device in others]
        if number == 4:
            block = self.total.at[one, two]
            return [self.copy(block, block, self.partners[1], 2 * rest)]
        if number == 5:
            block = self.total.at[one]
            return [self.copy(block, block, self.partners[0], 2 * rest + 1)]
        return []

    def step(self, number):
        one, two = self.bits
        rest = self.rest
        if number > 0:
            for copy in self.copies(number - 1):
                copy.wait()
        if number == 1:

            @pl.loop(0, 2 * rest)
            def _(i):
                j, z = i // rest, i % rest
                mine = self.total[one, j, z].astype(F32)
                self.half[j, z] = (mine + self.half[j, z].astype(F32)).astype(BF)

        elif number == 2:

            @pl.loop(0, rest)
            def _(z):
                mine = self.half[two, z].astype(F32)
                self.quarter[z] = (mine + self.quarter[z].astype(F32)).astype(BF)

        elif number == 3:
            mine = self.quarter[self.place].astype(F32)
            for step in range(1, rest):
                mine = mine + self.others[step - 1].astype(F32)
            self.total[one, two, self.place] = mine.astype(BF)
        for copy in self.copies(number):
            copy.start()

    @staticmethod
    def scratch(size, rows, columns):
        rest = size // 4
        count = 2 * rest + 2
        return [
            pltpu.VMEM((2, rest, rows, columns), BF),
            pltpu.VMEM((rest, rows, columns), BF),
            pltpu.VMEM((rest - 1, rows, columns), BF),
            pltpu.SemaphoreType.DMA((count,)),
            pltpu.SemaphoreType.DMA((count,)),
        ]


def reduction_parts(value, size):
    rows, columns = value.shape
    return value.reshape(2, 2, size // 4, rows // size, columns)


def reduction_whole(value):
    return value.reshape(-1, value.shape[-1])


def make_reductions(orders, totals, scratch):
    out = []
    for order, total in zip(orders, totals):
        out.append(Reduction(order, total, *scratch[:5]))
        scratch = scratch[5:]
    return out


def group_copies(branch, source, target, source_block, send_sems, recv_sems, local_sem):
    stride = 2**branch
    base, place = group_place(branch)
    first = stride - branch - 2
    copies = [
        pltpu.make_async_copy(source.at[source_block(place)], target.at[place], local_sem.at[branch - 1])
    ]
    for step in range(1, stride):
        member = (place + step) % stride
        copies.append(
            pltpu.make_async_remote_copy(
                src_ref=source.at[source_block(member)],
                dst_ref=target.at[place],
                send_sem=send_sems.at[first + step],
                recv_sem=recv_sems.at[first + step],
                device_id={"seq": base + member},
                device_id_type=pl.DeviceIdType.MESH,
            )
        )
    return copies


def exchange_forward_kernel(heads, own, *refs):
    count = BRANCHES - 1
    sends, refs = refs[:count], refs[count:]
    first, refs = refs[0], refs[1:]
    gots, refs = refs[:count], refs[count:]
    backs, refs = refs[:count], refs[count:]
    outs, refs = refs[:count], refs[count:]
    x, q_aug, in_send, in_recv, in_local, out_send, out_recv, out_local = refs
    tile = 256
    meet("seq")
    coming = {}
    for branch in range(1, BRANCHES):
        coming[branch] = group_copies(
            branch, sends[branch - 1], gots[branch - 1], lambda m: m, in_send, in_recv, in_local
        )
        for copy in coming[branch]:
            copy.start()

    @pl.loop(0, heads)
    def _(head):
        x[...] = own[0, head]

        def put(column, value):
            first[0, head, :, column : column + tile] = value

        forward_unit(x, q_aug, 0, SEG0, tile, put)

    leaving = []
    for branch in range(1, BRANCHES):
        stride, lanes, units, split = branch_shape(branch, heads)
        got, out = gots[branch - 1], outs[branch - 1]
        for copy in coming[branch]:
            copy.wait()
        queries = SEG0 // split
        base = 0 if split == 1 else lax.axis_index("seq") % split * queries

        @pl.loop(0, units)
        def _(unit):
            load_unit(got, unit, lanes, x)
            if split == 1:

                def put(column, value):
                    store_unit(out, unit, slice(None), value, column, value.shape[1])

            else:
                empty = row_block({0: -FAR}, 128)
                empty = jnp.concatenate([jnp.zeros((E, 128), F32), empty], axis=0).astype(BF)
                for block in range(SEG0 // 128):
                    store_unit(out, unit, slice(None), empty, block * 128, 128)

                def put(column, value):
                    width = out.shape[-1]
                    for start in range(0, value.shape[1], width):
                        block = (base + column + start) // width
                        out[block, unit] = value[:, start : start + width]

            forward_unit(x, q_aug, base, queries, min(tile, queries), put)

        per = out.shape[-1] // lanes
        copies = group_copies(
            branch, out, backs[branch - 1], lambda m: m // per, out_send, out_recv, out_local
        )
        for copy in copies:
            copy.start()
        leaving += copies
    for copy in leaving:
        copy.wait()


def exchange_scratch():
    copies = 2**BRANCHES - 2 - BRANCHES + 1
    one = [
        pltpu.SemaphoreType.DMA((copies,)),
        pltpu.SemaphoreType.DMA((copies,)),
        pltpu.SemaphoreType.DMA((BRANCHES - 1,)),
    ]
    return one + one


def unit_cost(units, dots):
    return pl.CostEstimate(
        flops=dots * 2 * units * SEG0 * SEG0 * 256,
        transcendentals=units * SEG0 * SEG0,
        bytes_accessed=units * SEG0 * 1000,
    )


def vmem_specs(count):
    return [pl.BlockSpec(memory_space=pltpu.VMEM)] * count


def out_blocks(heads, rows):
    shapes = []
    for branch in range(1, BRANCHES):
        stride, count, units, split = branch_shape(branch, heads)
        width = max(count, 128)
        shapes.append((SEG0 // width, units, rows, width))
    return shapes


def exchange_forward(heads, own, sends):
    backs = send_shapes(heads, ROWS_OUT)[0]
    gots = send_shapes(heads, ROWS_IN)[0]
    first = jax.ShapeDtypeStruct((1, heads, ROWS_OUT, SEG0), BF)
    results = pl.pallas_call(
        partial(exchange_forward_kernel, heads),
        in_specs=vmem_specs(1 + len(sends)),
        out_specs=vmem_specs(1 + len(gots) + len(backs)),
        out_shape=[first] + gots + backs,
        scratch_shapes=[pltpu.VMEM(shape, BF) for shape in out_blocks(heads, ROWS_OUT)]
        + [pltpu.VMEM((ROWS_IN, SEG0), BF), pltpu.VMEM((ROWS_OUT, SEG0), BF)]
        + exchange_scratch(),
        compiler_params=params(collective_id=0, has_side_effects=True),
        cost_estimate=unit_cost(2 * heads, 2),
        name="exchange_forward",
    )(own, *sends)
    return results[0], results[1 : 1 + len(gots)], results[1 + len(gots) :]


def backward_unit(x, g, q_aug, gk, gv, result, base, queries, tile):
    if isinstance(base, int):
        lanes = slice(base, base + queries)
    else:
        lanes = pl.ds(pl.multiple_of(base, 128), queries)
    extra = g[E:, lanes].astype(F32)
    ids = lax.broadcasted_iota(jnp.int32, extra.shape, 0)
    q = x[0:E, lanes]
    q_aug[0:E, :queries] = q
    q_aug[E:, :queries] = jnp.where(ids >= 12, extra, x[3 * E :, lanes].astype(F32) * -FAR).astype(BF)
    bits = x[3 * E :, :].astype(F32)
    k_aug = jnp.concatenate([x[E : 2 * E, :], (1.0 - bits).astype(BF)], axis=0)
    k_rows = k_aug.T
    v_ids = lax.broadcasted_iota(jnp.int32, bits.shape, 0)
    v_bits = jnp.where(v_ids < 3, 1.0, 0.0).astype(BF)
    v_rows = jnp.concatenate([x[2 * E : 3 * E, :], v_bits], axis=0).T
    q_rows = jnp.concatenate([q, jnp.zeros((BIT_ROWS, queries), BF)], axis=0).T
    g_all = g[:, lanes]
    g_rows = g_all.T
    if queries < SEG0:
        result[0:E, :] = jnp.zeros((E, SEG0), BF)
    for step in range(queries // tile):
        column = step * tile
        span = slice(column, column + tile)
        p = jnp.exp2(jnp.dot(k_rows, q_aug[:, span], preferred_element_type=F32))
        gs = p * jnp.dot(v_rows, g_all[:, span], preferred_element_type=F32)
        p, gs = p.astype(BF), gs.astype(BF)
        target = span if isinstance(base, int) else pl.ds(pl.multiple_of(base + column, 128), tile)
        result[0:E, target] = jnp.dot(k_aug, gs, preferred_element_type=F32)[:E].astype(BF)
        new_k = jnp.dot(gs, q_rows[span], preferred_element_type=F32)
        new_v = jnp.dot(p, g_rows[span], preferred_element_type=F32)
        if step == 0:
            gk[...] = new_k
            gv[...] = new_v
        else:
            gk[...] += new_k
            gv[...] += new_v
    result[E : 2 * E, :] = (gk[...].T[:E] * LN2).astype(BF)
    result[2 * E :, :] = gv[...].T[:E].astype(BF)


def stream_orders(count):
    return [((0, 1), (1, 0))[s % 2] for s in range(count)]


class Names:
    def __init__(self, refs):
        self.refs = list(refs)

    def take(self, count):
        taken, self.refs = self.refs[:count], self.refs[count:]
        return taken

    def one(self):
        return self.take(1)[0]


EARLY = [
    (6, 1, 1),
    (7, 0, 1),
    (9, 1, 2),
    (9, 0, 2),
    (10, 3, 1),
    (11, 2, 1),
    (11, 4, 1),
    (11, 1, 3),
    (11, 0, 3),
    (13, 3, 2),
    (13, 1, 4),
    (13, 0, 4),
    (14, 2, 2),
    (14, 4, 2),
    (15, 3, 3),
    (15, 1, 5),
    (15, 0, 5),
]


def backward_kernel(heads, streams, *refs):
    branches = BRANCHES - 1
    names = Names(refs)
    starts, own, own_g = names.take(3)
    units_in, sends, parts = names.take(branches), names.take(branches), names.take(streams)
    normed, in_proj, x_rows, grad_hidden, gain, gains_two = names.take(6)
    totals, in_totals = names.take(streams), names.take(3)
    grad_tokens, gains_out = names.take(2)
    first = names.one()
    backs, gots, outs = names.take(branches), names.take(branches), names.take(branches)
    x, g, q_aug, gk, gv, result = names.take(6)
    total, grads, grads_t, normed_t, spread_rows, head_send, head_recv = names.take(7)
    gain_head, gain_one, gain_two, gain_rest = names.take(4)
    in_send, in_recv, in_local, out_send, out_recv, out_local = names.take(6)
    part_sem, head_sems, gain_sems = names.take(3)
    orders = stream_orders(streams)
    reductions = make_reductions(orders, totals, names.take(5 * streams))
    lasts = make_reductions([(1, 0), (0, 1), (1, 0)], in_totals, names.take(15))

    shapes = [branch_shape(b, heads) for b in range(BRANCHES)]
    size, head_size = lax.axis_size("seq"), lax.axis_size("head")
    me, me_head = lax.axis_index("seq"), lax.axis_index("head")
    rest = size // 4
    tile = 256
    per_slot = x_rows.shape[0] // SLOTS
    width = x_rows.shape[1]

    fills = [pltpu.make_async_copy(parts[s], totals[s], part_sem.at[s]) for s in range(streams)]
    for fill in fills:
        fill.start()
    meet("seq", "head")

    def coming(branch):
        return group_copies(
            branch, sends[branch - 1], gots[branch - 1], lambda m: m, in_send, in_recv, in_local
        )

    def leaving(branch):
        out = outs[branch - 1]
        per = out.shape[-1] // shapes[branch][1]
        return group_copies(
            branch, out, backs[branch - 1], lambda m: m // per, out_send, out_recv, out_local
        )

    for branch in range(1, BRANCHES):
        for copy in coming(branch):
            copy.start()
    for s in range(streams):
        fills[s].wait()
        reductions[s].step(0)

    def split_branch(branch):
        stride, lanes, units, split = shapes[branch]
        queries = SEG0 // split
        for copy in coming(branch):
            copy.wait()
        load_unit(units_in[branch - 1], 0, lanes, x)
        load_unit(gots[branch - 1], 0, lanes, g)
        backward_unit(x, g, q_aug, gk, gv, result, me % split * queries, queries, min(tile, queries))
        store_unit(outs[branch - 1], 0, slice(None), result, 0, SEG0)

    runs, at = [(0, 0, 0, heads // 2)], heads // 2
    split_at = None
    for branch in range(1, BRANCHES):
        if shapes[branch][3] == 1:
            runs.append((branch, at, 0, shapes[branch][2]))
            at += shapes[branch][2]
    split_at = at
    runs.append((0, at, heads // 2, heads - heads // 2))
    blocks = at + heads - heads // 2
    plan = {}
    for block, stream, step in EARLY:
        if stream < streams:
            plan.setdefault(block * blocks // 16, []).append((stream, step))

    @pl.loop(0, blocks)
    def _(block):
        for after, events in plan.items():

            @pl.when(block == after)
            def _(events=events):
                for stream, step in events:
                    reductions[stream].step(step)

        @pl.when(block == split_at)
        def _():
            for branch in range(1, BRANCHES):
                if shapes[branch][3] > 1:
                    split_branch(branch)
                    for copy in leaving(branch):
                        copy.start()

        for branch, low, unit, count in runs:

            @pl.when((block >= low) & (block < low + count))
            def _(branch=branch, low=low, unit=unit):
                if branch == 0:
                    x[...] = own[0, block - low + unit]
                    g[...] = own_g[0, block - low + unit]
                else:

                    @pl.when(block == low)
                    def _():
                        for copy in coming(branch):
                            copy.wait()

                    load_unit(units_in[branch - 1], block - low, shapes[branch][1], x)
                    load_unit(gots[branch - 1], block - low, shapes[branch][1], g)

        backward_unit(x, g, q_aug, gk, gv, result, 0, SEG0, tile)
        for branch, low, unit, count in runs:

            @pl.when((block >= low) & (block < low + count))
            def _(branch=branch, low=low, unit=unit, count=count):
                if branch == 0:
                    first[block - low + unit] = result[...]
                else:
                    store_unit(outs[branch - 1], block - low, slice(None), result, 0, SEG0)

                    @pl.when(block == low + count - 1)
                    def _():
                        for copy in leaving(branch):
                            copy.start()

    for branch in range(1, BRANCHES):
        for copy in leaving(branch):
            copy.wait()

    later = []
    done = {s: 1 for s in range(streams)}
    for _, stream, step in EARLY:
        if stream < streams:
            done[stream] = step + 1
    for step in range(Reduction.STEPS):
        later += [(s, step) for s in (1, 0, 3, 2, 4) if s < streams and step >= done[s]]

    def advance(count):
        for stream, step in later[:count]:
            reductions[stream].step(step)
        del later[:count]

    @pl.loop(0, heads)
    def _(head):
        total[...] = first[head].astype(F32)
        for branch in range(1, BRANCHES):
            stride, lanes, per, split = shapes[branch]
            back, start = backs[branch - 1], starts[branch, head]
            if split == 1:
                value = back[head // per, head % per].astype(F32)
            else:
                value = back[head * split, 0].astype(F32)
                for copy in range(1, split):
                    value = value + back[head * split + copy, 0].astype(F32)
            if lanes < 128:
                share = 128 // lanes
                value = moved_part(value, lanes, me % share, start % share)
                start = start // share
                lanes = 128
            for block in range(SEG0 // lanes):
                span = slice(block * lanes, (block + 1) * lanes)
                total[:, span] += jnp.where(start == block, value, 0.0)
        grads[0, head] = (total[0:E, :] * E ** (-0.5)).astype(BF)
        grads[1, head] = total[E : 2 * E, :].astype(BF)
        grads[2, head] = total[2 * E :, :].astype(BF)

    normed_t[...] = normed[...].T
    rows_in = in_totals[0].shape[3]
    chunk = width // 2
    for j in range(3):
        grads_t[j] = grads[j].reshape(heads * E, SEG0).T
        for half in range(2):
            value = jnp.dot(
                normed_t[half * chunk : (half + 1) * chunk], grads_t[j], preferred_element_type=F32
            ).astype(BF)
            for part in range(chunk // rows_in):
                index = half * (chunk // rows_in) + part
                in_totals[j][index // (2 * rest), index // rest % 2, index % rest] = value[
                    part * rows_in : (part + 1) * rows_in
                ]
        lasts[j].step(0)
    advance(3)

    for half in range(2):
        rows = slice(half * SEG0 // 2, (half + 1) * SEG0 // 2)
        value = jnp.zeros((SEG0 // 2, width), F32)
        for j in range(3):
            value = value + lax.dot_general(
                grads_t[j, rows], in_proj[j], (((1,), (1,)), ((), ())), preferred_element_type=F32
            )
        value = value.astype(BF)
        for slot in range(SLOTS // 2):
            for device in range(head_size):
                begin = (slot * head_size + device) * per_slot
                place = (half * SLOTS // 2 + slot) * per_slot
                head_send[device, place : place + per_slot] = value[begin : begin + per_slot]
    swaps = []
    for step in range(1, head_size):
        device = (me_head + step) % head_size
        swaps.append(
            pltpu.make_async_remote_copy(
                src_ref=head_send.at[device],
                dst_ref=head_recv.at[step - 1],
                send_sem=head_sems.at[0, step - 1],
                recv_sem=head_sems.at[1, step - 1],
                device_id={"head": device},
                device_id_type=pl.DeviceIdType.MESH,
            )
        )
        swaps[-1].start()
    advance(3)
    for swap in swaps:
        swap.wait()

    gain_head[me_head] = jnp.zeros(gains_out.shape, F32)
    gain_head[me_head, 2:4] = gains_two[...]

    @pl.loop(0, SLOTS)
    def _(slot):
        rows = pl.ds(pl.multiple_of(slot * per_slot, per_slot), per_slot)
        grad = head_send[me_head, rows].astype(F32)
        for step in range(1, head_size):
            grad = grad + head_recv[step - 1, rows].astype(F32)
        values = x_rows[rows]
        centred = values - jnp.mean(values, axis=-1, keepdims=True)
        scale = lax.rsqrt(jnp.mean(centred * centred, axis=-1, keepdims=True) + EPS)
        unit = centred * scale
        scaled = grad * gain[...]
        inner = jnp.mean(scaled * unit, axis=-1, keepdims=True)
        out = grad_hidden[rows] + scale * (scaled - jnp.mean(scaled, axis=-1, keepdims=True) - unit * inner)
        place = slot % 2 * 8 + slot // 2 % 2 * 4 + slot // 4 % 2 * 2 + slot // 8
        for column in range(width // 128):
            lanes = slice(column * 128, (column + 1) * 128)
            spread_rows[column, pl.ds(place, per_slot, stride=SLOTS), :] = out[:, lanes]
        gain_head[me_head, 0:1] += jnp.sum(grad * unit, axis=0, keepdims=True)
        gain_head[me_head, 1:2] += jnp.sum(grad, axis=0, keepdims=True)

    for column in range(width // 128):
        grad_tokens[:, column * 128 : (column + 1) * 128] = spread_rows[column]

    def gain_copy(source, target, axis, device, sem):
        made = pltpu.make_async_remote_copy(
            src_ref=source,
            dst_ref=target,
            send_sem=gain_sems.at[0, sem],
            recv_sem=gain_sems.at[1, sem],
            device_id={axis: device},
            device_id_type=pl.DeviceIdType.MESH,
        )
        made.start()
        return made

    mine = gain_head.at[me_head]
    swaps = [
        gain_copy(mine, mine, "head", (me_head + step) % head_size, step - 1) for step in range(1, head_size)
    ]
    advance(3)
    for swap in swaps:
        swap.wait()
    value = gain_head[0]
    for device in range(1, head_size):
        value = value + gain_head[device]
    gain_one[0] = value
    swap = gain_copy(gain_one.at[0], gain_one.at[1], "seq", me + 1 - 2 * (me % 2), head_size)
    for last in lasts:
        last.step(1)
    advance(2)
    swap.wait()
    gain_two[0] = gain_one[0] + gain_one[1]
    swap = gain_copy(gain_two.at[0], gain_two.at[1], "seq", me + 2 - 4 * (me // 2 % 2), head_size + 1)
    advance(2)
    for last in lasts:
        last.step(2)
    swap.wait()
    spot = me // 4
    gain_rest[spot] = gain_two[0] + gain_two[1]
    block = gain_rest.at[spot]
    swaps = [
        gain_copy(block, block, "seq", (spot + step) % rest * 4 + me % 4, head_size + 1 + step)
        for step in range(1, rest)
    ]
    advance(2)
    for last in lasts:
        last.step(3)
    for swap in swaps:
        swap.wait()
    value = gain_rest[0]
    for z in range(1, rest):
        value = value + gain_rest[z]
    gains_out[...] = value
    advance(2)
    for last in lasts:
        last.step(4)
    advance(2)
    for last in lasts:
        last.step(5)
    advance(len(later))
    for last in lasts:
        last.step(6)


def backward(heads, starts, own, own_g, units, sends, terms, normed, in_proj, x_rows, grad_hidden, gain, gains_two):
    size, head_size = lax.axis_size("seq"), lax.axis_size("head")
    rest = size // 4
    rows, width = x_rows.shape
    parts = [reduction_parts(term, size) for term in terms]
    in_shape = (2, 2, rest, width // size, heads * E)
    scratch = []
    for part in parts:
        scratch += Reduction.scratch(size, *part.shape[-2:])
    for _ in range(3):
        scratch += Reduction.scratch(size, *in_shape[-2:])
    streams = len(parts)
    results = pl.pallas_call(
        partial(backward_kernel, heads, streams),
        in_specs=[pl.BlockSpec(memory_space=pltpu.SMEM)]
        + vmem_specs(2 + len(units) + len(sends))
        + [pl.BlockSpec(memory_space=pl.ANY)] * streams
        + vmem_specs(6),
        out_specs=vmem_specs(streams + 5),
        out_shape=[jax.ShapeDtypeStruct(part.shape, BF) for part in parts]
        + [jax.ShapeDtypeStruct(in_shape, BF)] * 3
        + [jax.ShapeDtypeStruct((rows, width), F32), jax.ShapeDtypeStruct((8, width), F32)],
        scratch_shapes=[pltpu.VMEM((heads, 3 * E, SEG0), BF)]
        + [pltpu.VMEM(shape.shape, BF) for shape in send_shapes(heads, 3 * E)[0]]
        + [pltpu.VMEM(shape.shape, BF) for shape in send_shapes(heads, ROWS_OUT)[0]]
        + [pltpu.VMEM(shape, BF) for shape in out_blocks(heads, 3 * E)]
        + [
            pltpu.VMEM((ROWS_IN, SEG0), BF),
            pltpu.VMEM((ROWS_OUT, SEG0), BF),
            pltpu.VMEM((ROWS_OUT, SEG0), BF),
            pltpu.VMEM((SEG0, ROWS_OUT), F32),
            pltpu.VMEM((SEG0, ROWS_OUT), F32),
            pltpu.VMEM((3 * E, SEG0), BF),
            pltpu.VMEM((3 * E, SEG0), F32),
            pltpu.VMEM((3, heads, E, SEG0), BF),
            pltpu.VMEM((3, SEG0, heads * E), BF),
            pltpu.VMEM((width, SEG0), BF),
            pltpu.VMEM((width // 128, rows, 128), F32),
            pltpu.VMEM((head_size, rows, width), BF),
            pltpu.VMEM((head_size - 1, rows, width), BF),
            pltpu.VMEM((head_size, 8, width), F32),
            pltpu.VMEM((2, 8, width), F32),
            pltpu.VMEM((2, 8, width), F32),
            pltpu.VMEM((rest, 8, width), F32),
        ]
        + exchange_scratch()
        + [
            pltpu.SemaphoreType.DMA((streams,)),
            pltpu.SemaphoreType.DMA((2, head_size - 1)),
            pltpu.SemaphoreType.DMA((2, head_size + 1 + rest)),
        ]
        + scratch,
        compiler_params=pltpu.CompilerParams(
            vmem_limit_bytes=60 * 2**20, collective_id=1, has_side_effects=True
        ),
        cost_estimate=unit_cost(2 * heads, 5),
        name="backward",
    )(starts, own, own_g, *units, *sends, *parts, normed, in_proj, x_rows, grad_hidden, gain, gains_two)
    sums = [reduction_whole(total) for total in results[: streams + 3]]
    return sums[:streams], sums[streams:], results[-2], results[-1]


def placed_part(value, count, start, place):
    if count >= 128:
        return value, None
    per = 128 // count
    lanes = lax.broadcasted_iota(jnp.int32, (1, 128), 1)
    return moved_part(value, count, place % per, start % per), lanes // count == start % per


def merge_kernel(heads, starts, place, first, *refs):
    seconds, (mixed, merged, lse) = refs[: BRANCHES - 1], refs[BRANCHES - 1 :]
    head = pl.program_id(0)
    extra = first[0, 0, E:, :].astype(F32)
    merged[0] = first[0, 0, :E, :].astype(F32)
    lse[0] = extra[0:1] + extra[1:2] + extra[2:3]
    for branch in range(1, BRANCHES):
        got = seconds[branch - 1]
        count = branch_shape(branch, heads)[1]
        start = starts[branch, head]
        lanes = aligned(start, count)
        for copy in range(got.shape[0]):
            value, mask = placed_part(got[copy, 0].astype(F32), count, start, place[0])
            new_lse = value[E : E + 1] + value[E + 1 : E + 2] + value[E + 2 : E + 3]
            if mask is not None:
                new_lse = jnp.where(mask, new_lse, -FAR)
            old_lse = lse[0, :, lanes]
            top = jnp.maximum(old_lse, new_lse)
            both = top + jnp.log2(jnp.exp2(old_lse - top) + jnp.exp2(new_lse - top))
            old_w = jnp.exp2(old_lse - both)
            new_w = jnp.exp2(new_lse - both)
            merged[0, :, lanes] = merged[0, :, lanes] * old_w + value[:E] * new_w
            lse[0, :, lanes] = both
    mixed[...] = merged[0].astype(BF)


def merge_heads(heads, starts, place, first, seconds):
    span = first.shape[-1]
    return pl.pallas_call(
        partial(merge_kernel, heads),
        grid_spec=pltpu.PrefetchScalarGridSpec(
            num_scalar_prefetch=2,
            grid=(heads,),
            in_specs=[pl.BlockSpec((1, 1, ROWS_OUT, span), lambda h, s, t: (0, h, 0, 0))]
            + send_shapes(heads, ROWS_OUT)[1],
            out_specs=[
                pl.BlockSpec((E, span), lambda h, s, t: (h, 0)),
                pl.BlockSpec((1, E, span), lambda h, s, t: (h, 0, 0)),
                pl.BlockSpec((1, 1, span), lambda h, s, t: (h, 0, 0)),
            ],
        ),
        out_shape=[
            jax.ShapeDtypeStruct((heads * E, span), BF),
            jax.ShapeDtypeStruct((heads, E, span), F32),
            jax.ShapeDtypeStruct((heads, 1, span), F32),
        ],
        compiler_params=params(),
        name="merge_heads",
    )(starts, place, first, *seconds)


def spread_kernel(heads, starts, place, grad, merged, lse, own, *sends):
    head = pl.program_id(0)
    low = grad[...].astype(BF)
    dots = jnp.sum(low.astype(F32) * merged[0], axis=0, keepdims=True)
    own[0, 0, :E, :] = low
    d = pieces_of(-dots)
    m = pieces_of(-lse[0])
    placed = {0: d[0], 1: d[1], 2: d[2], 12: m[0], 13: m[1], 14: m[2]}
    own[0, 0, E:, :] = row_block(placed, grad.shape[-1]).astype(BF)
    send_blocks(heads, head, starts, place, own, sends)


def spread_heads(heads, starts, place, grad, merged, lse):
    span = grad.shape[-1]
    sends, send_specs = send_shapes(heads, ROWS_OUT)
    return pl.pallas_call(
        partial(spread_kernel, heads),
        grid_spec=pltpu.PrefetchScalarGridSpec(
            num_scalar_prefetch=2,
            grid=(heads,),
            in_specs=[
                pl.BlockSpec((E, span), lambda h, s, t: (h, 0)),
                pl.BlockSpec((1, E, span), lambda h, s, t: (h, 0, 0)),
                pl.BlockSpec((1, 1, span), lambda h, s, t: (h, 0, 0)),
            ],
            out_specs=[pl.BlockSpec((1, 1, ROWS_OUT, span), lambda h, s, t: (0, h, 0, 0))] + send_specs,
        ),
        out_shape=[jax.ShapeDtypeStruct((1, heads, ROWS_OUT, span), BF)] + sends,
        compiler_params=params(),
        name="spread_heads",
    )(starts, place, grad, merged, lse)


def rolled(value, step):
    size = lax.axis_size("head")
    return lax.ppermute(value, "head", [(s, (s + step) % size) for s in range(size)])


def all_rows(own):
    size = lax.axis_size("head")
    me = lax.axis_index("head")
    got = [own] + [rolled(own, step) for step in range(1, size)]
    if size == 2:
        return [jnp.where(me == 0, got[0], got[1]), jnp.where(me == 0, got[1], got[0])]
    stacked = jnp.stack(got)
    return [stacked[(me - place) % size] for place in range(size)]


def sum_rows(parts):
    size = lax.axis_size("head")
    me = lax.axis_index("head")
    total = lax.dynamic_index_in_dim(parts, me, 0, keepdims=False).astype(F32)
    for step in range(1, size):
        sent = lax.dynamic_index_in_dim(parts, (me + step) % size, 0, keepdims=False)
        total = total + rolled(sent, step).astype(F32)
    return total


def local(
    tokens,
    documents,
    offsets,
    in_proj,
    out_proj,
    up_proj,
    down_proj,
    first_gain,
    first_shift,
    second_gain,
    second_shift,
    cotangent,
):
    head_count = lax.axis_size("head")
    seq_id = lax.axis_index("seq")
    row_count, width = tokens.shape
    seq_len = row_count * head_count
    heads = offsets.shape[1]
    per_slot = row_count // SLOTS
    gelu_exact = partial(jax.nn.gelu, approximate=False)

    ids = lax.broadcasted_iota(jnp.int32, (row_count, row_count), 0)
    slot = reversed_bits(ids // per_slot, 4)
    source = ids % per_slot * SLOTS + slot
    order = (source == lax.broadcasted_iota(jnp.int32, (row_count, row_count), 1)).astype(BF)

    def sorted_rows(values):
        return jnp.dot(order, values, preferred_element_type=F32)

    def shard_rows(own):
        parts = [part.reshape(SLOTS, per_slot, -1) for part in all_rows(own)]
        return jnp.stack(parts, axis=1).reshape(seq_len, -1)

    def device_parts(values):
        split = values.reshape(SLOTS, head_count, per_slot, -1)
        return jnp.moveaxis(split, 1, 0).reshape(head_count, row_count, -1)

    x_rows = sorted_rows(tokens)
    cot_low = sorted_rows(cotangent).astype(BF)
    normed_one = norm_rows(x_rows, first_gain, first_shift)
    gathered_one = shard_rows(normed_one.astype(BF))
    cot_all = shard_rows(cot_low)

    my_docs = lax.dynamic_slice_in_dim(documents, seq_id * seq_len, seq_len)
    my_docs = my_docs.reshape(head_count, per_slot, 2, 2, 2, 2).transpose(5, 4, 3, 2, 0, 1).reshape(seq_len)
    bit_ids = jnp.arange(BIT_ROWS, dtype=jnp.int32)[:, None]
    doc_bit = my_docs[None, :] // 2 ** (bit_ids % DOC_BITS) % 2
    bits = jnp.where(bit_ids < DOC_BITS, doc_bit, jnp.where(bit_ids < 2 * DOC_BITS, 1 - doc_bit, 0))
    bits = bits.astype(BF)
    starts = jnp.stack([reversed_bits(offsets[b], b) for b in range(BRANCHES)])

    scales = jnp.array([E ** (-0.5) * LOG2E, 1.0, 1.0], F32)[:, None, None]
    projected = jnp.einsum("td,jdc->jct", gathered_one, in_proj, preferred_element_type=F32)
    projected = (projected * scales).astype(BF)
    place = seq_id.astype(jnp.int32).reshape(1)
    own, *sends = pack_heads(heads, starts, place, projected, bits)
    first_out, units, outs = exchange_forward(heads, own, sends)
    mixed, merged, lse = merge_heads(heads, starts, place, first_out, outs)

    attn_part = jnp.einsum("ct,cd->td", mixed, out_proj, preferred_element_type=F32).astype(BF)
    hidden_one = x_rows + sum_rows(device_parts(attn_part))
    normed_two = norm_rows(hidden_one, second_gain, second_shift)
    gathered_two = shard_rows(normed_two.astype(BF))
    pre_act = jnp.dot(gathered_two, up_proj, preferred_element_type=F32)
    hidden, gelu_pull = jax.vjp(gelu_exact, pre_act)
    hidden = hidden.astype(BF)
    down_part = jnp.dot(hidden, down_proj, preferred_element_type=F32).astype(BF)
    block_rows = hidden_one + sum_rows(device_parts(down_part))
    block_out = jnp.dot(order.T, block_rows.astype(BF), preferred_element_type=F32).astype(BF)

    chunks = max(1, up_proj.shape[1] // width)

    def columns(values):
        return jnp.split(values, chunks, axis=1)

    grad_down = [
        jnp.einsum("tf,td->fd", part, cot_all, preferred_element_type=F32).astype(BF) for part in columns(hidden)
    ]
    grad_act = jnp.einsum("td,fd->tf", cot_all, down_proj, preferred_element_type=F32)
    grad_pre = gelu_pull(grad_act)[0].astype(BF)
    grad_up = [
        jnp.einsum("td,tf->df", gathered_two, part, preferred_element_type=F32).astype(BF)
        for part in columns(grad_pre)
    ]
    norm_part = jnp.einsum("tf,df->td", grad_pre, up_proj, preferred_element_type=F32).astype(BF)
    grad_normed_two = sum_rows(device_parts(norm_part))
    pull_two = jax.vjp(norm_rows, hidden_one, second_gain, second_shift)[1]
    grad_ln_two, grad_gain_two, grad_shift_two = pull_two(grad_normed_two)
    grad_hidden_one = cot_low.astype(F32) + grad_ln_two
    grad_attn = shard_rows(grad_hidden_one.astype(BF))
    grad_out = jnp.einsum("ct,td->cd", mixed, grad_attn, preferred_element_type=F32).astype(BF)
    grad_merged = jnp.einsum("td,cd->ct", grad_attn, out_proj, preferred_element_type=F32)

    own_g, *sends_g = spread_heads(heads, starts, place, grad_merged, merged, lse)
    terms = [term for pair in zip(grad_up, grad_down) for term in pair] + [grad_out]
    gains_two = jnp.stack([grad_gain_two, grad_shift_two])
    sums, grad_in, grad_tokens, gains = backward(
        heads, starts, own, own_g, units, sends_g, terms,
        gathered_one, in_proj, x_rows, grad_hidden_one, first_gain[None, :], gains_two,
    )
    return (
        block_out,
        grad_tokens,
        jnp.stack(grad_in).astype(F32),
        sums[-1].astype(F32),
        jnp.concatenate(sums[:-1:2], axis=1).astype(F32),
        jnp.concatenate(sums[1:-1:2], axis=0).astype(F32),
        gains[0],
        gains[1],
        gains[2],
        gains[3],
    )


def solution(mesh):
    placed = (
        P(("seq", "head"), None),
        P(),
        P(None, "head"),
        P(None, None, "head"),
        P("head", None),
        P(None, "head"),
        P("head", None),
        P(),
        P(),
        P(),
        P(),
        P(("seq", "head"), None),
    )
    return jax.shard_map(
        local,
        mesh=mesh,
        in_specs=placed,
        out_specs=(
            P(("seq", "head"), None),
            P(("seq", "head"), None),
            P(None, None, "head"),
            P("head", None),
            P(None, "head"),
            P("head", None),
            P(),
            P(),
            P(),
            P(),
        ),
        check_vma=False,
    )
```

```python
import math
from functools import partial

import jax
import jax.numpy as jnp
from jax import lax
from jax.experimental import pallas as pl
from jax.experimental.pallas import tpu as pltpu
from jax.sharding import PartitionSpec as P

E = 48
BRANCHES = 5
SEG0 = 1024
SLOTS = 16
BIT_ROWS = 16
DOC_BITS = 6
ROWS_IN = 3 * E + BIT_ROWS
ROWS_OUT = E + BIT_ROWS
EPS = 1e-05
FAR = 1e30
LOG2E = math.log2(math.e)
LN2 = math.log(2.0)
BF = jnp.bfloat16
F32 = jnp.float32
VMEM_LIMIT = 48 * 2**20


def params(**more):
    return pltpu.CompilerParams(vmem_limit_bytes=VMEM_LIMIT, **more)


def norm_rows(values, gain, shift):
    centre = jnp.mean(values, axis=-1, keepdims=True)
    centred = values - centre
    spread = jnp.mean(centred * centred, axis=-1, keepdims=True)
    return centred * lax.rsqrt(spread + EPS) * gain + shift


def reversed_bits(value, count):
    out = jnp.zeros_like(value)
    for bit in range(count):
        out = out * 2 + value // 2**bit % 2
    return out


def bit_reversed(value, count):
    return int(format(value, f"0{count}b")[::-1], 2)


def branch_shape(branch, heads):
    stride = 2**branch
    return (stride, SEG0 // stride, max(1, heads // stride), max(1, stride // heads))


def pieces_of(value):
    high = value.astype(BF).astype(F32)
    rest = value - high
    middle = rest.astype(BF).astype(F32)
    return high, middle, (rest - middle).astype(BF).astype(F32)


def row_block(placed, columns):
    ids = lax.broadcasted_iota(jnp.int32, (BIT_ROWS, columns), 0)
    block = jnp.zeros((BIT_ROWS, columns), F32)
    for row, value in placed.items():
        block = jnp.where(ids == row, value, block)
    return block


def lane_block(ref, rows, start, count):
    return ref[0, 0, rows, aligned(start, count)]


def aligned(start, count):
    if count >= 128:
        return pl.ds(pl.multiple_of(start * count, 128), count)
    return pl.ds(pl.multiple_of(start // (128 // count) * 128, 128), 128)


def moved_part(block, count, source, target):
    per = 128 // count
    lanes = lax.broadcasted_iota(jnp.int32, (1, 128), 1)
    out = block
    for shift in range(1, per):
        turned = jnp.concatenate([block[:, -shift * count :], block[:, : -shift * count]], axis=1)
        out = jnp.where((target - source) % per == shift, turned, out)
    return jnp.where(lanes // count == target, out, 0.0)


def pack_kernel(heads, starts, place, proj, bits, own, *sends):
    head = pl.program_id(0)
    for j in range(3):
        own[0, 0, j * E : (j + 1) * E, :] = proj[j]
    own[0, 0, 3 * E :, :] = bits[...]
    send_blocks(heads, head, starts, place, own, sends)


def send_blocks(heads, head, starts, place, own, sends):
    for branch in range(1, BRANCHES):
        count = branch_shape(branch, heads)[1]
        send = sends[branch - 1]
        start = starts[branch, head]
        block = lane_block(own, slice(None), start, count)
        if count < 128:
            per = 128 // count
            block = moved_part(block.astype(F32), count, start % per, place[0] % per).astype(BF)
        for copy in range(send.shape[0]):
            send[copy, 0] = block


def send_shapes(heads, rows):
    outs, specs = [], []
    for branch in range(1, BRANCHES):
        stride, count, per, split = branch_shape(branch, heads)
        count = max(count, 128)
        outs.append(jax.ShapeDtypeStruct((stride, per, rows, count), BF))
        specs.append(
            pl.BlockSpec((split, 1, rows, count), lambda h, s, t, per=per: (h // per, h % per, 0, 0))
        )
    return outs, specs


def pack_heads(heads, starts, place, proj, bits):
    span = proj.shape[-1]
    sends, send_specs = send_shapes(heads, ROWS_IN)
    return pl.pallas_call(
        partial(pack_kernel, heads),
        grid_spec=pltpu.PrefetchScalarGridSpec(
            num_scalar_prefetch=2,
            grid=(heads,),
            in_specs=[
                pl.BlockSpec((3, E, span), lambda h, s, t: (0, h, 0)),
                pl.BlockSpec((BIT_ROWS, span), lambda h, s, t: (0, 0)),
            ],
            out_specs=[pl.BlockSpec((1, 1, ROWS_IN, span), lambda h, s, t: (0, h, 0, 0))] + send_specs,
        ),
        out_shape=[jax.ShapeDtypeStruct((1, heads, ROWS_IN, span), BF)] + sends,
        compiler_params=params(),
        name="pack_heads",
    )(starts, place, proj, bits)


def load_unit(ref, unit, count, x):
    if ref.shape[0] == 1:
        x[...] = ref[0, unit]
        return
    width = ref.shape[-1]
    per = width // count
    for block in range(ref.shape[0] // per):
        value = ref[block * per, unit]
        for other in range(1, per):
            value = value + ref[block * per + other, unit]
        x[:, block * width : (block + 1) * width] = value


def store_unit(ref, unit, rows, value, column, count):
    width = ref.shape[-1]
    size = min(width, count)
    for start in range(column, column + count, size):
        lanes = slice(start % width, start % width + size)
        ref[start // width, unit, rows, lanes] = value[:, start - column : start - column + size]


def forward_unit(x, q_aug, base, queries, tile, put):
    if isinstance(base, int):
        lanes = slice(base, base + queries)
    else:
        lanes = pl.ds(pl.multiple_of(base, 128), queries)
    q_aug[0:E, :queries] = x[0:E, lanes]
    q_aug[E:, :queries] = (x[3 * E :, lanes].astype(F32) * -FAR).astype(BF)
    bits = x[3 * E :, :].astype(F32)
    k_rows = jnp.concatenate([x[E : 2 * E, :], (1.0 - bits).astype(BF)], axis=0).T
    v_aug = jnp.concatenate([x[2 * E : 3 * E, :], jnp.ones(bits.shape, BF)], axis=0)
    for step in range(queries // tile):
        column = step * tile
        s = jnp.dot(k_rows, q_aug[:, column : column + tile], preferred_element_type=F32)
        top = jnp.max(s, axis=0, keepdims=True)
        p = jnp.exp2(s - top).astype(BF)
        o = jnp.dot(v_aug, p, preferred_element_type=F32)
        total = o[E : E + 1]
        high, middle, low = pieces_of(top + jnp.log2(total))
        block = row_block({0: high, 1: middle, 2: low}, tile)
        put(column, jnp.concatenate([o[:E] * (1.0 / total), block], axis=0).astype(BF))


def group_place(branch):
    stride = 2**branch
    me = lax.axis_index("seq")
    return me // stride * stride, me % stride


def meet(*axes):
    barrier = pltpu.get_barrier_semaphore()
    count = 0
    for axis in axes:
        size = lax.axis_size(axis)
        me = lax.axis_index(axis)

        @pl.loop(1, size)
        def _(step):
            pl.semaphore_signal(
                barrier, inc=1, device_id={axis: (me + step) % size}, device_id_type=pl.DeviceIdType.MESH
            )

        count += size - 1
    pl.semaphore_wait(barrier, count)


class Reduction:
    STEPS = 7

    def __init__(self, order, total, half, quarter, others, send, recv):
        self.total = total
        self.half, self.quarter, self.others = half, quarter, others
        self.send, self.recv = send, recv
        me = lax.axis_index("seq")
        self.rest = lax.axis_size("seq") // 4
        self.me = me
        bits = (me % 2, me // 2 % 2)
        self.bits = [bits[bit] for bit in order]
        self.partners = [me + (1 - 2 * bits[bit]) * 2**bit for bit in order]
        self.place = me // 4

    def copy(self, source, target, device, sem):
        return pltpu.make_async_remote_copy(
            src_ref=source,
            dst_ref=target,
            send_sem=self.send.at[sem],
            recv_sem=self.recv.at[sem],
            device_id={"seq": device},
            device_id_type=pl.DeviceIdType.MESH,
        )

    def copies(self, number):
        one, two = self.bits
        rest = self.rest
        others = []
        for step in range(1, rest):
            place = (self.place + step) % rest
            others.append((step, place, place * 4 + self.me % 4))
        if number == 0:
            return [self.copy(self.total.at[1 - one], self.half, self.partners[0], 0)]
        if number == 1:
            return [self.copy(self.half.at[1 - two], self.quarter, self.partners[1], 1)]
        if number == 2:
            return [
                self.copy(self.quarter.at[place], self.others.at[step - 1], device, 1 + step)
                for step, place, device in others
            ]
        if number == 3:
            block = self.total.at[one, two, self.place]
            return [self.copy(block, block, device, rest + step) for step, place, device in others]
        if number == 4:
            block = self.total.at[one, two]
            return [self.copy(block, block, self.partners[1], 2 * rest)]
        if number == 5:
            block = self.total.at[one]
            return [self.copy(block, block, self.partners[0], 2 * rest + 1)]
        return []

    def step(self, number):
        one, two = self.bits
        rest = self.rest
        if number > 0:
            for copy in self.copies(number - 1):
                copy.wait()
        if number == 1:

            @pl.loop(0, 2 * rest)
            def _(i):
                j, z = i // rest, i % rest
                mine = self.total[one, j, z].astype(F32)
                self.half[j, z] = (mine + self.half[j, z].astype(F32)).astype(BF)

        elif number == 2:

            @pl.loop(0, rest)
            def _(z):
                mine = self.half[two, z].astype(F32)
                self.quarter[z] = (mine + self.quarter[z].astype(F32)).astype(BF)

        elif number == 3:
            mine = self.quarter[self.place].astype(F32)
            for step in range(1, rest):
                mine = mine + self.others[step - 1].astype(F32)
            self.total[one, two, self.place] = mine.astype(BF)
        for copy in self.copies(number):
            copy.start()

    @staticmethod
    def scratch(size, rows, columns):
        rest = size // 4
        count = 2 * rest + 2
        return [
            pltpu.VMEM((2, rest, rows, columns), BF),
            pltpu.VMEM((rest, rows, columns), BF),
            pltpu.VMEM((rest - 1, rows, columns), BF),
            pltpu.SemaphoreType.DMA((count,)),
            pltpu.SemaphoreType.DMA((count,)),
        ]


def reduction_parts(value, size):
    rows, columns = value.shape
    return value.reshape(2, 2, size // 4, rows // size, columns)


def reduction_whole(value):
    return value.reshape(-1, value.shape[-1])


def make_reductions(orders, totals, scratch):
    out = []
    for order, total in zip(orders, totals):
        out.append(Reduction(order, total, *scratch[:5]))
        scratch = scratch[5:]
    return out


def group_copies(branch, source, target, source_block, send_sems, recv_sems, local_sem):
    stride = 2**branch
    base, place = group_place(branch)
    first = stride - branch - 2
    copies = [
        pltpu.make_async_copy(source.at[source_block(place)], target.at[place], local_sem.at[branch - 1])
    ]
    for step in range(1, stride):
        member = (place + step) % stride
        copies.append(
            pltpu.make_async_remote_copy(
                src_ref=source.at[source_block(member)],
                dst_ref=target.at[place],
                send_sem=send_sems.at[first + step],
                recv_sem=recv_sems.at[first + step],
                device_id={"seq": base + member},
                device_id_type=pl.DeviceIdType.MESH,
            )
        )
    return copies


def exchange_forward_kernel(heads, own, *refs):
    count = BRANCHES - 1
    sends, refs = refs[:count], refs[count:]
    first, refs = refs[0], refs[1:]
    gots, refs = refs[:count], refs[count:]
    backs, refs = refs[:count], refs[count:]
    outs, refs = refs[:count], refs[count:]
    x, q_aug, in_send, in_recv, in_local, out_send, out_recv, out_local = refs
    tile = 256
    meet("seq")
    coming = {}
    for branch in range(1, BRANCHES):
        coming[branch] = group_copies(
            branch, sends[branch - 1], gots[branch - 1], lambda m: m, in_send, in_recv, in_local
        )
        for copy in coming[branch]:
            copy.start()

    @pl.loop(0, heads)
    def _(head):
        x[...] = own[0, head]

        def put(column, value):
            first[0, head, :, column : column + tile] = value

        forward_unit(x, q_aug, 0, SEG0, tile, put)

    leaving = []
    for branch in range(1, BRANCHES):
        stride, lanes, units, split = branch_shape(branch, heads)
        got, out = gots[branch - 1], outs[branch - 1]
        for copy in coming[branch]:
            copy.wait()
        queries = SEG0 // split
        base = 0 if split == 1 else lax.axis_index("seq") % split * queries

        @pl.loop(0, units)
        def _(unit):
            load_unit(got, unit, lanes, x)
            if split == 1:

                def put(column, value):
                    store_unit(out, unit, slice(None), value, column, value.shape[1])

            else:
                empty = row_block({0: -FAR}, 128)
                empty = jnp.concatenate([jnp.zeros((E, 128), F32), empty], axis=0).astype(BF)
                for block in range(SEG0 // 128):
                    store_unit(out, unit, slice(None), empty, block * 128, 128)

                def put(column, value):
                    width = out.shape[-1]
                    for start in range(0, value.shape[1], width):
                        block = (base + column + start) // width
                        out[block, unit] = value[:, start : start + width]

            forward_unit(x, q_aug, base, queries, min(tile, queries), put)

        per = out.shape[-1] // lanes
        copies = group_copies(
            branch, out, backs[branch - 1], lambda m: m // per, out_send, out_recv, out_local
        )
        for copy in copies:
            copy.start()
        leaving += copies
    for copy in leaving:
        copy.wait()


def exchange_scratch():
    copies = 2**BRANCHES - 2 - BRANCHES + 1
    one = [
        pltpu.SemaphoreType.DMA((copies,)),
        pltpu.SemaphoreType.DMA((copies,)),
        pltpu.SemaphoreType.DMA((BRANCHES - 1,)),
    ]
    return one + one


def unit_cost(units, dots):
    return pl.CostEstimate(
        flops=dots * 2 * units * SEG0 * SEG0 * 256,
        transcendentals=units * SEG0 * SEG0,
        bytes_accessed=units * SEG0 * 1000,
    )


def vmem_specs(count):
    return [pl.BlockSpec(memory_space=pltpu.VMEM)] * count


def out_blocks(heads, rows):
    shapes = []
    for branch in range(1, BRANCHES):
        stride, count, units, split = branch_shape(branch, heads)
        width = max(count, 128)
        shapes.append((SEG0 // width, units, rows, width))
    return shapes


def exchange_forward(heads, own, sends):
    backs = send_shapes(heads, ROWS_OUT)[0]
    gots = send_shapes(heads, ROWS_IN)[0]
    first = jax.ShapeDtypeStruct((1, heads, ROWS_OUT, SEG0), BF)
    results = pl.pallas_call(
        partial(exchange_forward_kernel, heads),
        in_specs=vmem_specs(1 + len(sends)),
        out_specs=vmem_specs(1 + len(gots) + len(backs)),
        out_shape=[first] + gots + backs,
        scratch_shapes=[pltpu.VMEM(shape, BF) for shape in out_blocks(heads, ROWS_OUT)]
        + [pltpu.VMEM((ROWS_IN, SEG0), BF), pltpu.VMEM((ROWS_OUT, SEG0), BF)]
        + exchange_scratch(),
        compiler_params=params(collective_id=0, has_side_effects=True),
        cost_estimate=unit_cost(2 * heads, 2),
        name="exchange_forward",
    )(own, *sends)
    return results[0], results[1 : 1 + len(gots)], results[1 + len(gots) :]


def backward_unit(x, g, q_aug, gk, gv, result, base, queries, tile):
    if isinstance(base, int):
        lanes = slice(base, base + queries)
    else:
        lanes = pl.ds(pl.multiple_of(base, 128), queries)
    extra = g[E:, lanes].astype(F32)
    ids = lax.broadcasted_iota(jnp.int32, extra.shape, 0)
    q = x[0:E, lanes]
    q_aug[0:E, :queries] = q
    q_aug[E:, :queries] = jnp.where(ids >= 12, extra, x[3 * E :, lanes].astype(F32) * -FAR).astype(BF)
    bits = x[3 * E :, :].astype(F32)
    k_aug = jnp.concatenate([x[E : 2 * E, :], (1.0 - bits).astype(BF)], axis=0)
    k_rows = k_aug.T
    v_ids = lax.broadcasted_iota(jnp.int32, bits.shape, 0)
    v_bits = jnp.where(v_ids < 3, 1.0, 0.0).astype(BF)
    v_rows = jnp.concatenate([x[2 * E : 3 * E, :], v_bits], axis=0).T
    q_rows = jnp.concatenate([q, jnp.zeros((BIT_ROWS, queries), BF)], axis=0).T
    g_all = g[:, lanes]
    g_rows = g_all.T
    if queries < SEG0:
        result[0:E, :] = jnp.zeros((E, SEG0), BF)
    for step in range(queries // tile):
        column = step * tile
        span = slice(column, column + tile)
        p = jnp.exp2(jnp.dot(k_rows, q_aug[:, span], preferred_element_type=F32))
        gs = p * jnp.dot(v_rows, g_all[:, span], preferred_element_type=F32)
        p, gs = p.astype(BF), gs.astype(BF)
        target = span if isinstance(base, int) else pl.ds(pl.multiple_of(base + column, 128), tile)
        result[0:E, target] = jnp.dot(k_aug, gs, preferred_element_type=F32)[:E].astype(BF)
        new_k = jnp.dot(gs, q_rows[span], preferred_element_type=F32)
        new_v = jnp.dot(p, g_rows[span], preferred_element_type=F32)
        if step == 0:
            gk[...] = new_k
            gv[...] = new_v
        else:
            gk[...] += new_k
            gv[...] += new_v
    result[E : 2 * E, :] = (gk[...].T[:E] * LN2).astype(BF)
    result[2 * E :, :] = gv[...].T[:E].astype(BF)


class Names:
    def __init__(self, refs):
        self.refs = list(refs)

    def take(self, count):
        taken, self.refs = self.refs[:count], self.refs[count:]
        return taken

    def one(self):
        return self.take(1)[0]


ORDERS = {
    'u1': (1, 0), 'u2': (0, 1), 'd1': (1, 0), 'd2': (1, 0), 'o': (1, 0), 'i0': (1, 0), 'i1': (0, 1), 'i2': (0,
    1),
}
EARLY = [
    (2, 'o', 0), (3, 'u1', 0), (3, 'u2', 0), (5, 'o', 1), (5, 'd1', 0), (8, 'u1', 1), (8, 'u2', 1), (8, 'o',
    2), (10, 'o', 3), (13, 'o', 4), (13, 'd2', 0), (13, 'd1', 1), (13, 'u1', 2), (13, 'u2', 2),
]
TAIL = [
    ('u1', 3), 'gather', 'in1', ('i1', 0), ('o', 5), ('u2', 3), ('d1', 2), 'in0', ('i0', 0), ('d2', 1), ('i1',
    1), ('u1', 4), ('d2', 2), ('u2', 4), ('i0', 1), 'in2', ('d1', 3), ('o', 6), ('i2', 0), ('u1', 5), ('i0',
    2), 'one', ('d1', 4), ('i0', 3), ('d2', 3), ('i2', 1), ('i0', 4), ('d1', 5), ('u2', 5), ('i2', 2), 'norm',
    ('i0', 5), 'gain0', ('i1', 2), ('d2', 4), 'gain1', ('i2', 3), ('i1', 3), 'gain2', ('i1', 4), ('d1', 6),
    'gain3', ('i0', 6), ('i2', 4), 'gain4', ('i1', 5), ('d2', 5), ('i2', 5), ('u1', 6), ('i2', 6), ('i1', 6),
    ('d2', 6), ('u2', 6),
]


def stream_names(streams):
    pairs = streams // 2
    return [kind + str(i + 1) for i in range(pairs) for kind in "ud"] + ["o"]


def backward_kernel(heads, streams, *refs):
    branches = BRANCHES - 1
    names = Names(refs)
    starts, own, own_g = names.take(3)
    units_in, sends, parts = names.take(branches), names.take(branches), names.take(streams)
    normed, in_proj, x_rows, grad_hidden, gain, gains_two = names.take(6)
    totals, in_totals = names.take(streams), names.take(3)
    grad_tokens, gains_out = names.take(2)
    first = names.one()
    backs, gots, outs = names.take(branches), names.take(branches), names.take(branches)
    x, g, q_aug, gk, gv, result = names.take(6)
    total, grads, grads_t, normed_t, spread_rows, head_send, head_recv = names.take(7)
    gain_head, gain_one, gain_two, gain_rest = names.take(4)
    in_send, in_recv, in_local, out_send, out_recv, out_local = names.take(6)
    part_sem, head_sems, gain_sems = names.take(3)
    labels = stream_names(streams) + ["i0", "i1", "i2"]
    reductions = make_reductions(
        [ORDERS[label] for label in labels], list(totals) + list(in_totals), names.take(5 * streams + 15)
    )
    reductions = dict(zip(labels, reductions))

    shapes = [branch_shape(b, heads) for b in range(BRANCHES)]
    size, head_size = lax.axis_size("seq"), lax.axis_size("head")
    me, me_head = lax.axis_index("seq"), lax.axis_index("head")
    rest = size // 4
    tile = 256
    per_slot = x_rows.shape[0] // SLOTS
    width = x_rows.shape[1]

    fills = [pltpu.make_async_copy(parts[s], totals[s], part_sem.at[s]) for s in range(streams)]
    for fill in fills:
        fill.start()
    meet("seq", "head")

    def coming(branch):
        return group_copies(
            branch, sends[branch - 1], gots[branch - 1], lambda m: m, in_send, in_recv, in_local
        )

    def leaving(branch):
        out = outs[branch - 1]
        per = out.shape[-1] // shapes[branch][1]
        return group_copies(
            branch, out, backs[branch - 1], lambda m: m // per, out_send, out_recv, out_local
        )

    for branch in range(1, BRANCHES):
        for copy in coming(branch):
            copy.start()
    for fill in fills:
        fill.wait()

    def split_branch(branch):
        stride, lanes, units, split = shapes[branch]
        queries = SEG0 // split
        for copy in coming(branch):
            copy.wait()
        load_unit(units_in[branch - 1], 0, lanes, x)
        load_unit(gots[branch - 1], 0, lanes, g)
        backward_unit(x, g, q_aug, gk, gv, result, me % split * queries, queries, min(tile, queries))
        store_unit(outs[branch - 1], 0, slice(None), result, 0, SEG0)

    runs, at = [(0, 0, 0, heads // 2)], heads // 2
    split_at = None
    for branch in range(1, BRANCHES):
        if shapes[branch][3] == 1:
            runs.append((branch, at, 0, shapes[branch][2]))
            at += shapes[branch][2]
    split_at = at
    runs.append((0, at, heads // 2, heads - heads // 2))
    blocks = at + heads - heads // 2
    plan = {}
    for block, stream, step in EARLY:
        if stream in labels:
            plan.setdefault(block * blocks // 15, []).append((stream, step))

    @pl.loop(0, blocks)
    def _(block):
        for after, events in plan.items():

            @pl.when(block == after)
            def _(events=events):
                for stream, step in events:
                    reductions[stream].step(step)

        @pl.when(block == split_at)
        def _():
            for branch in range(1, BRANCHES):
                if shapes[branch][3] > 1:
                    split_branch(branch)
                    for copy in leaving(branch):
                        copy.start()

        for branch, low, unit, count in runs:

            @pl.when((block >= low) & (block < low + count))
            def _(branch=branch, low=low, unit=unit):
                if branch == 0:
                    x[...] = own[0, block - low + unit]
                    g[...] = own_g[0, block - low + unit]
                else:

                    @pl.when(block == low)
                    def _():
                        for copy in coming(branch):
                            copy.wait()

                    load_unit(units_in[branch - 1], block - low, shapes[branch][1], x)
                    load_unit(gots[branch - 1], block - low, shapes[branch][1], g)

        backward_unit(x, g, q_aug, gk, gv, result, 0, SEG0, tile)
        for branch, low, unit, count in runs:

            @pl.when((block >= low) & (block < low + count))
            def _(branch=branch, low=low, unit=unit, count=count):
                if branch == 0:
                    first[block - low + unit] = result[...]
                else:
                    store_unit(outs[branch - 1], block - low, slice(None), result, 0, SEG0)

                    @pl.when(block == low + count - 1)
                    def _():
                        for copy in leaving(branch):
                            copy.start()

    tasks = {}

    def task(work):
        tasks[work.__name__] = work

    @task
    def gather():
        for branch in range(1, BRANCHES):
            for copy in leaving(branch):
                copy.wait()

        @pl.loop(0, heads)
        def _(head):
            total[...] = first[head].astype(F32)
            for branch in range(1, BRANCHES):
                stride, lanes, per, split = shapes[branch]
                back, start = backs[branch - 1], starts[branch, head]
                if split == 1:
                    value = back[head // per, head % per].astype(F32)
                else:
                    value = back[head * split, 0].astype(F32)
                    for copy in range(1, split):
                        value = value + back[head * split + copy, 0].astype(F32)
                if lanes < 128:
                    share = 128 // lanes
                    value = moved_part(value, lanes, me % share, start % share)
                    start = start // share
                    lanes = 128
                for block in range(SEG0 // lanes):
                    span = slice(block * lanes, (block + 1) * lanes)
                    total[:, span] += jnp.where(start == block, value, 0.0)
            grads[0, head] = (total[0:E, :] * E ** (-0.5)).astype(BF)
            grads[1, head] = total[E : 2 * E, :].astype(BF)
            grads[2, head] = total[2 * E :, :].astype(BF)

        normed_t[...] = normed[...].T

    def in_gradient(j):
        rows_in = in_totals[0].shape[3]
        chunk = width // 2
        grads_t[j] = grads[j].reshape(heads * E, SEG0).T
        for half in range(2):
            value = jnp.dot(
                normed_t[half * chunk : (half + 1) * chunk], grads_t[j], preferred_element_type=F32
            ).astype(BF)
            for part in range(chunk // rows_in):
                index = half * (chunk // rows_in) + part
                in_totals[j][index // (2 * rest), index // rest % 2, index % rest] = value[
                    part * rows_in : (part + 1) * rows_in
                ]

    for j in range(3):
        tasks[f"in{j}"] = partial(in_gradient, j)

    def head_swaps():
        swaps = []
        for step in range(1, head_size):
            device = (me_head + step) % head_size
            swaps.append(
                pltpu.make_async_remote_copy(
                    src_ref=head_send.at[device],
                    dst_ref=head_recv.at[step - 1],
                    send_sem=head_sems.at[0, step - 1],
                    recv_sem=head_sems.at[1, step - 1],
                    device_id={"head": device},
                    device_id_type=pl.DeviceIdType.MESH,
                )
            )
        return swaps

    @task
    def one():
        for half in range(2):
            rows = slice(half * SEG0 // 2, (half + 1) * SEG0 // 2)
            value = jnp.zeros((SEG0 // 2, width), F32)
            for j in range(3):
                value = value + lax.dot_general(
                    grads_t[j, rows], in_proj[j], (((1,), (1,)), ((), ())), preferred_element_type=F32
                )
            value = value.astype(BF)
            for slot in range(SLOTS // 2):
                for device in range(head_size):
                    begin = (slot * head_size + device) * per_slot
                    place = (half * SLOTS // 2 + slot) * per_slot
                    head_send[device, place : place + per_slot] = value[begin : begin + per_slot]
        for swap in head_swaps():
            swap.start()

    @task
    def norm():
        for swap in head_swaps():
            swap.wait()
        gain_head[me_head] = jnp.zeros(gains_out.shape, F32)
        gain_head[me_head, 2:4] = gains_two[...]

        @pl.loop(0, SLOTS)
        def _(slot):
            rows = pl.ds(pl.multiple_of(slot * per_slot, per_slot), per_slot)
            grad = head_send[me_head, rows].astype(F32)
            for step in range(1, head_size):
                grad = grad + head_recv[step - 1, rows].astype(F32)
            values = x_rows[rows]
            centred = values - jnp.mean(values, axis=-1, keepdims=True)
            scale = lax.rsqrt(jnp.mean(centred * centred, axis=-1, keepdims=True) + EPS)
            unit = centred * scale
            scaled = grad * gain[...]
            inner = jnp.mean(scaled * unit, axis=-1, keepdims=True)
            out = grad_hidden[rows] + scale * (
                scaled - jnp.mean(scaled, axis=-1, keepdims=True) - unit * inner
            )
            place = slot % 2 * 8 + slot // 2 % 2 * 4 + slot // 4 % 2 * 2 + slot // 8
            for column in range(width // 128):
                lanes = slice(column * 128, (column + 1) * 128)
                spread_rows[column, pl.ds(place, per_slot, stride=SLOTS), :] = out[:, lanes]
            gain_head[me_head, 0:1] += jnp.sum(grad * unit, axis=0, keepdims=True)
            gain_head[me_head, 1:2] += jnp.sum(grad, axis=0, keepdims=True)

        for column in range(width // 128):
            grad_tokens[:, column * 128 : (column + 1) * 128] = spread_rows[column]

    def gain_copy(source, target, axis, device, sem):
        return pltpu.make_async_remote_copy(
            src_ref=source,
            dst_ref=target,
            send_sem=gain_sems.at[0, sem],
            recv_sem=gain_sems.at[1, sem],
            device_id={axis: device},
            device_id_type=pl.DeviceIdType.MESH,
        )

    def gain_copies(stage):
        if stage == 0:
            mine = gain_head.at[me_head]
            return [
                gain_copy(mine, mine, "head", (me_head + step) % head_size, step - 1)
                for step in range(1, head_size)
            ]
        if stage == 1:
            return [gain_copy(gain_one.at[0], gain_one.at[1], "seq", me + 1 - 2 * (me % 2), head_size)]
        if stage == 2:
            device = me + 2 - 4 * (me // 2 % 2)
            return [gain_copy(gain_two.at[0], gain_two.at[1], "seq", device, head_size + 1)]
        spot = me // 4
        block = gain_rest.at[spot]
        return [
            gain_copy(block, block, "seq", (spot + step) % rest * 4 + me % 4, head_size + 1 + step)
            for step in range(1, rest)
        ]

    def summed(ref, count):
        value = ref[0]
        for index in range(1, count):
            value = value + ref[index]
        return value

    def gain_stage(stage):
        if stage > 0:
            for swap in gain_copies(stage - 1):
                swap.wait()
        if stage == 1:
            gain_one[0] = summed(gain_head, head_size)
        elif stage == 2:
            gain_two[0] = summed(gain_one, 2)
        elif stage == 3:
            gain_rest[me // 4] = summed(gain_two, 2)
        elif stage == 4:
            gains_out[...] = summed(gain_rest, rest)
            return
        for swap in gain_copies(stage):
            swap.start()

    for stage in range(5):
        tasks[f"gain{stage}"] = partial(gain_stage, stage)

    for item in TAIL:
        if isinstance(item, str):
            tasks[item]()
        elif item[0] in labels:
            reductions[item[0]].step(item[1])


def backward(heads, starts, own, own_g, units, sends, terms, normed, in_proj, x_rows, grad_hidden, gain, gains_two):
    size, head_size = lax.axis_size("seq"), lax.axis_size("head")
    rest = size // 4
    rows, width = x_rows.shape
    parts = [reduction_parts(term, size) for term in terms]
    in_shape = (2, 2, rest, width // size, heads * E)
    scratch = []
    for part in parts:
        scratch += Reduction.scratch(size, *part.shape[-2:])
    for _ in range(3):
        scratch += Reduction.scratch(size, *in_shape[-2:])
    streams = len(parts)
    results = pl.pallas_call(
        partial(backward_kernel, heads, streams),
        in_specs=[pl.BlockSpec(memory_space=pltpu.SMEM)]
        + vmem_specs(2 + len(units) + len(sends))
        + [pl.BlockSpec(memory_space=pl.ANY)] * streams
        + vmem_specs(6),
        out_specs=vmem_specs(streams + 5),
        out_shape=[jax.ShapeDtypeStruct(part.shape, BF) for part in parts]
        + [jax.ShapeDtypeStruct(in_shape, BF)] * 3
        + [jax.ShapeDtypeStruct((rows, width), F32), jax.ShapeDtypeStruct((8, width), F32)],
        scratch_shapes=[pltpu.VMEM((heads, 3 * E, SEG0), BF)]
        + [pltpu.VMEM(shape.shape, BF) for shape in send_shapes(heads, 3 * E)[0]]
        + [pltpu.VMEM(shape.shape, BF) for shape in send_shapes(heads, ROWS_OUT)[0]]
        + [pltpu.VMEM(shape, BF) for shape in out_blocks(heads, 3 * E)]
        + [
            pltpu.VMEM((ROWS_IN, SEG0), BF),
            pltpu.VMEM((ROWS_OUT, SEG0), BF),
            pltpu.VMEM((ROWS_OUT, SEG0), BF),
            pltpu.VMEM((SEG0, ROWS_OUT), F32),
            pltpu.VMEM((SEG0, ROWS_OUT), F32),
            pltpu.VMEM((3 * E, SEG0), BF),
            pltpu.VMEM((3 * E, SEG0), F32),
            pltpu.VMEM((3, heads, E, SEG0), BF),
            pltpu.VMEM((3, SEG0, heads * E), BF),
            pltpu.VMEM((width, SEG0), BF),
            pltpu.VMEM((width // 128, rows, 128), F32),
            pltpu.VMEM((head_size, rows, width), BF),
            pltpu.VMEM((head_size - 1, rows, width), BF),
            pltpu.VMEM((head_size, 8, width), F32),
            pltpu.VMEM((2, 8, width), F32),
            pltpu.VMEM((2, 8, width), F32),
            pltpu.VMEM((rest, 8, width), F32),
        ]
        + exchange_scratch()
        + [
            pltpu.SemaphoreType.DMA((streams,)),
            pltpu.SemaphoreType.DMA((2, head_size - 1)),
            pltpu.SemaphoreType.DMA((2, head_size + 1 + rest)),
        ]
        + scratch,
        compiler_params=pltpu.CompilerParams(
            vmem_limit_bytes=60 * 2**20, collective_id=1, has_side_effects=True
        ),
        cost_estimate=unit_cost(2 * heads, 5),
        name="backward",
    )(starts, own, own_g, *units, *sends, *parts, normed, in_proj, x_rows, grad_hidden, gain, gains_two)
    sums = [reduction_whole(total) for total in results[: streams + 3]]
    return sums[:streams], sums[streams:], results[-2], results[-1]


def placed_part(value, count, start, place):
    if count >= 128:
        return value, None
    per = 128 // count
    lanes = lax.broadcasted_iota(jnp.int32, (1, 128), 1)
    return moved_part(value, count, place % per, start % per), lanes // count == start % per


def merge_kernel(heads, starts, place, first, *refs):
    seconds, (mixed, merged, lse) = refs[: BRANCHES - 1], refs[BRANCHES - 1 :]
    head = pl.program_id(0)
    extra = first[0, 0, E:, :].astype(F32)
    merged[0] = first[0, 0, :E, :].astype(F32)
    lse[0] = extra[0:1] + extra[1:2] + extra[2:3]
    for branch in range(1, BRANCHES):
        got = seconds[branch - 1]
        count = branch_shape(branch, heads)[1]
        start = starts[branch, head]
        lanes = aligned(start, count)
        for copy in range(got.shape[0]):
            value, mask = placed_part(got[copy, 0].astype(F32), count, start, place[0])
            new_lse = value[E : E + 1] + value[E + 1 : E + 2] + value[E + 2 : E + 3]
            if mask is not None:
                new_lse = jnp.where(mask, new_lse, -FAR)
            old_lse = lse[0, :, lanes]
            top = jnp.maximum(old_lse, new_lse)
            both = top + jnp.log2(jnp.exp2(old_lse - top) + jnp.exp2(new_lse - top))
            old_w = jnp.exp2(old_lse - both)
            new_w = jnp.exp2(new_lse - both)
            merged[0, :, lanes] = merged[0, :, lanes] * old_w + value[:E] * new_w
            lse[0, :, lanes] = both
    mixed[...] = merged[0].astype(BF)


def merge_heads(heads, starts, place, first, seconds):
    span = first.shape[-1]
    return pl.pallas_call(
        partial(merge_kernel, heads),
        grid_spec=pltpu.PrefetchScalarGridSpec(
            num_scalar_prefetch=2,
            grid=(heads,),
            in_specs=[pl.BlockSpec((1, 1, ROWS_OUT, span), lambda h, s, t: (0, h, 0, 0))]
            + send_shapes(heads, ROWS_OUT)[1],
            out_specs=[
                pl.BlockSpec((E, span), lambda h, s, t: (h, 0)),
                pl.BlockSpec((1, E, span), lambda h, s, t: (h, 0, 0)),
                pl.BlockSpec((1, 1, span), lambda h, s, t: (h, 0, 0)),
            ],
        ),
        out_shape=[
            jax.ShapeDtypeStruct((heads * E, span), BF),
            jax.ShapeDtypeStruct((heads, E, span), F32),
            jax.ShapeDtypeStruct((heads, 1, span), F32),
        ],
        compiler_params=params(),
        name="merge_heads",
    )(starts, place, first, *seconds)


def spread_kernel(heads, starts, place, grad, merged, lse, own, *sends):
    head = pl.program_id(0)
    low = grad[...].astype(BF)
    dots = jnp.sum(low.astype(F32) * merged[0], axis=0, keepdims=True)
    own[0, 0, :E, :] = low
    d = pieces_of(-dots)
    m = pieces_of(-lse[0])
    placed = {0: d[0], 1: d[1], 2: d[2], 12: m[0], 13: m[1], 14: m[2]}
    own[0, 0, E:, :] = row_block(placed, grad.shape[-1]).astype(BF)
    send_blocks(heads, head, starts, place, own, sends)


def spread_heads(heads, starts, place, grad, merged, lse):
    span = grad.shape[-1]
    sends, send_specs = send_shapes(heads, ROWS_OUT)
    return pl.pallas_call(
        partial(spread_kernel, heads),
        grid_spec=pltpu.PrefetchScalarGridSpec(
            num_scalar_prefetch=2,
            grid=(heads,),
            in_specs=[
                pl.BlockSpec((E, span), lambda h, s, t: (h, 0)),
                pl.BlockSpec((1, E, span), lambda h, s, t: (h, 0, 0)),
                pl.BlockSpec((1, 1, span), lambda h, s, t: (h, 0, 0)),
            ],
            out_specs=[pl.BlockSpec((1, 1, ROWS_OUT, span), lambda h, s, t: (0, h, 0, 0))] + send_specs,
        ),
        out_shape=[jax.ShapeDtypeStruct((1, heads, ROWS_OUT, span), BF)] + sends,
        compiler_params=params(),
        name="spread_heads",
    )(starts, place, grad, merged, lse)


def rolled(value, step):
    size = lax.axis_size("head")
    return lax.ppermute(value, "head", [(s, (s + step) % size) for s in range(size)])


def all_rows(own):
    size = lax.axis_size("head")
    me = lax.axis_index("head")
    got = [own] + [rolled(own, step) for step in range(1, size)]
    if size == 2:
        return [jnp.where(me == 0, got[0], got[1]), jnp.where(me == 0, got[1], got[0])]
    stacked = jnp.stack(got)
    return [stacked[(me - place) % size] for place in range(size)]


def sum_rows(parts):
    size = lax.axis_size("head")
    me = lax.axis_index("head")
    total = lax.dynamic_index_in_dim(parts, me, 0, keepdims=False).astype(F32)
    for step in range(1, size):
        sent = lax.dynamic_index_in_dim(parts, (me + step) % size, 0, keepdims=False)
        total = total + rolled(sent, step).astype(F32)
    return total


def local(
    tokens,
    documents,
    offsets,
    in_proj,
    out_proj,
    up_proj,
    down_proj,
    first_gain,
    first_shift,
    second_gain,
    second_shift,
    cotangent,
):
    head_count = lax.axis_size("head")
    seq_id = lax.axis_index("seq")
    row_count, width = tokens.shape
    seq_len = row_count * head_count
    heads = offsets.shape[1]
    per_slot = row_count // SLOTS
    gelu_exact = partial(jax.nn.gelu, approximate=False)

    ids = lax.broadcasted_iota(jnp.int32, (row_count, row_count), 0)
    slot = reversed_bits(ids // per_slot, 4)
    source = ids % per_slot * SLOTS + slot
    order = (source == lax.broadcasted_iota(jnp.int32, (row_count, row_count), 1)).astype(BF)

    def sorted_rows(values):
        return jnp.dot(order, values, preferred_element_type=F32)

    def shard_rows(own):
        parts = [part.reshape(SLOTS, per_slot, -1) for part in all_rows(own)]
        return jnp.stack(parts, axis=1).reshape(seq_len, -1)

    def device_parts(values):
        split = values.reshape(SLOTS, head_count, per_slot, -1)
        return jnp.moveaxis(split, 1, 0).reshape(head_count, row_count, -1)

    x_rows = sorted_rows(tokens)
    cot_low = sorted_rows(cotangent).astype(BF)
    normed_one = norm_rows(x_rows, first_gain, first_shift)
    gathered_one = shard_rows(normed_one.astype(BF))
    cot_all = shard_rows(cot_low)

    my_docs = lax.dynamic_slice_in_dim(documents, seq_id * seq_len, seq_len)
    my_docs = my_docs.reshape(head_count, per_slot, 2, 2, 2, 2).transpose(5, 4, 3, 2, 0, 1).reshape(seq_len)
    bit_ids = jnp.arange(BIT_ROWS, dtype=jnp.int32)[:, None]
    doc_bit = my_docs[None, :] // 2 ** (bit_ids % DOC_BITS) % 2
    bits = jnp.where(bit_ids < DOC_BITS, doc_bit, jnp.where(bit_ids < 2 * DOC_BITS, 1 - doc_bit, 0))
    bits = bits.astype(BF)
    starts = jnp.stack([reversed_bits(offsets[b], b) for b in range(BRANCHES)])

    scales = jnp.array([E ** (-0.5) * LOG2E, 1.0, 1.0], F32)[:, None, None]
    projected = jnp.einsum("td,jdc->jct", gathered_one, in_proj, preferred_element_type=F32)
    projected = (projected * scales).astype(BF)
    place = seq_id.astype(jnp.int32).reshape(1)
    own, *sends = pack_heads(heads, starts, place, projected, bits)
    first_out, units, outs = exchange_forward(heads, own, sends)
    mixed, merged, lse = merge_heads(heads, starts, place, first_out, outs)

    attn_part = jnp.einsum("ct,cd->td", mixed, out_proj, preferred_element_type=F32).astype(BF)
    hidden_one = x_rows + sum_rows(device_parts(attn_part))
    normed_two = norm_rows(hidden_one, second_gain, second_shift)
    gathered_two = shard_rows(normed_two.astype(BF))
    pre_act = jnp.dot(gathered_two, up_proj, preferred_element_type=F32)
    hidden, gelu_pull = jax.vjp(gelu_exact, pre_act)
    hidden = hidden.astype(BF)
    down_part = jnp.dot(hidden, down_proj, preferred_element_type=F32).astype(BF)
    block_rows = hidden_one + sum_rows(device_parts(down_part))
    block_out = jnp.dot(order.T, block_rows.astype(BF), preferred_element_type=F32).astype(BF)

    chunks = max(1, up_proj.shape[1] // width)

    def columns(values):
        return jnp.split(values, chunks, axis=1)

    grad_down = [
        jnp.einsum("tf,td->fd", part, cot_all, preferred_element_type=F32).astype(BF) for part in columns(hidden)
    ]
    grad_act = jnp.einsum("td,fd->tf", cot_all, down_proj, preferred_element_type=F32)
    grad_pre = gelu_pull(grad_act)[0].astype(BF)
    grad_up = [
        jnp.einsum("td,tf->df", gathered_two, part, preferred_element_type=F32).astype(BF)
        for part in columns(grad_pre)
    ]
    norm_part = jnp.einsum("tf,df->td", grad_pre, up_proj, preferred_element_type=F32).astype(BF)
    grad_normed_two = sum_rows(device_parts(norm_part))
    pull_two = jax.vjp(norm_rows, hidden_one, second_gain, second_shift)[1]
    grad_ln_two, grad_gain_two, grad_shift_two = pull_two(grad_normed_two)
    grad_hidden_one = cot_low.astype(F32) + grad_ln_two
    grad_attn = shard_rows(grad_hidden_one.astype(BF))
    grad_out = jnp.einsum("ct,td->cd", mixed, grad_attn, preferred_element_type=F32).astype(BF)
    grad_merged = jnp.einsum("td,cd->ct", grad_attn, out_proj, preferred_element_type=F32)

    own_g, *sends_g = spread_heads(heads, starts, place, grad_merged, merged, lse)
    terms = [term for pair in zip(grad_up, grad_down) for term in pair] + [grad_out]
    gains_two = jnp.stack([grad_gain_two, grad_shift_two])
    sums, grad_in, grad_tokens, gains = backward(
        heads, starts, own, own_g, units, sends_g, terms,
        gathered_one, in_proj, x_rows, grad_hidden_one, first_gain[None, :], gains_two,
    )
    return (
        block_out,
        grad_tokens,
        jnp.stack(grad_in).astype(F32),
        sums[-1].astype(F32),
        jnp.concatenate(sums[:-1:2], axis=1).astype(F32),
        jnp.concatenate(sums[1:-1:2], axis=0).astype(F32),
        gains[0],
        gains[1],
        gains[2],
        gains[3],
    )


def solution(mesh):
    placed = (
        P(("seq", "head"), None),
        P(),
        P(None, "head"),
        P(None, None, "head"),
        P("head", None),
        P(None, "head"),
        P("head", None),
        P(),
        P(),
        P(),
        P(),
        P(("seq", "head"), None),
    )
    return jax.shard_map(
        local,
        mesh=mesh,
        in_specs=placed,
        out_specs=(
            P(("seq", "head"), None),
            P(("seq", "head"), None),
            P(None, None, "head"),
            P("head", None),
            P(None, "head"),
            P("head", None),
            P(),
            P(),
            P(),
            P(),
        ),
        check_vma=False,
    )
```

```python
import math
from functools import partial

import jax
import jax.numpy as jnp
from jax import lax
from jax.experimental import pallas as pl
from jax.experimental.pallas import tpu as pltpu
from jax.sharding import PartitionSpec as P

E = 48
BRANCHES = 5
SEG0 = 1024
SLOTS = 16
BIT_ROWS = 16
DOC_BITS = 6
ROWS_IN = 3 * E + BIT_ROWS
ROWS_OUT = E + BIT_ROWS
EPS = 1e-05
FAR = 1e30
LOG2E = math.log2(math.e)
LN2 = math.log(2.0)
BF = jnp.bfloat16
F32 = jnp.float32
VMEM_LIMIT = 48 * 2**20


def params(**more):
    return pltpu.CompilerParams(vmem_limit_bytes=VMEM_LIMIT, **more)


def norm_rows(values, gain, shift):
    centre = jnp.mean(values, axis=-1, keepdims=True)
    centred = values - centre
    spread = jnp.mean(centred * centred, axis=-1, keepdims=True)
    return centred * lax.rsqrt(spread + EPS) * gain + shift


def reversed_bits(value, count):
    out = jnp.zeros_like(value)
    for bit in range(count):
        out = out * 2 + value // 2**bit % 2
    return out


def bit_reversed(value, count):
    return int(format(value, f"0{count}b")[::-1], 2)


def branch_shape(branch, heads):
    stride = 2**branch
    return (stride, SEG0 // stride, max(1, heads // stride), max(1, stride // heads))


def pieces_of(value):
    high = value.astype(BF).astype(F32)
    rest = value - high
    middle = rest.astype(BF).astype(F32)
    return high, middle, (rest - middle).astype(BF).astype(F32)


def row_block(placed, columns):
    ids = lax.broadcasted_iota(jnp.int32, (BIT_ROWS, columns), 0)
    block = jnp.zeros((BIT_ROWS, columns), F32)
    for row, value in placed.items():
        block = jnp.where(ids == row, value, block)
    return block


def lane_block(ref, rows, start, count):
    return ref[0, 0, rows, aligned(start, count)]


def aligned(start, count):
    if count >= 128:
        return pl.ds(pl.multiple_of(start * count, 128), count)
    return pl.ds(pl.multiple_of(start // (128 // count) * 128, 128), 128)


def moved_part(block, count, source, target):
    per = 128 // count
    lanes = lax.broadcasted_iota(jnp.int32, (1, 128), 1)
    out = block
    for shift in range(1, per):
        turned = jnp.concatenate([block[:, -shift * count :], block[:, : -shift * count]], axis=1)
        out = jnp.where((target - source) % per == shift, turned, out)
    return jnp.where(lanes // count == target, out, 0.0)


def pack_kernel(heads, starts, place, proj, bits, own, *sends):
    head = pl.program_id(0)
    for j in range(3):
        own[0, 0, j * E : (j + 1) * E, :] = proj[j]
    own[0, 0, 3 * E :, :] = bits[...]
    send_blocks(heads, head, starts, place, own, sends)


def send_blocks(heads, head, starts, place, own, sends):
    for branch in range(1, BRANCHES):
        count = branch_shape(branch, heads)[1]
        send = sends[branch - 1]
        start = starts[branch, head]
        block = lane_block(own, slice(None), start, count)
        if count < 128:
            per = 128 // count
            block = moved_part(block.astype(F32), count, start % per, place[0] % per).astype(BF)
        for copy in range(send.shape[0]):
            send[copy, 0] = block


def send_shapes(heads, rows):
    outs, specs = [], []
    for branch in range(1, BRANCHES):
        stride, count, per, split = branch_shape(branch, heads)
        count = max(count, 128)
        outs.append(jax.ShapeDtypeStruct((stride, per, rows, count), BF))
        specs.append(
            pl.BlockSpec((split, 1, rows, count), lambda h, s, t, per=per: (h // per, h % per, 0, 0))
        )
    return outs, specs


def pack_heads(heads, starts, place, proj, bits):
    span = proj.shape[-1]
    sends, send_specs = send_shapes(heads, ROWS_IN)
    return pl.pallas_call(
        partial(pack_kernel, heads),
        grid_spec=pltpu.PrefetchScalarGridSpec(
            num_scalar_prefetch=2,
            grid=(heads,),
            in_specs=[
                pl.BlockSpec((3, E, span), lambda h, s, t: (0, h, 0)),
                pl.BlockSpec((BIT_ROWS, span), lambda h, s, t: (0, 0)),
            ],
            out_specs=[pl.BlockSpec((1, 1, ROWS_IN, span), lambda h, s, t: (0, h, 0, 0))] + send_specs,
        ),
        out_shape=[jax.ShapeDtypeStruct((1, heads, ROWS_IN, span), BF)] + sends,
        compiler_params=params(),
        name="pack_heads",
    )(starts, place, proj, bits)


def load_unit(ref, unit, count, x):
    if ref.shape[0] == 1:
        x[...] = ref[0, unit]
        return
    width = ref.shape[-1]
    per = width // count
    for block in range(ref.shape[0] // per):
        value = ref[block * per, unit]
        for other in range(1, per):
            value = value + ref[block * per + other, unit]
        x[:, block * width : (block + 1) * width] = value


def store_unit(ref, unit, rows, value, column, count):
    width = ref.shape[-1]
    size = min(width, count)
    for start in range(column, column + count, size):
        lanes = slice(start % width, start % width + size)
        ref[start // width, unit, rows, lanes] = value[:, start - column : start - column + size]


def forward_unit(x, q_aug, base, queries, tile, put):
    if isinstance(base, int):
        lanes = slice(base, base + queries)
    else:
        lanes = pl.ds(pl.multiple_of(base, 128), queries)
    q_aug[0:E, :queries] = x[0:E, lanes]
    q_aug[E:, :queries] = (x[3 * E :, lanes].astype(F32) * -FAR).astype(BF)
    bits = x[3 * E :, :].astype(F32)
    k_rows = jnp.concatenate([x[E : 2 * E, :], (1.0 - bits).astype(BF)], axis=0).T
    v_aug = jnp.concatenate([x[2 * E : 3 * E, :], jnp.ones(bits.shape, BF)], axis=0)
    for step in range(queries // tile):
        column = step * tile
        s = jnp.dot(k_rows, q_aug[:, column : column + tile], preferred_element_type=F32)
        top = jnp.max(s, axis=0, keepdims=True)
        p = jnp.exp2(s - top).astype(BF)
        o = jnp.dot(v_aug, p, preferred_element_type=F32)
        total = o[E : E + 1]
        high, middle, low = pieces_of(top + jnp.log2(total))
        block = row_block({0: high, 1: middle, 2: low}, tile)
        put(column, jnp.concatenate([o[:E] * (1.0 / total), block], axis=0).astype(BF))


def group_place(branch):
    stride = 2**branch
    me = lax.axis_index("seq")
    return me // stride * stride, me % stride


def meet(*axes):
    barrier = pltpu.get_barrier_semaphore()
    count = 0
    for axis in axes:
        size = lax.axis_size(axis)
        me = lax.axis_index(axis)

        @pl.loop(1, size)
        def _(step):
            pl.semaphore_signal(
                barrier, inc=1, device_id={axis: (me + step) % size}, device_id_type=pl.DeviceIdType.MESH
            )

        count += size - 1
    pl.semaphore_wait(barrier, count)


class Reduction:
    STEPS = 7

    def __init__(self, order, total, half, quarter, others, send, recv, begun=False):
        self.total, self.begun = total, begun
        self.half, self.quarter, self.others = half, quarter, others
        self.send, self.recv = send, recv
        me = lax.axis_index("seq")
        self.rest = lax.axis_size("seq") // 4
        self.me = me
        bits = (me % 2, me // 2 % 2)
        self.bits = [bits[bit] for bit in order]
        self.partners = [me + (1 - 2 * bits[bit]) * 2**bit for bit in order]
        self.place = me // 4

    def copy(self, source, target, device, sem):
        return pltpu.make_async_remote_copy(
            src_ref=source,
            dst_ref=target,
            send_sem=self.send.at[sem],
            recv_sem=self.recv.at[sem],
            device_id={"seq": device},
            device_id_type=pl.DeviceIdType.MESH,
        )

    def copies(self, number):
        one, two = self.bits
        rest = self.rest
        others = []
        for step in range(1, rest):
            place = (self.place + step) % rest
            others.append((step, place, place * 4 + self.me % 4))
        if number == 0:
            return [self.copy(self.total.at[1 - one], self.half, self.partners[0], 0)]
        if number == 1:
            return [self.copy(self.half.at[1 - two], self.quarter, self.partners[1], 1)]
        if number == 2:
            return [
                self.copy(self.quarter.at[place], self.others.at[step - 1], device, 1 + step)
                for step, place, device in others
            ]
        if number == 3:
            block = self.total.at[one, two, self.place]
            return [self.copy(block, block, device, rest + step) for step, place, device in others]
        if number == 4:
            block = self.total.at[one, two]
            return [self.copy(block, block, self.partners[1], 2 * rest)]
        if number == 5:
            block = self.total.at[one]
            return [self.copy(block, block, self.partners[0], 2 * rest + 1)]
        return []

    def finish_first(self):
        one, rest = self.bits[0], self.rest
        for copy in self.copies(0):
            copy.wait()

        @pl.loop(0, 2 * rest)
        def _(i):
            j, z = i // rest, i % rest
            mine = self.total[one, j, z].astype(F32)
            self.half[j, z] = (mine + self.half[j, z].astype(F32)).astype(BF)

    def step(self, number):
        one, two = self.bits
        rest = self.rest
        if number == 0 and self.begun:
            return
        if number == 1:
            if not self.begun:
                self.finish_first()
        elif number > 0:
            for copy in self.copies(number - 1):
                copy.wait()
        if number == 2:

            @pl.loop(0, rest)
            def _(z):
                mine = self.half[two, z].astype(F32)
                self.quarter[z] = (mine + self.quarter[z].astype(F32)).astype(BF)

        elif number == 3:
            mine = self.quarter[self.place].astype(F32)
            for step in range(1, rest):
                mine = mine + self.others[step - 1].astype(F32)
            self.total[one, two, self.place] = mine.astype(BF)
        for copy in self.copies(number):
            copy.start()

    @staticmethod
    def scratch(size, rows, columns):
        rest = size // 4
        count = 2 * rest + 2
        return [
            pltpu.VMEM((2, rest, rows, columns), BF),
            pltpu.VMEM((rest, rows, columns), BF),
            pltpu.VMEM((rest - 1, rows, columns), BF),
            pltpu.SemaphoreType.DMA((count,)),
            pltpu.SemaphoreType.DMA((count,)),
        ]


def reduction_parts(value, size):
    rows, columns = value.shape
    return value.reshape(2, 2, size // 4, rows // size, columns)


def reduction_whole(value):
    return value.reshape(-1, value.shape[-1])


def make_reductions(orders, totals, scratch):
    out = []
    for order, total in zip(orders, totals):
        out.append(Reduction(order, total, *scratch[:5]))
        scratch = scratch[5:]
    return out


def group_copies(branch, source, target, source_block, send_sems, recv_sems, local_sem):
    stride = 2**branch
    base, place = group_place(branch)
    first = stride - branch - 2
    copies = [
        pltpu.make_async_copy(source.at[source_block(place)], target.at[place], local_sem.at[branch - 1])
    ]
    for step in range(1, stride):
        member = (place + step) % stride
        copies.append(
            pltpu.make_async_remote_copy(
                src_ref=source.at[source_block(member)],
                dst_ref=target.at[place],
                send_sem=send_sems.at[first + step],
                recv_sem=recv_sems.at[first + step],
                device_id={"seq": base + member},
                device_id_type=pl.DeviceIdType.MESH,
            )
        )
    return copies


def exchange_forward_kernel(heads, own, *refs):
    count = BRANCHES - 1
    sends, refs = refs[:count], refs[count:]
    first, refs = refs[0], refs[1:]
    gots, refs = refs[:count], refs[count:]
    backs, refs = refs[:count], refs[count:]
    outs, refs = refs[:count], refs[count:]
    x, q_aug, in_send, in_recv, in_local, out_send, out_recv, out_local = refs
    tile = 256
    meet("seq")
    coming = {}
    for branch in range(1, BRANCHES):
        coming[branch] = group_copies(
            branch, sends[branch - 1], gots[branch - 1], lambda m: m, in_send, in_recv, in_local
        )
        for copy in coming[branch]:
            copy.start()

    @pl.loop(0, heads)
    def _(head):
        x[...] = own[0, head]

        def put(column, value):
            first[0, head, :, column : column + tile] = value

        forward_unit(x, q_aug, 0, SEG0, tile, put)

    leaving = []
    for branch in range(1, BRANCHES):
        stride, lanes, units, split = branch_shape(branch, heads)
        got, out = gots[branch - 1], outs[branch - 1]
        for copy in coming[branch]:
            copy.wait()
        queries = SEG0 // split
        base = 0 if split == 1 else lax.axis_index("seq") % split * queries

        @pl.loop(0, units)
        def _(unit):
            load_unit(got, unit, lanes, x)
            if split == 1:

                def put(column, value):
                    store_unit(out, unit, slice(None), value, column, value.shape[1])

            else:
                empty = row_block({0: -FAR}, 128)
                empty = jnp.concatenate([jnp.zeros((E, 128), F32), empty], axis=0).astype(BF)
                for block in range(SEG0 // 128):
                    store_unit(out, unit, slice(None), empty, block * 128, 128)

                def put(column, value):
                    width = out.shape[-1]
                    for start in range(0, value.shape[1], width):
                        block = (base + column + start) // width
                        out[block, unit] = value[:, start : start + width]

            forward_unit(x, q_aug, base, queries, min(tile, queries), put)

        per = out.shape[-1] // lanes
        copies = group_copies(
            branch, out, backs[branch - 1], lambda m: m // per, out_send, out_recv, out_local
        )
        for copy in copies:
            copy.start()
        leaving += copies
    for copy in leaving:
        copy.wait()


def exchange_scratch():
    copies = 2**BRANCHES - 2 - BRANCHES + 1
    one = [
        pltpu.SemaphoreType.DMA((copies,)),
        pltpu.SemaphoreType.DMA((copies,)),
        pltpu.SemaphoreType.DMA((BRANCHES - 1,)),
    ]
    return one + one


def unit_cost(units, dots):
    return pl.CostEstimate(
        flops=dots * 2 * units * SEG0 * SEG0 * 256,
        transcendentals=units * SEG0 * SEG0,
        bytes_accessed=units * SEG0 * 1000,
    )


def vmem_specs(count):
    return [pl.BlockSpec(memory_space=pltpu.VMEM)] * count


def out_blocks(heads, rows):
    shapes = []
    for branch in range(1, BRANCHES):
        stride, count, units, split = branch_shape(branch, heads)
        width = max(count, 128)
        shapes.append((SEG0 // width, units, rows, width))
    return shapes


def exchange_forward(heads, own, sends):
    backs = send_shapes(heads, ROWS_OUT)[0]
    gots = send_shapes(heads, ROWS_IN)[0]
    first = jax.ShapeDtypeStruct((1, heads, ROWS_OUT, SEG0), BF)
    results = pl.pallas_call(
        partial(exchange_forward_kernel, heads),
        in_specs=vmem_specs(1 + len(sends)),
        out_specs=vmem_specs(1 + len(gots) + len(backs)),
        out_shape=[first] + gots + backs,
        scratch_shapes=[pltpu.VMEM(shape, BF) for shape in out_blocks(heads, ROWS_OUT)]
        + [pltpu.VMEM((ROWS_IN, SEG0), BF), pltpu.VMEM((ROWS_OUT, SEG0), BF)]
        + exchange_scratch(),
        compiler_params=params(collective_id=0, has_side_effects=True),
        cost_estimate=unit_cost(2 * heads, 2),
        name="exchange_forward",
    )(own, *sends)
    return results[0], results[1 : 1 + len(gots)], results[1 + len(gots) :]


def backward_unit(x, g, q_aug, gk, gv, result, base, queries, tile):
    if isinstance(base, int):
        lanes = slice(base, base + queries)
    else:
        lanes = pl.ds(pl.multiple_of(base, 128), queries)
    extra = g[E:, lanes].astype(F32)
    ids = lax.broadcasted_iota(jnp.int32, extra.shape, 0)
    q = x[0:E, lanes]
    q_aug[0:E, :queries] = q
    q_aug[E:, :queries] = jnp.where(ids >= 12, extra, x[3 * E :, lanes].astype(F32) * -FAR).astype(BF)
    bits = x[3 * E :, :].astype(F32)
    k_aug = jnp.concatenate([x[E : 2 * E, :], (1.0 - bits).astype(BF)], axis=0)
    k_rows = k_aug.T
    v_ids = lax.broadcasted_iota(jnp.int32, bits.shape, 0)
    v_bits = jnp.where(v_ids < 3, 1.0, 0.0).astype(BF)
    v_rows = jnp.concatenate([x[2 * E : 3 * E, :], v_bits], axis=0).T
    q_rows = jnp.concatenate([q, jnp.zeros((BIT_ROWS, queries), BF)], axis=0).T
    g_all = g[:, lanes]
    g_rows = g_all.T
    if queries < SEG0:
        result[0:E, :] = jnp.zeros((E, SEG0), BF)
    for step in range(queries // tile):
        column = step * tile
        span = slice(column, column + tile)
        p = jnp.exp2(jnp.dot(k_rows, q_aug[:, span], preferred_element_type=F32))
        gs = p * jnp.dot(v_rows, g_all[:, span], preferred_element_type=F32)
        p, gs = p.astype(BF), gs.astype(BF)
        target = span if isinstance(base, int) else pl.ds(pl.multiple_of(base + column, 128), tile)
        result[0:E, target] = jnp.dot(k_aug, gs, preferred_element_type=F32)[:E].astype(BF)
        new_k = jnp.dot(gs, q_rows[span], preferred_element_type=F32)
        new_v = jnp.dot(p, g_rows[span], preferred_element_type=F32)
        if step == 0:
            gk[...] = new_k
            gv[...] = new_v
        else:
            gk[...] += new_k
            gv[...] += new_v
    result[E : 2 * E, :] = (gk[...].T[:E] * LN2).astype(BF)
    result[2 * E :, :] = gv[...].T[:E].astype(BF)


class Names:
    def __init__(self, refs):
        self.refs = list(refs)

    def take(self, count):
        taken, self.refs = self.refs[:count], self.refs[count:]
        return taken

    def one(self):
        return self.take(1)[0]


ORDERS = {
    'u1': (0, 1), 'u2': (0, 1), 'd1': (1, 0), 'd2': (1, 0), 'o': (0, 1), 'i0': (1, 0), 'i1': (1, 0), 'i2': (0,
    1),
}
EARLY = [
    (0, 'd1', 0), (0, 'u1', 0), (0, 'd1', 1), (0, 'u2', 0), (0, 'u1', 1), (2, 'o', 0), (4, 'u2', 1), (5, 'u1',
    2), (7, 'd1', 2), (9, 'u1', 3), (10, 'd2', 0), (12, 'd2', 1), (12, 'o', 1), (12, 'd1', 3), (13, 'u2', 2),
    (14, 'u1', 4),
]
TAIL = [
    'gather', ('d1', 4), 'in1', ('i1', 0), ('d2', 2), 'in2', ('u2', 3), ('i2', 0), 'in0', ('i0', 0), ('d2',
    3), ('i1', 1), ('i2', 1), ('u1', 5), ('u2', 4), ('d2', 4), ('d1', 5), ('o', 2), ('i2', 2), ('i0', 1),
    ('i1', 2), ('i2', 3), 'one', ('d2', 5), ('o', 3), ('i1', 3), ('u1', 6), ('u2', 5), 'norm', ('i2', 4),
    'gain0', ('i0', 2), ('i1', 4), ('i0', 3), 'gain1', ('o', 4), ('i0', 4), ('i2', 5), 'gain2', ('i1', 5),
    ('o', 5), ('i0', 5), 'gain3', ('i0', 6), ('d2', 6), ('u2', 6), 'gain4', ('d1', 6), ('i1', 6), ('i2', 6),
    ('o', 6),
]


def stream_names(streams):
    pairs = streams // 2
    return [kind + str(i + 1) for i in range(pairs) for kind in "ud"] + ["o"]


def backward_kernel(heads, streams, *refs):
    branches = BRANCHES - 1
    names = Names(refs)
    starts, own, own_g = names.take(3)
    units_in, sends, parts = names.take(branches), names.take(branches), names.take(streams)
    normed, in_proj, x_rows, grad_hidden, gain, gains_two = names.take(6)
    totals, in_totals = names.take(streams), names.take(3)
    grad_tokens, gains_out = names.take(2)
    first = names.one()
    backs, gots, outs = names.take(branches), names.take(branches), names.take(branches)
    x, g, q_aug, gk, gv, result = names.take(6)
    total, grads, grads_t, normed_t, spread_rows, head_send, head_recv = names.take(7)
    gain_head, gain_one, gain_two, gain_rest = names.take(4)
    in_send, in_recv, in_local, out_send, out_recv, out_local = names.take(6)
    part_sem, head_sems, gain_sems = names.take(3)
    labels = stream_names(streams) + ["i0", "i1", "i2"]
    reductions = make_reductions(
        [ORDERS[label] for label in labels], list(totals) + list(in_totals), names.take(5 * streams + 15)
    )
    reductions = dict(zip(labels, reductions))
    for label in labels[: streams - 1]:
        reductions[label].begun = True

    shapes = [branch_shape(b, heads) for b in range(BRANCHES)]
    size, head_size = lax.axis_size("seq"), lax.axis_size("head")
    me, me_head = lax.axis_index("seq"), lax.axis_index("head")
    rest = size // 4
    tile = 256
    per_slot = x_rows.shape[0] // SLOTS
    width = x_rows.shape[1]

    fills = [
        pltpu.make_async_copy(parts[s], reductions[labels[s]].half, part_sem.at[s]) for s in range(streams - 1)
    ] + [pltpu.make_async_copy(parts[-1], totals[-1], part_sem.at[streams - 1])]
    for fill in fills:
        fill.start()
    meet("seq", "head")

    def coming(branch):
        return group_copies(
            branch, sends[branch - 1], gots[branch - 1], lambda m: m, in_send, in_recv, in_local
        )

    def leaving(branch):
        out = outs[branch - 1]
        per = out.shape[-1] // shapes[branch][1]
        return group_copies(
            branch, out, backs[branch - 1], lambda m: m // per, out_send, out_recv, out_local
        )

    for branch in range(1, BRANCHES):
        for copy in coming(branch):
            copy.start()
    for fill in fills:
        fill.wait()

    def split_branch(branch):
        stride, lanes, units, split = shapes[branch]
        queries = SEG0 // split
        for copy in coming(branch):
            copy.wait()
        load_unit(units_in[branch - 1], 0, lanes, x)
        load_unit(gots[branch - 1], 0, lanes, g)
        backward_unit(x, g, q_aug, gk, gv, result, me % split * queries, queries, min(tile, queries))
        store_unit(outs[branch - 1], 0, slice(None), result, 0, SEG0)

    runs, at = [(0, 0, 0, heads // 2)], heads // 2
    split_at = None
    for branch in range(1, BRANCHES):
        if shapes[branch][3] == 1:
            runs.append((branch, at, 0, shapes[branch][2]))
            at += shapes[branch][2]
    split_at = at
    runs.append((0, at, heads // 2, heads - heads // 2))
    blocks = at + heads - heads // 2
    plan = {}
    for block, stream, step in EARLY:
        if stream in labels:
            plan.setdefault(block * blocks // 15, []).append((stream, step))

    @pl.loop(0, blocks)
    def _(block):
        for after, events in plan.items():

            @pl.when(block == after)
            def _(events=events):
                for stream, step in events:
                    reductions[stream].step(step)

        @pl.when(block == split_at)
        def _():
            for branch in range(1, BRANCHES):
                if shapes[branch][3] > 1:
                    split_branch(branch)
                    for copy in leaving(branch):
                        copy.start()

        for branch, low, unit, count in runs:

            @pl.when((block >= low) & (block < low + count))
            def _(branch=branch, low=low, unit=unit):
                if branch == 0:
                    x[...] = own[0, block - low + unit]
                    g[...] = own_g[0, block - low + unit]
                else:

                    @pl.when(block == low)
                    def _():
                        for copy in coming(branch):
                            copy.wait()

                    load_unit(units_in[branch - 1], block - low, shapes[branch][1], x)
                    load_unit(gots[branch - 1], block - low, shapes[branch][1], g)

        backward_unit(x, g, q_aug, gk, gv, result, 0, SEG0, tile)
        for branch, low, unit, count in runs:

            @pl.when((block >= low) & (block < low + count))
            def _(branch=branch, low=low, unit=unit, count=count):
                if branch == 0:
                    first[block - low + unit] = result[...]
                else:
                    store_unit(outs[branch - 1], block - low, slice(None), result, 0, SEG0)

                    @pl.when(block == low + count - 1)
                    def _():
                        for copy in leaving(branch):
                            copy.start()

    tasks = {}

    def task(work):
        tasks[work.__name__] = work

    @task
    def gather():
        for branch in range(1, BRANCHES):
            for copy in leaving(branch):
                copy.wait()

        @pl.loop(0, heads)
        def _(head):
            total[...] = first[head].astype(F32)
            for branch in range(1, BRANCHES):
                stride, lanes, per, split = shapes[branch]
                back, start = backs[branch - 1], starts[branch, head]
                if split == 1:
                    value = back[head // per, head % per].astype(F32)
                else:
                    value = back[head * split, 0].astype(F32)
                    for copy in range(1, split):
                        value = value + back[head * split + copy, 0].astype(F32)
                if lanes < 128:
                    share = 128 // lanes
                    value = moved_part(value, lanes, me % share, start % share)
                    start = start // share
                    lanes = 128
                for block in range(SEG0 // lanes):
                    span = slice(block * lanes, (block + 1) * lanes)
                    total[:, span] += jnp.where(start == block, value, 0.0)
            grads[0, head] = (total[0:E, :] * E ** (-0.5)).astype(BF)
            grads[1, head] = total[E : 2 * E, :].astype(BF)
            grads[2, head] = total[2 * E :, :].astype(BF)

        normed_t[...] = normed[...].T

    def in_gradient(j):
        rows_in = in_totals[0].shape[3]
        chunk = width // 2
        grads_t[j] = grads[j].reshape(heads * E, SEG0).T
        for half in range(2):
            value = jnp.dot(
                normed_t[half * chunk : (half + 1) * chunk], grads_t[j], preferred_element_type=F32
            ).astype(BF)
            for part in range(chunk // rows_in):
                index = half * (chunk // rows_in) + part
                in_totals[j][index // (2 * rest), index // rest % 2, index % rest] = value[
                    part * rows_in : (part + 1) * rows_in
                ]

    for j in range(3):
        tasks[f"in{j}"] = partial(in_gradient, j)

    def head_swaps():
        swaps = []
        for step in range(1, head_size):
            device = (me_head + step) % head_size
            swaps.append(
                pltpu.make_async_remote_copy(
                    src_ref=head_send.at[device],
                    dst_ref=head_recv.at[step - 1],
                    send_sem=head_sems.at[0, step - 1],
                    recv_sem=head_sems.at[1, step - 1],
                    device_id={"head": device},
                    device_id_type=pl.DeviceIdType.MESH,
                )
            )
        return swaps

    @task
    def one():
        for half in range(2):
            rows = slice(half * SEG0 // 2, (half + 1) * SEG0 // 2)
            value = jnp.zeros((SEG0 // 2, width), F32)
            for j in range(3):
                value = value + lax.dot_general(
                    grads_t[j, rows], in_proj[j], (((1,), (1,)), ((), ())), preferred_element_type=F32
                )
            value = value.astype(BF)
            for slot in range(SLOTS // 2):
                for device in range(head_size):
                    begin = (slot * head_size + device) * per_slot
                    place = (half * SLOTS // 2 + slot) * per_slot
                    head_send[device, place : place + per_slot] = value[begin : begin + per_slot]
        for swap in head_swaps():
            swap.start()

    @task
    def norm():
        for swap in head_swaps():
            swap.wait()
        gain_head[me_head] = jnp.zeros(gains_out.shape, F32)
        gain_head[me_head, 2:4] = gains_two[...]

        @pl.loop(0, SLOTS)
        def _(slot):
            rows = pl.ds(pl.multiple_of(slot * per_slot, per_slot), per_slot)
            grad = head_send[me_head, rows].astype(F32)
            for step in range(1, head_size):
                grad = grad + head_recv[step - 1, rows].astype(F32)
            values = x_rows[rows]
            centred = values - jnp.mean(values, axis=-1, keepdims=True)
            scale = lax.rsqrt(jnp.mean(centred * centred, axis=-1, keepdims=True) + EPS)
            unit = centred * scale
            scaled = grad * gain[...]
            inner = jnp.mean(scaled * unit, axis=-1, keepdims=True)
            out = grad_hidden[rows] + scale * (
                scaled - jnp.mean(scaled, axis=-1, keepdims=True) - unit * inner
            )
            place = slot % 2 * 8 + slot // 2 % 2 * 4 + slot // 4 % 2 * 2 + slot // 8
            for column in range(width // 128):
                lanes = slice(column * 128, (column + 1) * 128)
                spread_rows[column, pl.ds(place, per_slot, stride=SLOTS), :] = out[:, lanes]
            gain_head[me_head, 0:1] += jnp.sum(grad * unit, axis=0, keepdims=True)
            gain_head[me_head, 1:2] += jnp.sum(grad, axis=0, keepdims=True)

        for column in range(width // 128):
            grad_tokens[:, column * 128 : (column + 1) * 128] = spread_rows[column]

    def gain_copy(source, target, axis, device, sem):
        return pltpu.make_async_remote_copy(
            src_ref=source,
            dst_ref=target,
            send_sem=gain_sems.at[0, sem],
            recv_sem=gain_sems.at[1, sem],
            device_id={axis: device},
            device_id_type=pl.DeviceIdType.MESH,
        )

    def gain_copies(stage):
        if stage == 0:
            mine = gain_head.at[me_head]
            return [
                gain_copy(mine, mine, "head", (me_head + step) % head_size, step - 1)
                for step in range(1, head_size)
            ]
        if stage == 1:
            return [gain_copy(gain_one.at[0], gain_one.at[1], "seq", me + 1 - 2 * (me % 2), head_size)]
        if stage == 2:
            device = me + 2 - 4 * (me // 2 % 2)
            return [gain_copy(gain_two.at[0], gain_two.at[1], "seq", device, head_size + 1)]
        spot = me // 4
        block = gain_rest.at[spot]
        return [
            gain_copy(block, block, "seq", (spot + step) % rest * 4 + me % 4, head_size + 1 + step)
            for step in range(1, rest)
        ]

    def summed(ref, count):
        value = ref[0]
        for index in range(1, count):
            value = value + ref[index]
        return value

    def gain_stage(stage):
        if stage > 0:
            for swap in gain_copies(stage - 1):
                swap.wait()
        if stage == 1:
            gain_one[0] = summed(gain_head, head_size)
        elif stage == 2:
            gain_two[0] = summed(gain_one, 2)
        elif stage == 3:
            gain_rest[me // 4] = summed(gain_two, 2)
        elif stage == 4:
            gains_out[...] = summed(gain_rest, rest)
            return
        for swap in gain_copies(stage):
            swap.start()

    for stage in range(5):
        tasks[f"gain{stage}"] = partial(gain_stage, stage)

    for item in TAIL:
        if isinstance(item, str):
            tasks[item]()
        elif item[0] in labels:
            reductions[item[0]].step(item[1])


def backward(heads, starts, own, own_g, units, sends, parts, normed, in_proj, x_rows, grad_hidden, gain, gains_two):
    size, head_size = lax.axis_size("seq"), lax.axis_size("head")
    rest = size // 4
    rows, width = x_rows.shape
    in_shape = (2, 2, rest, width // size, heads * E)
    scratch = []
    for part in parts:
        scratch += Reduction.scratch(size, *part.shape[-2:])
    for _ in range(3):
        scratch += Reduction.scratch(size, *in_shape[-2:])
    streams = len(parts)
    results = pl.pallas_call(
        partial(backward_kernel, heads, streams),
        in_specs=[pl.BlockSpec(memory_space=pltpu.SMEM)]
        + vmem_specs(2 + len(units) + len(sends))
        + [pl.BlockSpec(memory_space=pl.ANY)] * streams
        + vmem_specs(6),
        out_specs=vmem_specs(streams + 5),
        out_shape=[jax.ShapeDtypeStruct((2, 2, rest) + part.shape[-2:], BF) for part in parts]
        + [jax.ShapeDtypeStruct(in_shape, BF)] * 3
        + [jax.ShapeDtypeStruct((rows, width), F32), jax.ShapeDtypeStruct((8, width), F32)],
        scratch_shapes=[pltpu.VMEM((heads, 3 * E, SEG0), BF)]
        + [pltpu.VMEM(shape.shape, BF) for shape in send_shapes(heads, 3 * E)[0]]
        + [pltpu.VMEM(shape.shape, BF) for shape in send_shapes(heads, ROWS_OUT)[0]]
        + [pltpu.VMEM(shape, BF) for shape in out_blocks(heads, 3 * E)]
        + [
            pltpu.VMEM((ROWS_IN, SEG0), BF),
            pltpu.VMEM((ROWS_OUT, SEG0), BF),
            pltpu.VMEM((ROWS_OUT, SEG0), BF),
            pltpu.VMEM((SEG0, ROWS_OUT), F32),
            pltpu.VMEM((SEG0, ROWS_OUT), F32),
            pltpu.VMEM((3 * E, SEG0), BF),
            pltpu.VMEM((3 * E, SEG0), F32),
            pltpu.VMEM((3, heads, E, SEG0), BF),
            pltpu.VMEM((3, SEG0, heads * E), BF),
            pltpu.VMEM((width, SEG0), BF),
            pltpu.VMEM((width // 128, rows, 128), F32),
            pltpu.VMEM((head_size, rows, width), BF),
            pltpu.VMEM((head_size - 1, rows, width), BF),
            pltpu.VMEM((head_size, 8, width), F32),
            pltpu.VMEM((2, 8, width), F32),
            pltpu.VMEM((2, 8, width), F32),
            pltpu.VMEM((rest, 8, width), F32),
        ]
        + exchange_scratch()
        + [
            pltpu.SemaphoreType.DMA((streams,)),
            pltpu.SemaphoreType.DMA((2, head_size - 1)),
            pltpu.SemaphoreType.DMA((2, head_size + 1 + rest)),
        ]
        + scratch,
        compiler_params=pltpu.CompilerParams(
            vmem_limit_bytes=60 * 2**20, collective_id=1, has_side_effects=True
        ),
        cost_estimate=unit_cost(2 * heads, 5),
        name="backward",
    )(starts, own, own_g, *units, *sends, *parts, normed, in_proj, x_rows, grad_hidden, gain, gains_two)
    sums = [reduction_whole(total) for total in results[: streams + 3]]
    return sums[:streams], sums[streams:], results[-2], results[-1]


def placed_part(value, count, start, place):
    if count >= 128:
        return value, None
    per = 128 // count
    lanes = lax.broadcasted_iota(jnp.int32, (1, 128), 1)
    return moved_part(value, count, place % per, start % per), lanes // count == start % per


def middle_kernel(heads, *refs):
    branches = BRANCHES - 1
    names = Names(refs)
    starts, first = names.take(2)
    backs = names.take(branches)
    x_rows, cot, out_proj, up, down, gain, shift = names.take(7)
    block_out, grad_hidden, gains_two, own_g = names.take(4)
    sends = names.take(branches)
    chunks = up.shape[1] // min(up.shape[1], x_rows.shape[1])
    halves = names.take(2 * chunks)
    out_total = names.one()
    merged, lse, mixed, turned, part, got, part_two, got_two = names.take(8)
    hidden_one, normed_own, normed, spread_rows, normed_t, cot_t = names.take(6)
    down_sum, norm_sum, up_grad, down_grad, totals = names.take(5)
    head_sems, first_sems = names.take(2)

    head_size, me_head = lax.axis_size("head"), lax.axis_index("head")
    me = lax.axis_index("seq")
    rest = lax.axis_size("seq") // 4
    width = x_rows.shape[1]
    per_slot = x_rows.shape[0] // SLOTS
    tile = 256

    meet("seq", "head")

    @pl.loop(0, heads)
    def _(head):
        own = first[0, head].astype(F32)
        merged[head] = own[:E]
        lse[head] = own[E : E + 1] + own[E + 1 : E + 2] + own[E + 2 : E + 3]
        for branch in range(1, BRANCHES):
            stride, lanes, per, split = branch_shape(branch, heads)
            back, start = backs[branch - 1], starts[branch, head]
            share = max(1, 128 // lanes)
            for copy in range(split):
                if split == 1:
                    value = back[head // per, head % per].astype(F32)
                else:
                    value = back[head * split + copy, 0].astype(F32)
                if share > 1:
                    value = moved_part(value, lanes, me % share, start % share)
                new_lse = value[E : E + 1] + value[E + 1 : E + 2] + value[E + 2 : E + 3]
                if share > 1:
                    ids = lax.broadcasted_iota(jnp.int32, new_lse.shape, 1)
                    new_lse = jnp.where(ids // lanes == start % share, new_lse, -FAR)
                span = lanes * share
                for block in range(SEG0 // span):
                    at = slice(block * span, (block + 1) * span)
                    new = jnp.where(start // share == block, new_lse, -FAR)
                    old = lse[head, :, at]
                    top = jnp.maximum(old, new)
                    both = top + jnp.log2(jnp.exp2(old - top) + jnp.exp2(new - top))
                    lse[head, :, at] = both
                    merged[head, :, at] = merged[head, :, at] * jnp.exp2(old - both) + value[:E] * jnp.exp2(
                        new - both
                    )
        mixed[head] = merged[head].astype(BF)

    def head_copies(kind, source, target, sem):
        copies = []
        for step in range(1, head_size):
            device = (me_head + step) % head_size
            copies.append(
                pltpu.make_async_remote_copy(
                    src_ref=source.at[:, device] if kind == 0 else source,
                    dst_ref=target.at[step - 1] if kind == 0 else target.at[:, me_head],
                    send_sem=head_sems.at[0, sem, step - 1],
                    recv_sem=head_sems.at[1, sem, step - 1],
                    device_id={"head": device},
                    device_id_type=pl.DeviceIdType.MESH,
                )
            )
        return copies

    def rows_of(ref):
        return ref[...].reshape(SEG0, width)

    turned[...] = mixed[...].reshape(heads * E, SEG0).T
    for step in range(SEG0 // tile):
        at = slice(step * tile // (head_size * per_slot), (step + 1) * tile // (head_size * per_slot))
        value = jnp.dot(turned[step * tile : (step + 1) * tile], out_proj[...], preferred_element_type=F32)
        part[at] = value.astype(BF).reshape(-1, head_size, per_slot, width)
    for copy in head_copies(0, part, got, 0):
        copy.start()
    cot_t[...] = rows_of(cot).T
    for copy in head_copies(0, part, got, 0):
        copy.wait()

    def norm_of(values):
        centred = values - jnp.mean(values, axis=-1, keepdims=True)
        scale = lax.rsqrt(jnp.mean(centred * centred, axis=-1, keepdims=True) + EPS)
        return centred * scale, scale

    def rows_at(slot):
        return pl.ds(pl.multiple_of(slot * per_slot, per_slot), per_slot)

    @pl.loop(0, SLOTS)
    def _(slot):
        value = x_rows[rows_at(slot)] + part[slot, me_head].astype(F32)
        for step in range(1, head_size):
            value = value + got[step - 1, slot].astype(F32)
        hidden_one[rows_at(slot)] = value
        unit, scale = norm_of(value)
        low = (unit * gain[...] + shift[...]).astype(BF)
        normed_own[slot] = low
        normed[slot, me_head] = low

    for copy in head_copies(1, normed_own, normed, 1):
        copy.start()
    for copy in head_copies(1, normed_own, normed, 1):
        copy.wait()
    normed_t[...] = rows_of(normed).T

    chunk_width = up.shape[1] // chunks
    orders = {0: ORDERS["u1"], 1: ORDERS["d1"]}
    firsts = []
    for chunk in range(chunks):
        for kind in range(2):
            index = 2 * chunk + kind
            firsts.append(
                Reduction(
                    orders[kind], totals.at[index], halves[index], None, None,
                    first_sems.at[0, pl.ds(index, 1)], first_sems.at[1, pl.ds(index, 1)],
                )
            )
    down_sum[...] = jnp.zeros_like(down_sum)
    norm_sum[...] = jnp.zeros_like(norm_sum)
    slots = tile // (head_size * per_slot)
    contract_last = (((1,), (1,)), ((), ()))

    for chunk in range(chunks):
        units = slice(chunk * chunk_width, (chunk + 1) * chunk_width)
        up_grad[...] = jnp.zeros_like(up_grad)
        down_grad[...] = jnp.zeros_like(down_grad)

        @pl.loop(0, SEG0 // tile)
        def _(step):
            rows = pl.ds(pl.multiple_of(step * tile, tile), tile)
            low = normed[pl.ds(step * slots, slots)].reshape(tile, width)
            back = cot[pl.ds(step * slots, slots)].reshape(tile, width)
            pre = jnp.dot(low, up[:, units], preferred_element_type=F32)
            grad = lax.dot_general(back, down[units], contract_last, preferred_element_type=F32)
            share = 0.5 + 0.5 * lax.erf(pre * math.sqrt(0.5))
            density = jnp.exp2(pre * pre * (-0.5 * LOG2E)) * (1.0 / math.sqrt(2.0 * math.pi))
            hidden = (pre * share).astype(BF)
            grad = (grad * (share + pre * density)).astype(BF)
            down_sum[rows] += jnp.dot(hidden, down[units], preferred_element_type=F32)
            norm_sum[rows] += lax.dot_general(grad, up[:, units], contract_last, preferred_element_type=F32)
            up_grad[...] += jnp.dot(normed_t[:, rows], grad, preferred_element_type=F32)
            down_grad[...] += jnp.dot(cot_t[:, rows], hidden, preferred_element_type=F32)

        pieces = totals.shape[3] * 4
        size = totals.shape[4]
        turned_down = down_grad[...].T
        for piece in range(pieces):
            spot = (piece // (2 * rest), piece // rest % 2, piece % rest)
            span = slice(piece * size, (piece + 1) * size)
            totals[(2 * chunk,) + spot] = up_grad[span].astype(BF)
            totals[(2 * chunk + 1,) + spot] = turned_down[span].astype(BF)
        firsts[2 * chunk].step(0)
        firsts[2 * chunk + 1].step(0)

    for ref, value in ((part, down_sum), (part_two, norm_sum)):

        @pl.loop(0, SLOTS)
        def _(slot):
            for device in range(head_size):
                begin = pl.multiple_of((slot * head_size + device) * per_slot, per_slot)
                ref[slot, device] = value[pl.ds(begin, per_slot)].astype(BF)

    for copy in head_copies(0, part_two, got_two, 2) + head_copies(0, part, got, 3):
        copy.start()
    for copy in head_copies(0, part_two, got_two, 2):
        copy.wait()
    gains_two[...] = jnp.zeros_like(gains_two)

    @pl.loop(0, SLOTS)
    def _(slot):
        grad = part_two[slot, me_head].astype(F32)
        for step in range(1, head_size):
            grad = grad + got_two[step - 1, slot].astype(F32)
        unit, scale = norm_of(hidden_one[rows_at(slot)])
        scaled = grad * gain[...]
        inner = jnp.mean(scaled * unit, axis=-1, keepdims=True)
        out = cot[slot, me_head].astype(F32) + scale * (
            scaled - jnp.mean(scaled, axis=-1, keepdims=True) - unit * inner
        )
        grad_hidden[rows_at(slot)] = out
        normed_own[slot] = out.astype(BF)
        normed[slot, me_head] = out.astype(BF)
        gains_two[0:1] += jnp.sum(grad * unit, axis=0, keepdims=True)
        gains_two[1:2] += jnp.sum(grad, axis=0, keepdims=True)

    for copy in head_copies(1, normed_own, normed, 4):
        copy.start()
    for copy in head_copies(0, part, got, 3):
        copy.wait()

    @pl.loop(0, SLOTS)
    def _(slot):
        value = hidden_one[rows_at(slot)] + part[slot, me_head].astype(F32)
        for step in range(1, head_size):
            value = value + got[step - 1, slot].astype(F32)
        place = slot % 2 * 8 + slot // 2 % 2 * 4 + slot // 4 % 2 * 2 + slot // 8
        for column in range(width // 128):
            lanes = slice(column * 128, (column + 1) * 128)
            spread_rows[column, pl.ds(place, per_slot, stride=SLOTS), :] = value[:, lanes]

    for column in range(width // 128):
        block_out[:, column * 128 : (column + 1) * 128] = spread_rows[column].astype(BF)
    for copy in head_copies(1, normed_own, normed, 4):
        copy.wait()

    value = jnp.dot(mixed[...].reshape(heads * E, SEG0), rows_of(normed), preferred_element_type=F32)
    size = out_total.shape[3]
    for piece in range(4 * rest):
        spot = (piece // (2 * rest), piece // rest % 2, piece % rest)
        out_total[spot] = value[piece * size : (piece + 1) * size].astype(BF)

    @pl.loop(0, heads)
    def _(head):
        rows = pl.ds(pl.multiple_of(head * E, 16), E)
        grad = lax.dot_general(out_proj[rows], rows_of(normed), contract_last, preferred_element_type=F32)
        low = grad.astype(BF)
        dots = jnp.sum(low.astype(F32) * merged[head], axis=0, keepdims=True)
        own_g[0, head, :E, :] = low
        d = pieces_of(-dots)
        m = pieces_of(-lse[head])
        placed = {0: d[0], 1: d[1], 2: d[2], 12: m[0], 13: m[1], 14: m[2]}
        own_g[0, head, E:, :] = row_block(placed, SEG0).astype(BF)
        own = jnp.concatenate([low.astype(F32), row_block(placed, SEG0)], axis=0)
        for branch in range(1, BRANCHES):
            stride, lanes, per, split = branch_shape(branch, heads)
            send, start = sends[branch - 1], starts[branch, head]
            share = max(1, 128 // lanes)
            span = lanes * share
            block = own[:, :span]
            for part_at in range(1, SEG0 // span):
                block = jnp.where(start // share == part_at, own[:, part_at * span : (part_at + 1) * span], block)
            if share > 1:
                block = moved_part(block, lanes, start % share, me % share)
            block = block.astype(BF)
            if split == 1:
                send[head // per, head % per] = block
            else:
                for copy in range(split):
                    send[head * split + copy, 0] = block

    for reduction in firsts:
        reduction.finish_first()


def middle(heads, starts, first, backs, x_rows, cot, out_proj, up, down, gain, shift):
    size, head_size = lax.axis_size("seq"), lax.axis_size("head")
    rest = size // 4
    rows, width = x_rows.shape
    per_slot = rows // SLOTS
    chunks = max(1, up.shape[1] // width)
    shard = (SLOTS, head_size, per_slot, width)
    own = (SLOTS, per_slot, width)
    got = (head_size - 1,) + own
    sends = send_shapes(heads, ROWS_OUT)[0]
    piece = (2, rest, width // size, up.shape[1] // chunks)
    out_piece = (2, 2, rest, heads * E // size, width)
    results = pl.pallas_call(
        partial(middle_kernel, heads),
        in_specs=[pl.BlockSpec(memory_space=pltpu.SMEM)] + vmem_specs(1 + len(backs) + 7),
        out_specs=vmem_specs(4 + len(sends) + 2 * chunks + 1),
        out_shape=[
            jax.ShapeDtypeStruct((rows, width), BF),
            jax.ShapeDtypeStruct((rows, width), F32),
            jax.ShapeDtypeStruct((2, width), F32),
            jax.ShapeDtypeStruct((1, heads, ROWS_OUT, SEG0), BF),
        ]
        + sends
        + [jax.ShapeDtypeStruct(piece, BF)] * (2 * chunks)
        + [jax.ShapeDtypeStruct(out_piece, BF)],
        scratch_shapes=[
            pltpu.VMEM((heads, E, SEG0), F32),
            pltpu.VMEM((heads, 1, SEG0), F32),
            pltpu.VMEM((heads, E, SEG0), BF),
            pltpu.VMEM((SEG0, heads * E), BF),
            pltpu.VMEM(shard, BF),
            pltpu.VMEM(got, BF),
            pltpu.VMEM(shard, BF),
            pltpu.VMEM(got, BF),
            pltpu.VMEM((rows, width), F32),
            pltpu.VMEM(own, BF),
            pltpu.VMEM(shard, BF),
            pltpu.VMEM((width // 128, rows, 128), F32),
            pltpu.VMEM((width, SEG0), BF),
            pltpu.VMEM((width, SEG0), BF),
            pltpu.VMEM((SEG0, width), F32),
            pltpu.VMEM((SEG0, width), F32),
            pltpu.VMEM((width, up.shape[1] // chunks), F32),
            pltpu.VMEM((width, up.shape[1] // chunks), F32),
            pltpu.VMEM((2 * chunks, 2) + piece, BF),
            pltpu.SemaphoreType.DMA((2, 5, head_size - 1)),
            pltpu.SemaphoreType.DMA((2, 2 * chunks)),
        ],
        compiler_params=pltpu.CompilerParams(
            vmem_limit_bytes=60 * 2**20, collective_id=2, has_side_effects=True
        ),
        cost_estimate=pl.CostEstimate(
            flops=14 * SEG0 * width * up.shape[1], transcendentals=0, bytes_accessed=40 * 2**20
        ),
        name="middle",
    )(starts, first, *backs, x_rows, cot.reshape(shard), out_proj, up, down, gain, shift)
    block_out, grad_hidden, gains_two, own_g = results[:4]
    return block_out, grad_hidden, gains_two, own_g, results[4 : 4 + len(sends)], results[4 + len(sends) :]


def rolled(value, step):
    size = lax.axis_size("head")
    return lax.ppermute(value, "head", [(s, (s + step) % size) for s in range(size)])


def all_rows(own):
    size = lax.axis_size("head")
    me = lax.axis_index("head")
    got = [own] + [rolled(own, step) for step in range(1, size)]
    if size == 2:
        return [jnp.where(me == 0, got[0], got[1]), jnp.where(me == 0, got[1], got[0])]
    stacked = jnp.stack(got)
    return [stacked[(me - place) % size] for place in range(size)]


def sum_rows(parts):
    size = lax.axis_size("head")
    me = lax.axis_index("head")
    total = lax.dynamic_index_in_dim(parts, me, 0, keepdims=False).astype(F32)
    for step in range(1, size):
        sent = lax.dynamic_index_in_dim(parts, (me + step) % size, 0, keepdims=False)
        total = total + rolled(sent, step).astype(F32)
    return total


def local(
    tokens,
    documents,
    offsets,
    in_proj,
    out_proj,
    up_proj,
    down_proj,
    first_gain,
    first_shift,
    second_gain,
    second_shift,
    cotangent,
):
    head_count = lax.axis_size("head")
    seq_id = lax.axis_index("seq")
    row_count, width = tokens.shape
    seq_len = row_count * head_count
    heads = offsets.shape[1]
    per_slot = row_count // SLOTS

    ids = lax.broadcasted_iota(jnp.int32, (row_count, row_count), 0)
    slot = reversed_bits(ids // per_slot, 4)
    source = ids % per_slot * SLOTS + slot
    order = (source == lax.broadcasted_iota(jnp.int32, (row_count, row_count), 1)).astype(BF)

    def sorted_rows(values):
        return jnp.dot(order, values, preferred_element_type=F32)

    def shard_rows(own):
        parts = [part.reshape(SLOTS, per_slot, -1) for part in all_rows(own)]
        return jnp.stack(parts, axis=1).reshape(seq_len, -1)

    def device_parts(values):
        split = values.reshape(SLOTS, head_count, per_slot, -1)
        return jnp.moveaxis(split, 1, 0).reshape(head_count, row_count, -1)

    x_rows = sorted_rows(tokens)
    cot_low = sorted_rows(cotangent).astype(BF)
    normed_one = norm_rows(x_rows, first_gain, first_shift)
    gathered_one = shard_rows(normed_one.astype(BF))
    cot_all = shard_rows(cot_low)

    my_docs = lax.dynamic_slice_in_dim(documents, seq_id * seq_len, seq_len)
    my_docs = my_docs.reshape(head_count, per_slot, 2, 2, 2, 2).transpose(5, 4, 3, 2, 0, 1).reshape(seq_len)
    bit_ids = jnp.arange(BIT_ROWS, dtype=jnp.int32)[:, None]
    doc_bit = my_docs[None, :] // 2 ** (bit_ids % DOC_BITS) % 2
    bits = jnp.where(bit_ids < DOC_BITS, doc_bit, jnp.where(bit_ids < 2 * DOC_BITS, 1 - doc_bit, 0))
    bits = bits.astype(BF)
    starts = jnp.stack([reversed_bits(offsets[b], b) for b in range(BRANCHES)])

    scales = jnp.array([E ** (-0.5) * LOG2E, 1.0, 1.0], F32)[:, None, None]
    projected = jnp.einsum("td,jdc->jct", gathered_one, in_proj, preferred_element_type=F32)
    projected = (projected * scales).astype(BF)
    place = seq_id.astype(jnp.int32).reshape(1)
    own, *sends = pack_heads(heads, starts, place, projected, bits)
    first_out, units, outs = exchange_forward(heads, own, sends)
    block_out, grad_hidden, gains_two, own_g, sends_g, parts = middle(
        heads, starts, first_out, outs, x_rows, cot_all, out_proj, up_proj, down_proj,
        second_gain[None, :], second_shift[None, :],
    )
    sums, grad_in, grad_tokens, gains = backward(
        heads, starts, own, own_g, units, sends_g, parts,
        gathered_one, in_proj, x_rows, grad_hidden, first_gain[None, :], gains_two,
    )
    return (
        block_out,
        grad_tokens,
        jnp.stack(grad_in).astype(F32),
        sums[-1].astype(F32),
        jnp.concatenate(sums[:-1:2], axis=1).astype(F32),
        jnp.concatenate(sums[1:-1:2], axis=0).astype(F32),
        gains[0],
        gains[1],
        gains[2],
        gains[3],
    )


def solution(mesh):
    placed = (
        P(("seq", "head"), None),
        P(),
        P(None, "head"),
        P(None, None, "head"),
        P("head", None),
        P(None, "head"),
        P("head", None),
        P(),
        P(),
        P(),
        P(),
        P(("seq", "head"), None),
    )
    return jax.shard_map(
        local,
        mesh=mesh,
        in_specs=placed,
        out_specs=(
            P(("seq", "head"), None),
            P(("seq", "head"), None),
            P(None, None, "head"),
            P("head", None),
            P(None, "head"),
            P("head", None),
            P(),
            P(),
            P(),
            P(),
        ),
        check_vma=False,
    )
```

```python
import math
from functools import partial

import jax
import jax.numpy as jnp
from jax import lax
from jax.experimental import pallas as pl
from jax.experimental.pallas import tpu as pltpu
from jax.sharding import PartitionSpec as P

E = 48
BRANCHES = 5
SEG0 = 1024
SLOTS = 16
BIT_ROWS = 16
DOC_BITS = 6
ROWS_IN = 3 * E + BIT_ROWS
ROWS_OUT = E + BIT_ROWS
EPS = 1e-05
FAR = 1e30
LOG2E = math.log2(math.e)
LN2 = math.log(2.0)
BF = jnp.bfloat16
F32 = jnp.float32
VMEM_LIMIT = 48 * 2**20


def params(**more):
    return pltpu.CompilerParams(vmem_limit_bytes=VMEM_LIMIT, **more)


def norm_rows(values, gain, shift):
    centre = jnp.mean(values, axis=-1, keepdims=True)
    centred = values - centre
    spread = jnp.mean(centred * centred, axis=-1, keepdims=True)
    return centred * lax.rsqrt(spread + EPS) * gain + shift


def reversed_bits(value, count):
    out = jnp.zeros_like(value)
    for bit in range(count):
        out = out * 2 + value // 2**bit % 2
    return out


def bit_reversed(value, count):
    return int(format(value, f"0{count}b")[::-1], 2)


def branch_shape(branch, heads):
    stride = 2**branch
    return (stride, SEG0 // stride, max(1, heads // stride), max(1, stride // heads))


def pieces_of(value):
    high = value.astype(BF).astype(F32)
    rest = value - high
    middle = rest.astype(BF).astype(F32)
    return high, middle, (rest - middle).astype(BF).astype(F32)


def row_block(placed, columns):
    ids = lax.broadcasted_iota(jnp.int32, (BIT_ROWS, columns), 0)
    block = jnp.zeros((BIT_ROWS, columns), F32)
    for row, value in placed.items():
        block = jnp.where(ids == row, value, block)
    return block


def lane_block(ref, rows, start, count):
    return ref[0, 0, rows, aligned(start, count)]


def aligned(start, count):
    if count >= 128:
        return pl.ds(pl.multiple_of(start * count, 128), count)
    return pl.ds(pl.multiple_of(start // (128 // count) * 128, 128), 128)


def turned_half(block):
    return jnp.concatenate([block[:, 64:], block[:, :64]], axis=1)


def low_half():
    return lax.broadcasted_iota(jnp.int32, (1, 128), 1) < 64


def packed_rows(rows, count):
    return rows if count >= 128 else (rows // 2 + 15) // 16 * 16


def packed(block, half):
    rows = packed_rows(block.shape[0], 64)
    upper, lower = block[:rows], block[block.shape[0] - rows :]
    if isinstance(half, int):
        return jnp.where(low_half(), turned_half(upper) if half else upper, lower if half else turned_half(lower))
    upper = jnp.where(half == 0, upper, turned_half(upper))
    lower = jnp.where(half == 0, turned_half(lower), lower)
    return jnp.where(low_half(), upper, lower)


def unpacked(value, rows, half):
    size = value.shape[0]
    other = turned_half(value)
    upper = jnp.where(half == 0, value, other)
    lower = jnp.where(half == 0, other, value)
    both = jnp.concatenate([upper, lower[2 * size - rows :]], axis=0)
    return jnp.where(low_half() == (half == 0), both, 0.0)


def pack_kernel(heads, starts, proj, bits, own, *sends):
    head = pl.program_id(0)
    for j in range(3):
        own[0, 0, j * E : (j + 1) * E, :] = proj[j]
    own[0, 0, 3 * E :, :] = bits[...]
    send_blocks(heads, head, starts, own, sends)


def send_blocks(heads, head, starts, own, sends):
    for branch in range(1, BRANCHES):
        count = branch_shape(branch, heads)[1]
        send = sends[branch - 1]
        start = starts[branch, head]
        block = lane_block(own, slice(None), start, count)
        if count < 128:
            block = packed(block.astype(F32), start % 2).astype(BF)
        for copy in range(send.shape[0]):
            send[copy, 0] = block


def send_shapes(heads, rows):
    outs, specs = [], []
    for branch in range(1, BRANCHES):
        stride, count, per, split = branch_shape(branch, heads)
        block = (packed_rows(rows, count), max(count, 128))
        outs.append(jax.ShapeDtypeStruct((stride, per) + block, BF))
        specs.append(pl.BlockSpec((split, 1) + block, lambda h, s, per=per: (h // per, h % per, 0, 0)))
    return outs, specs


def pack_heads(heads, starts, proj, bits):
    span = proj.shape[-1]
    sends, send_specs = send_shapes(heads, ROWS_IN)
    return pl.pallas_call(
        partial(pack_kernel, heads),
        grid_spec=pltpu.PrefetchScalarGridSpec(
            num_scalar_prefetch=1,
            grid=(heads,),
            in_specs=[
                pl.BlockSpec((3, E, span), lambda h, s: (0, h, 0)),
                pl.BlockSpec((BIT_ROWS, span), lambda h, s: (0, 0)),
            ],
            out_specs=[pl.BlockSpec((1, 1, ROWS_IN, span), lambda h, s: (0, h, 0, 0))] + send_specs,
        ),
        out_shape=[jax.ShapeDtypeStruct((1, heads, ROWS_IN, span), BF)] + sends,
        compiler_params=params(),
        name="pack_heads",
    )(starts, proj, bits)


def load_unit(ref, unit, count, x):
    width = ref.shape[-1]
    if count >= 128:
        for block in range(ref.shape[0]):
            x[:, block * width : (block + 1) * width] = ref[block, unit]
        return
    rows, size = x.shape[0], ref.shape[2]
    for block in range(ref.shape[0] // 2):
        lanes = slice(block * 128, (block + 1) * 128)
        left = ref[2 * block, unit].astype(F32)
        right = ref[2 * block + 1, unit].astype(F32)
        x[:size, lanes] = jnp.where(low_half(), left, turned_half(right)).astype(BF)
        x[rows - size :, lanes] = jnp.where(low_half(), turned_half(left), right).astype(BF)


def store_unit(ref, unit, count, result):
    width = ref.shape[-1]
    for block in range(SEG0 // width):
        value = result[:, block * width : (block + 1) * width]
        if count >= 128:
            ref[block, unit] = value
        else:
            value = value.astype(F32)
            ref[2 * block, unit] = packed(value, 0).astype(BF)
            ref[2 * block + 1, unit] = packed(value, 1).astype(BF)


def forward_unit(x, q_aug, result, base, queries):
    if isinstance(base, int):
        lanes = slice(base, base + queries)
    else:
        lanes = pl.ds(pl.multiple_of(base, 128), queries)
    q_aug[0:E, :queries] = x[0:E, lanes]
    q_aug[E:, :queries] = (x[3 * E :, lanes].astype(F32) * -FAR).astype(BF)
    bits = x[3 * E :, :].astype(F32)
    k_rows = jnp.concatenate([x[E : 2 * E, :], (1.0 - bits).astype(BF)], axis=0).T
    v_aug = jnp.concatenate([x[2 * E : 3 * E, :], jnp.ones(bits.shape, BF)], axis=0)
    if queries < SEG0:
        result[0:E, :] = jnp.zeros((E, SEG0), BF)
        result[E:, :] = row_block({0: -FAR}, SEG0).astype(BF)
    s = jnp.dot(k_rows, q_aug[:, :queries], preferred_element_type=F32)
    top = jnp.max(s, axis=0, keepdims=True)
    p = jnp.exp2(s - top).astype(BF)
    o = jnp.dot(v_aug, p, preferred_element_type=F32)
    total = o[E : E + 1]
    high, middle_part, low = pieces_of(top + jnp.log2(total))
    block = row_block({0: high, 1: middle_part, 2: low}, queries)
    result[:, lanes] = jnp.concatenate([o[:E] * (1.0 / total), block], axis=0).astype(BF)


class Names:
    def __init__(self, refs):
        self.refs = list(refs)

    def take(self, count):
        taken, self.refs = self.refs[:count], self.refs[count:]
        return taken

    def one(self):
        return self.take(1)[0]


def group_place(branch):
    stride = 2**branch
    me = lax.axis_index("seq")
    return me // stride * stride, me % stride


def meet(*axes):
    barrier = pltpu.get_barrier_semaphore()
    count = 0
    for axis in axes:
        size = lax.axis_size(axis)
        me = lax.axis_index(axis)

        @pl.loop(1, size)
        def _(step):
            pl.semaphore_signal(
                barrier, inc=1, device_id={axis: (me + step) % size}, device_id_type=pl.DeviceIdType.MESH
            )

        count += size - 1
    pl.semaphore_wait(barrier, count)


class Reduction:
    STEPS = 7

    def __init__(self, order, total, half, quarter, others, send, recv, begun=False):
        self.total, self.begun = total, begun
        self.half, self.quarter, self.others = half, quarter, others
        self.send, self.recv = send, recv
        me = lax.axis_index("seq")
        self.rest = lax.axis_size("seq") // 4
        self.me = me
        bits = (me % 2, me // 2 % 2)
        self.bits = [bits[bit] for bit in order]
        self.partners = [me + (1 - 2 * bits[bit]) * 2**bit for bit in order]
        self.place = me // 4

    def copy(self, source, target, device, sem):
        return pltpu.make_async_remote_copy(
            src_ref=source,
            dst_ref=target,
            send_sem=self.send.at[sem],
            recv_sem=self.recv.at[sem],
            device_id={"seq": device},
            device_id_type=pl.DeviceIdType.MESH,
        )

    def copies(self, number):
        one, two = self.bits
        rest = self.rest
        others = []
        for step in range(1, rest):
            place = (self.place + step) % rest
            others.append((step, place, place * 4 + self.me % 4))
        if number == 0:
            return [self.copy(self.total.at[1 - one], self.half, self.partners[0], 0)]
        if number == 1:
            return [self.copy(self.half.at[1 - two], self.quarter, self.partners[1], 1)]
        if number == 2:
            return [
                self.copy(self.quarter.at[place], self.others.at[step - 1], device, 1 + step)
                for step, place, device in others
            ]
        if number == 3:
            block = self.total.at[one, two, self.place]
            return [self.copy(block, block, device, rest + step) for step, place, device in others]
        if number == 4:
            block = self.total.at[one, two]
            return [self.copy(block, block, self.partners[1], 2 * rest)]
        if number == 5:
            block = self.total.at[one]
            return [self.copy(block, block, self.partners[0], 2 * rest + 1)]
        return []

    def finish_first(self):
        one, rest = self.bits[0], self.rest
        for copy in self.copies(0):
            copy.wait()

        @pl.loop(0, 2 * rest)
        def _(i):
            j, z = i // rest, i % rest
            mine = self.total[one, j, z].astype(F32)
            self.half[j, z] = (mine + self.half[j, z].astype(F32)).astype(BF)

    def step(self, number):
        one, two = self.bits
        rest = self.rest
        if number == 0 and self.begun:
            return
        if number == 1:
            if not self.begun:
                self.finish_first()
        elif number > 0:
            for copy in self.copies(number - 1):
                copy.wait()
        if number == 2:

            @pl.loop(0, rest)
            def _(z):
                mine = self.half[two, z].astype(F32)
                self.quarter[z] = (mine + self.quarter[z].astype(F32)).astype(BF)

        elif number == 3:
            mine = self.quarter[self.place].astype(F32)
            for step in range(1, rest):
                mine = mine + self.others[step - 1].astype(F32)
            self.total[one, two, self.place] = mine.astype(BF)
        for copy in self.copies(number):
            copy.start()

    @staticmethod
    def scratch(size, rows, columns):
        rest = size // 4
        count = 2 * rest + 2
        return [
            pltpu.VMEM((2, rest, rows, columns), BF),
            pltpu.VMEM((rest, rows, columns), BF),
            pltpu.VMEM((rest - 1, rows, columns), BF),
            pltpu.SemaphoreType.DMA((count,)),
            pltpu.SemaphoreType.DMA((count,)),
        ]


def reduction_parts(value, size):
    rows, columns = value.shape
    return value.reshape(2, 2, size // 4, rows // size, columns)


def reduction_whole(value):
    return value.reshape(-1, value.shape[-1])


def make_reductions(orders, totals, scratch):
    out = []
    for order, total in zip(orders, totals):
        out.append(Reduction(order, total, *scratch[:5]))
        scratch = scratch[5:]
    return out


def group_copies(branch, source, target, send_sems, recv_sems, local_sem):
    stride = 2**branch
    base, place = group_place(branch)
    first = stride - branch - 2
    copies = [
        pltpu.make_async_copy(source.at[place], target.at[place], local_sem.at[branch - 1])
    ]
    for step in range(1, stride):
        member = (place + step) % stride
        copies.append(
            pltpu.make_async_remote_copy(
                src_ref=source.at[member],
                dst_ref=target.at[place],
                send_sem=send_sems.at[first + step],
                recv_sem=recv_sems.at[first + step],
                device_id={"seq": base + member},
                device_id_type=pl.DeviceIdType.MESH,
            )
        )
    return copies


def exchange_forward_kernel(heads, own, *refs):
    count = BRANCHES - 1
    names = Names(refs)
    sends = names.take(count)
    first = names.one()
    gots, backs, outs = names.take(count), names.take(count), names.take(count)
    x, q_aug, result, in_send, in_recv, in_local, out_send, out_recv, out_local = names.take(9)
    meet("seq")
    coming = {}
    for branch in range(1, BRANCHES):
        coming[branch] = group_copies(branch, sends[branch - 1], gots[branch - 1], in_send, in_recv, in_local)
        for copy in coming[branch]:
            copy.start()

    @pl.loop(0, heads)
    def _(head):
        x[...] = own[0, head]
        forward_unit(x, q_aug, result, 0, SEG0)
        first[0, head] = result[...]

    leaving = []
    for branch in range(1, BRANCHES):
        stride, lanes, units, split = branch_shape(branch, heads)
        got, out = gots[branch - 1], outs[branch - 1]
        for copy in coming[branch]:
            copy.wait()
        queries = SEG0 // split
        base = 0 if split == 1 else lax.axis_index("seq") % split * queries

        @pl.loop(0, units)
        def _(unit):
            load_unit(got, unit, lanes, x)
            forward_unit(x, q_aug, result, base, queries)
            store_unit(out, unit, lanes, result)

        copies = group_copies(branch, out, backs[branch - 1], out_send, out_recv, out_local)
        for copy in copies:
            copy.start()
        leaving += copies
    for copy in leaving:
        copy.wait()


def exchange_scratch():
    copies = 2**BRANCHES - 2 - BRANCHES + 1
    one = [
        pltpu.SemaphoreType.DMA((copies,)),
        pltpu.SemaphoreType.DMA((copies,)),
        pltpu.SemaphoreType.DMA((BRANCHES - 1,)),
    ]
    return one + one


def unit_cost(units, dots):
    return pl.CostEstimate(
        flops=dots * 2 * units * SEG0 * SEG0 * 256,
        transcendentals=units * SEG0 * SEG0,
        bytes_accessed=units * SEG0 * 1000,
    )


def vmem_specs(count):
    return [pl.BlockSpec(memory_space=pltpu.VMEM)] * count


def exchange_forward(heads, own, sends):
    backs = send_shapes(heads, ROWS_OUT)[0]
    gots = send_shapes(heads, ROWS_IN)[0]
    first = jax.ShapeDtypeStruct((1, heads, ROWS_OUT, SEG0), BF)
    results = pl.pallas_call(
        partial(exchange_forward_kernel, heads),
        in_specs=vmem_specs(1 + len(sends)),
        out_specs=vmem_specs(1 + len(gots) + len(backs)),
        out_shape=[first] + gots + backs,
        scratch_shapes=[pltpu.VMEM(shape.shape, BF) for shape in backs]
        + [
            pltpu.VMEM((ROWS_IN, SEG0), BF),
            pltpu.VMEM((ROWS_OUT, SEG0), BF),
            pltpu.VMEM((ROWS_OUT, SEG0), BF),
        ]
        + exchange_scratch(),
        compiler_params=pltpu.CompilerParams(
            vmem_limit_bytes=60 * 2**20, collective_id=0, has_side_effects=True
        ),
        cost_estimate=unit_cost(2 * heads, 2),
        name="exchange_forward",
    )(own, *sends)
    return results[0], results[1 : 1 + len(gots)], results[1 + len(gots) :]


def backward_unit(x, g, q_aug, gk, gv, result, base, queries, tile):
    if isinstance(base, int):
        lanes = slice(base, base + queries)
    else:
        lanes = pl.ds(pl.multiple_of(base, 128), queries)
    extra = g[E:, lanes].astype(F32)
    ids = lax.broadcasted_iota(jnp.int32, extra.shape, 0)
    q = x[0:E, lanes]
    q_aug[0:E, :queries] = q
    q_aug[E:, :queries] = jnp.where(ids >= 12, extra, x[3 * E :, lanes].astype(F32) * -FAR).astype(BF)
    bits = x[3 * E :, :].astype(F32)
    k_aug = jnp.concatenate([x[E : 2 * E, :], (1.0 - bits).astype(BF)], axis=0)
    k_rows = k_aug.T
    v_ids = lax.broadcasted_iota(jnp.int32, bits.shape, 0)
    v_bits = jnp.where(v_ids < 3, 1.0, 0.0).astype(BF)
    v_rows = jnp.concatenate([x[2 * E : 3 * E, :], v_bits], axis=0).T
    q_rows = jnp.concatenate([q, jnp.zeros((BIT_ROWS, queries), BF)], axis=0).T
    g_all = g[:, lanes]
    g_rows = g_all.T
    if queries < SEG0:
        result[0:E, :] = jnp.zeros((E, SEG0), BF)
    for step in range(queries // tile):
        column = step * tile
        span = slice(column, column + tile)
        p = jnp.exp2(jnp.dot(k_rows, q_aug[:, span], preferred_element_type=F32))
        gs = p * jnp.dot(v_rows, g_all[:, span], preferred_element_type=F32)
        p, gs = p.astype(BF), gs.astype(BF)
        target = span if isinstance(base, int) else pl.ds(pl.multiple_of(base + column, 128), tile)
        result[0:E, target] = jnp.dot(k_aug, gs, preferred_element_type=F32)[:E].astype(BF)
        new_k = jnp.dot(gs, q_rows[span], preferred_element_type=F32)
        new_v = jnp.dot(p, g_rows[span], preferred_element_type=F32)
        if step == 0:
            gk[...] = new_k
            gv[...] = new_v
        else:
            gk[...] += new_k
            gv[...] += new_v
    result[E : 2 * E, :] = (gk[...].T[:E] * LN2).astype(BF)
    result[2 * E :, :] = gv[...].T[:E].astype(BF)


ORDERS = {
    'u1': (0, 1), 'u2': (0, 1), 'd1': (1, 0), 'd2': (1, 0), 'o': (0, 1), 'i0': (1, 0), 'i1': (1, 0), 'i2': (0,
    1),
}
EARLY = [
    (0, 'd1', 0), (0, 'u1', 0), (0, 'd1', 1), (0, 'u2', 0), (0, 'u1', 1), (2, 'o', 0), (4, 'u2', 1), (5, 'u1',
    2), (7, 'd1', 2), (9, 'u1', 3), (10, 'd2', 0), (12, 'd2', 1), (12, 'o', 1), (12, 'd1', 3), (13, 'u2', 2),
    (14, 'u1', 4),
]
TAIL = [
    'gather', ('d1', 4), 'in1', ('i1', 0), ('d2', 2), 'in2', ('u2', 3), ('i2', 0), 'in0', ('i0', 0), ('d2',
    3), ('i1', 1), ('i2', 1), ('u1', 5), ('u2', 4), ('d2', 4), ('d1', 5), ('o', 2), ('i2', 2), ('i0', 1),
    ('i1', 2), ('i2', 3), 'one', ('d2', 5), ('o', 3), ('i1', 3), ('u1', 6), ('u2', 5), 'norm', ('i2', 4),
    'gain0', ('i0', 2), ('i1', 4), ('i0', 3), 'gain1', ('o', 4), ('i0', 4), ('i2', 5), 'gain2', ('i1', 5),
    ('o', 5), ('i0', 5), 'gain3', ('i0', 6), ('d2', 6), ('u2', 6), 'gain4', ('d1', 6), ('i1', 6), ('i2', 6),
    ('o', 6),
]


def stream_names(streams):
    pairs = streams // 2
    return [kind + str(i + 1) for i in range(pairs) for kind in "ud"] + ["o"]


def backward_kernel(heads, streams, *refs):
    branches = BRANCHES - 1
    names = Names(refs)
    starts, own, own_g = names.take(3)
    sends, gain, gains_two = names.take(branches), *names.take(2)
    far = names.take(branches + 4)
    parts = names.take(streams)
    up_total, down_total, out_total, in_total = names.take(4)
    chunks = (streams - 1) // 2
    totals = []
    for chunk in range(chunks):
        lanes = pl.ds(chunk * (up_total.shape[-1] // chunks), up_total.shape[-1] // chunks)
        totals += [up_total.at[:, :, :, :, lanes], down_total.at[chunk]]
    totals.append(out_total)
    in_totals = [in_total.at[j] for j in range(3)]
    grad_tokens, gains_out = names.take(2)
    near = names.take(branches + 4)
    units_in, (normed, in_proj, x_rows, grad_hidden) = near[:branches], near[branches:]
    far_sem = names.one()
    first = names.one()
    backs, gots, outs = names.take(branches), names.take(branches), names.take(branches)
    x, g, q_aug, gk, gv, result = names.take(6)
    total, grads, grads_t, normed_t, spread_rows, head_send, head_recv = names.take(7)
    gain_head, gain_one, gain_two, gain_rest = names.take(4)
    in_send, in_recv, in_local, out_send, out_recv, out_local = names.take(6)
    part_sem, head_sems, gain_sems = names.take(3)
    labels = stream_names(streams) + ["i0", "i1", "i2"]
    reductions = make_reductions(
        [ORDERS[label] for label in labels], list(totals) + list(in_totals), names.take(5 * streams + 15)
    )
    reductions = dict(zip(labels, reductions))
    for label in labels[: streams - 1]:
        reductions[label].begun = True

    shapes = [branch_shape(b, heads) for b in range(BRANCHES)]
    size, head_size = lax.axis_size("seq"), lax.axis_size("head")
    me, me_head = lax.axis_index("seq"), lax.axis_index("head")
    rest = size // 4
    tile = 512
    per_slot = x_rows.shape[0] // SLOTS
    width = x_rows.shape[1]

    fills = [
        pltpu.make_async_copy(parts[s], reductions[labels[s]].half, part_sem.at[s]) for s in range(streams - 1)
    ] + [pltpu.make_async_copy(parts[-1], totals[-1], part_sem.at[streams - 1])]
    loads = [pltpu.make_async_copy(far[i], near[i], far_sem.at[i]) for i in range(branches + 4)]
    for copy in fills + loads:
        copy.start()
    meet("seq", "head")

    def coming(branch):
        return group_copies(branch, sends[branch - 1], gots[branch - 1], in_send, in_recv, in_local)

    def leaving(branch):
        return group_copies(branch, outs[branch - 1], backs[branch - 1], out_send, out_recv, out_local)

    for branch in range(1, BRANCHES):
        for copy in coming(branch):
            copy.start()
    for copy in fills + loads:
        copy.wait()

    def split_branch(branch):
        stride, lanes, units, split = shapes[branch]
        queries = SEG0 // split
        for copy in coming(branch):
            copy.wait()
        load_unit(units_in[branch - 1], 0, lanes, x)
        load_unit(gots[branch - 1], 0, lanes, g)
        backward_unit(x, g, q_aug, gk, gv, result, me % split * queries, queries, min(tile, queries))
        store_unit(outs[branch - 1], 0, lanes, result)

    runs, at = [(0, 0, 0, heads // 2)], heads // 2
    split_at = None
    for branch in range(1, BRANCHES):
        if shapes[branch][3] == 1:
            runs.append((branch, at, 0, shapes[branch][2]))
            at += shapes[branch][2]
    split_at = at
    runs.append((0, at, heads // 2, heads - heads // 2))
    blocks = at + heads - heads // 2
    plan = {}
    for block, stream, step in EARLY:
        if stream in labels:
            plan.setdefault(block * blocks // 15, []).append((stream, step))

    @pl.loop(0, blocks)
    def _(block):
        for after, events in plan.items():

            @pl.when(block == after)
            def _(events=events):
                for stream, step in events:
                    reductions[stream].step(step)

        @pl.when(block == split_at)
        def _():
            for branch in range(1, BRANCHES):
                if shapes[branch][3] > 1:
                    split_branch(branch)
                    for copy in leaving(branch):
                        copy.start()

        for branch, low, unit, count in runs:

            @pl.when((block >= low) & (block < low + count))
            def _(branch=branch, low=low, unit=unit):
                if branch == 0:
                    x[...] = own[0, block - low + unit]
                    g[...] = own_g[0, block - low + unit]
                else:

                    @pl.when(block == low)
                    def _():
                        for copy in coming(branch):
                            copy.wait()

                    load_unit(units_in[branch - 1], block - low, shapes[branch][1], x)
                    load_unit(gots[branch - 1], block - low, shapes[branch][1], g)

        backward_unit(x, g, q_aug, gk, gv, result, 0, SEG0, tile)
        for branch, low, unit, count in runs:

            @pl.when((block >= low) & (block < low + count))
            def _(branch=branch, low=low, unit=unit, count=count):
                if branch == 0:
                    first[block - low + unit] = result[...]
                else:
                    store_unit(outs[branch - 1], block - low, shapes[branch][1], result)

                    @pl.when(block == low + count - 1)
                    def _():
                        for copy in leaving(branch):
                            copy.start()

    tasks = {}

    def task(work):
        tasks[work.__name__] = work

    @task
    def gather():
        for branch in range(1, BRANCHES):
            for copy in leaving(branch):
                copy.wait()

        @pl.loop(0, heads)
        def _(head):
            total[...] = first[head].astype(F32)
            for branch in range(1, BRANCHES):
                stride, lanes, per, split = shapes[branch]
                back, start = backs[branch - 1], starts[branch, head]
                if split == 1:
                    value = back[head // per, head % per].astype(F32)
                else:
                    value = back[head * split, 0].astype(F32)
                    for copy in range(1, split):
                        value = value + back[head * split + copy, 0].astype(F32)
                if lanes < 128:
                    value = unpacked(value, 3 * E, start % 2)
                    start = start // 2
                    lanes = 128
                for block in range(SEG0 // lanes):
                    span = slice(block * lanes, (block + 1) * lanes)
                    total[:, span] += jnp.where(start == block, value, 0.0)
            grads[0, head] = (total[0:E, :] * E ** (-0.5)).astype(BF)
            grads[1, head] = total[E : 2 * E, :].astype(BF)
            grads[2, head] = total[2 * E :, :].astype(BF)

        normed_t[...] = normed[...].T

    def in_gradient(j):
        rows_in = in_totals[0].shape[3]
        chunk = width // 2
        grads_t[j] = grads[j].reshape(heads * E, SEG0).T
        for half in range(2):
            value = jnp.dot(
                normed_t[half * chunk : (half + 1) * chunk], grads_t[j], preferred_element_type=F32
            ).astype(BF)
            for part in range(chunk // rows_in):
                index = half * (chunk // rows_in) + part
                in_totals[j][index // (2 * rest), index // rest % 2, index % rest] = value[
                    part * rows_in : (part + 1) * rows_in
                ]

    for j in range(3):
        tasks[f"in{j}"] = partial(in_gradient, j)

    def head_swaps():
        swaps = []
        for step in range(1, head_size):
            device = (me_head + step) % head_size
            swaps.append(
                pltpu.make_async_remote_copy(
                    src_ref=head_send.at[device],
                    dst_ref=head_recv.at[step - 1],
                    send_sem=head_sems.at[0, step - 1],
                    recv_sem=head_sems.at[1, step - 1],
                    device_id={"head": device},
                    device_id_type=pl.DeviceIdType.MESH,
                )
            )
        return swaps

    @task
    def one():
        for half in range(2):
            rows = slice(half * SEG0 // 2, (half + 1) * SEG0 // 2)
            value = jnp.zeros((SEG0 // 2, width), F32)
            for j in range(3):
                value = value + lax.dot_general(
                    grads_t[j, rows], in_proj[j], (((1,), (1,)), ((), ())), preferred_element_type=F32
                )
            value = value.astype(BF)
            for slot in range(SLOTS // 2):
                for device in range(head_size):
                    begin = (slot * head_size + device) * per_slot
                    place = (half * SLOTS // 2 + slot) * per_slot
                    head_send[device, place : place + per_slot] = value[begin : begin + per_slot]
        for swap in head_swaps():
            swap.start()

    @task
    def norm():
        for swap in head_swaps():
            swap.wait()
        gain_head[me_head] = jnp.zeros(gains_out.shape, F32)
        gain_head[me_head, 2:4] = gains_two[...]

        @pl.loop(0, SLOTS)
        def _(slot):
            rows = pl.ds(pl.multiple_of(slot * per_slot, per_slot), per_slot)
            grad = head_send[me_head, rows].astype(F32)
            for step in range(1, head_size):
                grad = grad + head_recv[step - 1, rows].astype(F32)
            values = x_rows[rows]
            centred = values - jnp.mean(values, axis=-1, keepdims=True)
            scale = lax.rsqrt(jnp.mean(centred * centred, axis=-1, keepdims=True) + EPS)
            unit = centred * scale
            scaled = grad * gain[...]
            inner = jnp.mean(scaled * unit, axis=-1, keepdims=True)
            out = grad_hidden[rows] + scale * (
                scaled - jnp.mean(scaled, axis=-1, keepdims=True) - unit * inner
            )
            place = slot % 2 * 8 + slot // 2 % 2 * 4 + slot // 4 % 2 * 2 + slot // 8
            for column in range(width // 128):
                lanes = slice(column * 128, (column + 1) * 128)
                spread_rows[column, pl.ds(place, per_slot, stride=SLOTS), :] = out[:, lanes]
            gain_head[me_head, 0:1] += jnp.sum(grad * unit, axis=0, keepdims=True)
            gain_head[me_head, 1:2] += jnp.sum(grad, axis=0, keepdims=True)

        for column in range(width // 128):
            grad_tokens[:, column * 128 : (column + 1) * 128] = spread_rows[column]

    def gain_copy(source, target, axis, device, sem):
        return pltpu.make_async_remote_copy(
            src_ref=source,
            dst_ref=target,
            send_sem=gain_sems.at[0, sem],
            recv_sem=gain_sems.at[1, sem],
            device_id={axis: device},
            device_id_type=pl.DeviceIdType.MESH,
        )

    def gain_copies(stage):
        if stage == 0:
            mine = gain_head.at[me_head]
            return [
                gain_copy(mine, mine, "head", (me_head + step) % head_size, step - 1)
                for step in range(1, head_size)
            ]
        if stage == 1:
            return [gain_copy(gain_one.at[0], gain_one.at[1], "seq", me + 1 - 2 * (me % 2), head_size)]
        if stage == 2:
            device = me + 2 - 4 * (me // 2 % 2)
            return [gain_copy(gain_two.at[0], gain_two.at[1], "seq", device, head_size + 1)]
        spot = me // 4
        block = gain_rest.at[spot]
        return [
            gain_copy(block, block, "seq", (spot + step) % rest * 4 + me % 4, head_size + 1 + step)
            for step in range(1, rest)
        ]

    def summed(ref, count):
        value = ref[0]
        for index in range(1, count):
            value = value + ref[index]
        return value

    def gain_stage(stage):
        if stage > 0:
            for swap in gain_copies(stage - 1):
                swap.wait()
        if stage == 1:
            gain_one[0] = summed(gain_head, head_size)
        elif stage == 2:
            gain_two[0] = summed(gain_one, 2)
        elif stage == 3:
            gain_rest[me // 4] = summed(gain_two, 2)
        elif stage == 4:
            gains_out[...] = summed(gain_rest, rest)
            return
        for swap in gain_copies(stage):
            swap.start()

    for stage in range(5):
        tasks[f"gain{stage}"] = partial(gain_stage, stage)

    for item in TAIL:
        if isinstance(item, str):
            tasks[item]()
        elif item[0] in labels:
            reductions[item[0]].step(item[1])


def backward(heads, starts, own, own_g, units, sends, parts, normed, in_proj, x_rows, grad_hidden, gain, gains_two):
    size, head_size = lax.axis_size("seq"), lax.axis_size("head")
    rest = size // 4
    rows, width = x_rows.shape
    in_shape = (2, 2, rest, width // size, heads * E)
    scratch = []
    for part in parts:
        scratch += Reduction.scratch(size, *part.shape[-2:])
    for _ in range(3):
        scratch += Reduction.scratch(size, *in_shape[-2:])
    streams = len(parts)
    chunks = (streams - 1) // 2
    far = list(units) + [normed, in_proj, x_rows, grad_hidden]
    results = pl.pallas_call(
        partial(backward_kernel, heads, streams),
        in_specs=[pl.BlockSpec(memory_space=pltpu.SMEM)]
        + vmem_specs(2 + len(sends) + 2)
        + [pl.BlockSpec(memory_space=pl.ANY)] * (len(far) + streams),
        out_specs=vmem_specs(6),
        out_shape=[
            jax.ShapeDtypeStruct((2, 2, rest, width // size, chunks * parts[0].shape[-1]), BF),
            jax.ShapeDtypeStruct((chunks, 2, 2, rest) + parts[1].shape[-2:], BF),
            jax.ShapeDtypeStruct(parts[-1].shape, BF),
            jax.ShapeDtypeStruct((3,) + in_shape, BF),
        ]
        + [jax.ShapeDtypeStruct((rows, width), F32), jax.ShapeDtypeStruct((8, width), F32)],
        scratch_shapes=[pltpu.VMEM(value.shape, value.dtype) for value in far]
        + [pltpu.SemaphoreType.DMA((len(far),)), pltpu.VMEM((heads, 3 * E, SEG0), BF)]
        + [pltpu.VMEM(shape.shape, BF) for shape in send_shapes(heads, 3 * E)[0]]
        + [pltpu.VMEM(shape.shape, BF) for shape in send_shapes(heads, ROWS_OUT)[0]]
        + [pltpu.VMEM(shape.shape, BF) for shape in send_shapes(heads, 3 * E)[0]]
        + [
            pltpu.VMEM((ROWS_IN, SEG0), BF),
            pltpu.VMEM((ROWS_OUT, SEG0), BF),
            pltpu.VMEM((ROWS_OUT, SEG0), BF),
            pltpu.VMEM((SEG0, ROWS_OUT), F32),
            pltpu.VMEM((SEG0, ROWS_OUT), F32),
            pltpu.VMEM((3 * E, SEG0), BF),
            pltpu.VMEM((3 * E, SEG0), F32),
            pltpu.VMEM((3, heads, E, SEG0), BF),
            pltpu.VMEM((3, SEG0, heads * E), BF),
            pltpu.VMEM((width, SEG0), BF),
            pltpu.VMEM((width // 128, rows, 128), F32),
            pltpu.VMEM((head_size, rows, width), BF),
            pltpu.VMEM((head_size - 1, rows, width), BF),
            pltpu.VMEM((head_size, 8, width), F32),
            pltpu.VMEM((2, 8, width), F32),
            pltpu.VMEM((2, 8, width), F32),
            pltpu.VMEM((rest, 8, width), F32),
        ]
        + exchange_scratch()
        + [
            pltpu.SemaphoreType.DMA((streams,)),
            pltpu.SemaphoreType.DMA((2, head_size - 1)),
            pltpu.SemaphoreType.DMA((2, head_size + 1 + rest)),
        ]
        + scratch,
        compiler_params=pltpu.CompilerParams(
            vmem_limit_bytes=60 * 2**20, collective_id=1, has_side_effects=True
        ),
        cost_estimate=unit_cost(2 * heads, 5),
        name="backward",
    )(starts, own, own_g, *sends, gain, gains_two, *far, *parts)
    up_total, down_total, out_total, in_total = results[:4]
    sums = [
        up_total.reshape(width, -1).astype(F32),
        down_total.reshape(-1, width).astype(F32),
        out_total.reshape(-1, width).astype(F32),
        in_total.reshape(3, width, heads * E).astype(F32),
    ]
    return sums, results[4], results[5]


def middle_kernel(heads, *refs):
    branches = BRANCHES - 1
    names = Names(refs)
    starts, first = names.take(2)
    backs = names.take(branches)
    gain, shift = names.take(2)
    far = names.take(5)
    block_out, grad_hidden, gains_two, own_g = names.take(4)
    sends = names.take(branches)
    chunks = max(1, far[3].shape[1] // far[0].shape[1])
    halves = names.take(2 * chunks)
    out_total = names.one()
    merged, lse, mixed, turned, part, got, part_two, got_two = names.take(8)
    hidden_one, normed_own, normed, spread_rows, normed_t, cot_t = names.take(6)
    down_sum, norm_sum, up_grad, down_grad, totals = names.take(5)
    head_sems, first_sems, far_sem = names.take(3)
    near = names.take(5)
    out_proj, x_rows, cot, up, down = near[2], near[0], near[1], near[3], near[4]
    loads = [pltpu.make_async_copy(far[i], near[i], far_sem.at[i]) for i in range(5)]
    for copy in loads:
        copy.start()

    head_size, me_head = lax.axis_size("head"), lax.axis_index("head")
    me = lax.axis_index("seq")
    rest = lax.axis_size("seq") // 4
    width = x_rows.shape[1]
    per_slot = x_rows.shape[0] // SLOTS
    tile = 256

    meet("seq", "head")

    @pl.loop(0, heads)
    def _(head):
        own = first[0, head].astype(F32)
        merged[head] = own[:E]
        lse[head] = own[E : E + 1] + own[E + 1 : E + 2] + own[E + 2 : E + 3]
        for branch in range(1, BRANCHES):
            stride, lanes, per, split = branch_shape(branch, heads)
            back, start = backs[branch - 1], starts[branch, head]
            share = max(1, 128 // lanes)
            for copy in range(split):
                if split == 1:
                    value = back[head // per, head % per].astype(F32)
                else:
                    value = back[head * split + copy, 0].astype(F32)
                if share > 1:
                    value = unpacked(value, ROWS_OUT, start % share)
                new_lse = value[E : E + 1] + value[E + 1 : E + 2] + value[E + 2 : E + 3]
                if share > 1:
                    ids = lax.broadcasted_iota(jnp.int32, new_lse.shape, 1)
                    new_lse = jnp.where(ids // lanes == start % share, new_lse, -FAR)
                span = lanes * share
                for block in range(SEG0 // span):
                    at = slice(block * span, (block + 1) * span)
                    new = jnp.where(start // share == block, new_lse, -FAR)
                    old = lse[head, :, at]
                    top = jnp.maximum(old, new)
                    both = top + jnp.log2(jnp.exp2(old - top) + jnp.exp2(new - top))
                    lse[head, :, at] = both
                    merged[head, :, at] = merged[head, :, at] * jnp.exp2(old - both) + value[:E] * jnp.exp2(
                        new - both
                    )
        mixed[head] = merged[head].astype(BF)

    def head_copies(kind, source, target, sem):
        copies = []
        for step in range(1, head_size):
            device = (me_head + step) % head_size
            copies.append(
                pltpu.make_async_remote_copy(
                    src_ref=source.at[:, device] if kind == 0 else source,
                    dst_ref=target.at[step - 1] if kind == 0 else target.at[:, me_head],
                    send_sem=head_sems.at[0, sem, step - 1],
                    recv_sem=head_sems.at[1, sem, step - 1],
                    device_id={"head": device},
                    device_id_type=pl.DeviceIdType.MESH,
                )
            )
        return copies

    def rows_of(ref):
        return ref[...].reshape(SEG0, width)

    turned[...] = mixed[...].reshape(heads * E, SEG0).T
    for copy in loads:
        copy.wait()
    for step in range(SEG0 // tile):
        at = slice(step * tile // (head_size * per_slot), (step + 1) * tile // (head_size * per_slot))
        value = jnp.dot(turned[step * tile : (step + 1) * tile], out_proj[...], preferred_element_type=F32)
        part[at] = value.astype(BF).reshape(-1, head_size, per_slot, width)
    for copy in head_copies(0, part, got, 0):
        copy.start()
    cot_t[...] = rows_of(cot).T
    for copy in head_copies(0, part, got, 0):
        copy.wait()

    def norm_of(values):
        centred = values - jnp.mean(values, axis=-1, keepdims=True)
        scale = lax.rsqrt(jnp.mean(centred * centred, axis=-1, keepdims=True) + EPS)
        return centred * scale, scale

    def rows_at(slot):
        return pl.ds(pl.multiple_of(slot * per_slot, per_slot), per_slot)

    @pl.loop(0, SLOTS)
    def _(slot):
        value = x_rows[rows_at(slot)] + part[slot, me_head].astype(F32)
        for step in range(1, head_size):
            value = value + got[step - 1, slot].astype(F32)
        hidden_one[rows_at(slot)] = value
        unit, scale = norm_of(value)
        low = (unit * gain[...] + shift[...]).astype(BF)
        normed_own[slot] = low
        normed[slot, me_head] = low

    for copy in head_copies(1, normed_own, normed, 1):
        copy.start()
    for copy in head_copies(1, normed_own, normed, 1):
        copy.wait()
    normed_t[...] = rows_of(normed).T

    chunk_width = up.shape[1] // chunks
    orders = {0: ORDERS["u1"], 1: ORDERS["d1"]}
    firsts = []
    for chunk in range(chunks):
        for kind in range(2):
            index = 2 * chunk + kind
            firsts.append(
                Reduction(
                    orders[kind], totals.at[index], halves[index], None, None,
                    first_sems.at[0, pl.ds(index, 1)], first_sems.at[1, pl.ds(index, 1)],
                )
            )
    down_sum[...] = jnp.zeros_like(down_sum)
    norm_sum[...] = jnp.zeros_like(norm_sum)
    slots = tile // (head_size * per_slot)
    contract_last = (((1,), (1,)), ((), ()))

    for chunk in range(chunks):
        units = slice(chunk * chunk_width, (chunk + 1) * chunk_width)
        up_grad[...] = jnp.zeros_like(up_grad)
        down_grad[...] = jnp.zeros_like(down_grad)

        @pl.loop(0, SEG0 // tile)
        def _(step):
            rows = pl.ds(pl.multiple_of(step * tile, tile), tile)
            low = normed[pl.ds(step * slots, slots)].reshape(tile, width)
            back = cot[pl.ds(step * slots, slots)].reshape(tile, width)
            pre = jnp.dot(low, up[:, units], preferred_element_type=F32)
            grad = lax.dot_general(back, down[units], contract_last, preferred_element_type=F32)
            share = 0.5 + 0.5 * lax.erf(pre * math.sqrt(0.5))
            density = jnp.exp2(pre * pre * (-0.5 * LOG2E)) * (1.0 / math.sqrt(2.0 * math.pi))
            hidden = (pre * share).astype(BF)
            grad = (grad * (share + pre * density)).astype(BF)
            down_sum[rows] += jnp.dot(hidden, down[units], preferred_element_type=F32)
            norm_sum[rows] += lax.dot_general(grad, up[:, units], contract_last, preferred_element_type=F32)
            up_grad[...] += jnp.dot(normed_t[:, rows], grad, preferred_element_type=F32)
            down_grad[...] += jnp.dot(cot_t[:, rows], hidden, preferred_element_type=F32)

        pieces = totals.shape[3] * 4
        size = totals.shape[4]
        turned_down = down_grad[...].T
        for piece in range(pieces):
            spot = (piece // (2 * rest), piece // rest % 2, piece % rest)
            span = slice(piece * size, (piece + 1) * size)
            totals[(2 * chunk,) + spot] = up_grad[span].astype(BF)
            totals[(2 * chunk + 1,) + spot] = turned_down[span].astype(BF)
        firsts[2 * chunk].step(0)
        firsts[2 * chunk + 1].step(0)

    for ref, value in ((part, down_sum), (part_two, norm_sum)):

        @pl.loop(0, SLOTS)
        def _(slot):
            for device in range(head_size):
                begin = pl.multiple_of((slot * head_size + device) * per_slot, per_slot)
                ref[slot, device] = value[pl.ds(begin, per_slot)].astype(BF)

    for copy in head_copies(0, part_two, got_two, 2) + head_copies(0, part, got, 3):
        copy.start()
    for copy in head_copies(0, part_two, got_two, 2):
        copy.wait()
    gains_two[...] = jnp.zeros_like(gains_two)

    @pl.loop(0, SLOTS)
    def _(slot):
        grad = part_two[slot, me_head].astype(F32)
        for step in range(1, head_size):
            grad = grad + got_two[step - 1, slot].astype(F32)
        unit, scale = norm_of(hidden_one[rows_at(slot)])
        scaled = grad * gain[...]
        inner = jnp.mean(scaled * unit, axis=-1, keepdims=True)
        out = cot[slot, me_head].astype(F32) + scale * (
            scaled - jnp.mean(scaled, axis=-1, keepdims=True) - unit * inner
        )
        grad_hidden[rows_at(slot)] = out
        normed_own[slot] = out.astype(BF)
        normed[slot, me_head] = out.astype(BF)
        gains_two[0:1] += jnp.sum(grad * unit, axis=0, keepdims=True)
        gains_two[1:2] += jnp.sum(grad, axis=0, keepdims=True)

    for copy in head_copies(1, normed_own, normed, 4):
        copy.start()
    for copy in head_copies(0, part, got, 3):
        copy.wait()

    @pl.loop(0, SLOTS)
    def _(slot):
        value = hidden_one[rows_at(slot)] + part[slot, me_head].astype(F32)
        for step in range(1, head_size):
            value = value + got[step - 1, slot].astype(F32)
        place = slot % 2 * 8 + slot // 2 % 2 * 4 + slot // 4 % 2 * 2 + slot // 8
        for column in range(width // 128):
            lanes = slice(column * 128, (column + 1) * 128)
            spread_rows[column, pl.ds(place, per_slot, stride=SLOTS), :] = value[:, lanes]

    for column in range(width // 128):
        block_out[:, column * 128 : (column + 1) * 128] = spread_rows[column].astype(BF)
    for copy in head_copies(1, normed_own, normed, 4):
        copy.wait()

    value = jnp.dot(mixed[...].reshape(heads * E, SEG0), rows_of(normed), preferred_element_type=F32)
    size = out_total.shape[3]
    for piece in range(4 * rest):
        spot = (piece // (2 * rest), piece // rest % 2, piece % rest)
        out_total[spot] = value[piece * size : (piece + 1) * size].astype(BF)

    normed_t[...] = rows_of(normed).T
    value = jnp.dot(out_proj[...], normed_t[...], preferred_element_type=F32)
    own_g[0, :, :E, :] = value.astype(BF).reshape(heads, E, SEG0)

    @pl.loop(0, heads)
    def _(head):
        low = own_g[0, head, :E, :]
        dots = jnp.sum(low.astype(F32) * merged[head], axis=0, keepdims=True)
        d = pieces_of(-dots)
        m = pieces_of(-lse[head])
        placed = {0: d[0], 1: d[1], 2: d[2], 12: m[0], 13: m[1], 14: m[2]}
        own_g[0, head, E:, :] = row_block(placed, SEG0).astype(BF)
        own = jnp.concatenate([low.astype(F32), row_block(placed, SEG0)], axis=0)
        for branch in range(1, BRANCHES):
            stride, lanes, per, split = branch_shape(branch, heads)
            send, start = sends[branch - 1], starts[branch, head]
            share = max(1, 128 // lanes)
            span = lanes * share
            block = own[:, :span]
            for part_at in range(1, SEG0 // span):
                block = jnp.where(start // share == part_at, own[:, part_at * span : (part_at + 1) * span], block)
            if share > 1:
                block = packed(block, start % share)
            block = block.astype(BF)
            if split == 1:
                send[head // per, head % per] = block
            else:
                for copy in range(split):
                    send[head * split + copy, 0] = block

    for reduction in firsts:
        reduction.finish_first()


def middle(heads, starts, first, backs, x_rows, cot, out_proj, up, down, gain, shift):
    size, head_size = lax.axis_size("seq"), lax.axis_size("head")
    rest = size // 4
    rows, width = x_rows.shape
    per_slot = rows // SLOTS
    chunks = max(1, up.shape[1] // width)
    shard = (SLOTS, head_size, per_slot, width)
    own = (SLOTS, per_slot, width)
    got = (head_size - 1,) + own
    sends = send_shapes(heads, ROWS_OUT)[0]
    piece = (2, rest, width // size, up.shape[1] // chunks)
    out_piece = (2, 2, rest, heads * E // size, width)
    far = [x_rows, cot.reshape(shard), out_proj, up, down]
    results = pl.pallas_call(
        partial(middle_kernel, heads),
        in_specs=[pl.BlockSpec(memory_space=pltpu.SMEM)]
        + vmem_specs(1 + len(backs) + 2)
        + [pl.BlockSpec(memory_space=pl.ANY)] * 5,
        out_specs=vmem_specs(4 + len(sends) + 2 * chunks + 1),
        out_shape=[
            jax.ShapeDtypeStruct((rows, width), BF),
            jax.ShapeDtypeStruct((rows, width), F32),
            jax.ShapeDtypeStruct((2, width), F32),
            jax.ShapeDtypeStruct((1, heads, ROWS_OUT, SEG0), BF),
        ]
        + sends
        + [jax.ShapeDtypeStruct(piece, BF)] * (2 * chunks)
        + [jax.ShapeDtypeStruct(out_piece, BF)],
        scratch_shapes=[
            pltpu.VMEM((heads, E, SEG0), F32),
            pltpu.VMEM((heads, 1, SEG0), F32),
            pltpu.VMEM((heads, E, SEG0), BF),
            pltpu.VMEM((SEG0, heads * E), BF),
            pltpu.VMEM(shard, BF),
            pltpu.VMEM(got, BF),
            pltpu.VMEM(shard, BF),
            pltpu.VMEM(got, BF),
            pltpu.VMEM((rows, width), F32),
            pltpu.VMEM(own, BF),
            pltpu.VMEM(shard, BF),
            pltpu.VMEM((width // 128, rows, 128), F32),
            pltpu.VMEM((width, SEG0), BF),
            pltpu.VMEM((width, SEG0), BF),
            pltpu.VMEM((SEG0, width), F32),
            pltpu.VMEM((SEG0, width), F32),
            pltpu.VMEM((width, up.shape[1] // chunks), F32),
            pltpu.VMEM((width, up.shape[1] // chunks), F32),
            pltpu.VMEM((2 * chunks, 2) + piece, BF),
            pltpu.SemaphoreType.DMA((2, 5, head_size - 1)),
            pltpu.SemaphoreType.DMA((2, 2 * chunks)),
            pltpu.SemaphoreType.DMA((5,)),
        ]
        + [pltpu.VMEM(value.shape, value.dtype) for value in far],
        compiler_params=pltpu.CompilerParams(
            vmem_limit_bytes=60 * 2**20, collective_id=2, has_side_effects=True
        ),
        cost_estimate=pl.CostEstimate(
            flops=14 * SEG0 * width * up.shape[1], transcendentals=0, bytes_accessed=40 * 2**20
        ),
        name="middle",
    )(starts, first, *backs, gain, shift, *far)
    block_out, grad_hidden, gains_two, own_g = results[:4]
    return block_out, grad_hidden, gains_two, own_g, results[4 : 4 + len(sends)], results[4 + len(sends) :]


def rolled(value, step):
    size = lax.axis_size("head")
    return lax.ppermute(value, "head", [(s, (s + step) % size) for s in range(size)])


def all_rows(own):
    size = lax.axis_size("head")
    me = lax.axis_index("head")
    got = [own] + [rolled(own, step) for step in range(1, size)]
    if size == 2:
        return [jnp.where(me == 0, got[0], got[1]), jnp.where(me == 0, got[1], got[0])]
    stacked = jnp.stack(got)
    return [stacked[(me - place) % size] for place in range(size)]


def sum_rows(parts):
    size = lax.axis_size("head")
    me = lax.axis_index("head")
    total = lax.dynamic_index_in_dim(parts, me, 0, keepdims=False).astype(F32)
    for step in range(1, size):
        sent = lax.dynamic_index_in_dim(parts, (me + step) % size, 0, keepdims=False)
        total = total + rolled(sent, step).astype(F32)
    return total


def local(
    tokens,
    documents,
    offsets,
    in_proj,
    out_proj,
    up_proj,
    down_proj,
    first_gain,
    first_shift,
    second_gain,
    second_shift,
    cotangent,
):
    head_count = lax.axis_size("head")
    seq_id = lax.axis_index("seq")
    row_count, width = tokens.shape
    seq_len = row_count * head_count
    heads = offsets.shape[1]
    per_slot = row_count // SLOTS

    ids = lax.broadcasted_iota(jnp.int32, (row_count, row_count), 0)
    slot = reversed_bits(ids // per_slot, 4)
    source = ids % per_slot * SLOTS + slot
    order = (source == lax.broadcasted_iota(jnp.int32, (row_count, row_count), 1)).astype(BF)

    def sorted_rows(values):
        return jnp.dot(order, values, preferred_element_type=F32)

    def shard_rows(own):
        parts = [part.reshape(SLOTS, per_slot, -1) for part in all_rows(own)]
        return jnp.stack(parts, axis=1).reshape(seq_len, -1)

    def device_parts(values):
        split = values.reshape(SLOTS, head_count, per_slot, -1)
        return jnp.moveaxis(split, 1, 0).reshape(head_count, row_count, -1)

    x_rows = sorted_rows(tokens)
    cot_low = sorted_rows(cotangent).astype(BF)
    normed_one = norm_rows(x_rows, first_gain, first_shift)
    gathered_one = shard_rows(normed_one.astype(BF))
    cot_all = shard_rows(cot_low)

    my_docs = lax.dynamic_slice_in_dim(documents, seq_id * seq_len, seq_len)
    my_docs = my_docs.reshape(head_count, per_slot, 2, 2, 2, 2).transpose(5, 4, 3, 2, 0, 1).reshape(seq_len)
    bit_ids = jnp.arange(BIT_ROWS, dtype=jnp.int32)[:, None]
    doc_bit = my_docs[None, :] // 2 ** (bit_ids % DOC_BITS) % 2
    bits = jnp.where(bit_ids < DOC_BITS, doc_bit, jnp.where(bit_ids < 2 * DOC_BITS, 1 - doc_bit, 0))
    bits = bits.astype(BF)
    starts = jnp.stack([reversed_bits(offsets[b], b) for b in range(BRANCHES)])

    scales = jnp.array([E ** (-0.5) * LOG2E, 1.0, 1.0], F32)[:, None, None]
    projected = jnp.einsum("td,jdc->jct", gathered_one, in_proj, preferred_element_type=F32)
    projected = (projected * scales).astype(BF)
    own, *sends = pack_heads(heads, starts, projected, bits)
    first_out, units, outs = exchange_forward(heads, own, sends)
    block_out, grad_hidden, gains_two, own_g, sends_g, parts = middle(
        heads, starts, first_out, outs, x_rows, cot_all, out_proj, up_proj, down_proj,
        second_gain[None, :], second_shift[None, :],
    )
    (grad_up, grad_down, grad_out, grad_in), grad_tokens, gains = backward(
        heads, starts, own, own_g, units, sends_g, parts,
        gathered_one, in_proj, x_rows, grad_hidden, first_gain[None, :], gains_two,
    )
    return (
        block_out,
        grad_tokens,
        grad_in,
        grad_out,
        grad_up,
        grad_down,
        gains[0],
        gains[1],
        gains[2],
        gains[3],
    )


def solution(mesh):
    placed = (
        P(("seq", "head"), None),
        P(),
        P(None, "head"),
        P(None, None, "head"),
        P("head", None),
        P(None, "head"),
        P("head", None),
        P(),
        P(),
        P(),
        P(),
        P(("seq", "head"), None),
    )
    return jax.shard_map(
        local,
        mesh=mesh,
        in_specs=placed,
        out_specs=(
            P(("seq", "head"), None),
            P(("seq", "head"), None),
            P(None, None, "head"),
            P("head", None),
            P(None, "head"),
            P("head", None),
            P(),
            P(),
            P(),
            P(),
        ),
        check_vma=False,
    )
```

```python
import math
from functools import partial

import jax
import jax.numpy as jnp
from jax import lax
from jax.experimental import pallas as pl
from jax.experimental.pallas import tpu as pltpu
from jax.sharding import PartitionSpec as P

E = 48
BRANCHES = 5
SEG0 = 1024
SLOTS = 16
BIT_ROWS = 16
DOC_BITS = 6
ROWS_IN = 3 * E + BIT_ROWS
ROWS_OUT = E + BIT_ROWS
EPS = 1e-05
FAR = 1e30
LOG2E = math.log2(math.e)
LN2 = math.log(2.0)
BF = jnp.bfloat16
F32 = jnp.float32
VMEM_LIMIT = 48 * 2**20


def reversed_bits(value, count):
    out = jnp.zeros_like(value)
    for bit in range(count):
        out = out * 2 + value // 2**bit % 2
    return out


def branch_shape(branch, heads):
    stride = 2**branch
    return (stride, SEG0 // stride, max(1, heads // stride), max(1, stride // heads))


def pieces_of(value):
    high = value.astype(BF).astype(F32)
    rest = value - high
    middle = rest.astype(BF).astype(F32)
    return high, middle, (rest - middle).astype(BF).astype(F32)


def row_block(placed, columns):
    ids = lax.broadcasted_iota(jnp.int32, (BIT_ROWS, columns), 0)
    block = jnp.zeros((BIT_ROWS, columns), F32)
    for row, value in placed.items():
        block = jnp.where(ids == row, value, block)
    return block


def turned_half(block):
    return jnp.concatenate([block[:, 64:], block[:, :64]], axis=1)


def low_half():
    return lax.broadcasted_iota(jnp.int32, (1, 128), 1) < 64


def packed_rows(rows, count):
    return rows if count >= 128 else (rows // 2 + 15) // 16 * 16


def packed(block, half):
    rows = packed_rows(block.shape[0], 64)
    upper, lower = block[:rows], block[block.shape[0] - rows :]
    if isinstance(half, int):
        return jnp.where(low_half(), turned_half(upper) if half else upper, lower if half else turned_half(lower))
    upper = jnp.where(half == 0, upper, turned_half(upper))
    lower = jnp.where(half == 0, turned_half(lower), lower)
    return jnp.where(low_half(), upper, lower)


def unpacked(value, rows, half):
    size = value.shape[0]
    other = turned_half(value)
    upper = jnp.where(half == 0, value, other)
    lower = jnp.where(half == 0, other, value)
    both = jnp.concatenate([upper, lower[2 * size - rows :]], axis=0)
    return jnp.where(low_half() == (half == 0), both, 0.0)


def send_shapes(heads, rows):
    outs = []
    for branch in range(1, BRANCHES):
        stride, count, per, split = branch_shape(branch, heads)
        outs.append(jax.ShapeDtypeStruct((stride, per, packed_rows(rows, count), max(count, 128)), BF))
    return outs


def spread_blocks(heads, head, starts, value, sends):
    for branch in range(1, BRANCHES):
        stride, lanes, per, split = branch_shape(branch, heads)
        send, start = sends[branch - 1], starts[branch, head]
        share = max(1, 128 // lanes)
        span = lanes * share
        block = value[:, :span]
        for part in range(1, SEG0 // span):
            block = jnp.where(start // share == part, value[:, part * span : (part + 1) * span], block)
        if share > 1:
            block = packed(block, start % share)
        block = block.astype(BF)
        if split == 1:
            send[head // per, head % per] = block
        else:
            for copy in range(split):
                send[head * split + copy, 0] = block


def norm_of(values):
    centred = values - jnp.mean(values, axis=-1, keepdims=True)
    scale = lax.rsqrt(jnp.mean(centred * centred, axis=-1, keepdims=True) + EPS)
    return centred * scale, scale


def slot_place(slot):
    return slot % 2 * 8 + slot // 2 % 2 * 4 + slot // 4 % 2 * 2 + slot // 8


def over_slots(body, unroll=4):
    @pl.loop(0, SLOTS // unroll)
    def _(step):
        for part in range(unroll):
            body(step * unroll + part)


def head_copies(source, target, sems, index, scatter):
    size, me = lax.axis_size("head"), lax.axis_index("head")
    copies = []
    for step in range(1, size):
        device = (me + step) % size
        copies.append(
            pltpu.make_async_remote_copy(
                src_ref=source.at[:, device] if scatter else source,
                dst_ref=target.at[step - 1] if scatter else target.at[:, me],
                send_sem=sems.at[0, index, step - 1],
                recv_sem=sems.at[1, index, step - 1],
                device_id={"head": device},
                device_id_type=pl.DeviceIdType.MESH,
            )
        )
    return copies


def load_unit(ref, unit, count, x):
    width = ref.shape[-1]
    if count >= 128:
        for block in range(ref.shape[0]):
            x[:, block * width : (block + 1) * width] = ref[block, unit]
        return
    rows, size = x.shape[0], ref.shape[2]
    for block in range(ref.shape[0] // 2):
        lanes = slice(block * 128, (block + 1) * 128)
        left = ref[2 * block, unit].astype(F32)
        right = ref[2 * block + 1, unit].astype(F32)
        x[:size, lanes] = jnp.where(low_half(), left, turned_half(right)).astype(BF)
        x[rows - size :, lanes] = jnp.where(low_half(), turned_half(left), right).astype(BF)


def store_unit(ref, unit, count, result):
    width = ref.shape[-1]
    for block in range(SEG0 // width):
        value = result[:, block * width : (block + 1) * width]
        if count >= 128:
            ref[block, unit] = value
        else:
            value = value.astype(F32)
            ref[2 * block, unit] = packed(value, 0).astype(BF)
            ref[2 * block + 1, unit] = packed(value, 1).astype(BF)


def forward_unit(x, q_aug, result, base, queries):
    if isinstance(base, int):
        lanes = slice(base, base + queries)
    else:
        lanes = pl.ds(pl.multiple_of(base, 128), queries)
    q_aug[0:E, :queries] = x[0:E, lanes]
    q_aug[E:, :queries] = (x[3 * E :, lanes].astype(F32) * -FAR).astype(BF)
    bits = x[3 * E :, :].astype(F32)
    k_rows = jnp.concatenate([x[E : 2 * E, :], (1.0 - bits).astype(BF)], axis=0).T
    v_aug = jnp.concatenate([x[2 * E : 3 * E, :], jnp.ones(bits.shape, BF)], axis=0)
    if queries < SEG0:
        result[0:E, :] = jnp.zeros((E, SEG0), BF)
        result[E:, :] = row_block({0: -FAR}, SEG0).astype(BF)
    s = jnp.dot(k_rows, q_aug[:, :queries], preferred_element_type=F32)
    top = jnp.max(s, axis=0, keepdims=True)
    p = jnp.exp2(s - top).astype(BF)
    o = jnp.dot(v_aug, p, preferred_element_type=F32)
    total = o[E : E + 1]
    high, middle_part, low = pieces_of(top + jnp.log2(total))
    block = row_block({0: high, 1: middle_part, 2: low}, queries)
    result[:, lanes] = jnp.concatenate([o[:E] * (1.0 / total), block], axis=0).astype(BF)


class Names:
    def __init__(self, refs):
        self.refs = list(refs)

    def take(self, count):
        taken, self.refs = self.refs[:count], self.refs[count:]
        return taken

    def one(self):
        return self.take(1)[0]


def group_place(branch):
    stride = 2**branch
    me = lax.axis_index("seq")
    return me // stride * stride, me % stride


def meet(*axes):
    barrier = pltpu.get_barrier_semaphore()
    count = 0
    for axis in axes:
        size = lax.axis_size(axis)
        me = lax.axis_index(axis)

        @pl.loop(1, size)
        def _(step):
            pl.semaphore_signal(
                barrier, inc=1, device_id={axis: (me + step) % size}, device_id_type=pl.DeviceIdType.MESH
            )

        count += size - 1
    pl.semaphore_wait(barrier, count)


class Reduction:
    STEPS = 7

    def __init__(self, order, total, half, quarter, others, send, recv, begun=False):
        self.total, self.begun = total, begun
        self.half, self.quarter, self.others = half, quarter, others
        self.send, self.recv = send, recv
        me = lax.axis_index("seq")
        self.rest = lax.axis_size("seq") // 4
        self.me = me
        bits = (me % 2, me // 2 % 2)
        self.bits = [bits[bit] for bit in order]
        self.partners = [me + (1 - 2 * bits[bit]) * 2**bit for bit in order]
        self.place = me // 4

    def copy(self, source, target, device, sem):
        return pltpu.make_async_remote_copy(
            src_ref=source,
            dst_ref=target,
            send_sem=self.send.at[sem],
            recv_sem=self.recv.at[sem],
            device_id={"seq": device},
            device_id_type=pl.DeviceIdType.MESH,
        )

    def copies(self, number):
        one, two = self.bits
        rest = self.rest
        others = []
        for step in range(1, rest):
            place = (self.place + step) % rest
            others.append((step, place, place * 4 + self.me % 4))
        if number == 0:
            return [self.copy(self.total.at[1 - one], self.half, self.partners[0], 0)]
        if number == 1:
            return [self.copy(self.half.at[1 - two], self.quarter, self.partners[1], 1)]
        if number == 2:
            return [
                self.copy(self.quarter.at[place], self.others.at[step - 1], device, 1 + step)
                for step, place, device in others
            ]
        if number == 3:
            block = self.total.at[one, two, self.place]
            return [self.copy(block, block, device, rest + step) for step, place, device in others]
        if number == 4:
            block = self.total.at[one, two]
            return [self.copy(block, block, self.partners[1], 2 * rest)]
        if number == 5:
            block = self.total.at[one]
            return [self.copy(block, block, self.partners[0], 2 * rest + 1)]
        return []

    def finish_first(self):
        one, rest = self.bits[0], self.rest
        for copy in self.copies(0):
            copy.wait()

        @pl.loop(0, 2 * rest)
        def _(i):
            j, z = i // rest, i % rest
            mine = self.total[one, j, z].astype(F32)
            self.half[j, z] = (mine + self.half[j, z].astype(F32)).astype(BF)

    def step(self, number):
        one, two = self.bits
        rest = self.rest
        if number == 0 and self.begun:
            return
        if number == 1:
            if not self.begun:
                self.finish_first()
        elif number > 0:
            for copy in self.copies(number - 1):
                copy.wait()
        if number == 2:

            @pl.loop(0, rest)
            def _(z):
                mine = self.half[two, z].astype(F32)
                self.quarter[z] = (mine + self.quarter[z].astype(F32)).astype(BF)

        elif number == 3:
            mine = self.quarter[self.place].astype(F32)
            for step in range(1, rest):
                mine = mine + self.others[step - 1].astype(F32)
            self.total[one, two, self.place] = mine.astype(BF)
        for copy in self.copies(number):
            copy.start()

    @staticmethod
    def scratch(size, rows, columns):
        rest = size // 4
        count = 2 * rest + 2
        return [
            pltpu.VMEM((2, rest, rows, columns), BF),
            pltpu.VMEM((rest, rows, columns), BF),
            pltpu.VMEM((rest - 1, rows, columns), BF),
            pltpu.SemaphoreType.DMA((count,)),
            pltpu.SemaphoreType.DMA((count,)),
        ]


def reduction_parts(value, size):
    rows, columns = value.shape
    return value.reshape(2, 2, size // 4, rows // size, columns)


def reduction_whole(value):
    return value.reshape(-1, value.shape[-1])


def make_reductions(orders, totals, scratch):
    out = []
    for order, total in zip(orders, totals):
        out.append(Reduction(order, total, *scratch[:5]))
        scratch = scratch[5:]
    return out


def group_copies(branch, source, target, send_sems, recv_sems, local_sem):
    stride = 2**branch
    base, place = group_place(branch)
    first = stride - branch - 2
    copies = [
        pltpu.make_async_copy(source.at[place], target.at[place], local_sem.at[branch - 1])
    ]
    for step in range(1, stride):
        member = (place + step) % stride
        copies.append(
            pltpu.make_async_remote_copy(
                src_ref=source.at[member],
                dst_ref=target.at[place],
                send_sem=send_sems.at[first + step],
                recv_sem=recv_sems.at[first + step],
                device_id={"seq": base + member},
                device_id_type=pl.DeviceIdType.MESH,
            )
        )
    return copies


def forward_kernel(heads, starts, tokens, cotangent, bits, scales, in_proj, *refs):
    count = BRANCHES - 1
    names = Names(refs)
    x_rows, normed, cot, own, first = names.take(5)
    gots, backs, outs, sends = names.take(count), names.take(count), names.take(count), names.take(count)
    x, q_aug, result, in_send, in_recv, in_local, out_send, out_recv, out_local = names.take(9)
    spread_rows, normed_own, cot_own, normed_t, head_sems = names.take(5)
    me_head = lax.axis_index("head")
    rows, width = tokens.shape
    per_slot = rows // SLOTS

    def fill(source):
        for column in range(width // 128):
            spread_rows[column] = source[:, column * 128 : (column + 1) * 128].astype(F32)

    def picked(slot):
        at = pl.ds(slot_place(slot), per_slot, stride=SLOTS)
        return jnp.concatenate([spread_rows[column, at, :] for column in range(width // 128)], axis=1)

    fill(tokens)

    @over_slots
    def _(slot):
        value = picked(slot)
        x_rows[pl.ds(pl.multiple_of(slot * per_slot, per_slot), per_slot)] = value
        low = (norm_of(value)[0] * scales[0:1] + scales[1:2]).astype(BF)
        normed_own[slot] = low
        normed[slot, me_head] = low

    meet("seq", "head")
    for copy in head_copies(normed_own, normed, head_sems, 0, False):
        copy.start()
    fill(cotangent)

    @over_slots
    def _(slot):
        low = picked(slot).astype(BF)
        cot_own[slot] = low
        cot[slot, me_head] = low

    for copy in head_copies(cot_own, cot, head_sems, 1, False):
        copy.start()
    own[0, :, 3 * E :, :] = jnp.broadcast_to(bits[...][None], (heads,) + bits.shape)
    turned = [in_proj[j].T for j in range(3)]
    for copy in head_copies(normed_own, normed, head_sems, 0, False):
        copy.wait()
    normed_t[...] = normed[...].reshape(SEG0, width).T
    for j in range(3):
        value = jnp.dot(turned[j], normed_t[...], preferred_element_type=F32)
        if j == 0:
            value = value * (E ** (-0.5) * LOG2E)
        own[0, :, j * E : (j + 1) * E, :] = value.astype(BF).reshape(heads, E, SEG0)

    @pl.loop(0, heads)
    def _(head):
        spread_blocks(heads, head, starts, own[0, head].astype(F32), sends)

    coming = {}
    for branch in range(1, BRANCHES):
        coming[branch] = group_copies(branch, sends[branch - 1], gots[branch - 1], in_send, in_recv, in_local)
        for copy in coming[branch]:
            copy.start()

    @pl.loop(0, heads)
    def _(head):
        x[...] = own[0, head]
        forward_unit(x, q_aug, result, 0, SEG0)
        first[0, head] = result[...]

    leaving = []
    for branch in range(1, BRANCHES):
        stride, lanes, units, split = branch_shape(branch, heads)
        got, out = gots[branch - 1], outs[branch - 1]
        for copy in coming[branch]:
            copy.wait()
        queries = SEG0 // split
        base = 0 if split == 1 else lax.axis_index("seq") % split * queries

        @pl.loop(0, units)
        def _(unit):
            load_unit(got, unit, lanes, x)
            forward_unit(x, q_aug, result, base, queries)
            store_unit(out, unit, lanes, result)

        copies = group_copies(branch, out, backs[branch - 1], out_send, out_recv, out_local)
        for copy in copies:
            copy.start()
        leaving += copies
    for copy in leaving + head_copies(cot_own, cot, head_sems, 1, False):
        copy.wait()


def exchange_scratch():
    copies = 2**BRANCHES - 2 - BRANCHES + 1
    one = [
        pltpu.SemaphoreType.DMA((copies,)),
        pltpu.SemaphoreType.DMA((copies,)),
        pltpu.SemaphoreType.DMA((BRANCHES - 1,)),
    ]
    return one + one


def unit_cost(units, dots):
    return pl.CostEstimate(
        flops=dots * 2 * units * SEG0 * SEG0 * 256,
        transcendentals=units * SEG0 * SEG0,
        bytes_accessed=units * SEG0 * 1000,
    )


def vmem_specs(count):
    return [pl.BlockSpec(memory_space=pltpu.VMEM)] * count


def forward(heads, starts, tokens, cotangent, bits, scales, in_proj):
    head_size = lax.axis_size("head")
    rows, width = tokens.shape
    shard = jax.ShapeDtypeStruct((SLOTS, head_size, rows // SLOTS, width), BF)
    own_rows = pltpu.VMEM((SLOTS, rows // SLOTS, width), BF)
    backs = send_shapes(heads, ROWS_OUT)
    gots = send_shapes(heads, ROWS_IN)
    results = pl.pallas_call(
        partial(forward_kernel, heads),
        in_specs=[pl.BlockSpec(memory_space=pltpu.SMEM)] + vmem_specs(5),
        out_specs=vmem_specs(5 + len(gots) + len(backs)),
        out_shape=[
            jax.ShapeDtypeStruct((rows, width), F32),
            shard,
            shard,
            jax.ShapeDtypeStruct((1, heads, ROWS_IN, SEG0), BF),
            jax.ShapeDtypeStruct((1, heads, ROWS_OUT, SEG0), BF),
        ]
        + gots
        + backs,
        scratch_shapes=[pltpu.VMEM(shape.shape, BF) for shape in backs + gots]
        + [
            pltpu.VMEM((ROWS_IN, SEG0), BF),
            pltpu.VMEM((ROWS_OUT, SEG0), BF),
            pltpu.VMEM((ROWS_OUT, SEG0), BF),
        ]
        + exchange_scratch()
        + [
            pltpu.VMEM((width // 128, rows, 128), F32),
            own_rows,
            own_rows,
            pltpu.VMEM((width, SEG0), BF),
            pltpu.SemaphoreType.DMA((2, 2, head_size - 1)),
        ],
        compiler_params=pltpu.CompilerParams(
            vmem_limit_bytes=60 * 2**20, collective_id=0, has_side_effects=True
        ),
        cost_estimate=unit_cost(2 * heads, 2),
        name="forward",
    )(starts, tokens, cotangent, bits, scales, in_proj)
    return results[:5], results[5 : 5 + len(gots)], results[5 + len(gots) :]


def backward_unit(x, g, q_aug, gk, gv, result, base, queries, tile):
    if isinstance(base, int):
        lanes = slice(base, base + queries)
    else:
        lanes = pl.ds(pl.multiple_of(base, 128), queries)
    extra = g[E:, lanes].astype(F32)
    ids = lax.broadcasted_iota(jnp.int32, extra.shape, 0)
    q = x[0:E, lanes]
    q_aug[0:E, :queries] = q
    q_aug[E:, :queries] = jnp.where(ids >= 12, extra, x[3 * E :, lanes].astype(F32) * -FAR).astype(BF)
    bits = x[3 * E :, :].astype(F32)
    k_aug = jnp.concatenate([x[E : 2 * E, :], (1.0 - bits).astype(BF)], axis=0)
    k_rows = k_aug.T
    v_ids = lax.broadcasted_iota(jnp.int32, bits.shape, 0)
    v_bits = jnp.where(v_ids < 3, 1.0, 0.0).astype(BF)
    v_rows = jnp.concatenate([x[2 * E : 3 * E, :], v_bits], axis=0).T
    q_rows = jnp.concatenate([q, jnp.zeros((BIT_ROWS, queries), BF)], axis=0).T
    g_all = g[:, lanes]
    g_rows = g_all.T
    if queries < SEG0:
        result[0:E, :] = jnp.zeros((E, SEG0), BF)
    for step in range(queries // tile):
        column = step * tile
        span = slice(column, column + tile)
        p = jnp.exp2(jnp.dot(k_rows, q_aug[:, span], preferred_element_type=F32))
        gs = p * jnp.dot(v_rows, g_all[:, span], preferred_element_type=F32)
        p, gs = p.astype(BF), gs.astype(BF)
        target = span if isinstance(base, int) else pl.ds(pl.multiple_of(base + column, 128), tile)
        result[0:E, target] = jnp.dot(k_aug, gs, preferred_element_type=F32)[:E].astype(BF)
        new_k = jnp.dot(gs, q_rows[span], preferred_element_type=F32)
        new_v = jnp.dot(p, g_rows[span], preferred_element_type=F32)
        if step == 0:
            gk[...] = new_k
            gv[...] = new_v
        else:
            gk[...] += new_k
            gv[...] += new_v
    result[E : 2 * E, :] = (gk[...].T[:E] * LN2).astype(BF)
    result[2 * E :, :] = gv[...].T[:E].astype(BF)


ORDERS = {
    'u1': (0, 1), 'u2': (0, 1), 'd1': (1, 0), 'd2': (1, 0), 'o': (0, 1), 'i0': (1, 0), 'i1': (1, 0), 'i2': (0,
    1),
}
EARLY = [
    (0, 'd1', 0), (0, 'u1', 0), (0, 'd1', 1), (0, 'u2', 0), (0, 'u1', 1), (2, 'o', 0), (4, 'u2', 1), (5, 'u1',
    2), (7, 'd1', 2), (9, 'u1', 3), (10, 'd2', 0), (12, 'd2', 1), (12, 'o', 1), (12, 'd1', 3), (13, 'u2', 2),
    (14, 'u1', 4),
]
TAIL = [
    'gather', ('d1', 4), 'in1', ('i1', 0), ('d2', 2), 'in2', ('u2', 3), ('i2', 0), 'in0', ('i0', 0), ('d2',
    3), ('i1', 1), ('i2', 1), ('u1', 5), ('u2', 4), ('d2', 4), ('d1', 5), ('o', 2), ('i2', 2), ('i0', 1),
    ('i1', 2), ('i2', 3), 'one', ('d2', 5), ('o', 3), ('i1', 3), ('u1', 6), ('u2', 5), 'norm', ('i2', 4),
    'gain0', ('i0', 2), ('i1', 4), ('i0', 3), 'gain1', ('o', 4), ('i0', 4), ('i2', 5), 'gain2', ('i1', 5),
    ('o', 5), ('i0', 5), 'gain3', ('i0', 6), ('d2', 6), ('u2', 6), 'gain4', ('d1', 6), ('i1', 6), ('i2', 6),
    ('o', 6),
]


def stream_names(streams):
    pairs = streams // 2
    return [kind + str(i + 1) for i in range(pairs) for kind in "ud"] + ["o"]


def backward_kernel(heads, streams, *refs):
    branches = BRANCHES - 1
    names = Names(refs)
    starts, own, own_g = names.take(3)
    sends, gain, gains_two = names.take(branches), *names.take(2)
    far = names.take(branches + 4)
    parts = names.take(streams)
    up_total, down_total, out_total, in_total = names.take(4)
    chunks = (streams - 1) // 2
    totals = []
    for chunk in range(chunks):
        lanes = pl.ds(chunk * (up_total.shape[-1] // chunks), up_total.shape[-1] // chunks)
        totals += [up_total.at[:, :, :, :, lanes], down_total.at[chunk]]
    totals.append(out_total)
    in_totals = [in_total.at[j] for j in range(3)]
    grad_tokens, gains_out = names.take(2)
    near = names.take(branches + 4)
    units_in, (normed, in_proj, x_rows, grad_hidden) = near[:branches], near[branches:]
    far_sem = names.one()
    first = names.one()
    backs, gots, outs = names.take(branches), names.take(branches), names.take(branches)
    x, g, q_aug, gk, gv, result = names.take(6)
    total, grads, grads_t, normed_t, spread_rows, head_send, head_recv = names.take(7)
    gain_head, gain_one, gain_two, gain_rest = names.take(4)
    in_send, in_recv, in_local, out_send, out_recv, out_local = names.take(6)
    part_sem, head_sems, gain_sems = names.take(3)
    labels = stream_names(streams) + ["i0", "i1", "i2"]
    reductions = make_reductions(
        [ORDERS[label] for label in labels], list(totals) + list(in_totals), names.take(5 * streams + 15)
    )
    reductions = dict(zip(labels, reductions))
    for label in labels[: streams - 1]:
        reductions[label].begun = True

    shapes = [branch_shape(b, heads) for b in range(BRANCHES)]
    size, head_size = lax.axis_size("seq"), lax.axis_size("head")
    me, me_head = lax.axis_index("seq"), lax.axis_index("head")
    rest = size // 4
    tile = 512
    per_slot = x_rows.shape[0] // SLOTS
    width = x_rows.shape[1]

    fills = [
        pltpu.make_async_copy(parts[s], reductions[labels[s]].half, part_sem.at[s]) for s in range(streams - 1)
    ] + [pltpu.make_async_copy(parts[-1], totals[-1], part_sem.at[streams - 1])]
    loads = [pltpu.make_async_copy(far[i], near[i], far_sem.at[i]) for i in range(branches + 4)]
    for copy in fills + loads:
        copy.start()
    meet("seq", "head")

    def coming(branch):
        return group_copies(branch, sends[branch - 1], gots[branch - 1], in_send, in_recv, in_local)

    def leaving(branch):
        return group_copies(branch, outs[branch - 1], backs[branch - 1], out_send, out_recv, out_local)

    for branch in range(1, BRANCHES):
        for copy in coming(branch):
            copy.start()
    for copy in fills + loads:
        copy.wait()

    def split_branch(branch):
        stride, lanes, units, split = shapes[branch]
        queries = SEG0 // split
        for copy in coming(branch):
            copy.wait()
        load_unit(units_in[branch - 1], 0, lanes, x)
        load_unit(gots[branch - 1], 0, lanes, g)
        backward_unit(x, g, q_aug, gk, gv, result, me % split * queries, queries, min(tile, queries))
        store_unit(outs[branch - 1], 0, lanes, result)

    runs, at = [(0, 0, 0, heads // 2)], heads // 2
    split_at = None
    for branch in range(1, BRANCHES):
        if shapes[branch][3] == 1:
            runs.append((branch, at, 0, shapes[branch][2]))
            at += shapes[branch][2]
    split_at = at
    runs.append((0, at, heads // 2, heads - heads // 2))
    blocks = at + heads - heads // 2
    plan = {}
    for block, stream, step in EARLY:
        if stream in labels:
            plan.setdefault(block * blocks // 15, []).append((stream, step))

    @pl.loop(0, blocks)
    def _(block):
        for after, events in plan.items():

            @pl.when(block == after)
            def _(events=events):
                for stream, step in events:
                    reductions[stream].step(step)

        @pl.when(block == split_at)
        def _():
            for branch in range(1, BRANCHES):
                if shapes[branch][3] > 1:
                    split_branch(branch)
                    for copy in leaving(branch):
                        copy.start()

        for branch, low, unit, count in runs:

            @pl.when((block >= low) & (block < low + count))
            def _(branch=branch, low=low, unit=unit):
                if branch == 0:
                    x[...] = own[0, block - low + unit]
                    g[...] = own_g[0, block - low + unit]
                else:

                    @pl.when(block == low)
                    def _():
                        for copy in coming(branch):
                            copy.wait()

                    load_unit(units_in[branch - 1], block - low, shapes[branch][1], x)
                    load_unit(gots[branch - 1], block - low, shapes[branch][1], g)

        backward_unit(x, g, q_aug, gk, gv, result, 0, SEG0, tile)
        for branch, low, unit, count in runs:

            @pl.when((block >= low) & (block < low + count))
            def _(branch=branch, low=low, unit=unit, count=count):
                if branch == 0:
                    first[block - low + unit] = result[...]
                else:
                    store_unit(outs[branch - 1], block - low, shapes[branch][1], result)

                    @pl.when(block == low + count - 1)
                    def _():
                        for copy in leaving(branch):
                            copy.start()

    tasks = {}

    def task(work):
        tasks[work.__name__] = work

    @task
    def gather():
        for branch in range(1, BRANCHES):
            for copy in leaving(branch):
                copy.wait()

        @pl.loop(0, heads)
        def _(head):
            total[...] = first[head].astype(F32)
            for branch in range(1, BRANCHES):
                stride, lanes, per, split = shapes[branch]
                back, start = backs[branch - 1], starts[branch, head]
                if split == 1:
                    value = back[head // per, head % per].astype(F32)
                else:
                    value = back[head * split, 0].astype(F32)
                    for copy in range(1, split):
                        value = value + back[head * split + copy, 0].astype(F32)
                if lanes < 128:
                    value = unpacked(value, 3 * E, start % 2)
                    start = start // 2
                    lanes = 128
                for block in range(SEG0 // lanes):
                    span = slice(block * lanes, (block + 1) * lanes)
                    total[:, span] += jnp.where(start == block, value, 0.0)
            grads[0, head] = (total[0:E, :] * E ** (-0.5)).astype(BF)
            grads[1, head] = total[E : 2 * E, :].astype(BF)
            grads[2, head] = total[2 * E :, :].astype(BF)

        normed_t[...] = normed[...].reshape(SEG0, width).T

    def in_gradient(j):
        rows_in = in_totals[0].shape[3]
        chunk = width // 2
        grads_t[j] = grads[j].reshape(heads * E, SEG0).T
        for half in range(2):
            value = jnp.dot(
                normed_t[half * chunk : (half + 1) * chunk], grads_t[j], preferred_element_type=F32
            ).astype(BF)
            for part in range(chunk // rows_in):
                index = half * (chunk // rows_in) + part
                in_totals[j][index // (2 * rest), index // rest % 2, index % rest] = value[
                    part * rows_in : (part + 1) * rows_in
                ]

    for j in range(3):
        tasks[f"in{j}"] = partial(in_gradient, j)

    def head_swaps():
        swaps = []
        for step in range(1, head_size):
            device = (me_head + step) % head_size
            swaps.append(
                pltpu.make_async_remote_copy(
                    src_ref=head_send.at[device],
                    dst_ref=head_recv.at[step - 1],
                    send_sem=head_sems.at[0, step - 1],
                    recv_sem=head_sems.at[1, step - 1],
                    device_id={"head": device},
                    device_id_type=pl.DeviceIdType.MESH,
                )
            )
        return swaps

    @task
    def one():
        for half in range(2):
            rows = slice(half * SEG0 // 2, (half + 1) * SEG0 // 2)
            value = jnp.zeros((SEG0 // 2, width), F32)
            for j in range(3):
                value = value + lax.dot_general(
                    grads_t[j, rows], in_proj[j], (((1,), (1,)), ((), ())), preferred_element_type=F32
                )
            value = value.astype(BF)
            for slot in range(SLOTS // 2):
                for device in range(head_size):
                    begin = (slot * head_size + device) * per_slot
                    place = (half * SLOTS // 2 + slot) * per_slot
                    head_send[device, place : place + per_slot] = value[begin : begin + per_slot]
        for swap in head_swaps():
            swap.start()

    @task
    def norm():
        for swap in head_swaps():
            swap.wait()
        gain_head[me_head] = jnp.zeros(gains_out.shape, F32)
        gain_head[me_head, 2:4] = gains_two[...]

        @pl.loop(0, SLOTS)
        def _(slot):
            rows = pl.ds(pl.multiple_of(slot * per_slot, per_slot), per_slot)
            grad = head_send[me_head, rows].astype(F32)
            for step in range(1, head_size):
                grad = grad + head_recv[step - 1, rows].astype(F32)
            values = x_rows[rows]
            centred = values - jnp.mean(values, axis=-1, keepdims=True)
            scale = lax.rsqrt(jnp.mean(centred * centred, axis=-1, keepdims=True) + EPS)
            unit = centred * scale
            scaled = grad * gain[0:1]
            inner = jnp.mean(scaled * unit, axis=-1, keepdims=True)
            out = grad_hidden[rows] + scale * (
                scaled - jnp.mean(scaled, axis=-1, keepdims=True) - unit * inner
            )
            place = slot_place(slot)
            for column in range(width // 128):
                lanes = slice(column * 128, (column + 1) * 128)
                spread_rows[column, pl.ds(place, per_slot, stride=SLOTS), :] = out[:, lanes]
            gain_head[me_head, 0:1] += jnp.sum(grad * unit, axis=0, keepdims=True)
            gain_head[me_head, 1:2] += jnp.sum(grad, axis=0, keepdims=True)

        for column in range(width // 128):
            grad_tokens[:, column * 128 : (column + 1) * 128] = spread_rows[column]

    def gain_copy(source, target, axis, device, sem):
        return pltpu.make_async_remote_copy(
            src_ref=source,
            dst_ref=target,
            send_sem=gain_sems.at[0, sem],
            recv_sem=gain_sems.at[1, sem],
            device_id={axis: device},
            device_id_type=pl.DeviceIdType.MESH,
        )

    def gain_copies(stage):
        if stage == 0:
            mine = gain_head.at[me_head]
            return [
                gain_copy(mine, mine, "head", (me_head + step) % head_size, step - 1)
                for step in range(1, head_size)
            ]
        if stage == 1:
            return [gain_copy(gain_one.at[0], gain_one.at[1], "seq", me + 1 - 2 * (me % 2), head_size)]
        if stage == 2:
            device = me + 2 - 4 * (me // 2 % 2)
            return [gain_copy(gain_two.at[0], gain_two.at[1], "seq", device, head_size + 1)]
        spot = me // 4
        block = gain_rest.at[spot]
        return [
            gain_copy(block, block, "seq", (spot + step) % rest * 4 + me % 4, head_size + 1 + step)
            for step in range(1, rest)
        ]

    def summed(ref, count):
        value = ref[0]
        for index in range(1, count):
            value = value + ref[index]
        return value

    def gain_stage(stage):
        if stage > 0:
            for swap in gain_copies(stage - 1):
                swap.wait()
        if stage == 1:
            gain_one[0] = summed(gain_head, head_size)
        elif stage == 2:
            gain_two[0] = summed(gain_one, 2)
        elif stage == 3:
            gain_rest[me // 4] = summed(gain_two, 2)
        elif stage == 4:
            gains_out[...] = summed(gain_rest, rest)
            return
        for swap in gain_copies(stage):
            swap.start()

    for stage in range(5):
        tasks[f"gain{stage}"] = partial(gain_stage, stage)

    for item in TAIL:
        if isinstance(item, str):
            tasks[item]()
        elif item[0] in labels:
            reductions[item[0]].step(item[1])


def backward(heads, starts, own, own_g, units, sends, parts, normed, in_proj, x_rows, grad_hidden, gain, gains_two):
    size, head_size = lax.axis_size("seq"), lax.axis_size("head")
    rest = size // 4
    rows, width = x_rows.shape
    in_shape = (2, 2, rest, width // size, heads * E)
    scratch = []
    for part in parts:
        scratch += Reduction.scratch(size, *part.shape[-2:])
    for _ in range(3):
        scratch += Reduction.scratch(size, *in_shape[-2:])
    streams = len(parts)
    chunks = (streams - 1) // 2
    far = list(units) + [normed, in_proj, x_rows, grad_hidden]
    results = pl.pallas_call(
        partial(backward_kernel, heads, streams),
        in_specs=[pl.BlockSpec(memory_space=pltpu.SMEM)]
        + vmem_specs(2 + len(sends) + 2)
        + [pl.BlockSpec(memory_space=pl.ANY)] * (len(far) + streams),
        out_specs=vmem_specs(6),
        out_shape=[
            jax.ShapeDtypeStruct((2, 2, rest, width // size, chunks * parts[0].shape[-1]), BF),
            jax.ShapeDtypeStruct((chunks, 2, 2, rest) + parts[1].shape[-2:], BF),
            jax.ShapeDtypeStruct(parts[-1].shape, BF),
            jax.ShapeDtypeStruct((3,) + in_shape, BF),
        ]
        + [jax.ShapeDtypeStruct((rows, width), F32), jax.ShapeDtypeStruct((8, width), F32)],
        scratch_shapes=[pltpu.VMEM(value.shape, value.dtype) for value in far]
        + [pltpu.SemaphoreType.DMA((len(far),)), pltpu.VMEM((heads, 3 * E, SEG0), BF)]
        + [pltpu.VMEM(shape.shape, BF) for shape in send_shapes(heads, 3 * E)]
        + [pltpu.VMEM(shape.shape, BF) for shape in send_shapes(heads, ROWS_OUT)]
        + [pltpu.VMEM(shape.shape, BF) for shape in send_shapes(heads, 3 * E)]
        + [
            pltpu.VMEM((ROWS_IN, SEG0), BF),
            pltpu.VMEM((ROWS_OUT, SEG0), BF),
            pltpu.VMEM((ROWS_OUT, SEG0), BF),
            pltpu.VMEM((SEG0, ROWS_OUT), F32),
            pltpu.VMEM((SEG0, ROWS_OUT), F32),
            pltpu.VMEM((3 * E, SEG0), BF),
            pltpu.VMEM((3 * E, SEG0), F32),
            pltpu.VMEM((3, heads, E, SEG0), BF),
            pltpu.VMEM((3, SEG0, heads * E), BF),
            pltpu.VMEM((width, SEG0), BF),
            pltpu.VMEM((width // 128, rows, 128), F32),
            pltpu.VMEM((head_size, rows, width), BF),
            pltpu.VMEM((head_size - 1, rows, width), BF),
            pltpu.VMEM((head_size, 8, width), F32),
            pltpu.VMEM((2, 8, width), F32),
            pltpu.VMEM((2, 8, width), F32),
            pltpu.VMEM((rest, 8, width), F32),
        ]
        + exchange_scratch()
        + [
            pltpu.SemaphoreType.DMA((streams,)),
            pltpu.SemaphoreType.DMA((2, head_size - 1)),
            pltpu.SemaphoreType.DMA((2, head_size + 1 + rest)),
        ]
        + scratch,
        compiler_params=pltpu.CompilerParams(
            vmem_limit_bytes=60 * 2**20, collective_id=1, has_side_effects=True
        ),
        cost_estimate=unit_cost(2 * heads, 5),
        name="backward",
    )(starts, own, own_g, *sends, gain, gains_two, *far, *parts)
    up_total, down_total, out_total, in_total = results[:4]
    sums = [
        up_total.reshape(width, -1).astype(F32),
        down_total.reshape(-1, width).astype(F32),
        out_total.reshape(-1, width).astype(F32),
        in_total.reshape(3, width, heads * E).astype(F32),
    ]
    return sums, results[4], results[5]


def middle_kernel(heads, *refs):
    branches = BRANCHES - 1
    names = Names(refs)
    starts, first = names.take(2)
    backs = names.take(branches)
    scales = names.one()
    far = names.take(5)
    block_out, grad_hidden, gains_two, own_g = names.take(4)
    sends = names.take(branches)
    chunks = max(1, far[3].shape[1] // far[0].shape[1])
    halves = names.take(2 * chunks)
    out_total = names.one()
    merged, lse, mixed, turned, part, got, part_two, got_two = names.take(8)
    hidden_one, normed_own, normed, spread_rows, normed_t, cot_t = names.take(6)
    down_sum, norm_sum, up_grad, down_grad, totals = names.take(5)
    head_sems, first_sems, far_sem = names.take(3)
    near = names.take(5)
    out_proj, x_rows, cot, up, down = near[2], near[0], near[1], near[3], near[4]
    loads = [pltpu.make_async_copy(far[i], near[i], far_sem.at[i]) for i in range(5)]
    for copy in loads:
        copy.start()

    head_size, me_head = lax.axis_size("head"), lax.axis_index("head")
    me = lax.axis_index("seq")
    rest = lax.axis_size("seq") // 4
    width = x_rows.shape[1]
    per_slot = x_rows.shape[0] // SLOTS
    tile = 256

    meet("seq", "head")

    @pl.loop(0, heads)
    def _(head):
        own = first[0, head].astype(F32)
        merged[head] = own[:E]
        lse[head] = own[E : E + 1] + own[E + 1 : E + 2] + own[E + 2 : E + 3]
        for branch in range(1, BRANCHES):
            stride, lanes, per, split = branch_shape(branch, heads)
            back, start = backs[branch - 1], starts[branch, head]
            share = max(1, 128 // lanes)
            for copy in range(split):
                if split == 1:
                    value = back[head // per, head % per].astype(F32)
                else:
                    value = back[head * split + copy, 0].astype(F32)
                if share > 1:
                    value = unpacked(value, ROWS_OUT, start % share)
                new_lse = value[E : E + 1] + value[E + 1 : E + 2] + value[E + 2 : E + 3]
                if share > 1:
                    ids = lax.broadcasted_iota(jnp.int32, new_lse.shape, 1)
                    new_lse = jnp.where(ids // lanes == start % share, new_lse, -FAR)
                span = lanes * share
                for block in range(SEG0 // span):
                    at = slice(block * span, (block + 1) * span)
                    new = jnp.where(start // share == block, new_lse, -FAR)
                    old = lse[head, :, at]
                    top = jnp.maximum(old, new)
                    both = top + jnp.log2(jnp.exp2(old - top) + jnp.exp2(new - top))
                    lse[head, :, at] = both
                    merged[head, :, at] = merged[head, :, at] * jnp.exp2(old - both) + value[:E] * jnp.exp2(
                        new - both
                    )
        mixed[head] = merged[head].astype(BF)

    def rows_of(ref):
        return ref[...].reshape(SEG0, width)

    turned[...] = mixed[...].reshape(heads * E, SEG0).T
    for copy in loads:
        copy.wait()
    for step in range(SEG0 // tile):
        at = slice(step * tile // (head_size * per_slot), (step + 1) * tile // (head_size * per_slot))
        value = jnp.dot(turned[step * tile : (step + 1) * tile], out_proj[...], preferred_element_type=F32)
        part[at] = value.astype(BF).reshape(-1, head_size, per_slot, width)
    for copy in head_copies(part, got, head_sems, 0, True):
        copy.start()
    cot_t[...] = rows_of(cot).T
    for copy in head_copies(part, got, head_sems, 0, True):
        copy.wait()

    def rows_at(slot):
        return pl.ds(pl.multiple_of(slot * per_slot, per_slot), per_slot)

    @over_slots
    def _(slot):
        value = x_rows[rows_at(slot)] + part[slot, me_head].astype(F32)
        for step in range(1, head_size):
            value = value + got[step - 1, slot].astype(F32)
        hidden_one[rows_at(slot)] = value
        unit, scale = norm_of(value)
        low = (unit * scales[2:3] + scales[3:4]).astype(BF)
        normed_own[slot] = low
        normed[slot, me_head] = low

    for copy in head_copies(normed_own, normed, head_sems, 1, False):
        copy.start()
    for copy in head_copies(normed_own, normed, head_sems, 1, False):
        copy.wait()
    normed_t[...] = rows_of(normed).T

    chunk_width = up.shape[1] // chunks
    orders = {0: ORDERS["u1"], 1: ORDERS["d1"]}
    firsts = []
    for chunk in range(chunks):
        for kind in range(2):
            index = 2 * chunk + kind
            firsts.append(
                Reduction(
                    orders[kind], totals.at[index], halves[index], None, None,
                    first_sems.at[0, pl.ds(index, 1)], first_sems.at[1, pl.ds(index, 1)],
                )
            )
    down_sum[...] = jnp.zeros_like(down_sum)
    norm_sum[...] = jnp.zeros_like(norm_sum)
    slots = tile // (head_size * per_slot)
    contract_last = (((1,), (1,)), ((), ()))

    for chunk in range(chunks):
        units = slice(chunk * chunk_width, (chunk + 1) * chunk_width)
        up_grad[...] = jnp.zeros_like(up_grad)
        down_grad[...] = jnp.zeros_like(down_grad)

        @pl.loop(0, SEG0 // tile)
        def _(step):
            rows = pl.ds(pl.multiple_of(step * tile, tile), tile)
            low = normed[pl.ds(step * slots, slots)].reshape(tile, width)
            back = cot[pl.ds(step * slots, slots)].reshape(tile, width)
            pre = jnp.dot(low, up[:, units], preferred_element_type=F32)
            grad = lax.dot_general(back, down[units], contract_last, preferred_element_type=F32)
            share = 0.5 + 0.5 * lax.erf(pre * math.sqrt(0.5))
            density = jnp.exp2(pre * pre * (-0.5 * LOG2E)) * (1.0 / math.sqrt(2.0 * math.pi))
            hidden = (pre * share).astype(BF)
            grad = (grad * (share + pre * density)).astype(BF)
            down_sum[rows] += jnp.dot(hidden, down[units], preferred_element_type=F32)
            norm_sum[rows] += lax.dot_general(grad, up[:, units], contract_last, preferred_element_type=F32)
            up_grad[...] += jnp.dot(normed_t[:, rows], grad, preferred_element_type=F32)
            down_grad[...] += jnp.dot(cot_t[:, rows], hidden, preferred_element_type=F32)

        pieces = totals.shape[3] * 4
        size = totals.shape[4]
        turned_down = down_grad[...].T
        for piece in range(pieces):
            spot = (piece // (2 * rest), piece // rest % 2, piece % rest)
            span = slice(piece * size, (piece + 1) * size)
            totals[(2 * chunk,) + spot] = up_grad[span].astype(BF)
            totals[(2 * chunk + 1,) + spot] = turned_down[span].astype(BF)
        firsts[2 * chunk].step(0)
        firsts[2 * chunk + 1].step(0)

    for ref, value in ((part, down_sum), (part_two, norm_sum)):

        @pl.loop(0, SLOTS)
        def _(slot):
            for device in range(head_size):
                begin = pl.multiple_of((slot * head_size + device) * per_slot, per_slot)
                ref[slot, device] = value[pl.ds(begin, per_slot)].astype(BF)

    for copy in head_copies(part_two, got_two, head_sems, 2, True) + head_copies(part, got, head_sems, 3, True):
        copy.start()
    for copy in head_copies(part_two, got_two, head_sems, 2, True):
        copy.wait()
    gains_two[...] = jnp.zeros_like(gains_two)

    @over_slots
    def _(slot):
        grad = part_two[slot, me_head].astype(F32)
        for step in range(1, head_size):
            grad = grad + got_two[step - 1, slot].astype(F32)
        unit, scale = norm_of(hidden_one[rows_at(slot)])
        scaled = grad * scales[2:3]
        inner = jnp.mean(scaled * unit, axis=-1, keepdims=True)
        out = cot[slot, me_head].astype(F32) + scale * (
            scaled - jnp.mean(scaled, axis=-1, keepdims=True) - unit * inner
        )
        grad_hidden[rows_at(slot)] = out
        normed_own[slot] = out.astype(BF)
        normed[slot, me_head] = out.astype(BF)
        gains_two[0:1] += jnp.sum(grad * unit, axis=0, keepdims=True)
        gains_two[1:2] += jnp.sum(grad, axis=0, keepdims=True)

    for copy in head_copies(normed_own, normed, head_sems, 4, False):
        copy.start()
    for copy in head_copies(part, got, head_sems, 3, True):
        copy.wait()

    @pl.loop(0, SLOTS)
    def _(slot):
        value = hidden_one[rows_at(slot)] + part[slot, me_head].astype(F32)
        for step in range(1, head_size):
            value = value + got[step - 1, slot].astype(F32)
        place = slot_place(slot)
        for column in range(width // 128):
            lanes = slice(column * 128, (column + 1) * 128)
            spread_rows[column, pl.ds(place, per_slot, stride=SLOTS), :] = value[:, lanes]

    for column in range(width // 128):
        block_out[:, column * 128 : (column + 1) * 128] = spread_rows[column].astype(BF)
    for copy in head_copies(normed_own, normed, head_sems, 4, False):
        copy.wait()

    value = jnp.dot(mixed[...].reshape(heads * E, SEG0), rows_of(normed), preferred_element_type=F32)
    size = out_total.shape[3]
    for piece in range(4 * rest):
        spot = (piece // (2 * rest), piece // rest % 2, piece % rest)
        out_total[spot] = value[piece * size : (piece + 1) * size].astype(BF)

    normed_t[...] = rows_of(normed).T
    value = jnp.dot(out_proj[...], normed_t[...], preferred_element_type=F32)
    own_g[0, :, :E, :] = value.astype(BF).reshape(heads, E, SEG0)

    @pl.loop(0, heads)
    def _(head):
        low = own_g[0, head, :E, :]
        dots = jnp.sum(low.astype(F32) * merged[head], axis=0, keepdims=True)
        d = pieces_of(-dots)
        m = pieces_of(-lse[head])
        placed = {0: d[0], 1: d[1], 2: d[2], 12: m[0], 13: m[1], 14: m[2]}
        own_g[0, head, E:, :] = row_block(placed, SEG0).astype(BF)
        own = jnp.concatenate([low.astype(F32), row_block(placed, SEG0)], axis=0)
        spread_blocks(heads, head, starts, own, sends)

    for reduction in firsts:
        reduction.finish_first()


def middle(heads, starts, first, backs, x_rows, cot, out_proj, up, down, scales):
    size, head_size = lax.axis_size("seq"), lax.axis_size("head")
    rest = size // 4
    rows, width = x_rows.shape
    per_slot = rows // SLOTS
    chunks = max(1, up.shape[1] // width)
    shard = (SLOTS, head_size, per_slot, width)
    own = (SLOTS, per_slot, width)
    got = (head_size - 1,) + own
    sends = send_shapes(heads, ROWS_OUT)
    piece = (2, rest, width // size, up.shape[1] // chunks)
    out_piece = (2, 2, rest, heads * E // size, width)
    far = [x_rows, cot, out_proj, up, down]
    results = pl.pallas_call(
        partial(middle_kernel, heads),
        in_specs=[pl.BlockSpec(memory_space=pltpu.SMEM)]
        + vmem_specs(1 + len(backs) + 1)
        + [pl.BlockSpec(memory_space=pl.ANY)] * 5,
        out_specs=vmem_specs(4 + len(sends) + 2 * chunks + 1),
        out_shape=[
            jax.ShapeDtypeStruct((rows, width), BF),
            jax.ShapeDtypeStruct((rows, width), F32),
            jax.ShapeDtypeStruct((2, width), F32),
            jax.ShapeDtypeStruct((1, heads, ROWS_OUT, SEG0), BF),
        ]
        + sends
        + [jax.ShapeDtypeStruct(piece, BF)] * (2 * chunks)
        + [jax.ShapeDtypeStruct(out_piece, BF)],
        scratch_shapes=[
            pltpu.VMEM((heads, E, SEG0), F32),
            pltpu.VMEM((heads, 1, SEG0), F32),
            pltpu.VMEM((heads, E, SEG0), BF),
            pltpu.VMEM((SEG0, heads * E), BF),
            pltpu.VMEM(shard, BF),
            pltpu.VMEM(got, BF),
            pltpu.VMEM(shard, BF),
            pltpu.VMEM(got, BF),
            pltpu.VMEM((rows, width), F32),
            pltpu.VMEM(own, BF),
            pltpu.VMEM(shard, BF),
            pltpu.VMEM((width // 128, rows, 128), F32),
            pltpu.VMEM((width, SEG0), BF),
            pltpu.VMEM((width, SEG0), BF),
            pltpu.VMEM((SEG0, width), F32),
            pltpu.VMEM((SEG0, width), F32),
            pltpu.VMEM((width, up.shape[1] // chunks), F32),
            pltpu.VMEM((width, up.shape[1] // chunks), F32),
            pltpu.VMEM((2 * chunks, 2) + piece, BF),
            pltpu.SemaphoreType.DMA((2, 5, head_size - 1)),
            pltpu.SemaphoreType.DMA((2, 2 * chunks)),
            pltpu.SemaphoreType.DMA((5,)),
        ]
        + [pltpu.VMEM(value.shape, value.dtype) for value in far],
        compiler_params=pltpu.CompilerParams(
            vmem_limit_bytes=60 * 2**20, collective_id=2, has_side_effects=True
        ),
        cost_estimate=pl.CostEstimate(
            flops=14 * SEG0 * width * up.shape[1], transcendentals=0, bytes_accessed=40 * 2**20
        ),
        name="middle",
    )(starts, first, *backs, scales, *far)
    block_out, grad_hidden, gains_two, own_g = results[:4]
    return block_out, grad_hidden, gains_two, own_g, results[4 : 4 + len(sends)], results[4 + len(sends) :]


def local(
    tokens,
    documents,
    offsets,
    in_proj,
    out_proj,
    up_proj,
    down_proj,
    first_gain,
    first_shift,
    second_gain,
    second_shift,
    cotangent,
):
    head_count = lax.axis_size("head")
    seq_id = lax.axis_index("seq")
    row_count = tokens.shape[0]
    seq_len = row_count * head_count
    heads = offsets.shape[1]
    per_slot = row_count // SLOTS

    my_docs = lax.dynamic_slice_in_dim(documents, seq_id * seq_len, seq_len)
    my_docs = my_docs.reshape(head_count, per_slot, 2, 2, 2, 2).transpose(5, 4, 3, 2, 0, 1).reshape(seq_len)
    bit_ids = jnp.arange(BIT_ROWS, dtype=jnp.int32)[:, None]
    doc_bit = my_docs[None, :] // 2 ** (bit_ids % DOC_BITS) % 2
    bits = jnp.where(bit_ids < DOC_BITS, doc_bit, jnp.where(bit_ids < 2 * DOC_BITS, 1 - doc_bit, 0))
    bits = bits.astype(BF)
    starts = jnp.stack([reversed_bits(offsets[b], b) for b in range(BRANCHES)])

    scales = jnp.stack([first_gain, first_shift, second_gain, second_shift])
    (x_rows, normed, cot_all, own, first_out), units, outs = forward(
        heads, starts, tokens, cotangent, bits, scales, in_proj
    )
    block_out, grad_hidden, gains_two, own_g, sends_g, parts = middle(
        heads, starts, first_out, outs, x_rows, cot_all, out_proj, up_proj, down_proj, scales
    )
    (grad_up, grad_down, grad_out, grad_in), grad_tokens, gains = backward(
        heads, starts, own, own_g, units, sends_g, parts,
        normed, in_proj, x_rows, grad_hidden, scales, gains_two,
    )
    return (
        block_out,
        grad_tokens,
        grad_in,
        grad_out,
        grad_up,
        grad_down,
        gains[0],
        gains[1],
        gains[2],
        gains[3],
    )


def solution(mesh):
    placed = (
        P(("seq", "head"), None),
        P(),
        P(None, "head"),
        P(None, None, "head"),
        P("head", None),
        P(None, "head"),
        P("head", None),
        P(),
        P(),
        P(),
        P(),
        P(("seq", "head"), None),
    )
    return jax.shard_map(
        local,
        mesh=mesh,
        in_specs=placed,
        out_specs=(
            P(("seq", "head"), None),
            P(("seq", "head"), None),
            P(None, None, "head"),
            P("head", None),
            P(None, "head"),
            P("head", None),
            P(),
            P(),
            P(),
            P(),
        ),
        check_vma=False,
    )
```

```python
import math
from functools import partial

import jax
import jax.numpy as jnp
from jax import lax
from jax.experimental import pallas as pl
from jax.experimental.pallas import tpu as pltpu
from jax.sharding import PartitionSpec as P

E = 48
BRANCHES = 5
SEG0 = 1024
SLOTS = 16
BIT_ROWS = 16
DOC_BITS = 6
ROWS_IN = 3 * E + BIT_ROWS
ROWS_OUT = E + BIT_ROWS
EPS = 1e-05
FAR = 1e30
LOG2E = math.log2(math.e)
LN2 = math.log(2.0)
BF = jnp.bfloat16
F32 = jnp.float32
VMEM_LIMIT = 48 * 2**20


def reversed_bits(value, count):
    out = jnp.zeros_like(value)
    for bit in range(count):
        out = out * 2 + value // 2**bit % 2
    return out


def branch_shape(branch, heads):
    stride = 2**branch
    return (stride, SEG0 // stride, max(1, heads // stride), max(1, stride // heads))


def pieces_of(value):
    high = value.astype(BF).astype(F32)
    rest = value - high
    middle = rest.astype(BF).astype(F32)
    return high, middle, (rest - middle).astype(BF).astype(F32)


def row_block(placed, columns):
    ids = lax.broadcasted_iota(jnp.int32, (BIT_ROWS, columns), 0)
    block = jnp.zeros((BIT_ROWS, columns), F32)
    for row, value in placed.items():
        block = jnp.where(ids == row, value, block)
    return block


def turned_half(block):
    return jnp.concatenate([block[:, 64:], block[:, :64]], axis=1)


def low_half():
    return lax.broadcasted_iota(jnp.int32, (1, 128), 1) < 64


def packed_rows(rows, count):
    return rows if count >= 128 else (rows // 2 + 15) // 16 * 16


def packed(block, half):
    rows = packed_rows(block.shape[0], 64)
    upper, lower = block[:rows], block[block.shape[0] - rows :]
    if isinstance(half, int):
        return jnp.where(low_half(), turned_half(upper) if half else upper, lower if half else turned_half(lower))
    upper = jnp.where(half == 0, upper, turned_half(upper))
    lower = jnp.where(half == 0, turned_half(lower), lower)
    return jnp.where(low_half(), upper, lower)


def unpacked(value, rows, half):
    size = value.shape[0]
    other = turned_half(value)
    upper = jnp.where(half == 0, value, other)
    lower = jnp.where(half == 0, other, value)
    both = jnp.concatenate([upper, lower[2 * size - rows :]], axis=0)
    return jnp.where(low_half() == (half == 0), both, 0.0)


def send_shapes(heads, rows):
    outs = []
    for branch in range(1, BRANCHES):
        stride, count, per, split = branch_shape(branch, heads)
        outs.append(jax.ShapeDtypeStruct((stride, per, packed_rows(rows, count), max(count, 128)), BF))
    return outs


def spread_blocks(heads, head, starts, value, sends):
    for branch in range(1, BRANCHES):
        stride, lanes, per, split = branch_shape(branch, heads)
        send, start = sends[branch - 1], starts[branch, head]
        share = max(1, 128 // lanes)
        span = lanes * share
        block = value[:, :span]
        for part in range(1, SEG0 // span):
            block = jnp.where(start // share == part, value[:, part * span : (part + 1) * span], block)
        if share > 1:
            block = packed(block, start % share)
        block = block.astype(BF)
        if split == 1:
            send[head // per, head % per] = block
        else:
            for copy in range(split):
                send[head * split + copy, 0] = block


def norm_of(values):
    centred = values - jnp.mean(values, axis=-1, keepdims=True)
    scale = lax.rsqrt(jnp.mean(centred * centred, axis=-1, keepdims=True) + EPS)
    return centred * scale, scale


def slot_place(slot):
    return slot % 2 * 8 + slot // 2 % 2 * 4 + slot // 4 % 2 * 2 + slot // 8


def over_slots(body, unroll=4):
    @pl.loop(0, SLOTS // unroll)
    def _(step):
        for part in range(unroll):
            body(step * unroll + part)


def head_copies(source, target, sems, index, scatter):
    size, me = lax.axis_size("head"), lax.axis_index("head")
    copies = []
    for step in range(1, size):
        device = (me + step) % size
        copies.append(
            pltpu.make_async_remote_copy(
                src_ref=source.at[:, device] if scatter else source,
                dst_ref=target.at[step - 1] if scatter else target.at[:, me],
                send_sem=sems.at[0, index, step - 1],
                recv_sem=sems.at[1, index, step - 1],
                device_id={"head": device},
                device_id_type=pl.DeviceIdType.MESH,
            )
        )
    return copies


def load_unit(ref, unit, count, x):
    width = ref.shape[-1]
    if count >= 128:
        for block in range(ref.shape[0]):
            x[:, block * width : (block + 1) * width] = ref[block, unit]
        return
    rows, size = x.shape[0], ref.shape[2]
    for block in range(ref.shape[0] // 2):
        lanes = slice(block * 128, (block + 1) * 128)
        left = ref[2 * block, unit].astype(F32)
        right = ref[2 * block + 1, unit].astype(F32)
        x[:size, lanes] = jnp.where(low_half(), left, turned_half(right)).astype(BF)
        x[rows - size :, lanes] = jnp.where(low_half(), turned_half(left), right).astype(BF)


def store_unit(ref, unit, count, result):
    width = ref.shape[-1]
    for block in range(SEG0 // width):
        value = result[:, block * width : (block + 1) * width]
        if count >= 128:
            ref[block, unit] = value
        else:
            value = value.astype(F32)
            ref[2 * block, unit] = packed(value, 0).astype(BF)
            ref[2 * block + 1, unit] = packed(value, 1).astype(BF)


def forward_unit(x, q_aug, result, base, queries):
    if isinstance(base, int):
        lanes = slice(base, base + queries)
    else:
        lanes = pl.ds(pl.multiple_of(base, 128), queries)
    q_aug[0:E, :queries] = x[0:E, lanes]
    q_aug[E:, :queries] = (x[3 * E :, lanes].astype(F32) * -FAR).astype(BF)
    bits = x[3 * E :, :].astype(F32)
    k_rows = jnp.concatenate([x[E : 2 * E, :], (1.0 - bits).astype(BF)], axis=0).T
    v_aug = jnp.concatenate([x[2 * E : 3 * E, :], jnp.ones(bits.shape, BF)], axis=0)
    if queries < SEG0:
        result[0:E, :] = jnp.zeros((E, SEG0), BF)
        result[E:, :] = row_block({0: -FAR}, SEG0).astype(BF)
    s = jnp.dot(k_rows, q_aug[:, :queries], preferred_element_type=F32)
    top = jnp.max(s, axis=0, keepdims=True)
    p = jnp.exp2(s - top).astype(BF)
    o = jnp.dot(v_aug, p, preferred_element_type=F32)
    total = o[E : E + 1]
    high, middle_part, low = pieces_of(top + jnp.log2(total))
    block = row_block({0: high, 1: middle_part, 2: low}, queries)
    result[:, lanes] = jnp.concatenate([o[:E] * (1.0 / total), block], axis=0).astype(BF)


class Names:
    def __init__(self, refs):
        self.refs = list(refs)

    def take(self, count):
        taken, self.refs = self.refs[:count], self.refs[count:]
        return taken

    def one(self):
        return self.take(1)[0]


def group_place(branch):
    stride = 2**branch
    me = lax.axis_index("seq")
    return me // stride * stride, me % stride


def meet(*axes):
    barrier = pltpu.get_barrier_semaphore()
    count = 0
    for axis in axes:
        size = lax.axis_size(axis)
        me = lax.axis_index(axis)

        @pl.loop(1, size)
        def _(step):
            pl.semaphore_signal(
                barrier, inc=1, device_id={axis: (me + step) % size}, device_id_type=pl.DeviceIdType.MESH
            )

        count += size - 1
    pl.semaphore_wait(barrier, count)


class Reduction:
    STEPS = 7

    def __init__(self, order, total, half, quarter, others, send, recv, begun=False):
        self.total, self.begun = total, begun
        self.half, self.quarter, self.others = half, quarter, others
        self.send, self.recv = send, recv
        me = lax.axis_index("seq")
        self.rest = lax.axis_size("seq") // 4
        self.me = me
        bits = (me % 2, me // 2 % 2)
        self.bits = [bits[bit] for bit in order]
        self.partners = [me + (1 - 2 * bits[bit]) * 2**bit for bit in order]
        self.place = me // 4

    def copy(self, source, target, device, sem):
        return pltpu.make_async_remote_copy(
            src_ref=source,
            dst_ref=target,
            send_sem=self.send.at[sem],
            recv_sem=self.recv.at[sem],
            device_id={"seq": device},
            device_id_type=pl.DeviceIdType.MESH,
        )

    def copies(self, number):
        one, two = self.bits
        rest = self.rest
        others = []
        for step in range(1, rest):
            place = (self.place + step) % rest
            others.append((step, place, place * 4 + self.me % 4))
        if number == 0:
            return [self.copy(self.total.at[1 - one], self.half, self.partners[0], 0)]
        if number == 1:
            return [self.copy(self.half.at[1 - two], self.quarter, self.partners[1], 1)]
        if number == 2:
            return [
                self.copy(self.quarter.at[place], self.others.at[step - 1], device, 1 + step)
                for step, place, device in others
            ]
        if number == 3:
            block = self.total.at[one, two, self.place]
            return [self.copy(block, block, device, rest + step) for step, place, device in others]
        if number == 4:
            block = self.total.at[one, two]
            return [self.copy(block, block, self.partners[1], 2 * rest)]
        if number == 5:
            block = self.total.at[one]
            return [self.copy(block, block, self.partners[0], 2 * rest + 1)]
        return []

    def finish_first(self):
        one, rest = self.bits[0], self.rest
        for copy in self.copies(0):
            copy.wait()

        @pl.loop(0, 2 * rest)
        def _(i):
            j, z = i // rest, i % rest
            mine = self.total[one, j, z].astype(F32)
            self.half[j, z] = (mine + self.half[j, z].astype(F32)).astype(BF)

    def step(self, number):
        one, two = self.bits
        rest = self.rest
        if number == 0 and self.begun:
            return
        if number == 1:
            if not self.begun:
                self.finish_first()
        elif number > 0:
            for copy in self.copies(number - 1):
                copy.wait()
        if number == 2:

            @pl.loop(0, rest)
            def _(z):
                mine = self.half[two, z].astype(F32)
                self.quarter[z] = (mine + self.quarter[z].astype(F32)).astype(BF)

        elif number == 3:
            mine = self.quarter[self.place].astype(F32)
            for step in range(1, rest):
                mine = mine + self.others[step - 1].astype(F32)
            self.total[one, two, self.place] = mine.astype(BF)
        for copy in self.copies(number):
            copy.start()

    @staticmethod
    def scratch(size, rows, columns):
        rest = size // 4
        count = 2 * rest + 2
        return [
            pltpu.VMEM((2, rest, rows, columns), BF),
            pltpu.VMEM((rest, rows, columns), BF),
            pltpu.VMEM((rest - 1, rows, columns), BF),
            pltpu.SemaphoreType.DMA((count,)),
            pltpu.SemaphoreType.DMA((count,)),
        ]


def reduction_parts(value, size):
    rows, columns = value.shape
    return value.reshape(2, 2, size // 4, rows // size, columns)


def reduction_whole(value):
    return value.reshape(-1, value.shape[-1])


def make_reductions(orders, totals, scratch):
    out = []
    for order, total in zip(orders, totals):
        out.append(Reduction(order, total, *scratch[:5]))
        scratch = scratch[5:]
    return out


def group_copies(branch, source, target, send_sems, recv_sems, local_sem):
    stride = 2**branch
    base, place = group_place(branch)
    first = stride - branch - 2
    copies = [
        pltpu.make_async_copy(source.at[place], target.at[place], local_sem.at[branch - 1])
    ]
    for step in range(1, stride):
        member = (place + step) % stride
        copies.append(
            pltpu.make_async_remote_copy(
                src_ref=source.at[member],
                dst_ref=target.at[place],
                send_sem=send_sems.at[first + step],
                recv_sem=recv_sems.at[first + step],
                device_id={"seq": base + member},
                device_id_type=pl.DeviceIdType.MESH,
            )
        )
    return copies


def forward_kernel(heads, starts, tokens, cotangent, bits, gain, shift, in_proj, *refs):
    count = BRANCHES - 1
    names = Names(refs)
    far = names.take(4 + count)
    first, backs = names.one(), names.take(count)
    near = names.take(4 + count)
    (x_rows, normed, cot, own), gots = near[:4], near[4:]
    outs, sends = names.take(count), names.take(count)
    x, q_aug, result, in_send, in_recv, in_local, out_send, out_recv, out_local = names.take(9)
    spread_rows, normed_own, cot_own, normed_t, head_sems, far_sem = names.take(6)
    saves = [pltpu.make_async_copy(near[i], far[i], far_sem.at[i]) for i in range(4 + count)]
    me_head = lax.axis_index("head")
    rows, width = tokens.shape
    per_slot = rows // SLOTS

    def fill(source):
        for column in range(width // 128):
            spread_rows[column] = source[:, column * 128 : (column + 1) * 128].astype(F32)

    def picked(slot):
        at = pl.ds(slot_place(slot), per_slot, stride=SLOTS)
        return jnp.concatenate([spread_rows[column, at, :] for column in range(width // 128)], axis=1)

    fill(tokens)

    @over_slots
    def _(slot):
        value = picked(slot)
        x_rows[pl.ds(pl.multiple_of(slot * per_slot, per_slot), per_slot)] = value
        low = (norm_of(value)[0] * gain[...][None] + shift[...][None]).astype(BF)
        normed_own[slot] = low
        normed[slot, me_head] = low

    meet("seq", "head")
    for copy in head_copies(normed_own, normed, head_sems, 0, False):
        copy.start()
    saves[0].start()
    fill(cotangent)

    @over_slots
    def _(slot):
        low = picked(slot).astype(BF)
        cot_own[slot] = low
        cot[slot, me_head] = low

    for copy in head_copies(cot_own, cot, head_sems, 1, False):
        copy.start()
    own[0, :, 3 * E :, :] = jnp.broadcast_to(bits[...][None], (heads,) + bits.shape)
    turned = [in_proj[j].T for j in range(3)]
    for copy in head_copies(normed_own, normed, head_sems, 0, False):
        copy.wait()
    normed_t[...] = normed[...].reshape(SEG0, width).T
    for j in range(3):
        value = jnp.dot(turned[j], normed_t[...], preferred_element_type=F32)
        if j == 0:
            value = value * (E ** (-0.5) * LOG2E)
        own[0, :, j * E : (j + 1) * E, :] = value.astype(BF).reshape(heads, E, SEG0)
    saves[1].start()
    saves[3].start()

    @pl.loop(0, heads)
    def _(head):
        spread_blocks(heads, head, starts, own[0, head].astype(F32), sends)

    coming = {}
    for branch in range(1, BRANCHES):
        coming[branch] = group_copies(branch, sends[branch - 1], gots[branch - 1], in_send, in_recv, in_local)
        for copy in coming[branch]:
            copy.start()

    @pl.loop(0, heads)
    def _(head):
        x[...] = own[0, head]
        forward_unit(x, q_aug, result, 0, SEG0)
        first[0, head] = result[...]

    for copy in head_copies(cot_own, cot, head_sems, 1, False):
        copy.wait()
    saves[2].start()
    leaving = []
    for branch in range(1, BRANCHES):
        stride, lanes, units, split = branch_shape(branch, heads)
        got, out = gots[branch - 1], outs[branch - 1]
        for copy in coming[branch]:
            copy.wait()
        saves[3 + branch].start()
        queries = SEG0 // split
        base = 0 if split == 1 else lax.axis_index("seq") % split * queries

        @pl.loop(0, units)
        def _(unit):
            load_unit(got, unit, lanes, x)
            forward_unit(x, q_aug, result, base, queries)
            store_unit(out, unit, lanes, result)

        copies = group_copies(branch, out, backs[branch - 1], out_send, out_recv, out_local)
        for copy in copies:
            copy.start()
        leaving += copies
    for copy in leaving + saves:
        copy.wait()


def exchange_scratch():
    copies = 2**BRANCHES - 2 - BRANCHES + 1
    one = [
        pltpu.SemaphoreType.DMA((copies,)),
        pltpu.SemaphoreType.DMA((copies,)),
        pltpu.SemaphoreType.DMA((BRANCHES - 1,)),
    ]
    return one + one


def unit_cost(units, dots):
    return pl.CostEstimate(
        flops=dots * 2 * units * SEG0 * SEG0 * 256,
        transcendentals=units * SEG0 * SEG0,
        bytes_accessed=units * SEG0 * 1000,
    )


def vmem_specs(count):
    return [pl.BlockSpec(memory_space=pltpu.VMEM)] * count


def forward(heads, starts, tokens, cotangent, bits, gain, shift, in_proj):
    head_size = lax.axis_size("head")
    rows, width = tokens.shape
    shard = jax.ShapeDtypeStruct((SLOTS, head_size, rows // SLOTS, width), BF)
    own_rows = pltpu.VMEM((SLOTS, rows // SLOTS, width), BF)
    backs = send_shapes(heads, ROWS_OUT)
    gots = send_shapes(heads, ROWS_IN)
    own = jax.ShapeDtypeStruct((1, heads, ROWS_IN, SEG0), BF)
    far = [jax.ShapeDtypeStruct((rows, width), F32), shard, shard, own] + gots
    results = pl.pallas_call(
        partial(forward_kernel, heads),
        in_specs=[pl.BlockSpec(memory_space=pltpu.SMEM)] + vmem_specs(6),
        out_specs=[pl.BlockSpec(memory_space=pl.ANY)] * len(far) + vmem_specs(1 + len(backs)),
        out_shape=far + [jax.ShapeDtypeStruct((1, heads, ROWS_OUT, SEG0), BF)] + backs,
        scratch_shapes=[pltpu.VMEM(shape.shape, shape.dtype) for shape in far + backs + gots]
        + [
            pltpu.VMEM((ROWS_IN, SEG0), BF),
            pltpu.VMEM((ROWS_OUT, SEG0), BF),
            pltpu.VMEM((ROWS_OUT, SEG0), BF),
        ]
        + exchange_scratch()
        + [
            pltpu.VMEM((width // 128, rows, 128), F32),
            own_rows,
            own_rows,
            pltpu.VMEM((width, SEG0), BF),
            pltpu.SemaphoreType.DMA((2, 2, head_size - 1)),
            pltpu.SemaphoreType.DMA((len(far),)),
        ],
        compiler_params=pltpu.CompilerParams(
            vmem_limit_bytes=60 * 2**20, collective_id=0, has_side_effects=True
        ),
        cost_estimate=unit_cost(2 * heads, 2),
        name="forward",
    )(starts, tokens, cotangent, bits, gain, shift, in_proj)
    return results[:4], results[4 : len(far)], results[len(far)], results[len(far) + 1 :]


def backward_unit(x, g, q_aug, gk, gv, result, base, queries, tile):
    if isinstance(base, int):
        lanes = slice(base, base + queries)
    else:
        lanes = pl.ds(pl.multiple_of(base, 128), queries)
    extra = g[E:, lanes].astype(F32)
    ids = lax.broadcasted_iota(jnp.int32, extra.shape, 0)
    q = x[0:E, lanes]
    q_aug[0:E, :queries] = q
    q_aug[E:, :queries] = jnp.where(ids >= 12, extra, x[3 * E :, lanes].astype(F32) * -FAR).astype(BF)
    bits = x[3 * E :, :].astype(F32)
    k_aug = jnp.concatenate([x[E : 2 * E, :], (1.0 - bits).astype(BF)], axis=0)
    k_rows = k_aug.T
    v_ids = lax.broadcasted_iota(jnp.int32, bits.shape, 0)
    v_bits = jnp.where(v_ids < 3, 1.0, 0.0).astype(BF)
    v_rows = jnp.concatenate([x[2 * E : 3 * E, :], v_bits], axis=0).T
    q_rows = jnp.concatenate([q, jnp.zeros((BIT_ROWS, queries), BF)], axis=0).T
    g_all = g[:, lanes]
    g_rows = g_all.T
    if queries < SEG0:
        result[0:E, :] = jnp.zeros((E, SEG0), BF)
    for step in range(queries // tile):
        column = step * tile
        span = slice(column, column + tile)
        p = jnp.exp2(jnp.dot(k_rows, q_aug[:, span], preferred_element_type=F32))
        gs = p * jnp.dot(v_rows, g_all[:, span], preferred_element_type=F32)
        p, gs = p.astype(BF), gs.astype(BF)
        target = span if isinstance(base, int) else pl.ds(pl.multiple_of(base + column, 128), tile)
        result[0:E, target] = jnp.dot(k_aug, gs, preferred_element_type=F32)[:E].astype(BF)
        new_k = jnp.dot(gs, q_rows[span], preferred_element_type=F32)
        new_v = jnp.dot(p, g_rows[span], preferred_element_type=F32)
        if step == 0:
            gk[...] = new_k
            gv[...] = new_v
        else:
            gk[...] += new_k
            gv[...] += new_v
    result[E : 2 * E, :] = (gk[...].T[:E] * LN2).astype(BF)
    result[2 * E :, :] = gv[...].T[:E].astype(BF)


ORDERS = {
    'u1': (0, 1), 'u2': (0, 1), 'd1': (1, 0), 'd2': (1, 0), 'o': (0, 1), 'i0': (1, 0), 'i1': (1, 0), 'i2': (0,
    1),
}
EARLY = [
    (0, 'd1', 0), (0, 'u1', 0), (0, 'd1', 1), (0, 'u2', 0), (0, 'u1', 1), (2, 'o', 0), (4, 'u2', 1), (5, 'u1',
    2), (7, 'd1', 2), (9, 'u1', 3), (10, 'd2', 0), (12, 'd2', 1), (12, 'o', 1), (12, 'd1', 3), (13, 'u2', 2),
    (14, 'u1', 4),
]
TAIL = [
    'gather', ('d1', 4), 'in1', ('i1', 0), ('d2', 2), 'in2', ('u2', 3), ('i2', 0), 'in0', ('i0', 0), ('d2',
    3), ('i1', 1), ('i2', 1), ('u1', 5), ('u2', 4), ('d2', 4), ('d1', 5), ('o', 2), ('i2', 2), ('i0', 1),
    ('i1', 2), ('i2', 3), 'one', ('d2', 5), ('o', 3), ('i1', 3), ('u1', 6), ('u2', 5), 'norm', ('i2', 4),
    'gain0', ('i0', 2), ('i1', 4), ('i0', 3), 'gain1', ('o', 4), ('i0', 4), ('i2', 5), 'gain2', ('i1', 5),
    ('o', 5), ('i0', 5), 'gain3', ('i0', 6), ('d2', 6), ('u2', 6), 'gain4', ('d1', 6), ('i1', 6), ('i2', 6),
    ('o', 6),
]


def stream_names(streams):
    pairs = streams // 2
    return [kind + str(i + 1) for i in range(pairs) for kind in "ud"] + ["o"]


def backward_kernel(heads, streams, *refs):
    branches = BRANCHES - 1
    names = Names(refs)
    starts, own, own_g = names.take(3)
    sends, gain, gains_two = names.take(branches), *names.take(2)
    far = names.take(branches + 4)
    parts = names.take(streams)
    up_total, down_total, out_total, in_total = names.take(4)
    chunks = (streams - 1) // 2
    totals = []
    for chunk in range(chunks):
        lanes = pl.ds(chunk * (up_total.shape[-1] // chunks), up_total.shape[-1] // chunks)
        totals += [up_total.at[:, :, :, :, lanes], down_total.at[chunk]]
    totals.append(out_total)
    in_totals = [in_total.at[j] for j in range(3)]
    grad_tokens, gains_out = names.take(2)
    near = names.take(branches + 4)
    units_in, (normed, in_proj, x_rows, grad_hidden) = near[:branches], near[branches:]
    far_sem = names.one()
    first = names.one()
    backs, gots, outs = names.take(branches), names.take(branches), names.take(branches)
    x, g, q_aug, gk, gv, result = names.take(6)
    total, grads, grads_t, normed_t, spread_rows, head_send, head_recv = names.take(7)
    gain_head, gain_one, gain_two, gain_rest = names.take(4)
    in_send, in_recv, in_local, out_send, out_recv, out_local = names.take(6)
    part_sem, head_sems, gain_sems = names.take(3)
    labels = stream_names(streams) + ["i0", "i1", "i2"]
    reductions = make_reductions(
        [ORDERS[label] for label in labels], list(totals) + list(in_totals), names.take(5 * streams + 15)
    )
    reductions = dict(zip(labels, reductions))
    for label in labels[: streams - 1]:
        reductions[label].begun = True

    shapes = [branch_shape(b, heads) for b in range(BRANCHES)]
    size, head_size = lax.axis_size("seq"), lax.axis_size("head")
    me, me_head = lax.axis_index("seq"), lax.axis_index("head")
    rest = size // 4
    tile = 512
    per_slot = x_rows.shape[0] // SLOTS
    width = x_rows.shape[1]

    fills = [
        pltpu.make_async_copy(parts[s], reductions[labels[s]].half, part_sem.at[s]) for s in range(streams - 1)
    ] + [pltpu.make_async_copy(parts[-1], totals[-1], part_sem.at[streams - 1])]
    loads = [pltpu.make_async_copy(far[i], near[i], far_sem.at[i]) for i in range(branches + 4)]
    for copy in fills + loads:
        copy.start()
    meet("seq", "head")

    def coming(branch):
        return group_copies(branch, sends[branch - 1], gots[branch - 1], in_send, in_recv, in_local)

    def leaving(branch):
        return group_copies(branch, outs[branch - 1], backs[branch - 1], out_send, out_recv, out_local)

    for branch in range(1, BRANCHES):
        for copy in coming(branch):
            copy.start()
    for copy in fills + loads:
        copy.wait()

    def split_branch(branch):
        stride, lanes, units, split = shapes[branch]
        queries = SEG0 // split
        for copy in coming(branch):
            copy.wait()
        load_unit(units_in[branch - 1], 0, lanes, x)
        load_unit(gots[branch - 1], 0, lanes, g)
        backward_unit(x, g, q_aug, gk, gv, result, me % split * queries, queries, min(tile, queries))
        store_unit(outs[branch - 1], 0, lanes, result)

    runs, at = [(0, 0, 0, heads // 2)], heads // 2
    split_at = None
    for branch in range(1, BRANCHES):
        if shapes[branch][3] == 1:
            runs.append((branch, at, 0, shapes[branch][2]))
            at += shapes[branch][2]
    split_at = at
    runs.append((0, at, heads // 2, heads - heads // 2))
    blocks = at + heads - heads // 2
    plan = {}
    for block, stream, step in EARLY:
        if stream in labels:
            plan.setdefault(block * blocks // 15, []).append((stream, step))

    @pl.loop(0, blocks)
    def _(block):
        for after, events in plan.items():

            @pl.when(block == after)
            def _(events=events):
                for stream, step in events:
                    reductions[stream].step(step)

        @pl.when(block == split_at)
        def _():
            for branch in range(1, BRANCHES):
                if shapes[branch][3] > 1:
                    split_branch(branch)
                    for copy in leaving(branch):
                        copy.start()

        for branch, low, unit, count in runs:

            @pl.when((block >= low) & (block < low + count))
            def _(branch=branch, low=low, unit=unit):
                if branch == 0:
                    x[...] = own[0, block - low + unit]
                    g[...] = own_g[0, block - low + unit]
                else:

                    @pl.when(block == low)
                    def _():
                        for copy in coming(branch):
                            copy.wait()

                    load_unit(units_in[branch - 1], block - low, shapes[branch][1], x)
                    load_unit(gots[branch - 1], block - low, shapes[branch][1], g)

        backward_unit(x, g, q_aug, gk, gv, result, 0, SEG0, tile)
        for branch, low, unit, count in runs:

            @pl.when((block >= low) & (block < low + count))
            def _(branch=branch, low=low, unit=unit, count=count):
                if branch == 0:
                    first[block - low + unit] = result[...]
                else:
                    store_unit(outs[branch - 1], block - low, shapes[branch][1], result)

                    @pl.when(block == low + count - 1)
                    def _():
                        for copy in leaving(branch):
                            copy.start()

    tasks = {}

    def task(work):
        tasks[work.__name__] = work

    @task
    def gather():
        for branch in range(1, BRANCHES):
            for copy in leaving(branch):
                copy.wait()

        @pl.loop(0, heads)
        def _(head):
            total[...] = first[head].astype(F32)
            for branch in range(1, BRANCHES):
                stride, lanes, per, split = shapes[branch]
                back, start = backs[branch - 1], starts[branch, head]
                if split == 1:
                    value = back[head // per, head % per].astype(F32)
                else:
                    value = back[head * split, 0].astype(F32)
                    for copy in range(1, split):
                        value = value + back[head * split + copy, 0].astype(F32)
                if lanes < 128:
                    value = unpacked(value, 3 * E, start % 2)
                    start = start // 2
                    lanes = 128
                for block in range(SEG0 // lanes):
                    span = slice(block * lanes, (block + 1) * lanes)
                    total[:, span] += jnp.where(start == block, value, 0.0)
            grads[0, head] = (total[0:E, :] * E ** (-0.5)).astype(BF)
            grads[1, head] = total[E : 2 * E, :].astype(BF)
            grads[2, head] = total[2 * E :, :].astype(BF)

        normed_t[...] = normed[...].reshape(SEG0, width).T

    def in_gradient(j):
        rows_in = in_totals[0].shape[3]
        chunk = width // 2
        grads_t[j] = grads[j].reshape(heads * E, SEG0).T
        for half in range(2):
            value = jnp.dot(
                normed_t[half * chunk : (half + 1) * chunk], grads_t[j], preferred_element_type=F32
            ).astype(BF)
            for part in range(chunk // rows_in):
                index = half * (chunk // rows_in) + part
                in_totals[j][index // (2 * rest), index // rest % 2, index % rest] = value[
                    part * rows_in : (part + 1) * rows_in
                ]

    for j in range(3):
        tasks[f"in{j}"] = partial(in_gradient, j)

    def head_swaps():
        swaps = []
        for step in range(1, head_size):
            device = (me_head + step) % head_size
            swaps.append(
                pltpu.make_async_remote_copy(
                    src_ref=head_send.at[device],
                    dst_ref=head_recv.at[step - 1],
                    send_sem=head_sems.at[0, step - 1],
                    recv_sem=head_sems.at[1, step - 1],
                    device_id={"head": device},
                    device_id_type=pl.DeviceIdType.MESH,
                )
            )
        return swaps

    @task
    def one():
        for half in range(2):
            rows = slice(half * SEG0 // 2, (half + 1) * SEG0 // 2)
            value = jnp.zeros((SEG0 // 2, width), F32)
            for j in range(3):
                value = value + lax.dot_general(
                    grads_t[j, rows], in_proj[j], (((1,), (1,)), ((), ())), preferred_element_type=F32
                )
            value = value.astype(BF)
            for slot in range(SLOTS // 2):
                for device in range(head_size):
                    begin = (slot * head_size + device) * per_slot
                    place = (half * SLOTS // 2 + slot) * per_slot
                    head_send[device, place : place + per_slot] = value[begin : begin + per_slot]
        for swap in head_swaps():
            swap.start()

    @task
    def norm():
        for swap in head_swaps():
            swap.wait()
        gain_head[me_head] = jnp.zeros(gains_out.shape, F32)
        gain_head[me_head, 2:4] = gains_two[...]

        @pl.loop(0, SLOTS)
        def _(slot):
            rows = pl.ds(pl.multiple_of(slot * per_slot, per_slot), per_slot)
            grad = head_send[me_head, rows].astype(F32)
            for step in range(1, head_size):
                grad = grad + head_recv[step - 1, rows].astype(F32)
            values = x_rows[rows]
            centred = values - jnp.mean(values, axis=-1, keepdims=True)
            scale = lax.rsqrt(jnp.mean(centred * centred, axis=-1, keepdims=True) + EPS)
            unit = centred * scale
            scaled = grad * gain[...][None]
            inner = jnp.mean(scaled * unit, axis=-1, keepdims=True)
            out = grad_hidden[rows] + scale * (
                scaled - jnp.mean(scaled, axis=-1, keepdims=True) - unit * inner
            )
            place = slot_place(slot)
            for column in range(width // 128):
                lanes = slice(column * 128, (column + 1) * 128)
                spread_rows[column, pl.ds(place, per_slot, stride=SLOTS), :] = out[:, lanes]
            gain_head[me_head, 0:1] += jnp.sum(grad * unit, axis=0, keepdims=True)
            gain_head[me_head, 1:2] += jnp.sum(grad, axis=0, keepdims=True)

        for column in range(width // 128):
            grad_tokens[:, column * 128 : (column + 1) * 128] = spread_rows[column]

    def gain_copy(source, target, axis, device, sem):
        return pltpu.make_async_remote_copy(
            src_ref=source,
            dst_ref=target,
            send_sem=gain_sems.at[0, sem],
            recv_sem=gain_sems.at[1, sem],
            device_id={axis: device},
            device_id_type=pl.DeviceIdType.MESH,
        )

    def gain_copies(stage):
        if stage == 0:
            mine = gain_head.at[me_head]
            return [
                gain_copy(mine, mine, "head", (me_head + step) % head_size, step - 1)
                for step in range(1, head_size)
            ]
        if stage == 1:
            return [gain_copy(gain_one.at[0], gain_one.at[1], "seq", me + 1 - 2 * (me % 2), head_size)]
        if stage == 2:
            device = me + 2 - 4 * (me // 2 % 2)
            return [gain_copy(gain_two.at[0], gain_two.at[1], "seq", device, head_size + 1)]
        spot = me // 4
        block = gain_rest.at[spot]
        return [
            gain_copy(block, block, "seq", (spot + step) % rest * 4 + me % 4, head_size + 1 + step)
            for step in range(1, rest)
        ]

    def summed(ref, count):
        value = ref[0]
        for index in range(1, count):
            value = value + ref[index]
        return value

    def gain_stage(stage):
        if stage > 0:
            for swap in gain_copies(stage - 1):
                swap.wait()
        if stage == 1:
            gain_one[0] = summed(gain_head, head_size)
        elif stage == 2:
            gain_two[0] = summed(gain_one, 2)
        elif stage == 3:
            gain_rest[me // 4] = summed(gain_two, 2)
        elif stage == 4:
            gains_out[...] = summed(gain_rest, rest)
            return
        for swap in gain_copies(stage):
            swap.start()

    for stage in range(5):
        tasks[f"gain{stage}"] = partial(gain_stage, stage)

    for item in TAIL:
        if isinstance(item, str):
            tasks[item]()
        elif item[0] in labels:
            reductions[item[0]].step(item[1])


def backward(heads, starts, own, own_g, units, sends, parts, normed, in_proj, x_rows, grad_hidden, gain, gains_two):
    size, head_size = lax.axis_size("seq"), lax.axis_size("head")
    rest = size // 4
    rows, width = x_rows.shape
    in_shape = (2, 2, rest, width // size, heads * E)
    scratch = []
    for part in parts:
        scratch += Reduction.scratch(size, *part.shape[-2:])
    for _ in range(3):
        scratch += Reduction.scratch(size, *in_shape[-2:])
    streams = len(parts)
    chunks = (streams - 1) // 2
    far = list(units) + [normed, in_proj, x_rows, grad_hidden]
    results = pl.pallas_call(
        partial(backward_kernel, heads, streams),
        in_specs=[pl.BlockSpec(memory_space=pltpu.SMEM)]
        + vmem_specs(2 + len(sends) + 2)
        + [pl.BlockSpec(memory_space=pl.ANY)] * (len(far) + streams),
        out_specs=vmem_specs(6),
        out_shape=[
            jax.ShapeDtypeStruct((2, 2, rest, width // size, chunks * parts[0].shape[-1]), BF),
            jax.ShapeDtypeStruct((chunks, 2, 2, rest) + parts[1].shape[-2:], BF),
            jax.ShapeDtypeStruct(parts[-1].shape, BF),
            jax.ShapeDtypeStruct((3,) + in_shape, BF),
        ]
        + [jax.ShapeDtypeStruct((rows, width), F32), jax.ShapeDtypeStruct((8, width), F32)],
        scratch_shapes=[pltpu.VMEM(value.shape, value.dtype) for value in far]
        + [pltpu.SemaphoreType.DMA((len(far),)), pltpu.VMEM((heads, 3 * E, SEG0), BF)]
        + [pltpu.VMEM(shape.shape, BF) for shape in send_shapes(heads, 3 * E)]
        + [pltpu.VMEM(shape.shape, BF) for shape in send_shapes(heads, ROWS_OUT)]
        + [pltpu.VMEM(shape.shape, BF) for shape in send_shapes(heads, 3 * E)]
        + [
            pltpu.VMEM((ROWS_IN, SEG0), BF),
            pltpu.VMEM((ROWS_OUT, SEG0), BF),
            pltpu.VMEM((ROWS_OUT, SEG0), BF),
            pltpu.VMEM((SEG0, ROWS_OUT), F32),
            pltpu.VMEM((SEG0, ROWS_OUT), F32),
            pltpu.VMEM((3 * E, SEG0), BF),
            pltpu.VMEM((3 * E, SEG0), F32),
            pltpu.VMEM((3, heads, E, SEG0), BF),
            pltpu.VMEM((3, SEG0, heads * E), BF),
            pltpu.VMEM((width, SEG0), BF),
            pltpu.VMEM((width // 128, rows, 128), F32),
            pltpu.VMEM((head_size, rows, width), BF),
            pltpu.VMEM((head_size - 1, rows, width), BF),
            pltpu.VMEM((head_size, 8, width), F32),
            pltpu.VMEM((2, 8, width), F32),
            pltpu.VMEM((2, 8, width), F32),
            pltpu.VMEM((rest, 8, width), F32),
        ]
        + exchange_scratch()
        + [
            pltpu.SemaphoreType.DMA((streams,)),
            pltpu.SemaphoreType.DMA((2, head_size - 1)),
            pltpu.SemaphoreType.DMA((2, head_size + 1 + rest)),
        ]
        + scratch,
        compiler_params=pltpu.CompilerParams(
            vmem_limit_bytes=60 * 2**20, collective_id=1, has_side_effects=True
        ),
        cost_estimate=unit_cost(2 * heads, 5),
        name="backward",
    )(starts, own, own_g, *sends, gain, gains_two, *far, *parts)
    up_total, down_total, out_total, in_total = results[:4]
    sums = [
        in_total.reshape(3, width, heads * E),
        out_total.reshape(-1, width),
        up_total.reshape(width, -1),
        down_total.reshape(-1, width),
    ]
    return sums, results[4], results[5]


def finish_kernel(*refs):
    count = len(refs) // 2
    for source, target in zip(refs[:count], refs[count:]):
        target[...] = source[...].astype(target.dtype)


def finish(values, types):
    steps = 8
    specs = []
    for value in values:
        shape = list(value.shape)
        shape[-2] //= steps
        if value.ndim == 3:
            specs.append(pl.BlockSpec(tuple(shape), lambda i: (0, i, 0)))
        else:
            specs.append(pl.BlockSpec(tuple(shape), lambda i: (i, 0)))
    return pl.pallas_call(
        finish_kernel,
        grid=(steps,),
        in_specs=specs,
        out_specs=specs,
        out_shape=[jax.ShapeDtypeStruct(value.shape, kind) for value, kind in zip(values, types)],
        compiler_params=pltpu.CompilerParams(vmem_limit_bytes=61 * 2**20),
        name="finish",
    )(*values)


def middle_kernel(heads, *refs):
    branches = BRANCHES - 1
    names = Names(refs)
    starts, first = names.take(2)
    backs = names.take(branches)
    gain, shift = names.take(2)
    far = names.take(5)
    block_out, grad_hidden, gains_two, own_g = names.take(4)
    sends = names.take(branches)
    chunks = max(1, far[3].shape[1] // far[0].shape[1])
    halves = names.take(2 * chunks)
    out_total = names.one()
    merged, lse, mixed, turned, part, got, part_two, got_two = names.take(8)
    hidden_one, normed_own, normed, spread_rows, normed_t, cot_t = names.take(6)
    down_sum, norm_sum, up_grad, down_grad, totals = names.take(5)
    head_sems, first_sems, far_sem = names.take(3)
    near = names.take(5)
    out_proj, x_rows, cot, up, down = near[2], near[0], near[1], near[3], near[4]
    loads = [pltpu.make_async_copy(far[i], near[i], far_sem.at[i]) for i in range(5)]
    for copy in loads:
        copy.start()

    head_size, me_head = lax.axis_size("head"), lax.axis_index("head")
    me = lax.axis_index("seq")
    rest = lax.axis_size("seq") // 4
    width = x_rows.shape[1]
    per_slot = x_rows.shape[0] // SLOTS
    tile = 256

    meet("seq", "head")

    @pl.loop(0, heads)
    def _(head):
        own = first[0, head].astype(F32)
        merged[head] = own[:E]
        lse[head] = own[E : E + 1] + own[E + 1 : E + 2] + own[E + 2 : E + 3]
        for branch in range(1, BRANCHES):
            stride, lanes, per, split = branch_shape(branch, heads)
            back, start = backs[branch - 1], starts[branch, head]
            share = max(1, 128 // lanes)
            for copy in range(split):
                if split == 1:
                    value = back[head // per, head % per].astype(F32)
                else:
                    value = back[head * split + copy, 0].astype(F32)
                if share > 1:
                    value = unpacked(value, ROWS_OUT, start % share)
                new_lse = value[E : E + 1] + value[E + 1 : E + 2] + value[E + 2 : E + 3]
                if share > 1:
                    ids = lax.broadcasted_iota(jnp.int32, new_lse.shape, 1)
                    new_lse = jnp.where(ids // lanes == start % share, new_lse, -FAR)
                span = lanes * share
                for block in range(SEG0 // span):
                    at = slice(block * span, (block + 1) * span)
                    new = jnp.where(start // share == block, new_lse, -FAR)
                    old = lse[head, :, at]
                    top = jnp.maximum(old, new)
                    both = top + jnp.log2(jnp.exp2(old - top) + jnp.exp2(new - top))
                    lse[head, :, at] = both
                    merged[head, :, at] = merged[head, :, at] * jnp.exp2(old - both) + value[:E] * jnp.exp2(
                        new - both
                    )
        mixed[head] = merged[head].astype(BF)

    def rows_of(ref):
        return ref[...].reshape(SEG0, width)

    turned[...] = mixed[...].reshape(heads * E, SEG0).T
    for copy in loads:
        copy.wait()
    for step in range(SEG0 // tile):
        at = slice(step * tile // (head_size * per_slot), (step + 1) * tile // (head_size * per_slot))
        value = jnp.dot(turned[step * tile : (step + 1) * tile], out_proj[...], preferred_element_type=F32)
        part[at] = value.astype(BF).reshape(-1, head_size, per_slot, width)
    for copy in head_copies(part, got, head_sems, 0, True):
        copy.start()
    cot_t[...] = rows_of(cot).T
    for copy in head_copies(part, got, head_sems, 0, True):
        copy.wait()

    def rows_at(slot):
        return pl.ds(pl.multiple_of(slot * per_slot, per_slot), per_slot)

    @over_slots
    def _(slot):
        value = x_rows[rows_at(slot)] + part[slot, me_head].astype(F32)
        for step in range(1, head_size):
            value = value + got[step - 1, slot].astype(F32)
        hidden_one[rows_at(slot)] = value
        unit, scale = norm_of(value)
        low = (unit * gain[...][None] + shift[...][None]).astype(BF)
        normed_own[slot] = low
        normed[slot, me_head] = low

    for copy in head_copies(normed_own, normed, head_sems, 1, False):
        copy.start()
    for copy in head_copies(normed_own, normed, head_sems, 1, False):
        copy.wait()
    normed_t[...] = rows_of(normed).T

    chunk_width = up.shape[1] // chunks
    orders = {0: ORDERS["u1"], 1: ORDERS["d1"]}
    firsts = []
    for chunk in range(chunks):
        for kind in range(2):
            index = 2 * chunk + kind
            firsts.append(
                Reduction(
                    orders[kind], totals.at[index], halves[index], None, None,
                    first_sems.at[0, pl.ds(index, 1)], first_sems.at[1, pl.ds(index, 1)],
                )
            )
    down_sum[...] = jnp.zeros_like(down_sum)
    norm_sum[...] = jnp.zeros_like(norm_sum)
    slots = tile // (head_size * per_slot)
    contract_last = (((1,), (1,)), ((), ()))

    for chunk in range(chunks):
        units = slice(chunk * chunk_width, (chunk + 1) * chunk_width)
        up_grad[...] = jnp.zeros_like(up_grad)
        down_grad[...] = jnp.zeros_like(down_grad)

        @pl.loop(0, SEG0 // tile)
        def _(step):
            rows = pl.ds(pl.multiple_of(step * tile, tile), tile)
            low = normed[pl.ds(step * slots, slots)].reshape(tile, width)
            back = cot[pl.ds(step * slots, slots)].reshape(tile, width)
            pre = jnp.dot(low, up[:, units], preferred_element_type=F32)
            grad = lax.dot_general(back, down[units], contract_last, preferred_element_type=F32)
            share = 0.5 + 0.5 * lax.erf(pre * math.sqrt(0.5))
            density = jnp.exp2(pre * pre * (-0.5 * LOG2E)) * (1.0 / math.sqrt(2.0 * math.pi))
            hidden = (pre * share).astype(BF)
            grad = (grad * (share + pre * density)).astype(BF)
            down_sum[rows] += jnp.dot(hidden, down[units], preferred_element_type=F32)
            norm_sum[rows] += lax.dot_general(grad, up[:, units], contract_last, preferred_element_type=F32)
            up_grad[...] += jnp.dot(normed_t[:, rows], grad, preferred_element_type=F32)
            down_grad[...] += jnp.dot(cot_t[:, rows], hidden, preferred_element_type=F32)

        pieces = totals.shape[3] * 4
        size = totals.shape[4]
        turned_down = down_grad[...].T
        for piece in range(pieces):
            spot = (piece // (2 * rest), piece // rest % 2, piece % rest)
            span = slice(piece * size, (piece + 1) * size)
            totals[(2 * chunk,) + spot] = up_grad[span].astype(BF)
            totals[(2 * chunk + 1,) + spot] = turned_down[span].astype(BF)
        firsts[2 * chunk].step(0)
        firsts[2 * chunk + 1].step(0)

    for ref, value in ((part, down_sum), (part_two, norm_sum)):

        @pl.loop(0, SLOTS)
        def _(slot):
            for device in range(head_size):
                begin = pl.multiple_of((slot * head_size + device) * per_slot, per_slot)
                ref[slot, device] = value[pl.ds(begin, per_slot)].astype(BF)

    for copy in head_copies(part_two, got_two, head_sems, 2, True) + head_copies(part, got, head_sems, 3, True):
        copy.start()
    for copy in head_copies(part_two, got_two, head_sems, 2, True):
        copy.wait()
    gains_two[...] = jnp.zeros_like(gains_two)

    @over_slots
    def _(slot):
        grad = part_two[slot, me_head].astype(F32)
        for step in range(1, head_size):
            grad = grad + got_two[step - 1, slot].astype(F32)
        unit, scale = norm_of(hidden_one[rows_at(slot)])
        scaled = grad * gain[...][None]
        inner = jnp.mean(scaled * unit, axis=-1, keepdims=True)
        out = cot[slot, me_head].astype(F32) + scale * (
            scaled - jnp.mean(scaled, axis=-1, keepdims=True) - unit * inner
        )
        grad_hidden[rows_at(slot)] = out
        normed_own[slot] = out.astype(BF)
        normed[slot, me_head] = out.astype(BF)
        gains_two[0:1] += jnp.sum(grad * unit, axis=0, keepdims=True)
        gains_two[1:2] += jnp.sum(grad, axis=0, keepdims=True)

    for copy in head_copies(normed_own, normed, head_sems, 4, False):
        copy.start()
    for copy in head_copies(part, got, head_sems, 3, True):
        copy.wait()

    @pl.loop(0, SLOTS)
    def _(slot):
        value = hidden_one[rows_at(slot)] + part[slot, me_head].astype(F32)
        for step in range(1, head_size):
            value = value + got[step - 1, slot].astype(F32)
        place = slot_place(slot)
        for column in range(width // 128):
            lanes = slice(column * 128, (column + 1) * 128)
            spread_rows[column, pl.ds(place, per_slot, stride=SLOTS), :] = value[:, lanes]

    for column in range(width // 128):
        block_out[:, column * 128 : (column + 1) * 128] = spread_rows[column].astype(BF)
    for copy in head_copies(normed_own, normed, head_sems, 4, False):
        copy.wait()

    value = jnp.dot(mixed[...].reshape(heads * E, SEG0), rows_of(normed), preferred_element_type=F32)
    size = out_total.shape[3]
    for piece in range(4 * rest):
        spot = (piece // (2 * rest), piece // rest % 2, piece % rest)
        out_total[spot] = value[piece * size : (piece + 1) * size].astype(BF)

    normed_t[...] = rows_of(normed).T
    value = jnp.dot(out_proj[...], normed_t[...], preferred_element_type=F32)
    own_g[0, :, :E, :] = value.astype(BF).reshape(heads, E, SEG0)

    @pl.loop(0, heads)
    def _(head):
        low = own_g[0, head, :E, :]
        dots = jnp.sum(low.astype(F32) * merged[head], axis=0, keepdims=True)
        d = pieces_of(-dots)
        m = pieces_of(-lse[head])
        placed = {0: d[0], 1: d[1], 2: d[2], 12: m[0], 13: m[1], 14: m[2]}
        own_g[0, head, E:, :] = row_block(placed, SEG0).astype(BF)
        own = jnp.concatenate([low.astype(F32), row_block(placed, SEG0)], axis=0)
        spread_blocks(heads, head, starts, own, sends)

    for reduction in firsts:
        reduction.finish_first()


def middle(heads, starts, first, backs, x_rows, cot, out_proj, up, down, gain, shift):
    size, head_size = lax.axis_size("seq"), lax.axis_size("head")
    rest = size // 4
    rows, width = x_rows.shape
    per_slot = rows // SLOTS
    chunks = max(1, up.shape[1] // width)
    shard = (SLOTS, head_size, per_slot, width)
    own = (SLOTS, per_slot, width)
    got = (head_size - 1,) + own
    sends = send_shapes(heads, ROWS_OUT)
    piece = (2, rest, width // size, up.shape[1] // chunks)
    out_piece = (2, 2, rest, heads * E // size, width)
    far = [x_rows, cot, out_proj, up, down]
    results = pl.pallas_call(
        partial(middle_kernel, heads),
        in_specs=[pl.BlockSpec(memory_space=pltpu.SMEM)]
        + vmem_specs(1 + len(backs) + 2)
        + [pl.BlockSpec(memory_space=pl.ANY)] * 5,
        out_specs=vmem_specs(4 + len(sends) + 2 * chunks + 1),
        out_shape=[
            jax.ShapeDtypeStruct((rows, width), BF),
            jax.ShapeDtypeStruct((rows, width), F32),
            jax.ShapeDtypeStruct((2, width), F32),
            jax.ShapeDtypeStruct((1, heads, ROWS_OUT, SEG0), BF),
        ]
        + sends
        + [jax.ShapeDtypeStruct(piece, BF)] * (2 * chunks)
        + [jax.ShapeDtypeStruct(out_piece, BF)],
        scratch_shapes=[
            pltpu.VMEM((heads, E, SEG0), F32),
            pltpu.VMEM((heads, 1, SEG0), F32),
            pltpu.VMEM((heads, E, SEG0), BF),
            pltpu.VMEM((SEG0, heads * E), BF),
            pltpu.VMEM(shard, BF),
            pltpu.VMEM(got, BF),
            pltpu.VMEM(shard, BF),
            pltpu.VMEM(got, BF),
            pltpu.VMEM((rows, width), F32),
            pltpu.VMEM(own, BF),
            pltpu.VMEM(shard, BF),
            pltpu.VMEM((width // 128, rows, 128), F32),
            pltpu.VMEM((width, SEG0), BF),
            pltpu.VMEM((width, SEG0), BF),
            pltpu.VMEM((SEG0, width), F32),
            pltpu.VMEM((SEG0, width), F32),
            pltpu.VMEM((width, up.shape[1] // chunks), F32),
            pltpu.VMEM((width, up.shape[1] // chunks), F32),
            pltpu.VMEM((2 * chunks, 2) + piece, BF),
            pltpu.SemaphoreType.DMA((2, 5, head_size - 1)),
            pltpu.SemaphoreType.DMA((2, 2 * chunks)),
            pltpu.SemaphoreType.DMA((5,)),
        ]
        + [pltpu.VMEM(value.shape, value.dtype) for value in far],
        compiler_params=pltpu.CompilerParams(
            vmem_limit_bytes=60 * 2**20, collective_id=2, has_side_effects=True
        ),
        cost_estimate=pl.CostEstimate(
            flops=14 * SEG0 * width * up.shape[1], transcendentals=0, bytes_accessed=40 * 2**20
        ),
        name="middle",
    )(starts, first, *backs, gain, shift, *far)
    block_out, grad_hidden, gains_two, own_g = results[:4]
    return block_out, grad_hidden, gains_two, own_g, results[4 : 4 + len(sends)], results[4 + len(sends) :]


def local(
    tokens,
    documents,
    offsets,
    in_proj,
    out_proj,
    up_proj,
    down_proj,
    first_gain,
    first_shift,
    second_gain,
    second_shift,
    cotangent,
):
    head_count = lax.axis_size("head")
    seq_id = lax.axis_index("seq")
    row_count = tokens.shape[0]
    seq_len = row_count * head_count
    heads = offsets.shape[1]
    per_slot = row_count // SLOTS

    my_docs = lax.dynamic_slice_in_dim(documents, seq_id * seq_len, seq_len)
    my_docs = my_docs.reshape(head_count, per_slot, 2, 2, 2, 2).transpose(5, 4, 3, 2, 0, 1).reshape(seq_len)
    bit_ids = jnp.arange(BIT_ROWS, dtype=jnp.int32)[:, None]
    doc_bit = my_docs[None, :] // 2 ** (bit_ids % DOC_BITS) % 2
    bits = jnp.where(bit_ids < DOC_BITS, doc_bit, jnp.where(bit_ids < 2 * DOC_BITS, 1 - doc_bit, 0))
    bits = bits.astype(BF)
    starts = jnp.stack([reversed_bits(offsets[b], b) for b in range(BRANCHES)])

    (x_rows, normed, cot_all, own), units, first_out, outs = forward(
        heads, starts, tokens, cotangent, bits, first_gain, first_shift, in_proj
    )
    block_out, grad_hidden, gains_two, own_g, sends_g, parts = middle(
        heads, starts, first_out, outs, x_rows, cot_all, out_proj, up_proj, down_proj, second_gain, second_shift
    )
    sums, grad_tokens, gains = backward(
        heads, starts, own, own_g, units, sends_g, parts,
        normed, in_proj, x_rows, grad_hidden, first_gain, gains_two,
    )
    results = finish([block_out, grad_tokens] + sums, [BF] + [F32] * 5)
    return (*results, gains[0], gains[1], gains[2], gains[3])


def solution(mesh):
    placed = (
        P(("seq", "head"), None),
        P(),
        P(None, "head"),
        P(None, None, "head"),
        P("head", None),
        P(None, "head"),
        P("head", None),
        P(),
        P(),
        P(),
        P(),
        P(("seq", "head"), None),
    )
    return jax.shard_map(
        local,
        mesh=mesh,
        in_specs=placed,
        out_specs=(
            P(("seq", "head"), None),
            P(("seq", "head"), None),
            P(None, None, "head"),
            P("head", None),
            P(None, "head"),
            P("head", None),
            P(),
            P(),
            P(),
            P(),
        ),
        check_vma=False,
    )
```

```python
import math
from functools import partial

import jax
import jax.numpy as jnp
from jax import lax
from jax.experimental import pallas as pl
from jax.experimental.pallas import tpu as pltpu
from jax.sharding import PartitionSpec as P

E = 48
BRANCHES = 5
SEG0 = 1024
SLOTS = 16
BIT_ROWS = 16
DOC_BITS = 6
ROWS_IN = 3 * E + BIT_ROWS
ROWS_OUT = E + BIT_ROWS
EPS = 1e-05
FAR = 1e30
LOG2E = math.log2(math.e)
LN2 = math.log(2.0)
BF = jnp.bfloat16
F32 = jnp.float32
VMEM_LIMIT = 48 * 2**20


def reversed_bits(value, count):
    out = value % 2
    for bit in range(1, count):
        out = out * 2 + value // 2**bit % 2
    return out


def branch_shape(branch, heads):
    stride = 2**branch
    return (stride, SEG0 // stride, max(1, heads // stride), max(1, stride // heads))


def pieces_of(value):
    high = value.astype(BF).astype(F32)
    rest = value - high
    middle = rest.astype(BF).astype(F32)
    return high, middle, (rest - middle).astype(BF).astype(F32)


def row_block(placed, columns):
    ids = lax.broadcasted_iota(jnp.int32, (BIT_ROWS, columns), 0)
    block = jnp.zeros((BIT_ROWS, columns), F32)
    for row, value in placed.items():
        block = jnp.where(ids == row, value, block)
    return block


def turned_half(block):
    return jnp.concatenate([block[:, 64:], block[:, :64]], axis=1)


def low_half():
    return lax.broadcasted_iota(jnp.int32, (1, 128), 1) < 64


def packed_rows(rows, count):
    return rows if count >= 128 else (rows // 2 + 15) // 16 * 16


def packed(block, half):
    rows = packed_rows(block.shape[0], 64)
    upper, lower = block[:rows], block[block.shape[0] - rows :]
    if isinstance(half, int):
        return jnp.where(low_half(), turned_half(upper) if half else upper, lower if half else turned_half(lower))
    upper = jnp.where(half == 0, upper, turned_half(upper))
    lower = jnp.where(half == 0, turned_half(lower), lower)
    return jnp.where(low_half(), upper, lower)


def unpacked(value, rows, half):
    size = value.shape[0]
    other = turned_half(value)
    upper = jnp.where(half == 0, value, other)
    lower = jnp.where(half == 0, other, value)
    both = jnp.concatenate([upper, lower[2 * size - rows :]], axis=0)
    return jnp.where(low_half() == (half == 0), both, 0.0)


def send_shapes(heads, rows):
    outs = []
    for branch in range(1, BRANCHES):
        stride, count, per, split = branch_shape(branch, heads)
        outs.append(jax.ShapeDtypeStruct((stride, per, packed_rows(rows, count), max(count, 128)), BF))
    return outs


def spread_blocks(heads, head, starts, value, sends, branches=range(1, BRANCHES)):
    for branch in branches:
        stride, lanes, per, split = branch_shape(branch, heads)
        send, start = sends[branch - 1], reversed_bits(starts[branch, head], branch)
        share = max(1, 128 // lanes)
        span = lanes * share
        block = value[:, :span]
        for part in range(1, SEG0 // span):
            block = jnp.where(start // share == part, value[:, part * span : (part + 1) * span], block)
        if share > 1:
            block = packed(block, start % share)
        block = block.astype(BF)
        if split == 1:
            send[head // per, head % per] = block
        else:
            for copy in range(split):
                send[head * split + copy, 0] = block


def norm_of(values):
    centred = values - jnp.mean(values, axis=-1, keepdims=True)
    scale = lax.rsqrt(jnp.mean(centred * centred, axis=-1, keepdims=True) + EPS)
    return centred * scale, scale


def slot_place(slot):
    return slot % 2 * 8 + slot // 2 % 2 * 4 + slot // 4 % 2 * 2 + slot // 8


def over_slots(body, unroll=4):
    @pl.loop(0, SLOTS // unroll)
    def _(step):
        for part in range(unroll):
            body(step * unroll + part)


def head_copies(source, target, sems, index, scatter):
    size, me = lax.axis_size("head"), lax.axis_index("head")
    copies = []
    for step in range(1, size):
        device = (me + step) % size
        copies.append(
            pltpu.make_async_remote_copy(
                src_ref=source.at[:, device] if scatter else source,
                dst_ref=target.at[step - 1] if scatter else target.at[:, me],
                send_sem=sems.at[0, index, step - 1],
                recv_sem=sems.at[1, index, step - 1],
                device_id={"head": device},
                device_id_type=pl.DeviceIdType.MESH,
            )
        )
    return copies


def load_unit(ref, unit, count, x):
    width = ref.shape[-1]
    if count >= 128:
        for block in range(ref.shape[0]):
            x[:, block * width : (block + 1) * width] = ref[block, unit]
        return
    rows, size = x.shape[0], ref.shape[2]
    for block in range(ref.shape[0] // 2):
        lanes = slice(block * 128, (block + 1) * 128)
        left = ref[2 * block, unit].astype(F32)
        right = ref[2 * block + 1, unit].astype(F32)
        x[:size, lanes] = jnp.where(low_half(), left, turned_half(right)).astype(BF)
        x[rows - size :, lanes] = jnp.where(low_half(), turned_half(left), right).astype(BF)


def store_unit(ref, unit, count, result):
    width = ref.shape[-1]
    for block in range(SEG0 // width):
        value = result[:, block * width : (block + 1) * width]
        if count >= 128:
            ref[block, unit] = value
        else:
            value = value.astype(F32)
            ref[2 * block, unit] = packed(value, 0).astype(BF)
            ref[2 * block + 1, unit] = packed(value, 1).astype(BF)


def forward_unit(x, q_aug, result, base, queries):
    if isinstance(base, int):
        lanes = slice(base, base + queries)
    else:
        lanes = pl.ds(pl.multiple_of(base, 128), queries)
    q_aug[0:E, :queries] = x[0:E, lanes]
    q_aug[E:, :queries] = (x[3 * E :, lanes].astype(F32) * -FAR).astype(BF)
    bits = x[3 * E :, :].astype(F32)
    k_rows = jnp.concatenate([x[E : 2 * E, :], (1.0 - bits).astype(BF)], axis=0).T
    v_aug = jnp.concatenate([x[2 * E : 3 * E, :], jnp.ones(bits.shape, BF)], axis=0)
    if queries < SEG0:
        result[0:E, :] = jnp.zeros((E, SEG0), BF)
        result[E:, :] = row_block({0: -FAR}, SEG0).astype(BF)
    s = jnp.dot(k_rows, q_aug[:, :queries], preferred_element_type=F32)
    top = jnp.max(s, axis=0, keepdims=True)
    p = jnp.exp2(s - top).astype(BF)
    o = jnp.dot(v_aug, p, preferred_element_type=F32)
    total = o[E : E + 1]
    high, middle_part, low = pieces_of(top + jnp.log2(total))
    block = row_block({0: high, 1: middle_part, 2: low}, queries)
    result[:, lanes] = jnp.concatenate([o[:E] * (1.0 / total), block], axis=0).astype(BF)


class Names:
    def __init__(self, refs):
        self.refs = list(refs)

    def take(self, count):
        taken, self.refs = self.refs[:count], self.refs[count:]
        return taken

    def one(self):
        return self.take(1)[0]


def group_place(branch):
    stride = 2**branch
    me = lax.axis_index("seq")
    return me // stride * stride, me % stride


def meet(*axes):
    barrier = pltpu.get_barrier_semaphore()
    count = 0
    for axis in axes:
        size = lax.axis_size(axis)
        me = lax.axis_index(axis)

        @pl.loop(1, size)
        def _(step):
            pl.semaphore_signal(
                barrier, inc=1, device_id={axis: (me + step) % size}, device_id_type=pl.DeviceIdType.MESH
            )

        count += size - 1
    pl.semaphore_wait(barrier, count)


class Reduction:
    STEPS = 7

    def __init__(self, order, total, half, quarter, others, send, recv, begun=False):
        self.total, self.begun = total, begun
        self.half, self.quarter, self.others = half, quarter, others
        self.send, self.recv = send, recv
        me = lax.axis_index("seq")
        self.rest = lax.axis_size("seq") // 4
        self.me = me
        bits = (me % 2, me // 2 % 2)
        self.bits = [bits[bit] for bit in order]
        self.partners = [me + (1 - 2 * bits[bit]) * 2**bit for bit in order]
        self.place = me // 4

    def copy(self, source, target, device, sem):
        return pltpu.make_async_remote_copy(
            src_ref=source,
            dst_ref=target,
            send_sem=self.send.at[sem],
            recv_sem=self.recv.at[sem],
            device_id={"seq": device},
            device_id_type=pl.DeviceIdType.MESH,
        )

    def copies(self, number):
        one, two = self.bits
        rest = self.rest
        others = []
        for step in range(1, rest):
            place = (self.place + step) % rest
            others.append((step, place, place * 4 + self.me % 4))
        if number == 0:
            return [self.copy(self.total.at[1 - one], self.half, self.partners[0], 0)]
        if number == 1:
            return [self.copy(self.half.at[1 - two], self.quarter, self.partners[1], 1)]
        if number == 2:
            return [
                self.copy(self.quarter.at[place], self.others.at[step - 1], device, 1 + step)
                for step, place, device in others
            ]
        if number == 3:
            block = self.total.at[one, two, self.place]
            return [self.copy(block, block, device, rest + step) for step, place, device in others]
        if number == 4:
            block = self.total.at[one, two]
            return [self.copy(block, block, self.partners[1], 2 * rest)]
        if number == 5:
            block = self.total.at[one]
            return [self.copy(block, block, self.partners[0], 2 * rest + 1)]
        return []

    def finish_first(self):
        one, rest = self.bits[0], self.rest
        for copy in self.copies(0):
            copy.wait()

        @pl.loop(0, 2 * rest)
        def _(i):
            j, z = i // rest, i % rest
            mine = self.total[one, j, z].astype(F32)
            self.half[j, z] = (mine + self.half[j, z].astype(F32)).astype(BF)

    def step(self, number):
        one, two = self.bits
        rest = self.rest
        if number == 0 and self.begun:
            return
        if number == 1:
            if not self.begun:
                self.finish_first()
        elif number > 0:
            for copy in self.copies(number - 1):
                copy.wait()
        if number == 2:

            @pl.loop(0, rest)
            def _(z):
                mine = self.half[two, z].astype(F32)
                self.quarter[z] = (mine + self.quarter[z].astype(F32)).astype(BF)

        elif number == 3:
            mine = self.quarter[self.place].astype(F32)
            for step in range(1, rest):
                mine = mine + self.others[step - 1].astype(F32)
            self.total[one, two, self.place] = mine.astype(BF)
        for copy in self.copies(number):
            copy.start()

    @staticmethod
    def scratch(size, rows, columns):
        rest = size // 4
        count = 2 * rest + 2
        return [
            pltpu.VMEM((2, rest, rows, columns), BF),
            pltpu.VMEM((rest, rows, columns), BF),
            pltpu.VMEM((rest - 1, rows, columns), BF),
            pltpu.SemaphoreType.DMA((count,)),
            pltpu.SemaphoreType.DMA((count,)),
        ]


def reduction_parts(value, size):
    rows, columns = value.shape
    return value.reshape(2, 2, size // 4, rows // size, columns)


def reduction_whole(value):
    return value.reshape(-1, value.shape[-1])


def make_reductions(orders, totals, scratch):
    out = []
    for order, total in zip(orders, totals):
        out.append(Reduction(order, total, *scratch[:5]))
        scratch = scratch[5:]
    return out


def group_copies(branch, source, target, send_sems, recv_sems, local_sem):
    stride = 2**branch
    base, place = group_place(branch)
    first = stride - branch - 2
    copies = [
        pltpu.make_async_copy(source.at[place], target.at[place], local_sem.at[branch - 1])
    ]
    for step in range(1, stride):
        member = (place + step) % stride
        copies.append(
            pltpu.make_async_remote_copy(
                src_ref=source.at[member],
                dst_ref=target.at[place],
                send_sem=send_sems.at[first + step],
                recv_sem=recv_sems.at[first + step],
                device_id={"seq": base + member},
                device_id_type=pl.DeviceIdType.MESH,
            )
        )
    return copies


def forward_kernel(heads, starts, tokens, cotangent, bits, gain, shift, in_proj, *refs):
    count = BRANCHES - 1
    names = Names(refs)
    far = names.take(4 + count)
    first, backs = names.one(), names.take(count)
    near = names.take(4 + count)
    (x_rows, normed, cot, own), gots = near[:4], near[4:]
    outs, sends = names.take(count), names.take(count)
    x, q_aug, result, in_send, in_recv, in_local, out_send, out_recv, out_local = names.take(9)
    spread_rows, normed_own, cot_own, normed_t, head_sems, far_sem = names.take(6)
    saves = [pltpu.make_async_copy(near[i], far[i], far_sem.at[i]) for i in range(4 + count)]
    me_head = lax.axis_index("head")
    rows, width = tokens.shape
    per_slot = rows // SLOTS

    def fill(source):
        for column in range(width // 128):
            spread_rows[column] = source[:, column * 128 : (column + 1) * 128].astype(F32)

    def picked(slot):
        at = pl.ds(slot_place(slot), per_slot, stride=SLOTS)
        return jnp.concatenate([spread_rows[column, at, :] for column in range(width // 128)], axis=1)

    fill(tokens)

    @over_slots
    def _(slot):
        value = picked(slot)
        x_rows[pl.ds(pl.multiple_of(slot * per_slot, per_slot), per_slot)] = value
        low = (norm_of(value)[0] * gain[...][None] + shift[...][None]).astype(BF)
        normed_own[slot] = low
        normed[slot, me_head] = low

    meet("seq", "head")
    for copy in head_copies(normed_own, normed, head_sems, 0, False):
        copy.start()
    saves[0].start()
    fill(cotangent)

    @over_slots
    def _(slot):
        low = picked(slot).astype(BF)
        cot_own[slot] = low
        cot[slot, me_head] = low

    for copy in head_copies(cot_own, cot, head_sems, 1, False):
        copy.start()
    own[0, :, 3 * E :, :] = jnp.broadcast_to(bits[...][None], (heads,) + bits.shape)
    turned = [in_proj[j].T for j in range(3)]
    for copy in head_copies(normed_own, normed, head_sems, 0, False):
        copy.wait()
    normed_t[...] = normed[...].reshape(SEG0, width).T
    for j in range(3):
        value = jnp.dot(turned[j], normed_t[...], preferred_element_type=F32)
        if j == 0:
            value = value * (E ** (-0.5) * LOG2E)
        own[0, :, j * E : (j + 1) * E, :] = value.astype(BF).reshape(heads, E, SEG0)
    saves[1].start()
    saves[3].start()

    coming = {}
    for branch in range(1, BRANCHES):

        @pl.loop(0, heads)
        def _(head):
            spread_blocks(heads, head, starts, own[0, head].astype(F32), sends, [branch])

        coming[branch] = group_copies(branch, sends[branch - 1], gots[branch - 1], in_send, in_recv, in_local)
        for copy in coming[branch]:
            copy.start()

    @pl.loop(0, heads)
    def _(head):
        x[...] = own[0, head]
        forward_unit(x, q_aug, result, 0, SEG0)
        first[0, head] = result[...]

    for copy in head_copies(cot_own, cot, head_sems, 1, False):
        copy.wait()
    saves[2].start()
    leaving = []
    for branch in range(1, BRANCHES):
        stride, lanes, units, split = branch_shape(branch, heads)
        got, out = gots[branch - 1], outs[branch - 1]
        for copy in coming[branch]:
            copy.wait()
        saves[3 + branch].start()
        queries = SEG0 // split
        base = 0 if split == 1 else lax.axis_index("seq") % split * queries

        @pl.loop(0, units)
        def _(unit):
            load_unit(got, unit, lanes, x)
            forward_unit(x, q_aug, result, base, queries)
            store_unit(out, unit, lanes, result)

        copies = group_copies(branch, out, backs[branch - 1], out_send, out_recv, out_local)
        for copy in copies:
            copy.start()
        leaving += copies
    for copy in leaving + saves:
        copy.wait()


def exchange_scratch():
    copies = 2**BRANCHES - 2 - BRANCHES + 1
    one = [
        pltpu.SemaphoreType.DMA((copies,)),
        pltpu.SemaphoreType.DMA((copies,)),
        pltpu.SemaphoreType.DMA((BRANCHES - 1,)),
    ]
    return one + one


def unit_cost(units, dots):
    return pl.CostEstimate(
        flops=dots * 2 * units * SEG0 * SEG0 * 256,
        transcendentals=units * SEG0 * SEG0,
        bytes_accessed=units * SEG0 * 1000,
    )


def vmem_specs(count):
    return [pl.BlockSpec(memory_space=pltpu.VMEM)] * count


def forward(heads, starts, tokens, cotangent, bits, gain, shift, in_proj):
    head_size = lax.axis_size("head")
    rows, width = tokens.shape
    shard = jax.ShapeDtypeStruct((SLOTS, head_size, rows // SLOTS, width), BF)
    own_rows = pltpu.VMEM((SLOTS, rows // SLOTS, width), BF)
    backs = send_shapes(heads, ROWS_OUT)
    gots = send_shapes(heads, ROWS_IN)
    own = jax.ShapeDtypeStruct((1, heads, ROWS_IN, SEG0), BF)
    far = [jax.ShapeDtypeStruct((rows, width), F32), shard, shard, own] + gots
    results = pl.pallas_call(
        partial(forward_kernel, heads),
        in_specs=[pl.BlockSpec(memory_space=pltpu.SMEM)] + vmem_specs(6),
        out_specs=[pl.BlockSpec(memory_space=pl.ANY)] * len(far) + vmem_specs(1 + len(backs)),
        out_shape=far + [jax.ShapeDtypeStruct((1, heads, ROWS_OUT, SEG0), BF)] + backs,
        scratch_shapes=[pltpu.VMEM(shape.shape, shape.dtype) for shape in far + backs + gots]
        + [
            pltpu.VMEM((ROWS_IN, SEG0), BF),
            pltpu.VMEM((ROWS_OUT, SEG0), BF),
            pltpu.VMEM((ROWS_OUT, SEG0), BF),
        ]
        + exchange_scratch()
        + [
            pltpu.VMEM((width // 128, rows, 128), F32),
            own_rows,
            own_rows,
            pltpu.VMEM((width, SEG0), BF),
            pltpu.SemaphoreType.DMA((2, 2, head_size - 1)),
            pltpu.SemaphoreType.DMA((len(far),)),
        ],
        compiler_params=pltpu.CompilerParams(
            vmem_limit_bytes=60 * 2**20, collective_id=0, has_side_effects=True
        ),
        cost_estimate=unit_cost(2 * heads, 2),
        name="forward",
    )(starts, tokens, cotangent, bits, gain, shift, in_proj)
    return results[:4], results[4 : len(far)], results[len(far)], results[len(far) + 1 :]


def backward_unit(x, g, q_aug, gk, gv, result, base, queries, tile):
    if isinstance(base, int):
        lanes = slice(base, base + queries)
    else:
        lanes = pl.ds(pl.multiple_of(base, 128), queries)
    extra = g[E:, lanes].astype(F32)
    ids = lax.broadcasted_iota(jnp.int32, extra.shape, 0)
    q = x[0:E, lanes]
    q_aug[0:E, :queries] = q
    q_aug[E:, :queries] = jnp.where(ids >= 12, extra, x[3 * E :, lanes].astype(F32) * -FAR).astype(BF)
    bits = x[3 * E :, :].astype(F32)
    k_aug = jnp.concatenate([x[E : 2 * E, :], (1.0 - bits).astype(BF)], axis=0)
    k_rows = k_aug.T
    v_ids = lax.broadcasted_iota(jnp.int32, bits.shape, 0)
    v_bits = jnp.where(v_ids < 3, 1.0, 0.0).astype(BF)
    v_rows = jnp.concatenate([x[2 * E : 3 * E, :], v_bits], axis=0).T
    q_rows = jnp.concatenate([q, jnp.zeros((BIT_ROWS, queries), BF)], axis=0).T
    g_all = g[:, lanes]
    g_rows = g_all.T
    if queries < SEG0:
        result[0:E, :] = jnp.zeros((E, SEG0), BF)
    for step in range(queries // tile):
        column = step * tile
        span = slice(column, column + tile)
        p = jnp.exp2(jnp.dot(k_rows, q_aug[:, span], preferred_element_type=F32))
        gs = p * jnp.dot(v_rows, g_all[:, span], preferred_element_type=F32)
        p, gs = p.astype(BF), gs.astype(BF)
        target = span if isinstance(base, int) else pl.ds(pl.multiple_of(base + column, 128), tile)
        result[0:E, target] = jnp.dot(k_aug, gs, preferred_element_type=F32)[:E].astype(BF)
        new_k = jnp.dot(gs, q_rows[span], preferred_element_type=F32)
        new_v = jnp.dot(p, g_rows[span], preferred_element_type=F32)
        if step == 0:
            gk[...] = new_k
            gv[...] = new_v
        else:
            gk[...] += new_k
            gv[...] += new_v
    result[E : 2 * E, :] = (gk[...].T[:E] * LN2).astype(BF)
    result[2 * E :, :] = gv[...].T[:E].astype(BF)


ORDERS = {
    'u1': (0, 1), 'u2': (0, 1), 'd1': (1, 0), 'd2': (1, 0), 'o': (0, 1), 'i0': (1, 0), 'i1': (1, 0), 'i2': (0,
    1),
}
EARLY = [
    (0, 'd1', 0), (0, 'u1', 0), (0, 'd1', 1), (0, 'u2', 0), (0, 'u1', 1), (2, 'o', 0), (4, 'u2', 1), (5, 'u1',
    2), (7, 'd1', 2), (9, 'u1', 3), (10, 'd2', 0), (12, 'd2', 1), (12, 'o', 1), (12, 'd1', 3), (13, 'u2', 2),
    (14, 'u1', 4),
]
TAIL = [
    'gather', ('d1', 4), 'in1', ('i1', 0), ('d2', 2), 'in2', ('u2', 3), ('i2', 0), 'in0', ('i0', 0), ('d2',
    3), ('i1', 1), ('i2', 1), ('u1', 5), ('u2', 4), ('d2', 4), ('d1', 5), ('o', 2), ('i2', 2), ('i0', 1),
    ('i1', 2), ('i2', 3), 'one', ('d2', 5), ('o', 3), ('i1', 3), ('u1', 6), ('u2', 5), 'norm', ('i2', 4),
    'gain0', ('i0', 2), ('i1', 4), ('i0', 3), 'gain1', ('o', 4), ('i0', 4), ('i2', 5), 'gain2', ('i1', 5),
    ('o', 5), ('i0', 5), 'gain3', ('i0', 6), ('d2', 6), ('u2', 6), 'gain4', ('d1', 6), ('i1', 6), ('i2', 6),
    ('o', 6),
]


def stream_names(streams):
    pairs = streams // 2
    return [kind + str(i + 1) for i in range(pairs) for kind in "ud"] + ["o"]


def backward_kernel(heads, streams, *refs):
    branches = BRANCHES - 1
    names = Names(refs)
    starts, gain, gains_two = names.take(3)
    sends = names.take(branches)
    far = names.take(branches + 6)
    parts = names.take(streams)
    far_totals, gains_out = names.take(5), names.one()
    near_totals, save_sem = names.take(5), names.one()
    up_total, down_total, out_total, in_total, grad_tokens = near_totals
    chunks = (streams - 1) // 2
    totals = []
    for chunk in range(chunks):
        lanes = pl.ds(chunk * (up_total.shape[-1] // chunks), up_total.shape[-1] // chunks)
        totals += [up_total.at[:, :, :, :, lanes], down_total.at[chunk]]
    totals.append(out_total)
    in_totals = [in_total.at[j] for j in range(3)]
    near = names.take(branches + 6)
    (own, own_g), units_in, (normed, in_proj, x_rows, grad_hidden) = near[:2], near[2:-4], near[-4:]
    far_sem = names.one()
    first = names.one()
    backs, gots, outs = names.take(branches), names.take(branches), names.take(branches)
    x, g, q_aug, gk, gv, result = names.take(6)
    total, grads, grads_t, normed_t, spread_rows, head_send, head_recv = names.take(7)
    gain_head, gain_one, gain_two, gain_rest = names.take(4)
    in_send, in_recv, in_local, out_send, out_recv, out_local = names.take(6)
    part_sem, head_sems, gain_sems = names.take(3)
    labels = stream_names(streams) + ["i0", "i1", "i2"]
    reductions = make_reductions(
        [ORDERS[label] for label in labels], list(totals) + list(in_totals), names.take(5 * streams + 15)
    )
    reductions = dict(zip(labels, reductions))
    for label in labels[: streams - 1]:
        reductions[label].begun = True

    shapes = [branch_shape(b, heads) for b in range(BRANCHES)]
    size, head_size = lax.axis_size("seq"), lax.axis_size("head")
    me, me_head = lax.axis_index("seq"), lax.axis_index("head")
    rest = size // 4
    tile = 512
    per_slot = x_rows.shape[0] // SLOTS
    width = x_rows.shape[1]

    fills = [
        pltpu.make_async_copy(parts[s], reductions[labels[s]].half, part_sem.at[s]) for s in range(streams - 1)
    ] + [pltpu.make_async_copy(parts[-1], totals[-1], part_sem.at[streams - 1])]
    loads = [pltpu.make_async_copy(far[i], near[i], far_sem.at[i]) for i in range(branches + 6)]
    for copy in fills + loads:
        copy.start()
    meet("seq", "head")

    def coming(branch):
        return group_copies(branch, sends[branch - 1], gots[branch - 1], in_send, in_recv, in_local)

    def leaving(branch):
        return group_copies(branch, outs[branch - 1], backs[branch - 1], out_send, out_recv, out_local)

    for branch in range(1, BRANCHES):
        for copy in coming(branch):
            copy.start()
    for copy in fills + loads:
        copy.wait()

    def split_branch(branch):
        stride, lanes, units, split = shapes[branch]
        queries = SEG0 // split
        for copy in coming(branch):
            copy.wait()
        load_unit(units_in[branch - 1], 0, lanes, x)
        load_unit(gots[branch - 1], 0, lanes, g)
        backward_unit(x, g, q_aug, gk, gv, result, me % split * queries, queries, min(tile, queries))
        store_unit(outs[branch - 1], 0, lanes, result)

    runs, at = [(0, 0, 0, heads // 2)], heads // 2
    split_at = None
    for branch in range(1, BRANCHES):
        if shapes[branch][3] == 1:
            runs.append((branch, at, 0, shapes[branch][2]))
            at += shapes[branch][2]
    split_at = at
    runs.append((0, at, heads // 2, heads - heads // 2))
    blocks = at + heads - heads // 2
    plan = {}
    for block, stream, step in EARLY:
        if stream in labels:
            plan.setdefault(block * blocks // 15, []).append((stream, step))

    @pl.loop(0, blocks)
    def _(block):
        for after, events in plan.items():

            @pl.when(block == after)
            def _(events=events):
                for stream, step in events:
                    reductions[stream].step(step)

        @pl.when(block == split_at)
        def _():
            for branch in range(1, BRANCHES):
                if shapes[branch][3] > 1:
                    split_branch(branch)
                    for copy in leaving(branch):
                        copy.start()

        for branch, low, unit, count in runs:

            @pl.when((block >= low) & (block < low + count))
            def _(branch=branch, low=low, unit=unit):
                if branch == 0:
                    x[...] = own[0, block - low + unit]
                    g[...] = own_g[0, block - low + unit]
                else:

                    @pl.when(block == low)
                    def _():
                        for copy in coming(branch):
                            copy.wait()

                    load_unit(units_in[branch - 1], block - low, shapes[branch][1], x)
                    load_unit(gots[branch - 1], block - low, shapes[branch][1], g)

        backward_unit(x, g, q_aug, gk, gv, result, 0, SEG0, tile)
        for branch, low, unit, count in runs:

            @pl.when((block >= low) & (block < low + count))
            def _(branch=branch, low=low, unit=unit, count=count):
                if branch == 0:
                    first[block - low + unit] = result[...]
                else:
                    store_unit(outs[branch - 1], block - low, shapes[branch][1], result)

                    @pl.when(block == low + count - 1)
                    def _():
                        for copy in leaving(branch):
                            copy.start()

    def saves(index):
        return pltpu.make_async_copy(near_totals[index], far_totals[index], save_sem.at[index])

    def save(index):
        saves(index).start()

    tasks = {}

    def task(work):
        tasks[work.__name__] = work

    @task
    def gather():
        for branch in range(1, BRANCHES):
            for copy in leaving(branch):
                copy.wait()

        @pl.loop(0, heads)
        def _(head):
            total[...] = first[head].astype(F32)
            for branch in range(1, BRANCHES):
                stride, lanes, per, split = shapes[branch]
                back, start = backs[branch - 1], reversed_bits(starts[branch, head], branch)
                if split == 1:
                    value = back[head // per, head % per].astype(F32)
                else:
                    value = back[head * split, 0].astype(F32)
                    for copy in range(1, split):
                        value = value + back[head * split + copy, 0].astype(F32)
                if lanes < 128:
                    value = unpacked(value, 3 * E, start % 2)
                    start = start // 2
                    lanes = 128
                for block in range(SEG0 // lanes):
                    span = slice(block * lanes, (block + 1) * lanes)
                    total[:, span] += jnp.where(start == block, value, 0.0)
            grads[0, head] = (total[0:E, :] * E ** (-0.5)).astype(BF)
            grads[1, head] = total[E : 2 * E, :].astype(BF)
            grads[2, head] = total[2 * E :, :].astype(BF)

        normed_t[...] = normed[...].reshape(SEG0, width).T

    def in_gradient(j):
        rows_in = in_totals[0].shape[3]
        chunk = width // 2
        grads_t[j] = grads[j].reshape(heads * E, SEG0).T
        for half in range(2):
            value = jnp.dot(
                normed_t[half * chunk : (half + 1) * chunk], grads_t[j], preferred_element_type=F32
            ).astype(BF)
            for part in range(chunk // rows_in):
                index = half * (chunk // rows_in) + part
                in_totals[j][index // (2 * rest), index // rest % 2, index % rest] = value[
                    part * rows_in : (part + 1) * rows_in
                ]

    for j in range(3):
        tasks[f"in{j}"] = partial(in_gradient, j)

    def head_swaps():
        swaps = []
        for step in range(1, head_size):
            device = (me_head + step) % head_size
            swaps.append(
                pltpu.make_async_remote_copy(
                    src_ref=head_send.at[device],
                    dst_ref=head_recv.at[step - 1],
                    send_sem=head_sems.at[0, step - 1],
                    recv_sem=head_sems.at[1, step - 1],
                    device_id={"head": device},
                    device_id_type=pl.DeviceIdType.MESH,
                )
            )
        return swaps

    @task
    def one():
        for half in range(2):
            rows = slice(half * SEG0 // 2, (half + 1) * SEG0 // 2)
            value = jnp.zeros((SEG0 // 2, width), F32)
            for j in range(3):
                value = value + lax.dot_general(
                    grads_t[j, rows], in_proj[j], (((1,), (1,)), ((), ())), preferred_element_type=F32
                )
            value = value.astype(BF)
            for slot in range(SLOTS // 2):
                for device in range(head_size):
                    begin = (slot * head_size + device) * per_slot
                    place = (half * SLOTS // 2 + slot) * per_slot
                    head_send[device, place : place + per_slot] = value[begin : begin + per_slot]
        for swap in head_swaps():
            swap.start()

    @task
    def norm():
        for swap in head_swaps():
            swap.wait()
        gain_head[me_head] = jnp.zeros(gains_out.shape, F32)
        gain_head[me_head, 2:4] = gains_two[...]

        @pl.loop(0, SLOTS)
        def _(slot):
            rows = pl.ds(pl.multiple_of(slot * per_slot, per_slot), per_slot)
            grad = head_send[me_head, rows].astype(F32)
            for step in range(1, head_size):
                grad = grad + head_recv[step - 1, rows].astype(F32)
            values = x_rows[rows]
            centred = values - jnp.mean(values, axis=-1, keepdims=True)
            scale = lax.rsqrt(jnp.mean(centred * centred, axis=-1, keepdims=True) + EPS)
            unit = centred * scale
            scaled = grad * gain[...][None]
            inner = jnp.mean(scaled * unit, axis=-1, keepdims=True)
            out = grad_hidden[rows] + scale * (
                scaled - jnp.mean(scaled, axis=-1, keepdims=True) - unit * inner
            )
            place = slot_place(slot)
            for column in range(width // 128):
                lanes = slice(column * 128, (column + 1) * 128)
                spread_rows[column, pl.ds(place, per_slot, stride=SLOTS), :] = out[:, lanes]
            gain_head[me_head, 0:1] += jnp.sum(grad * unit, axis=0, keepdims=True)
            gain_head[me_head, 1:2] += jnp.sum(grad, axis=0, keepdims=True)

        for column in range(width // 128):
            grad_tokens[:, column * 128 : (column + 1) * 128] = spread_rows[column]
        save(4)

    def gain_copy(source, target, axis, device, sem):
        return pltpu.make_async_remote_copy(
            src_ref=source,
            dst_ref=target,
            send_sem=gain_sems.at[0, sem],
            recv_sem=gain_sems.at[1, sem],
            device_id={axis: device},
            device_id_type=pl.DeviceIdType.MESH,
        )

    def gain_copies(stage):
        if stage == 0:
            mine = gain_head.at[me_head]
            return [
                gain_copy(mine, mine, "head", (me_head + step) % head_size, step - 1)
                for step in range(1, head_size)
            ]
        if stage == 1:
            return [gain_copy(gain_one.at[0], gain_one.at[1], "seq", me + 1 - 2 * (me % 2), head_size)]
        if stage == 2:
            device = me + 2 - 4 * (me // 2 % 2)
            return [gain_copy(gain_two.at[0], gain_two.at[1], "seq", device, head_size + 1)]
        spot = me // 4
        block = gain_rest.at[spot]
        return [
            gain_copy(block, block, "seq", (spot + step) % rest * 4 + me % 4, head_size + 1 + step)
            for step in range(1, rest)
        ]

    def summed(ref, count):
        value = ref[0]
        for index in range(1, count):
            value = value + ref[index]
        return value

    def gain_stage(stage):
        if stage > 0:
            for swap in gain_copies(stage - 1):
                swap.wait()
        if stage == 1:
            gain_one[0] = summed(gain_head, head_size)
        elif stage == 2:
            gain_two[0] = summed(gain_one, 2)
        elif stage == 3:
            gain_rest[me // 4] = summed(gain_two, 2)
        elif stage == 4:
            gains_out[...] = summed(gain_rest, rest)
            return
        for swap in gain_copies(stage):
            swap.start()

    for stage in range(5):
        tasks[f"gain{stage}"] = partial(gain_stage, stage)

    groups = [[], [], ["o"], ["i0", "i1", "i2"]]
    for chunk in range(chunks):
        groups[0].append(labels[2 * chunk])
        groups[1].append(labels[2 * chunk + 1])
    for item in TAIL:
        if isinstance(item, str):
            tasks[item]()
        elif item[0] in labels:
            reductions[item[0]].step(item[1])
            if item[1] == Reduction.STEPS - 1:
                for index, group in enumerate(groups):
                    if item[0] in group:
                        group.remove(item[0])
                        if not group:
                            save(index)
    for index in range(5):
        saves(index).wait()


def backward(heads, starts, own, own_g, units, sends, parts, normed, in_proj, x_rows, grad_hidden, gain, gains_two):
    size, head_size = lax.axis_size("seq"), lax.axis_size("head")
    rest = size // 4
    rows, width = x_rows.shape
    in_shape = (2, 2, rest, width // size, heads * E)
    scratch = []
    for part in parts:
        scratch += Reduction.scratch(size, *part.shape[-2:])
    for _ in range(3):
        scratch += Reduction.scratch(size, *in_shape[-2:])
    streams = len(parts)
    chunks = (streams - 1) // 2
    far = [own, own_g] + list(units) + [normed, in_proj, x_rows, grad_hidden]
    totals = [
        jax.ShapeDtypeStruct((2, 2, rest, width // size, chunks * parts[0].shape[-1]), BF),
        jax.ShapeDtypeStruct((chunks, 2, 2, rest) + parts[1].shape[-2:], BF),
        jax.ShapeDtypeStruct(parts[-1].shape, BF),
        jax.ShapeDtypeStruct((3,) + in_shape, BF),
        jax.ShapeDtypeStruct((rows, width), F32),
    ]
    results = pl.pallas_call(
        partial(backward_kernel, heads, streams),
        in_specs=[pl.BlockSpec(memory_space=pltpu.SMEM)]
        + vmem_specs(2)
        + [pl.BlockSpec(memory_space=pl.ANY)] * (len(sends) + len(far) + streams),
        out_specs=[pl.BlockSpec(memory_space=pl.ANY)] * len(totals) + vmem_specs(1),
        out_shape=totals + [jax.ShapeDtypeStruct((8, width), F32)],
        scratch_shapes=[pltpu.VMEM(value.shape, value.dtype) for value in totals]
        + [pltpu.SemaphoreType.DMA((len(totals),))]
        + [pltpu.VMEM(value.shape, value.dtype) for value in far]
        + [pltpu.SemaphoreType.DMA((len(far),)), pltpu.VMEM((heads, 3 * E, SEG0), BF)]
        + [pltpu.VMEM(shape.shape, BF) for shape in send_shapes(heads, 3 * E)]
        + [pltpu.VMEM(shape.shape, BF) for shape in send_shapes(heads, ROWS_OUT)]
        + [pltpu.VMEM(shape.shape, BF) for shape in send_shapes(heads, 3 * E)]
        + [
            pltpu.VMEM((ROWS_IN, SEG0), BF),
            pltpu.VMEM((ROWS_OUT, SEG0), BF),
            pltpu.VMEM((ROWS_OUT, SEG0), BF),
            pltpu.VMEM((SEG0, ROWS_OUT), F32),
            pltpu.VMEM((SEG0, ROWS_OUT), F32),
            pltpu.VMEM((3 * E, SEG0), BF),
            pltpu.VMEM((3 * E, SEG0), F32),
            pltpu.VMEM((3, heads, E, SEG0), BF),
            pltpu.VMEM((3, SEG0, heads * E), BF),
            pltpu.VMEM((width, SEG0), BF),
            pltpu.VMEM((width // 128, rows, 128), F32),
            pltpu.VMEM((head_size, rows, width), BF),
            pltpu.VMEM((head_size - 1, rows, width), BF),
            pltpu.VMEM((head_size, 8, width), F32),
            pltpu.VMEM((2, 8, width), F32),
            pltpu.VMEM((2, 8, width), F32),
            pltpu.VMEM((rest, 8, width), F32),
        ]
        + exchange_scratch()
        + [
            pltpu.SemaphoreType.DMA((streams,)),
            pltpu.SemaphoreType.DMA((2, head_size - 1)),
            pltpu.SemaphoreType.DMA((2, head_size + 1 + rest)),
        ]
        + scratch,
        compiler_params=pltpu.CompilerParams(
            vmem_limit_bytes=60 * 2**20, collective_id=1, has_side_effects=True
        ),
        cost_estimate=unit_cost(2 * heads, 5),
        name="backward",
    )(starts, gain, gains_two, *sends, *far, *parts)
    up_total, down_total, out_total, in_total = results[:4]
    sums = [
        in_total.reshape(3, width, heads * E),
        out_total.reshape(-1, width),
        up_total.reshape(width, -1),
        down_total.reshape(-1, width),
    ]
    return sums, results[4], results[5]


def finish_kernel(*refs):
    count = len(refs) // 2
    for source, target in zip(refs[:count], refs[count:]):
        target[...] = source[...].astype(target.dtype)


def finish(values, types):
    steps = 8
    specs = []
    for value in values:
        shape = list(value.shape)
        shape[-2] //= steps
        if value.ndim == 3:
            specs.append(pl.BlockSpec(tuple(shape), lambda i: (0, i, 0)))
        else:
            specs.append(pl.BlockSpec(tuple(shape), lambda i: (i, 0)))
    return pl.pallas_call(
        finish_kernel,
        grid=(steps,),
        in_specs=specs,
        out_specs=specs,
        out_shape=[jax.ShapeDtypeStruct(value.shape, kind) for value, kind in zip(values, types)],
        compiler_params=pltpu.CompilerParams(vmem_limit_bytes=61 * 2**20),
        name="finish",
    )(*values)


def middle_kernel(heads, *refs):
    branches = BRANCHES - 1
    names = Names(refs)
    starts, first = names.take(2)
    backs = names.take(branches)
    gain, shift = names.take(2)
    far = names.take(5)
    block_out, grad_hidden, gains_two, own_g = names.take(4)
    sends = names.take(branches)
    chunks = max(1, far[3].shape[1] // far[0].shape[1])
    halves = names.take(2 * chunks)
    out_total = names.one()
    merged, lse, mixed, turned, part, got, part_two, got_two = names.take(8)
    hidden_one, normed_own, normed, spread_rows, normed_t = names.take(5)
    down_sum, norm_sum, up_grad, down_grad, totals = names.take(5)
    head_sems, first_sems, far_sem = names.take(3)
    near = names.take(5)
    out_proj, x_rows, cot, up, down = near[2], near[0], near[1], near[3], near[4]
    loads = [pltpu.make_async_copy(far[i], near[i], far_sem.at[i]) for i in range(5)]
    for copy in loads:
        copy.start()

    head_size, me_head = lax.axis_size("head"), lax.axis_index("head")
    me = lax.axis_index("seq")
    rest = lax.axis_size("seq") // 4
    width = x_rows.shape[1]
    per_slot = x_rows.shape[0] // SLOTS
    tile = 256

    meet("seq", "head")

    @pl.loop(0, heads)
    def _(head):
        own = first[0, head].astype(F32)
        merged[head] = own[:E]
        lse[head] = own[E : E + 1] + own[E + 1 : E + 2] + own[E + 2 : E + 3]
        for branch in range(1, BRANCHES):
            stride, lanes, per, split = branch_shape(branch, heads)
            back, start = backs[branch - 1], reversed_bits(starts[branch, head], branch)
            share = max(1, 128 // lanes)
            for copy in range(split):
                if split == 1:
                    value = back[head // per, head % per].astype(F32)
                else:
                    value = back[head * split + copy, 0].astype(F32)
                if share > 1:
                    value = unpacked(value, ROWS_OUT, start % share)
                new_lse = value[E : E + 1] + value[E + 1 : E + 2] + value[E + 2 : E + 3]
                if share > 1:
                    ids = lax.broadcasted_iota(jnp.int32, new_lse.shape, 1)
                    new_lse = jnp.where(ids // lanes == start % share, new_lse, -FAR)
                span = lanes * share
                for block in range(SEG0 // span):
                    at = slice(block * span, (block + 1) * span)
                    new = jnp.where(start // share == block, new_lse, -FAR)
                    old = lse[head, :, at]
                    top = jnp.maximum(old, new)
                    both = top + jnp.log2(jnp.exp2(old - top) + jnp.exp2(new - top))
                    lse[head, :, at] = both
                    merged[head, :, at] = merged[head, :, at] * jnp.exp2(old - both) + value[:E] * jnp.exp2(
                        new - both
                    )
        mixed[head] = merged[head].astype(BF)

    def rows_of(ref):
        return ref[...].reshape(SEG0, width)

    turned[...] = mixed[...].reshape(heads * E, SEG0).T
    for copy in loads:
        copy.wait()
    for step in range(SEG0 // tile):
        at = slice(step * tile // (head_size * per_slot), (step + 1) * tile // (head_size * per_slot))
        value = jnp.dot(turned[step * tile : (step + 1) * tile], out_proj[...], preferred_element_type=F32)
        part[at] = value.astype(BF).reshape(-1, head_size, per_slot, width)
    for copy in head_copies(part, got, head_sems, 0, True):
        copy.start()
    for copy in head_copies(part, got, head_sems, 0, True):
        copy.wait()

    def rows_at(slot):
        return pl.ds(pl.multiple_of(slot * per_slot, per_slot), per_slot)

    @over_slots
    def _(slot):
        value = x_rows[rows_at(slot)] + part[slot, me_head].astype(F32)
        for step in range(1, head_size):
            value = value + got[step - 1, slot].astype(F32)
        hidden_one[rows_at(slot)] = value
        unit, scale = norm_of(value)
        low = (unit * gain[...][None] + shift[...][None]).astype(BF)
        normed_own[slot] = low
        normed[slot, me_head] = low

    for copy in head_copies(normed_own, normed, head_sems, 1, False):
        copy.start()
    for copy in head_copies(normed_own, normed, head_sems, 1, False):
        copy.wait()
    normed_t[...] = rows_of(normed).T

    chunk_width = up.shape[1] // chunks
    orders = {0: ORDERS["u1"], 1: ORDERS["d1"]}
    firsts = []
    for chunk in range(chunks):
        for kind in range(2):
            index = 2 * chunk + kind
            firsts.append(
                Reduction(
                    orders[kind], totals.at[index], halves[index], None, None,
                    first_sems.at[0, pl.ds(index, 1)], first_sems.at[1, pl.ds(index, 1)],
                )
            )
    down_sum[...] = jnp.zeros_like(down_sum)
    norm_sum[...] = jnp.zeros_like(norm_sum)
    slots = tile // (head_size * per_slot)
    contract_last = (((1,), (1,)), ((), ()))

    for chunk in range(chunks):
        units = slice(chunk * chunk_width, (chunk + 1) * chunk_width)
        up_grad[...] = jnp.zeros_like(up_grad)
        down_grad[...] = jnp.zeros_like(down_grad)

        @pl.loop(0, SEG0 // tile)
        def _(step):
            rows = pl.ds(pl.multiple_of(step * tile, tile), tile)
            low = normed[pl.ds(step * slots, slots)].reshape(tile, width)
            back = cot[pl.ds(step * slots, slots)].reshape(tile, width)
            pre = jnp.dot(low, up[:, units], preferred_element_type=F32)
            grad = lax.dot_general(back, down[units], contract_last, preferred_element_type=F32)
            share = 0.5 + 0.5 * lax.erf(pre * math.sqrt(0.5))
            density = jnp.exp2(pre * pre * (-0.5 * LOG2E)) * (1.0 / math.sqrt(2.0 * math.pi))
            hidden = (pre * share).astype(BF)
            grad = (grad * (share + pre * density)).astype(BF)
            down_sum[rows] += jnp.dot(hidden, down[units], preferred_element_type=F32)
            norm_sum[rows] += lax.dot_general(grad, up[:, units], contract_last, preferred_element_type=F32)
            up_grad[...] += jnp.dot(normed_t[:, rows], grad, preferred_element_type=F32)
            down_grad[...] += jnp.dot(hidden.T, back, preferred_element_type=F32)

        pieces = totals.shape[3] * 4
        size = totals.shape[4]
        for piece in range(pieces):
            spot = (piece // (2 * rest), piece // rest % 2, piece % rest)
            span = slice(piece * size, (piece + 1) * size)
            totals[(2 * chunk,) + spot] = up_grad[span].astype(BF)
            totals[(2 * chunk + 1,) + spot] = down_grad[span].astype(BF)
        firsts[2 * chunk].step(0)
        firsts[2 * chunk + 1].step(0)

    for ref, value in ((part, down_sum), (part_two, norm_sum)):

        @pl.loop(0, SLOTS)
        def _(slot):
            for device in range(head_size):
                begin = pl.multiple_of((slot * head_size + device) * per_slot, per_slot)
                ref[slot, device] = value[pl.ds(begin, per_slot)].astype(BF)

    for copy in head_copies(part_two, got_two, head_sems, 2, True) + head_copies(part, got, head_sems, 3, True):
        copy.start()
    for copy in head_copies(part_two, got_two, head_sems, 2, True):
        copy.wait()
    gains_two[...] = jnp.zeros_like(gains_two)

    @over_slots
    def _(slot):
        grad = part_two[slot, me_head].astype(F32)
        for step in range(1, head_size):
            grad = grad + got_two[step - 1, slot].astype(F32)
        unit, scale = norm_of(hidden_one[rows_at(slot)])
        scaled = grad * gain[...][None]
        inner = jnp.mean(scaled * unit, axis=-1, keepdims=True)
        out = cot[slot, me_head].astype(F32) + scale * (
            scaled - jnp.mean(scaled, axis=-1, keepdims=True) - unit * inner
        )
        grad_hidden[rows_at(slot)] = out
        normed_own[slot] = out.astype(BF)
        normed[slot, me_head] = out.astype(BF)
        gains_two[0:1] += jnp.sum(grad * unit, axis=0, keepdims=True)
        gains_two[1:2] += jnp.sum(grad, axis=0, keepdims=True)

    for copy in head_copies(normed_own, normed, head_sems, 4, False):
        copy.start()
    for copy in head_copies(part, got, head_sems, 3, True):
        copy.wait()

    @pl.loop(0, SLOTS)
    def _(slot):
        value = hidden_one[rows_at(slot)] + part[slot, me_head].astype(F32)
        for step in range(1, head_size):
            value = value + got[step - 1, slot].astype(F32)
        place = slot_place(slot)
        for column in range(width // 128):
            lanes = slice(column * 128, (column + 1) * 128)
            spread_rows[column, pl.ds(place, per_slot, stride=SLOTS), :] = value[:, lanes]

    for column in range(width // 128):
        block_out[:, column * 128 : (column + 1) * 128] = spread_rows[column].astype(BF)
    for copy in head_copies(normed_own, normed, head_sems, 4, False):
        copy.wait()

    value = jnp.dot(mixed[...].reshape(heads * E, SEG0), rows_of(normed), preferred_element_type=F32)
    size = out_total.shape[3]
    for piece in range(4 * rest):
        spot = (piece // (2 * rest), piece // rest % 2, piece % rest)
        out_total[spot] = value[piece * size : (piece + 1) * size].astype(BF)

    normed_t[...] = rows_of(normed).T
    value = jnp.dot(out_proj[...], normed_t[...], preferred_element_type=F32)
    own_g[0, :, :E, :] = value.astype(BF).reshape(heads, E, SEG0)

    @pl.loop(0, heads)
    def _(head):
        low = own_g[0, head, :E, :]
        dots = jnp.sum(low.astype(F32) * merged[head], axis=0, keepdims=True)
        d = pieces_of(-dots)
        m = pieces_of(-lse[head])
        placed = {0: d[0], 1: d[1], 2: d[2], 12: m[0], 13: m[1], 14: m[2]}
        own_g[0, head, E:, :] = row_block(placed, SEG0).astype(BF)
        own = jnp.concatenate([low.astype(F32), row_block(placed, SEG0)], axis=0)
        spread_blocks(heads, head, starts, own, sends)

    for reduction in firsts:
        reduction.finish_first()


def middle(heads, starts, first, backs, x_rows, cot, out_proj, up, down, gain, shift):
    size, head_size = lax.axis_size("seq"), lax.axis_size("head")
    rest = size // 4
    rows, width = x_rows.shape
    per_slot = rows // SLOTS
    chunks = max(1, up.shape[1] // width)
    shard = (SLOTS, head_size, per_slot, width)
    own = (SLOTS, per_slot, width)
    got = (head_size - 1,) + own
    sends = send_shapes(heads, ROWS_OUT)
    piece = (2, rest, width // size, up.shape[1] // chunks)
    out_piece = (2, 2, rest, heads * E // size, width)
    far = [x_rows, cot, out_proj, up, down]
    results = pl.pallas_call(
        partial(middle_kernel, heads),
        in_specs=[pl.BlockSpec(memory_space=pltpu.SMEM)]
        + vmem_specs(1 + len(backs) + 2)
        + [pl.BlockSpec(memory_space=pl.ANY)] * 5,
        out_specs=vmem_specs(4 + len(sends) + 2 * chunks + 1),
        out_shape=[
            jax.ShapeDtypeStruct((rows, width), BF),
            jax.ShapeDtypeStruct((rows, width), F32),
            jax.ShapeDtypeStruct((2, width), F32),
            jax.ShapeDtypeStruct((1, heads, ROWS_OUT, SEG0), BF),
        ]
        + sends
        + [jax.ShapeDtypeStruct(piece, BF)] * (2 * chunks)
        + [jax.ShapeDtypeStruct(out_piece, BF)],
        scratch_shapes=[
            pltpu.VMEM((heads, E, SEG0), F32),
            pltpu.VMEM((heads, 1, SEG0), F32),
            pltpu.VMEM((heads, E, SEG0), BF),
            pltpu.VMEM((SEG0, heads * E), BF),
            pltpu.VMEM(shard, BF),
            pltpu.VMEM(got, BF),
            pltpu.VMEM(shard, BF),
            pltpu.VMEM(got, BF),
            pltpu.VMEM((rows, width), F32),
            pltpu.VMEM(own, BF),
            pltpu.VMEM(shard, BF),
            pltpu.VMEM((width // 128, rows, 128), F32),
            pltpu.VMEM((width, SEG0), BF),
            pltpu.VMEM((SEG0, width), F32),
            pltpu.VMEM((SEG0, width), F32),
            pltpu.VMEM((width, up.shape[1] // chunks), F32),
            pltpu.VMEM((up.shape[1] // chunks, width), F32),
            pltpu.VMEM((2 * chunks, 2) + piece, BF),
            pltpu.SemaphoreType.DMA((2, 5, head_size - 1)),
            pltpu.SemaphoreType.DMA((2, 2 * chunks)),
            pltpu.SemaphoreType.DMA((5,)),
        ]
        + [pltpu.VMEM(value.shape, value.dtype) for value in far],
        compiler_params=pltpu.CompilerParams(
            vmem_limit_bytes=60 * 2**20, collective_id=2, has_side_effects=True
        ),
        cost_estimate=pl.CostEstimate(
            flops=14 * SEG0 * width * up.shape[1], transcendentals=0, bytes_accessed=40 * 2**20
        ),
        name="middle",
    )(starts, first, *backs, gain, shift, *far)
    block_out, grad_hidden, gains_two, own_g = results[:4]
    return block_out, grad_hidden, gains_two, own_g, results[4 : 4 + len(sends)], results[4 + len(sends) :]


def local(
    tokens,
    documents,
    offsets,
    in_proj,
    out_proj,
    up_proj,
    down_proj,
    first_gain,
    first_shift,
    second_gain,
    second_shift,
    cotangent,
):
    head_count = lax.axis_size("head")
    seq_id = lax.axis_index("seq")
    row_count = tokens.shape[0]
    seq_len = row_count * head_count
    heads = offsets.shape[1]
    per_slot = row_count // SLOTS

    my_docs = lax.dynamic_slice_in_dim(documents, seq_id * seq_len, seq_len)
    my_docs = my_docs.reshape(head_count, per_slot, 2, 2, 2, 2).transpose(5, 4, 3, 2, 0, 1).reshape(seq_len)
    bit_ids = jnp.arange(BIT_ROWS, dtype=jnp.int32)[:, None]
    doc_bit = my_docs[None, :] // 2 ** (bit_ids % DOC_BITS) % 2
    bits = jnp.where(bit_ids < DOC_BITS, doc_bit, jnp.where(bit_ids < 2 * DOC_BITS, 1 - doc_bit, 0))
    bits = bits.astype(BF)

    (x_rows, normed, cot_all, own), units, first_out, outs = forward(
        heads, offsets, tokens, cotangent, bits, first_gain, first_shift, in_proj
    )
    block_out, grad_hidden, gains_two, own_g, sends_g, parts = middle(
        heads, offsets, first_out, outs, x_rows, cot_all, out_proj, up_proj, down_proj, second_gain, second_shift
    )
    sums, grad_tokens, gains = backward(
        heads, offsets, own, own_g, units, sends_g, parts,
        normed, in_proj, x_rows, grad_hidden, first_gain, gains_two,
    )
    results = finish([block_out, grad_tokens] + sums, [BF] + [F32] * 5)
    return (*results, gains[0], gains[1], gains[2], gains[3])


def solution(mesh):
    placed = (
        P(("seq", "head"), None),
        P(),
        P(None, "head"),
        P(None, None, "head"),
        P("head", None),
        P(None, "head"),
        P("head", None),
        P(),
        P(),
        P(),
        P(),
        P(("seq", "head"), None),
    )
    return jax.shard_map(
        local,
        mesh=mesh,
        in_specs=placed,
        out_specs=(
            P(("seq", "head"), None),
            P(("seq", "head"), None),
            P(None, None, "head"),
            P("head", None),
            P(None, "head"),
            P("head", None),
            P(),
            P(),
            P(),
            P(),
        ),
        check_vma=False,
    )
```

```python
import math
from functools import partial

import jax
import jax.numpy as jnp
from jax import lax
from jax.experimental import pallas as pl
from jax.experimental.pallas import tpu as pltpu
from jax.sharding import PartitionSpec as P

E = 48
BRANCHES = 5
SEG0 = 1024
SLOTS = 16
BIT_ROWS = 16
DOC_BITS = 6
ROWS_IN = 3 * E + BIT_ROWS
ROWS_OUT = E + BIT_ROWS
EPS = 1e-05
FAR = 1e30
LOG2E = math.log2(math.e)
LN2 = math.log(2.0)
BF = jnp.bfloat16
F32 = jnp.float32
VMEM_LIMIT = 48 * 2**20


def reversed_bits(value, count):
    out = value % 2
    for bit in range(1, count):
        out = out * 2 + value // 2**bit % 2
    return out


def branch_shape(branch, heads):
    stride = 2**branch
    return (stride, SEG0 // stride, max(1, heads // stride), max(1, stride // heads))


def pieces_of(value):
    high = value.astype(BF).astype(F32)
    rest = value - high
    middle = rest.astype(BF).astype(F32)
    return high, middle, (rest - middle).astype(BF).astype(F32)


def row_block(placed, columns):
    ids = lax.broadcasted_iota(jnp.int32, (BIT_ROWS, columns), 0)
    block = jnp.zeros((BIT_ROWS, columns), F32)
    for row, value in placed.items():
        block = jnp.where(ids == row, value, block)
    return block


def turned_half(block):
    return jnp.concatenate([block[:, 64:], block[:, :64]], axis=1)


def low_half():
    return lax.broadcasted_iota(jnp.int32, (1, 128), 1) < 64


def packed_rows(rows, count):
    return rows if count >= 128 else (rows // 2 + 15) // 16 * 16


def packed(block, half):
    rows = packed_rows(block.shape[0], 64)
    upper, lower = block[:rows], block[block.shape[0] - rows :]
    if isinstance(half, int):
        return jnp.where(low_half(), turned_half(upper) if half else upper, lower if half else turned_half(lower))
    upper = jnp.where(half == 0, upper, turned_half(upper))
    lower = jnp.where(half == 0, turned_half(lower), lower)
    return jnp.where(low_half(), upper, lower)


def unpacked(value, rows, half):
    size = value.shape[0]
    other = turned_half(value)
    upper = jnp.where(half == 0, value, other)
    lower = jnp.where(half == 0, other, value)
    both = jnp.concatenate([upper, lower[2 * size - rows :]], axis=0)
    return jnp.where(low_half() == (half == 0), both, 0.0)


def send_shapes(heads, rows):
    outs = []
    for branch in range(1, BRANCHES):
        stride, count, per, split = branch_shape(branch, heads)
        outs.append(jax.ShapeDtypeStruct((stride, per, packed_rows(rows, count), max(count, 128)), BF))
    return outs


def spread_blocks(heads, head, starts, value, sends, branches=range(1, BRANCHES)):
    for branch in branches:
        stride, lanes, per, split = branch_shape(branch, heads)
        send, start = sends[branch - 1], reversed_bits(starts[branch, head], branch)
        share = max(1, 128 // lanes)
        span = lanes * share
        block = value[:, :span]
        for part in range(1, SEG0 // span):
            block = jnp.where(start // share == part, value[:, part * span : (part + 1) * span], block)
        if share > 1:
            block = packed(block, start % share)
        block = block.astype(BF)
        if split == 1:
            send[head // per, head % per] = block
        else:
            for copy in range(split):
                send[head * split + copy, 0] = block


def norm_of(values):
    centred = values - jnp.mean(values, axis=-1, keepdims=True)
    scale = lax.rsqrt(jnp.mean(centred * centred, axis=-1, keepdims=True) + EPS)
    return centred * scale, scale


def slot_place(slot):
    return slot % 2 * 8 + slot // 2 % 2 * 4 + slot // 4 % 2 * 2 + slot // 8


def over_slots(body, unroll=4):
    @pl.loop(0, SLOTS // unroll)
    def _(step):
        for part in range(unroll):
            body(step * unroll + part)


def head_copies(source, target, sems, index, scatter):
    size, me = lax.axis_size("head"), lax.axis_index("head")
    copies = []
    for step in range(1, size):
        device = (me + step) % size
        copies.append(
            pltpu.make_async_remote_copy(
                src_ref=source.at[:, device] if scatter else source,
                dst_ref=target.at[step - 1] if scatter else target.at[:, me],
                send_sem=sems.at[0, index, step - 1],
                recv_sem=sems.at[1, index, step - 1],
                device_id={"head": device},
                device_id_type=pl.DeviceIdType.MESH,
            )
        )
    return copies


def load_unit(ref, unit, count, x):
    width = ref.shape[-1]
    if count >= 128:
        for block in range(ref.shape[0]):
            x[:, block * width : (block + 1) * width] = ref[block, unit]
        return
    rows, size = x.shape[0], ref.shape[2]
    for block in range(ref.shape[0] // 2):
        lanes = slice(block * 128, (block + 1) * 128)
        left = ref[2 * block, unit].astype(F32)
        right = ref[2 * block + 1, unit].astype(F32)
        x[:size, lanes] = jnp.where(low_half(), left, turned_half(right)).astype(BF)
        x[rows - size :, lanes] = jnp.where(low_half(), turned_half(left), right).astype(BF)


def store_unit(ref, unit, count, result):
    width = ref.shape[-1]
    for block in range(SEG0 // width):
        value = result[:, block * width : (block + 1) * width]
        if count >= 128:
            ref[block, unit] = value
        else:
            value = value.astype(F32)
            ref[2 * block, unit] = packed(value, 0).astype(BF)
            ref[2 * block + 1, unit] = packed(value, 1).astype(BF)


def forward_unit(x, q_aug, result, base, queries):
    if isinstance(base, int):
        lanes = slice(base, base + queries)
    else:
        lanes = pl.ds(pl.multiple_of(base, 128), queries)
    q_aug[0:E, :queries] = x[0:E, lanes]
    q_aug[E:, :queries] = (x[3 * E :, lanes].astype(F32) * -FAR).astype(BF)
    bits = x[3 * E :, :].astype(F32)
    k_rows = jnp.concatenate([x[E : 2 * E, :], (1.0 - bits).astype(BF)], axis=0).T
    v_aug = jnp.concatenate([x[2 * E : 3 * E, :], jnp.ones(bits.shape, BF)], axis=0)
    if queries < SEG0:
        result[0:E, :] = jnp.zeros((E, SEG0), BF)
        result[E:, :] = row_block({0: -FAR}, SEG0).astype(BF)
    s = jnp.dot(k_rows, q_aug[:, :queries], preferred_element_type=F32)
    top = jnp.max(s, axis=0, keepdims=True)
    p = jnp.exp2(s - top).astype(BF)
    o = jnp.dot(v_aug, p, preferred_element_type=F32)
    total = o[E : E + 1]
    high, middle_part, low = pieces_of(top + jnp.log2(total))
    block = row_block({0: high, 1: middle_part, 2: low}, queries)
    result[:, lanes] = jnp.concatenate([o[:E] * (1.0 / total), block], axis=0).astype(BF)


class Names:
    def __init__(self, refs):
        self.refs = list(refs)

    def take(self, count):
        taken, self.refs = self.refs[:count], self.refs[count:]
        return taken

    def one(self):
        return self.take(1)[0]


def group_place(branch):
    stride = 2**branch
    me = lax.axis_index("seq")
    return me // stride * stride, me % stride


def meet(*axes):
    barrier = pltpu.get_barrier_semaphore()
    count = 0
    for axis in axes:
        size = lax.axis_size(axis)
        me = lax.axis_index(axis)

        @pl.loop(1, size)
        def _(step):
            pl.semaphore_signal(
                barrier, inc=1, device_id={axis: (me + step) % size}, device_id_type=pl.DeviceIdType.MESH
            )

        count += size - 1
    pl.semaphore_wait(barrier, count)


class Reduction:
    STEPS = 7

    def __init__(self, order, total, half, quarter, others, send, recv, begun=False):
        self.total, self.begun = total, begun
        self.half, self.quarter, self.others = half, quarter, others
        self.send, self.recv = send, recv
        me = lax.axis_index("seq")
        self.rest = lax.axis_size("seq") // 4
        self.me = me
        bits = (me % 2, me // 2 % 2)
        self.bits = [bits[bit] for bit in order]
        self.partners = [me + (1 - 2 * bits[bit]) * 2**bit for bit in order]
        self.place = me // 4

    def copy(self, source, target, device, sem):
        return pltpu.make_async_remote_copy(
            src_ref=source,
            dst_ref=target,
            send_sem=self.send.at[sem],
            recv_sem=self.recv.at[sem],
            device_id={"seq": device},
            device_id_type=pl.DeviceIdType.MESH,
        )

    def copies(self, number):
        one, two = self.bits
        rest = self.rest
        others = []
        for step in range(1, rest):
            place = (self.place + step) % rest
            others.append((step, place, place * 4 + self.me % 4))
        if number == 0:
            return [self.copy(self.total.at[1 - one], self.half, self.partners[0], 0)]
        if number == 1:
            return [self.copy(self.half.at[1 - two], self.quarter, self.partners[1], 1)]
        if number == 2:
            return [
                self.copy(self.quarter.at[place], self.others.at[step - 1], device, 1 + step)
                for step, place, device in others
            ]
        if number == 3:
            block = self.total.at[one, two, self.place]
            return [self.copy(block, block, device, rest + step) for step, place, device in others]
        if number == 4:
            block = self.total.at[one, two]
            return [self.copy(block, block, self.partners[1], 2 * rest)]
        if number == 5:
            block = self.total.at[one]
            return [self.copy(block, block, self.partners[0], 2 * rest + 1)]
        return []

    def finish_first(self):
        one, rest = self.bits[0], self.rest
        for copy in self.copies(0):
            copy.wait()

        @pl.loop(0, 2 * rest)
        def _(i):
            j, z = i // rest, i % rest
            mine = self.total[one, j, z].astype(F32)
            self.half[j, z] = (mine + self.half[j, z].astype(F32)).astype(BF)

    def step(self, number):
        one, two = self.bits
        rest = self.rest
        if number == 0 and self.begun:
            return
        if number == 1:
            if not self.begun:
                self.finish_first()
        elif number > 0:
            for copy in self.copies(number - 1):
                copy.wait()
        if number == 2:

            @pl.loop(0, rest)
            def _(z):
                mine = self.half[two, z].astype(F32)
                self.quarter[z] = (mine + self.quarter[z].astype(F32)).astype(BF)

        elif number == 3:
            mine = self.quarter[self.place].astype(F32)
            for step in range(1, rest):
                mine = mine + self.others[step - 1].astype(F32)
            self.total[one, two, self.place] = mine.astype(BF)
        for copy in self.copies(number):
            copy.start()

    @staticmethod
    def scratch(size, rows, columns):
        rest = size // 4
        count = 2 * rest + 2
        return [
            pltpu.VMEM((2, rest, rows, columns), BF),
            pltpu.VMEM((rest, rows, columns), BF),
            pltpu.VMEM((rest - 1, rows, columns), BF),
            pltpu.SemaphoreType.DMA((count,)),
            pltpu.SemaphoreType.DMA((count,)),
        ]


def reduction_parts(value, size):
    rows, columns = value.shape
    return value.reshape(2, 2, size // 4, rows // size, columns)


def reduction_whole(value):
    return value.reshape(-1, value.shape[-1])


def make_reductions(orders, totals, scratch):
    out = []
    for order, total in zip(orders, totals):
        out.append(Reduction(order, total, *scratch[:5]))
        scratch = scratch[5:]
    return out


def group_copies(branch, source, target, send_sems, recv_sems, local_sem):
    stride = 2**branch
    base, place = group_place(branch)
    first = stride - branch - 2
    copies = [
        pltpu.make_async_copy(source.at[place], target.at[place], local_sem.at[branch - 1])
    ]
    for step in range(1, stride):
        member = (place + step) % stride
        copies.append(
            pltpu.make_async_remote_copy(
                src_ref=source.at[member],
                dst_ref=target.at[place],
                send_sem=send_sems.at[first + step],
                recv_sem=recv_sems.at[first + step],
                device_id={"seq": base + member},
                device_id_type=pl.DeviceIdType.MESH,
            )
        )
    return copies


def forward_kernel(heads, starts, tokens, cotangent, bits, gain, shift, in_proj, *refs):
    count = BRANCHES - 1
    names = Names(refs)
    far = names.take(4 + count)
    first, backs = names.one(), names.take(count)
    near = names.take(4 + count)
    (x_rows, normed, cot, own), gots = near[:4], near[4:]
    outs, sends = names.take(count), names.take(count)
    x, q_aug, result, in_send, in_recv, in_local, out_send, out_recv, out_local = names.take(9)
    spread_rows, normed_own, cot_own, normed_t, head_sems, far_sem = names.take(6)
    saves = [pltpu.make_async_copy(near[i], far[i], far_sem.at[i]) for i in range(4 + count)]
    me_head = lax.axis_index("head")
    rows, width = tokens.shape
    per_slot = rows // SLOTS

    def fill(source):
        for column in range(width // 128):
            spread_rows[column] = source[:, column * 128 : (column + 1) * 128].astype(F32)

    def picked(slot):
        at = pl.ds(slot_place(slot), per_slot, stride=SLOTS)
        return jnp.concatenate([spread_rows[column, at, :] for column in range(width // 128)], axis=1)

    fill(tokens)

    @over_slots
    def _(slot):
        value = picked(slot)
        x_rows[pl.ds(pl.multiple_of(slot * per_slot, per_slot), per_slot)] = value
        low = (norm_of(value)[0] * gain[...][None] + shift[...][None]).astype(BF)
        normed_own[slot] = low
        normed[slot, me_head] = low

    meet("seq", "head")
    for copy in head_copies(normed_own, normed, head_sems, 0, False):
        copy.start()
    saves[0].start()
    fill(cotangent)

    @over_slots
    def _(slot):
        low = picked(slot).astype(BF)
        cot_own[slot] = low
        cot[slot, me_head] = low

    for copy in head_copies(cot_own, cot, head_sems, 1, False):
        copy.start()
    own[0, :, 3 * E :, :] = jnp.broadcast_to(bits[...][None], (heads,) + bits.shape)
    turned = [in_proj[j].T for j in range(3)]
    for copy in head_copies(normed_own, normed, head_sems, 0, False):
        copy.wait()
    normed_t[...] = normed[...].reshape(SEG0, width).T
    for j in range(3):
        value = jnp.dot(turned[j], normed_t[...], preferred_element_type=F32)
        if j == 0:
            value = value * (E ** (-0.5) * LOG2E)
        own[0, :, j * E : (j + 1) * E, :] = value.astype(BF).reshape(heads, E, SEG0)
    saves[1].start()
    saves[3].start()

    coming = {}
    for branch in range(1, BRANCHES):

        @pl.loop(0, heads)
        def _(head):
            spread_blocks(heads, head, starts, own[0, head].astype(F32), sends, [branch])

        coming[branch] = group_copies(branch, sends[branch - 1], gots[branch - 1], in_send, in_recv, in_local)
        for copy in coming[branch]:
            copy.start()

    @pl.loop(0, heads)
    def _(head):
        x[...] = own[0, head]
        forward_unit(x, q_aug, result, 0, SEG0)
        first[0, head] = result[...]

    for copy in head_copies(cot_own, cot, head_sems, 1, False):
        copy.wait()
    saves[2].start()
    leaving = []
    for branch in range(1, BRANCHES):
        stride, lanes, units, split = branch_shape(branch, heads)
        got, out = gots[branch - 1], outs[branch - 1]
        for copy in coming[branch]:
            copy.wait()
        saves[3 + branch].start()
        queries = SEG0 // split
        base = 0 if split == 1 else lax.axis_index("seq") % split * queries

        @pl.loop(0, units)
        def _(unit):
            load_unit(got, unit, lanes, x)
            forward_unit(x, q_aug, result, base, queries)
            store_unit(out, unit, lanes, result)

        copies = group_copies(branch, out, backs[branch - 1], out_send, out_recv, out_local)
        for copy in copies:
            copy.start()
        leaving += copies
    for copy in leaving + saves:
        copy.wait()


def exchange_scratch():
    copies = 2**BRANCHES - 2 - BRANCHES + 1
    one = [
        pltpu.SemaphoreType.DMA((copies,)),
        pltpu.SemaphoreType.DMA((copies,)),
        pltpu.SemaphoreType.DMA((BRANCHES - 1,)),
    ]
    return one + one


def unit_cost(units, dots):
    return pl.CostEstimate(
        flops=dots * 2 * units * SEG0 * SEG0 * 256,
        transcendentals=units * SEG0 * SEG0,
        bytes_accessed=units * SEG0 * 1000,
    )


def vmem_specs(count):
    return [pl.BlockSpec(memory_space=pltpu.VMEM)] * count


def forward(heads, starts, tokens, cotangent, bits, gain, shift, in_proj):
    head_size = lax.axis_size("head")
    rows, width = tokens.shape
    shard = jax.ShapeDtypeStruct((SLOTS, head_size, rows // SLOTS, width), BF)
    own_rows = pltpu.VMEM((SLOTS, rows // SLOTS, width), BF)
    backs = send_shapes(heads, ROWS_OUT)
    gots = send_shapes(heads, ROWS_IN)
    own = jax.ShapeDtypeStruct((1, heads, ROWS_IN, SEG0), BF)
    far = [jax.ShapeDtypeStruct((rows, width), F32), shard, shard, own] + gots
    results = pl.pallas_call(
        partial(forward_kernel, heads),
        in_specs=[pl.BlockSpec(memory_space=pltpu.SMEM)] + vmem_specs(6),
        out_specs=[pl.BlockSpec(memory_space=pl.ANY)] * len(far) + vmem_specs(1 + len(backs)),
        out_shape=far + [jax.ShapeDtypeStruct((1, heads, ROWS_OUT, SEG0), BF)] + backs,
        scratch_shapes=[pltpu.VMEM(shape.shape, shape.dtype) for shape in far + backs + gots]
        + [
            pltpu.VMEM((ROWS_IN, SEG0), BF),
            pltpu.VMEM((ROWS_OUT, SEG0), BF),
            pltpu.VMEM((ROWS_OUT, SEG0), BF),
        ]
        + exchange_scratch()
        + [
            pltpu.VMEM((width // 128, rows, 128), F32),
            own_rows,
            own_rows,
            pltpu.VMEM((width, SEG0), BF),
            pltpu.SemaphoreType.DMA((2, 2, head_size - 1)),
            pltpu.SemaphoreType.DMA((len(far),)),
        ],
        compiler_params=pltpu.CompilerParams(
            vmem_limit_bytes=60 * 2**20, collective_id=0, has_side_effects=True
        ),
        cost_estimate=unit_cost(2 * heads, 2),
        name="forward",
    )(starts, tokens, cotangent, bits, gain, shift, in_proj)
    return results[:4], results[4 : len(far)], results[len(far)], results[len(far) + 1 :]


def backward_unit(x, g, q_aug, gk, gv, result, base, queries, tile):
    if isinstance(base, int):
        lanes = slice(base, base + queries)
    else:
        lanes = pl.ds(pl.multiple_of(base, 128), queries)
    extra = g[E:, lanes].astype(F32)
    ids = lax.broadcasted_iota(jnp.int32, extra.shape, 0)
    q = x[0:E, lanes]
    q_aug[0:E, :queries] = q
    q_aug[E:, :queries] = jnp.where(ids >= 12, extra, x[3 * E :, lanes].astype(F32) * -FAR).astype(BF)
    bits = x[3 * E :, :].astype(F32)
    k_aug = jnp.concatenate([x[E : 2 * E, :], (1.0 - bits).astype(BF)], axis=0)
    k_rows = k_aug.T
    v_ids = lax.broadcasted_iota(jnp.int32, bits.shape, 0)
    v_bits = jnp.where(v_ids < 3, 1.0, 0.0).astype(BF)
    v_rows = jnp.concatenate([x[2 * E : 3 * E, :], v_bits], axis=0).T
    q_rows = jnp.concatenate([q, jnp.zeros((BIT_ROWS, queries), BF)], axis=0).T
    g_all = g[:, lanes]
    g_rows = g_all.T
    if queries < SEG0:
        result[0:E, :] = jnp.zeros((E, SEG0), BF)
    for step in range(queries // tile):
        column = step * tile
        span = slice(column, column + tile)
        p = jnp.exp2(jnp.dot(k_rows, q_aug[:, span], preferred_element_type=F32))
        gs = p * jnp.dot(v_rows, g_all[:, span], preferred_element_type=F32)
        p, gs = p.astype(BF), gs.astype(BF)
        target = span if isinstance(base, int) else pl.ds(pl.multiple_of(base + column, 128), tile)
        result[0:E, target] = jnp.dot(k_aug, gs, preferred_element_type=F32)[:E].astype(BF)
        new_k = jnp.dot(gs, q_rows[span], preferred_element_type=F32)
        new_v = jnp.dot(p, g_rows[span], preferred_element_type=F32)
        if step == 0:
            gk[...] = new_k
            gv[...] = new_v
        else:
            gk[...] += new_k
            gv[...] += new_v
    result[E : 2 * E, :] = (gk[...].T[:E] * LN2).astype(BF)
    result[2 * E :, :] = gv[...].T[:E].astype(BF)


ORDERS = {
    'u1': (0, 1), 'u2': (0, 1), 'd1': (1, 0), 'd2': (1, 0), 'o': (0, 1), 'i0': (1, 0), 'i1': (1, 0), 'i2': (0,
    1),
}
EARLY = [
    (0, 'd1', 0), (0, 'u1', 0), (0, 'd1', 1), (0, 'u2', 0), (0, 'u1', 1), (2, 'o', 0), (4, 'u2', 1), (5, 'u1',
    2), (7, 'd1', 2), (9, 'u1', 3), (10, 'd2', 0), (12, 'd2', 1), (12, 'o', 1), (12, 'd1', 3), (13, 'u2', 2),
    (14, 'u1', 4),
]
TAIL = [
    'gather', ('d1', 4), 'in1', ('i1', 0), ('d2', 2), 'in2', ('u2', 3), ('i2', 0), 'in0', ('i0', 0), ('d2',
    3), ('i1', 1), ('i2', 1), ('u1', 5), ('u2', 4), ('d2', 4), ('d1', 5), ('o', 2), ('i2', 2), ('i0', 1),
    ('i1', 2), ('i2', 3), 'one', ('d2', 5), ('o', 3), ('i1', 3), ('u1', 6), ('u2', 5), 'norm', ('i2', 4),
    'gain0', ('i0', 2), ('i1', 4), ('i0', 3), 'gain1', ('o', 4), ('i0', 4), ('i2', 5), 'gain2', ('i1', 5),
    ('o', 5), ('i0', 5), 'gain3', ('i0', 6), ('d2', 6), ('u2', 6), 'gain4', ('d1', 6), ('i1', 6), ('i2', 6),
    ('o', 6),
]


def stream_names(streams):
    pairs = streams // 2
    return [kind + str(i + 1) for i in range(pairs) for kind in "ud"] + ["o"]


def backward_kernel(heads, streams, *refs):
    branches = BRANCHES - 1
    names = Names(refs)
    starts, gain, gains_two = names.take(3)
    sends = names.take(branches)
    far = names.take(branches + 6)
    parts = names.take(streams)
    far_totals, gains_out = names.take(5), names.one()
    near_totals, save_sem = names.take(5), names.one()
    up_total, down_total, out_total, in_total, grad_tokens = near_totals
    chunks = (streams - 1) // 2
    totals = []
    for chunk in range(chunks):
        lanes = pl.ds(chunk * (up_total.shape[-1] // chunks), up_total.shape[-1] // chunks)
        totals += [up_total.at[:, :, :, :, lanes], down_total.at[chunk]]
    totals.append(out_total)
    in_totals = [in_total.at[j] for j in range(3)]
    near = names.take(branches + 6)
    (own, own_g), units_in, (normed, in_proj, x_rows, grad_hidden) = near[:2], near[2:-4], near[-4:]
    far_sem = names.one()
    first = names.one()
    backs, gots, outs = names.take(branches), names.take(branches), names.take(branches)
    x, g, q_aug, gk, gv, result = names.take(6)
    total, grads, grads_t, normed_t, spread_rows, head_send, head_recv = names.take(7)
    gain_head, gain_one, gain_two, gain_rest = names.take(4)
    in_send, in_recv, in_local, out_send, out_recv, out_local = names.take(6)
    part_sem, head_sems, gain_sems = names.take(3)
    labels = stream_names(streams) + ["i0", "i1", "i2"]
    reductions = make_reductions(
        [ORDERS[label] for label in labels], list(totals) + list(in_totals), names.take(5 * streams + 15)
    )
    reductions = dict(zip(labels, reductions))
    for label in labels[: streams - 1]:
        reductions[label].begun = True

    shapes = [branch_shape(b, heads) for b in range(BRANCHES)]
    size, head_size = lax.axis_size("seq"), lax.axis_size("head")
    me, me_head = lax.axis_index("seq"), lax.axis_index("head")
    rest = size // 4
    tile = 512
    per_slot = x_rows.shape[0] // SLOTS
    width = x_rows.shape[1]


    def fill(s):
        target = reductions[labels[s]].half if s < streams - 1 else totals[-1]
        return pltpu.make_async_copy(parts[s], target, part_sem.at[s])

    def load(i):
        return pltpu.make_async_copy(far[i], near[i], far_sem.at[i])

    for s in range(streams):
        fill(s).start()
    for i in range(branches + 6):
        load(i).start()
    meet("seq", "head")

    def coming(branch):
        return group_copies(branch, sends[branch - 1], gots[branch - 1], in_send, in_recv, in_local)

    def leaving(branch):
        return group_copies(branch, outs[branch - 1], backs[branch - 1], out_send, out_recv, out_local)

    for branch in range(1, BRANCHES):
        for copy in coming(branch):
            copy.start()
    for i in range(2):
        load(i).wait()

    def advance(label, number):
        if label in labels[:streams] and number == (1 if reductions[label].begun else 0):
            fill(labels.index(label)).wait()
        reductions[label].step(number)

    def split_branch(branch):
        stride, lanes, units, split = shapes[branch]
        queries = SEG0 // split
        load(1 + branch).wait()
        for copy in coming(branch):
            copy.wait()
        load_unit(units_in[branch - 1], 0, lanes, x)
        load_unit(gots[branch - 1], 0, lanes, g)
        backward_unit(x, g, q_aug, gk, gv, result, me % split * queries, queries, min(tile, queries))
        store_unit(outs[branch - 1], 0, lanes, result)

    runs, at = [(0, 0, 0, heads // 2)], heads // 2
    split_at = None
    for branch in range(1, BRANCHES):
        if shapes[branch][3] == 1:
            runs.append((branch, at, 0, shapes[branch][2]))
            at += shapes[branch][2]
    split_at = at
    runs.append((0, at, heads // 2, heads - heads // 2))
    blocks = at + heads - heads // 2
    plan = {}
    for block, stream, step in EARLY:
        if stream in labels:
            plan.setdefault(block * blocks // 15, []).append((stream, step))

    @pl.loop(0, blocks)
    def _(block):
        for after, events in plan.items():

            @pl.when(block == after)
            def _(events=events):
                for stream, step in events:
                    advance(stream, step)

        @pl.when(block == split_at)
        def _():
            for branch in range(1, BRANCHES):
                if shapes[branch][3] > 1:
                    split_branch(branch)
                    for copy in leaving(branch):
                        copy.start()

        for branch, low, unit, count in runs:

            @pl.when((block >= low) & (block < low + count))
            def _(branch=branch, low=low, unit=unit):
                if branch == 0:
                    x[...] = own[0, block - low + unit]
                    g[...] = own_g[0, block - low + unit]
                else:

                    @pl.when(block == low)
                    def _():
                        load(1 + branch).wait()
                        for copy in coming(branch):
                            copy.wait()

                    load_unit(units_in[branch - 1], block - low, shapes[branch][1], x)
                    load_unit(gots[branch - 1], block - low, shapes[branch][1], g)

        backward_unit(x, g, q_aug, gk, gv, result, 0, SEG0, tile)
        for branch, low, unit, count in runs:

            @pl.when((block >= low) & (block < low + count))
            def _(branch=branch, low=low, unit=unit, count=count):
                if branch == 0:
                    first[block - low + unit] = result[...]
                else:
                    store_unit(outs[branch - 1], block - low, shapes[branch][1], result)

                    @pl.when(block == low + count - 1)
                    def _():
                        for copy in leaving(branch):
                            copy.start()

    def saves(index):
        return pltpu.make_async_copy(near_totals[index], far_totals[index], save_sem.at[index])

    def save(index):
        saves(index).start()

    tasks = {}

    def task(work):
        tasks[work.__name__] = work

    @task
    def gather():
        for i in range(4):
            load(branches + 2 + i).wait()
        for branch in range(1, BRANCHES):
            for copy in leaving(branch):
                copy.wait()

        @pl.loop(0, heads)
        def _(head):
            total[...] = first[head].astype(F32)
            for branch in range(1, BRANCHES):
                stride, lanes, per, split = shapes[branch]
                back, start = backs[branch - 1], reversed_bits(starts[branch, head], branch)
                if split == 1:
                    value = back[head // per, head % per].astype(F32)
                else:
                    value = back[head * split, 0].astype(F32)
                    for copy in range(1, split):
                        value = value + back[head * split + copy, 0].astype(F32)
                if lanes < 128:
                    value = unpacked(value, 3 * E, start % 2)
                    start = start // 2
                    lanes = 128
                for block in range(SEG0 // lanes):
                    span = slice(block * lanes, (block + 1) * lanes)
                    total[:, span] += jnp.where(start == block, value, 0.0)
            grads[0, head] = (total[0:E, :] * E ** (-0.5)).astype(BF)
            grads[1, head] = total[E : 2 * E, :].astype(BF)
            grads[2, head] = total[2 * E :, :].astype(BF)

        normed_t[...] = normed[...].reshape(SEG0, width).T

    def in_gradient(j):
        rows_in = in_totals[0].shape[3]
        chunk = width // 2
        grads_t[j] = grads[j].reshape(heads * E, SEG0).T
        for half in range(2):
            value = jnp.dot(
                normed_t[half * chunk : (half + 1) * chunk], grads_t[j], preferred_element_type=F32
            ).astype(BF)
            for part in range(chunk // rows_in):
                index = half * (chunk // rows_in) + part
                in_totals[j][index // (2 * rest), index // rest % 2, index % rest] = value[
                    part * rows_in : (part + 1) * rows_in
                ]

    for j in range(3):
        tasks[f"in{j}"] = partial(in_gradient, j)

    def head_swaps():
        swaps = []
        for step in range(1, head_size):
            device = (me_head + step) % head_size
            swaps.append(
                pltpu.make_async_remote_copy(
                    src_ref=head_send.at[device],
                    dst_ref=head_recv.at[step - 1],
                    send_sem=head_sems.at[0, step - 1],
                    recv_sem=head_sems.at[1, step - 1],
                    device_id={"head": device},
                    device_id_type=pl.DeviceIdType.MESH,
                )
            )
        return swaps

    @task
    def one():
        for half in range(2):
            rows = slice(half * SEG0 // 2, (half + 1) * SEG0 // 2)
            value = jnp.zeros((SEG0 // 2, width), F32)
            for j in range(3):
                value = value + lax.dot_general(
                    grads_t[j, rows], in_proj[j], (((1,), (1,)), ((), ())), preferred_element_type=F32
                )
            value = value.astype(BF)
            for slot in range(SLOTS // 2):
                for device in range(head_size):
                    begin = (slot * head_size + device) * per_slot
                    place = (half * SLOTS // 2 + slot) * per_slot
                    head_send[device, place : place + per_slot] = value[begin : begin + per_slot]
        for swap in head_swaps():
            swap.start()

    @task
    def norm():
        for swap in head_swaps():
            swap.wait()
        gain_head[me_head] = jnp.zeros(gains_out.shape, F32)
        gain_head[me_head, 2:4] = gains_two[...]

        @pl.loop(0, SLOTS)
        def _(slot):
            rows = pl.ds(pl.multiple_of(slot * per_slot, per_slot), per_slot)
            grad = head_send[me_head, rows].astype(F32)
            for step in range(1, head_size):
                grad = grad + head_recv[step - 1, rows].astype(F32)
            values = x_rows[rows]
            centred = values - jnp.mean(values, axis=-1, keepdims=True)
            scale = lax.rsqrt(jnp.mean(centred * centred, axis=-1, keepdims=True) + EPS)
            unit = centred * scale
            scaled = grad * gain[...][None]
            inner = jnp.mean(scaled * unit, axis=-1, keepdims=True)
            out = grad_hidden[rows] + scale * (
                scaled - jnp.mean(scaled, axis=-1, keepdims=True) - unit * inner
            )
            place = slot_place(slot)
            for column in range(width // 128):
                lanes = slice(column * 128, (column + 1) * 128)
                spread_rows[column, pl.ds(place, per_slot, stride=SLOTS), :] = out[:, lanes]
            gain_head[me_head, 0:1] += jnp.sum(grad * unit, axis=0, keepdims=True)
            gain_head[me_head, 1:2] += jnp.sum(grad, axis=0, keepdims=True)

        for column in range(width // 128):
            grad_tokens[:, column * 128 : (column + 1) * 128] = spread_rows[column]
        save(4)

    def gain_copy(source, target, axis, device, sem):
        return pltpu.make_async_remote_copy(
            src_ref=source,
            dst_ref=target,
            send_sem=gain_sems.at[0, sem],
            recv_sem=gain_sems.at[1, sem],
            device_id={axis: device},
            device_id_type=pl.DeviceIdType.MESH,
        )

    def gain_copies(stage):
        if stage == 0:
            mine = gain_head.at[me_head]
            return [
                gain_copy(mine, mine, "head", (me_head + step) % head_size, step - 1)
                for step in range(1, head_size)
            ]
        if stage == 1:
            return [gain_copy(gain_one.at[0], gain_one.at[1], "seq", me + 1 - 2 * (me % 2), head_size)]
        if stage == 2:
            device = me + 2 - 4 * (me // 2 % 2)
            return [gain_copy(gain_two.at[0], gain_two.at[1], "seq", device, head_size + 1)]
        spot = me // 4
        block = gain_rest.at[spot]
        return [
            gain_copy(block, block, "seq", (spot + step) % rest * 4 + me % 4, head_size + 1 + step)
            for step in range(1, rest)
        ]

    def summed(ref, count):
        value = ref[0]
        for index in range(1, count):
            value = value + ref[index]
        return value

    def gain_stage(stage):
        if stage > 0:
            for swap in gain_copies(stage - 1):
                swap.wait()
        if stage == 1:
            gain_one[0] = summed(gain_head, head_size)
        elif stage == 2:
            gain_two[0] = summed(gain_one, 2)
        elif stage == 3:
            gain_rest[me // 4] = summed(gain_two, 2)
        elif stage == 4:
            gains_out[...] = summed(gain_rest, rest)
            return
        for swap in gain_copies(stage):
            swap.start()

    for stage in range(5):
        tasks[f"gain{stage}"] = partial(gain_stage, stage)

    groups = [[], [], ["o"], ["i0", "i1", "i2"]]
    for chunk in range(chunks):
        groups[0].append(labels[2 * chunk])
        groups[1].append(labels[2 * chunk + 1])
    for item in TAIL:
        if isinstance(item, str):
            tasks[item]()
        elif item[0] in labels:
            advance(item[0], item[1])
            if item[1] == Reduction.STEPS - 1:
                for index, group in enumerate(groups):
                    if item[0] in group:
                        group.remove(item[0])
                        if not group:
                            save(index)
    for index in range(5):
        saves(index).wait()


def backward(heads, starts, own, own_g, units, sends, parts, normed, in_proj, x_rows, grad_hidden, gain, gains_two):
    size, head_size = lax.axis_size("seq"), lax.axis_size("head")
    rest = size // 4
    rows, width = x_rows.shape
    in_shape = (2, 2, rest, width // size, heads * E)
    scratch = []
    for part in parts:
        scratch += Reduction.scratch(size, *part.shape[-2:])
    for _ in range(3):
        scratch += Reduction.scratch(size, *in_shape[-2:])
    streams = len(parts)
    chunks = (streams - 1) // 2
    far = [own, own_g] + list(units) + [normed, in_proj, x_rows, grad_hidden]
    totals = [
        jax.ShapeDtypeStruct((2, 2, rest, width // size, chunks * parts[0].shape[-1]), BF),
        jax.ShapeDtypeStruct((chunks, 2, 2, rest) + parts[1].shape[-2:], BF),
        jax.ShapeDtypeStruct(parts[-1].shape, BF),
        jax.ShapeDtypeStruct((3,) + in_shape, BF),
        jax.ShapeDtypeStruct((rows, width), F32),
    ]
    results = pl.pallas_call(
        partial(backward_kernel, heads, streams),
        in_specs=[pl.BlockSpec(memory_space=pltpu.SMEM)]
        + vmem_specs(2)
        + [pl.BlockSpec(memory_space=pl.ANY)] * (len(sends) + len(far) + streams),
        out_specs=[pl.BlockSpec(memory_space=pl.ANY)] * len(totals) + vmem_specs(1),
        out_shape=totals + [jax.ShapeDtypeStruct((8, width), F32)],
        scratch_shapes=[pltpu.VMEM(value.shape, value.dtype) for value in totals]
        + [pltpu.SemaphoreType.DMA((len(totals),))]
        + [pltpu.VMEM(value.shape, value.dtype) for value in far]
        + [pltpu.SemaphoreType.DMA((len(far),)), pltpu.VMEM((heads, 3 * E, SEG0), BF)]
        + [pltpu.VMEM(shape.shape, BF) for shape in send_shapes(heads, 3 * E)]
        + [pltpu.VMEM(shape.shape, BF) for shape in send_shapes(heads, ROWS_OUT)]
        + [pltpu.VMEM(shape.shape, BF) for shape in send_shapes(heads, 3 * E)]
        + [
            pltpu.VMEM((ROWS_IN, SEG0), BF),
            pltpu.VMEM((ROWS_OUT, SEG0), BF),
            pltpu.VMEM((ROWS_OUT, SEG0), BF),
            pltpu.VMEM((SEG0, ROWS_OUT), F32),
            pltpu.VMEM((SEG0, ROWS_OUT), F32),
            pltpu.VMEM((3 * E, SEG0), BF),
            pltpu.VMEM((3 * E, SEG0), F32),
            pltpu.VMEM((3, heads, E, SEG0), BF),
            pltpu.VMEM((3, SEG0, heads * E), BF),
            pltpu.VMEM((width, SEG0), BF),
            pltpu.VMEM((width // 128, rows, 128), F32),
            pltpu.VMEM((head_size, rows, width), BF),
            pltpu.VMEM((head_size - 1, rows, width), BF),
            pltpu.VMEM((head_size, 8, width), F32),
            pltpu.VMEM((2, 8, width), F32),
            pltpu.VMEM((2, 8, width), F32),
            pltpu.VMEM((rest, 8, width), F32),
        ]
        + exchange_scratch()
        + [
            pltpu.SemaphoreType.DMA((streams,)),
            pltpu.SemaphoreType.DMA((2, head_size - 1)),
            pltpu.SemaphoreType.DMA((2, head_size + 1 + rest)),
        ]
        + scratch,
        compiler_params=pltpu.CompilerParams(
            vmem_limit_bytes=60 * 2**20, collective_id=1, has_side_effects=True
        ),
        cost_estimate=unit_cost(2 * heads, 5),
        name="backward",
    )(starts, gain, gains_two, *sends, *far, *parts)
    up_total, down_total, out_total, in_total = results[:4]
    sums = [
        in_total.reshape(3, width, heads * E),
        out_total.reshape(-1, width),
        up_total.reshape(width, -1),
        down_total.reshape(-1, width),
    ]
    return sums, results[4], results[5]


def finish_kernel(*refs):
    count = len(refs) // 2
    for source, target in zip(refs[:count], refs[count:]):
        target[...] = source[...].astype(target.dtype)


def finish(values, types):
    steps = 2
    specs = []
    for value in values:
        shape = list(value.shape)
        shape[-2] //= steps
        if value.ndim == 3:
            specs.append(pl.BlockSpec(tuple(shape), lambda i: (0, i, 0)))
        else:
            specs.append(pl.BlockSpec(tuple(shape), lambda i: (i, 0)))
    return pl.pallas_call(
        finish_kernel,
        grid=(steps,),
        in_specs=specs,
        out_specs=specs,
        out_shape=[jax.ShapeDtypeStruct(value.shape, kind) for value, kind in zip(values, types)],
        compiler_params=pltpu.CompilerParams(vmem_limit_bytes=61 * 2**20),
        name="finish",
    )(*values)


def middle_kernel(heads, *refs):
    branches = BRANCHES - 1
    names = Names(refs)
    starts, first = names.take(2)
    backs = names.take(branches)
    gain, shift = names.take(2)
    far = names.take(5)
    block_out, grad_hidden, gains_two, own_g = names.take(4)
    sends = names.take(branches)
    chunks = max(1, far[3].shape[1] // far[0].shape[1])
    halves = names.take(2 * chunks)
    out_total = names.one()
    merged, lse, mixed, turned, part, got, part_two, got_two = names.take(8)
    hidden_one, normed_own, normed, spread_rows, normed_t = names.take(5)
    down_sum, norm_sum, up_grad, down_grad, totals = names.take(5)
    head_sems, first_sems, far_sem = names.take(3)
    near = names.take(5)
    out_proj, x_rows, cot, up, down = near[2], near[0], near[1], near[3], near[4]
    loads = [pltpu.make_async_copy(far[i], near[i], far_sem.at[i]) for i in range(5)]
    for i in (2, 0, 1, 3, 4):
        loads[i].start()

    head_size, me_head = lax.axis_size("head"), lax.axis_index("head")
    me = lax.axis_index("seq")
    rest = lax.axis_size("seq") // 4
    width = x_rows.shape[1]
    per_slot = x_rows.shape[0] // SLOTS
    tile = 256

    meet("seq", "head")

    @pl.loop(0, heads)
    def _(head):
        own = first[0, head].astype(F32)
        merged[head] = own[:E]
        lse[head] = own[E : E + 1] + own[E + 1 : E + 2] + own[E + 2 : E + 3]
        for branch in range(1, BRANCHES):
            stride, lanes, per, split = branch_shape(branch, heads)
            back, start = backs[branch - 1], reversed_bits(starts[branch, head], branch)
            share = max(1, 128 // lanes)
            for copy in range(split):
                if split == 1:
                    value = back[head // per, head % per].astype(F32)
                else:
                    value = back[head * split + copy, 0].astype(F32)
                if share > 1:
                    value = unpacked(value, ROWS_OUT, start % share)
                new_lse = value[E : E + 1] + value[E + 1 : E + 2] + value[E + 2 : E + 3]
                if share > 1:
                    ids = lax.broadcasted_iota(jnp.int32, new_lse.shape, 1)
                    new_lse = jnp.where(ids // lanes == start % share, new_lse, -FAR)
                span = lanes * share
                for block in range(SEG0 // span):
                    at = slice(block * span, (block + 1) * span)
                    new = jnp.where(start // share == block, new_lse, -FAR)
                    old = lse[head, :, at]
                    top = jnp.maximum(old, new)
                    both = top + jnp.log2(jnp.exp2(old - top) + jnp.exp2(new - top))
                    lse[head, :, at] = both
                    merged[head, :, at] = merged[head, :, at] * jnp.exp2(old - both) + value[:E] * jnp.exp2(
                        new - both
                    )
        mixed[head] = merged[head].astype(BF)

    def rows_of(ref):
        return ref[...].reshape(SEG0, width)

    turned[...] = mixed[...].reshape(heads * E, SEG0).T
    loads[2].wait()
    for step in range(SEG0 // tile):
        at = slice(step * tile // (head_size * per_slot), (step + 1) * tile // (head_size * per_slot))
        value = jnp.dot(turned[step * tile : (step + 1) * tile], out_proj[...], preferred_element_type=F32)
        part[at] = value.astype(BF).reshape(-1, head_size, per_slot, width)
    for copy in head_copies(part, got, head_sems, 0, True):
        copy.start()
    for ref in (down_sum, norm_sum, up_grad, down_grad):
        ref[...] = jnp.zeros_like(ref)
    loads[0].wait()
    for copy in head_copies(part, got, head_sems, 0, True):
        copy.wait()

    def rows_at(slot):
        return pl.ds(pl.multiple_of(slot * per_slot, per_slot), per_slot)

    @over_slots
    def _(slot):
        value = x_rows[rows_at(slot)] + part[slot, me_head].astype(F32)
        for step in range(1, head_size):
            value = value + got[step - 1, slot].astype(F32)
        hidden_one[rows_at(slot)] = value
        unit, scale = norm_of(value)
        low = (unit * gain[...][None] + shift[...][None]).astype(BF)
        normed_own[slot] = low
        normed[slot, me_head] = low

    for copy in head_copies(normed_own, normed, head_sems, 1, False):
        copy.start()
    for copy in head_copies(normed_own, normed, head_sems, 1, False):
        copy.wait()
    normed_t[...] = rows_of(normed).T
    for i in (1, 3, 4):
        loads[i].wait()

    chunk_width = up.shape[1] // chunks
    orders = {0: ORDERS["u1"], 1: ORDERS["d1"]}
    firsts = []
    for chunk in range(chunks):
        for kind in range(2):
            index = 2 * chunk + kind
            firsts.append(
                Reduction(
                    orders[kind], totals.at[index], halves[index], None, None,
                    first_sems.at[0, pl.ds(index, 1)], first_sems.at[1, pl.ds(index, 1)],
                )
            )
    slots = tile // (head_size * per_slot)
    contract_last = (((1,), (1,)), ((), ()))

    for chunk in range(chunks):
        units = slice(chunk * chunk_width, (chunk + 1) * chunk_width)
        if chunk > 0:
            up_grad[...] = jnp.zeros_like(up_grad)
            down_grad[...] = jnp.zeros_like(down_grad)

        @pl.loop(0, SEG0 // tile)
        def _(step):
            rows = pl.ds(pl.multiple_of(step * tile, tile), tile)
            low = normed[pl.ds(step * slots, slots)].reshape(tile, width)
            back = cot[pl.ds(step * slots, slots)].reshape(tile, width)
            pre = jnp.dot(low, up[:, units], preferred_element_type=F32)
            grad = lax.dot_general(back, down[units], contract_last, preferred_element_type=F32)
            share = 0.5 + 0.5 * lax.erf(pre * math.sqrt(0.5))
            density = jnp.exp2(pre * pre * (-0.5 * LOG2E)) * (1.0 / math.sqrt(2.0 * math.pi))
            hidden = (pre * share).astype(BF)
            grad = (grad * (share + pre * density)).astype(BF)
            down_sum[rows] += jnp.dot(hidden, down[units], preferred_element_type=F32)
            norm_sum[rows] += lax.dot_general(grad, up[:, units], contract_last, preferred_element_type=F32)
            up_grad[...] += jnp.dot(normed_t[:, rows], grad, preferred_element_type=F32)
            down_grad[...] += jnp.dot(hidden.T, back, preferred_element_type=F32)

        pieces = totals.shape[3] * 4
        size = totals.shape[4]
        for piece in range(pieces):
            spot = (piece // (2 * rest), piece // rest % 2, piece % rest)
            span = slice(piece * size, (piece + 1) * size)
            totals[(2 * chunk,) + spot] = up_grad[span].astype(BF)
            totals[(2 * chunk + 1,) + spot] = down_grad[span].astype(BF)
        firsts[2 * chunk].step(0)
        firsts[2 * chunk + 1].step(0)

    for ref, value in ((part, down_sum), (part_two, norm_sum)):

        @pl.loop(0, SLOTS)
        def _(slot):
            for device in range(head_size):
                begin = pl.multiple_of((slot * head_size + device) * per_slot, per_slot)
                ref[slot, device] = value[pl.ds(begin, per_slot)].astype(BF)

    for copy in head_copies(part_two, got_two, head_sems, 2, True) + head_copies(part, got, head_sems, 3, True):
        copy.start()
    for copy in head_copies(part_two, got_two, head_sems, 2, True):
        copy.wait()
    gains_two[...] = jnp.zeros_like(gains_two)

    @over_slots
    def _(slot):
        grad = part_two[slot, me_head].astype(F32)
        for step in range(1, head_size):
            grad = grad + got_two[step - 1, slot].astype(F32)
        unit, scale = norm_of(hidden_one[rows_at(slot)])
        scaled = grad * gain[...][None]
        inner = jnp.mean(scaled * unit, axis=-1, keepdims=True)
        out = cot[slot, me_head].astype(F32) + scale * (
            scaled - jnp.mean(scaled, axis=-1, keepdims=True) - unit * inner
        )
        grad_hidden[rows_at(slot)] = out
        normed_own[slot] = out.astype(BF)
        normed[slot, me_head] = out.astype(BF)
        gains_two[0:1] += jnp.sum(grad * unit, axis=0, keepdims=True)
        gains_two[1:2] += jnp.sum(grad, axis=0, keepdims=True)

    for copy in head_copies(normed_own, normed, head_sems, 4, False):
        copy.start()
    for copy in head_copies(part, got, head_sems, 3, True):
        copy.wait()

    @pl.loop(0, SLOTS)
    def _(slot):
        value = hidden_one[rows_at(slot)] + part[slot, me_head].astype(F32)
        for step in range(1, head_size):
            value = value + got[step - 1, slot].astype(F32)
        place = slot_place(slot)
        for column in range(width // 128):
            lanes = slice(column * 128, (column + 1) * 128)
            spread_rows[column, pl.ds(place, per_slot, stride=SLOTS), :] = value[:, lanes]

    for column in range(width // 128):
        block_out[:, column * 128 : (column + 1) * 128] = spread_rows[column].astype(BF)
    for copy in head_copies(normed_own, normed, head_sems, 4, False):
        copy.wait()

    value = jnp.dot(mixed[...].reshape(heads * E, SEG0), rows_of(normed), preferred_element_type=F32)
    size = out_total.shape[3]
    for piece in range(4 * rest):
        spot = (piece // (2 * rest), piece // rest % 2, piece % rest)
        out_total[spot] = value[piece * size : (piece + 1) * size].astype(BF)

    normed_t[...] = rows_of(normed).T
    value = jnp.dot(out_proj[...], normed_t[...], preferred_element_type=F32)
    own_g[0, :, :E, :] = value.astype(BF).reshape(heads, E, SEG0)

    @pl.loop(0, heads)
    def _(head):
        low = own_g[0, head, :E, :]
        dots = jnp.sum(low.astype(F32) * merged[head], axis=0, keepdims=True)
        d = pieces_of(-dots)
        m = pieces_of(-lse[head])
        placed = {0: d[0], 1: d[1], 2: d[2], 12: m[0], 13: m[1], 14: m[2]}
        own_g[0, head, E:, :] = row_block(placed, SEG0).astype(BF)
        own = jnp.concatenate([low.astype(F32), row_block(placed, SEG0)], axis=0)
        spread_blocks(heads, head, starts, own, sends)

    for reduction in firsts:
        reduction.finish_first()


def middle(heads, starts, first, backs, x_rows, cot, out_proj, up, down, gain, shift):
    size, head_size = lax.axis_size("seq"), lax.axis_size("head")
    rest = size // 4
    rows, width = x_rows.shape
    per_slot = rows // SLOTS
    chunks = max(1, up.shape[1] // width)
    shard = (SLOTS, head_size, per_slot, width)
    own = (SLOTS, per_slot, width)
    got = (head_size - 1,) + own
    sends = send_shapes(heads, ROWS_OUT)
    piece = (2, rest, width // size, up.shape[1] // chunks)
    out_piece = (2, 2, rest, heads * E // size, width)
    far = [x_rows, cot, out_proj, up, down]
    results = pl.pallas_call(
        partial(middle_kernel, heads),
        in_specs=[pl.BlockSpec(memory_space=pltpu.SMEM)]
        + vmem_specs(1 + len(backs) + 2)
        + [pl.BlockSpec(memory_space=pl.ANY)] * 5,
        out_specs=vmem_specs(4 + len(sends) + 2 * chunks + 1),
        out_shape=[
            jax.ShapeDtypeStruct((rows, width), BF),
            jax.ShapeDtypeStruct((rows, width), F32),
            jax.ShapeDtypeStruct((2, width), F32),
            jax.ShapeDtypeStruct((1, heads, ROWS_OUT, SEG0), BF),
        ]
        + sends
        + [jax.ShapeDtypeStruct(piece, BF)] * (2 * chunks)
        + [jax.ShapeDtypeStruct(out_piece, BF)],
        scratch_shapes=[
            pltpu.VMEM((heads, E, SEG0), F32),
            pltpu.VMEM((heads, 1, SEG0), F32),
            pltpu.VMEM((heads, E, SEG0), BF),
            pltpu.VMEM((SEG0, heads * E), BF),
            pltpu.VMEM(shard, BF),
            pltpu.VMEM(got, BF),
            pltpu.VMEM(shard, BF),
            pltpu.VMEM(got, BF),
            pltpu.VMEM((rows, width), F32),
            pltpu.VMEM(own, BF),
            pltpu.VMEM(shard, BF),
            pltpu.VMEM((width // 128, rows, 128), F32),
            pltpu.VMEM((width, SEG0), BF),
            pltpu.VMEM((SEG0, width), F32),
            pltpu.VMEM((SEG0, width), F32),
            pltpu.VMEM((width, up.shape[1] // chunks), F32),
            pltpu.VMEM((up.shape[1] // chunks, width), F32),
            pltpu.VMEM((2 * chunks, 2) + piece, BF),
            pltpu.SemaphoreType.DMA((2, 5, head_size - 1)),
            pltpu.SemaphoreType.DMA((2, 2 * chunks)),
            pltpu.SemaphoreType.DMA((5,)),
        ]
        + [pltpu.VMEM(value.shape, value.dtype) for value in far],
        compiler_params=pltpu.CompilerParams(
            vmem_limit_bytes=60 * 2**20, collective_id=2, has_side_effects=True
        ),
        cost_estimate=pl.CostEstimate(
            flops=14 * SEG0 * width * up.shape[1], transcendentals=0, bytes_accessed=40 * 2**20
        ),
        name="middle",
    )(starts, first, *backs, gain, shift, *far)
    block_out, grad_hidden, gains_two, own_g = results[:4]
    return block_out, grad_hidden, gains_two, own_g, results[4 : 4 + len(sends)], results[4 + len(sends) :]


def local(
    tokens,
    documents,
    offsets,
    in_proj,
    out_proj,
    up_proj,
    down_proj,
    first_gain,
    first_shift,
    second_gain,
    second_shift,
    cotangent,
):
    head_count = lax.axis_size("head")
    seq_id = lax.axis_index("seq")
    row_count = tokens.shape[0]
    seq_len = row_count * head_count
    heads = offsets.shape[1]
    per_slot = row_count // SLOTS

    my_docs = lax.dynamic_slice_in_dim(documents, seq_id * seq_len, seq_len)
    my_docs = my_docs.reshape(head_count, per_slot, 2, 2, 2, 2).transpose(5, 4, 3, 2, 0, 1).reshape(seq_len)
    bit_ids = jnp.arange(BIT_ROWS, dtype=jnp.int32)[:, None]
    doc_bit = my_docs[None, :] // 2 ** (bit_ids % DOC_BITS) % 2
    bits = jnp.where(bit_ids < DOC_BITS, doc_bit, jnp.where(bit_ids < 2 * DOC_BITS, 1 - doc_bit, 0))
    bits = bits.astype(BF)

    (x_rows, normed, cot_all, own), units, first_out, outs = forward(
        heads, offsets, tokens, cotangent, bits, first_gain, first_shift, in_proj
    )
    block_out, grad_hidden, gains_two, own_g, sends_g, parts = middle(
        heads, offsets, first_out, outs, x_rows, cot_all, out_proj, up_proj, down_proj, second_gain, second_shift
    )
    sums, grad_tokens, gains = backward(
        heads, offsets, own, own_g, units, sends_g, parts,
        normed, in_proj, x_rows, grad_hidden, first_gain, gains_two,
    )
    results = finish([block_out, grad_tokens] + sums, [BF] + [F32] * 5)
    return (*results, gains[0], gains[1], gains[2], gains[3])


def solution(mesh):
    placed = (
        P(("seq", "head"), None),
        P(),
        P(None, "head"),
        P(None, None, "head"),
        P("head", None),
        P(None, "head"),
        P("head", None),
        P(),
        P(),
        P(),
        P(),
        P(("seq", "head"), None),
    )
    return jax.shard_map(
        local,
        mesh=mesh,
        in_specs=placed,
        out_specs=(
            P(("seq", "head"), None),
            P(("seq", "head"), None),
            P(None, None, "head"),
            P("head", None),
            P(None, "head"),
            P("head", None),
            P(),
            P(),
            P(),
            P(),
        ),
        check_vma=False,
    )
```

```python
import math
from functools import partial

import jax
import jax.numpy as jnp
from jax import lax
from jax.experimental import pallas as pl
from jax.experimental.pallas import tpu as pltpu
from jax.sharding import PartitionSpec as P

E = 48
BRANCHES = 5
SEG0 = 1024
SLOTS = 16
BIT_ROWS = 16
DOC_BITS = 6
ROWS_IN = 3 * E + BIT_ROWS
ROWS_OUT = E + BIT_ROWS
EPS = 1e-05
FAR = 1e30
LOG2E = math.log2(math.e)
LN2 = math.log(2.0)
BF = jnp.bfloat16
F32 = jnp.float32
VMEM_LIMIT = 48 * 2**20


def reversed_bits(value, count):
    out = value % 2
    for bit in range(1, count):
        out = out * 2 + value // 2**bit % 2
    return out


def branch_shape(branch, heads):
    stride = 2**branch
    return (stride, SEG0 // stride, max(1, heads // stride), max(1, stride // heads))


def pieces_of(value):
    high = value.astype(BF).astype(F32)
    rest = value - high
    middle = rest.astype(BF).astype(F32)
    return high, middle, (rest - middle).astype(BF).astype(F32)


def row_block(placed, columns):
    ids = lax.broadcasted_iota(jnp.int32, (BIT_ROWS, columns), 0)
    block = jnp.zeros((BIT_ROWS, columns), F32)
    for row, value in placed.items():
        block = jnp.where(ids == row, value, block)
    return block


def turned_half(block):
    return jnp.concatenate([block[:, 64:], block[:, :64]], axis=1)


def low_half():
    return lax.broadcasted_iota(jnp.int32, (1, 128), 1) < 64


def packed_rows(rows, count):
    return rows if count >= 128 else (rows // 2 + 15) // 16 * 16


def packed(block, half):
    rows = packed_rows(block.shape[0], 64)
    upper, lower = block[:rows], block[block.shape[0] - rows :]
    if isinstance(half, int):
        return jnp.where(low_half(), turned_half(upper) if half else upper, lower if half else turned_half(lower))
    upper = jnp.where(half == 0, upper, turned_half(upper))
    lower = jnp.where(half == 0, turned_half(lower), lower)
    return jnp.where(low_half(), upper, lower)


def unpacked(value, rows, half):
    size = value.shape[0]
    other = turned_half(value)
    upper = jnp.where(half == 0, value, other)
    lower = jnp.where(half == 0, other, value)
    both = jnp.concatenate([upper, lower[2 * size - rows :]], axis=0)
    return jnp.where(low_half() == (half == 0), both, 0.0)


def send_shapes(heads, rows):
    outs = []
    for branch in range(1, BRANCHES):
        stride, count, per, split = branch_shape(branch, heads)
        outs.append(jax.ShapeDtypeStruct((stride, per, packed_rows(rows, count), max(count, 128)), BF))
    return outs


def spread_blocks(heads, head, starts, value, sends, branches=range(1, BRANCHES)):
    for branch in branches:
        stride, lanes, per, split = branch_shape(branch, heads)
        send, start = sends[branch - 1], reversed_bits(starts[branch, head], branch)
        share = max(1, 128 // lanes)
        span = lanes * share
        block = value[:, :span]
        for part in range(1, SEG0 // span):
            block = jnp.where(start // share == part, value[:, part * span : (part + 1) * span], block)
        if share > 1:
            block = packed(block, start % share)
        block = block.astype(BF)
        if split == 1:
            send[head // per, head % per] = block
        else:
            for copy in range(split):
                send[head * split + copy, 0] = block


def norm_of(values):
    centred = values - jnp.mean(values, axis=-1, keepdims=True)
    scale = lax.rsqrt(jnp.mean(centred * centred, axis=-1, keepdims=True) + EPS)
    return centred * scale, scale


def slot_place(slot):
    return slot % 2 * 8 + slot // 2 % 2 * 4 + slot // 4 % 2 * 2 + slot // 8


def over_slots(body, unroll=4):
    @pl.loop(0, SLOTS // unroll)
    def _(step):
        for part in range(unroll):
            body(step * unroll + part)


def head_copies(source, target, sems, index, scatter):
    size, me = lax.axis_size("head"), lax.axis_index("head")
    copies = []
    for step in range(1, size):
        device = (me + step) % size
        copies.append(
            pltpu.make_async_remote_copy(
                src_ref=source.at[:, device] if scatter else source,
                dst_ref=target.at[step - 1] if scatter else target.at[:, me],
                send_sem=sems.at[0, index, step - 1],
                recv_sem=sems.at[1, index, step - 1],
                device_id={"head": device},
                device_id_type=pl.DeviceIdType.MESH,
            )
        )
    return copies


def load_unit(ref, unit, count, x):
    width = ref.shape[-1]
    if count >= 128:
        for block in range(ref.shape[0]):
            x[:, block * width : (block + 1) * width] = ref[block, unit]
        return
    rows, size = x.shape[0], ref.shape[2]
    for block in range(ref.shape[0] // 2):
        lanes = slice(block * 128, (block + 1) * 128)
        left = ref[2 * block, unit].astype(F32)
        right = ref[2 * block + 1, unit].astype(F32)
        x[:size, lanes] = jnp.where(low_half(), left, turned_half(right)).astype(BF)
        x[rows - size :, lanes] = jnp.where(low_half(), turned_half(left), right).astype(BF)


def store_unit(ref, unit, count, result):
    width = ref.shape[-1]
    for block in range(SEG0 // width):
        value = result[:, block * width : (block + 1) * width]
        if count >= 128:
            ref[block, unit] = value
        else:
            value = value.astype(F32)
            ref[2 * block, unit] = packed(value, 0).astype(BF)
            ref[2 * block + 1, unit] = packed(value, 1).astype(BF)


def forward_unit(x, q_aug, result, base, queries):
    if isinstance(base, int):
        lanes = slice(base, base + queries)
    else:
        lanes = pl.ds(pl.multiple_of(base, 128), queries)
    q_aug[0:E, :queries] = x[0:E, lanes]
    q_aug[E:, :queries] = (x[3 * E :, lanes].astype(F32) * -FAR).astype(BF)
    bits = x[3 * E :, :].astype(F32)
    k_rows = jnp.concatenate([x[E : 2 * E, :], (1.0 - bits).astype(BF)], axis=0).T
    v_aug = jnp.concatenate([x[2 * E : 3 * E, :], jnp.ones(bits.shape, BF)], axis=0)
    if queries < SEG0:
        result[0:E, :] = jnp.zeros((E, SEG0), BF)
        result[E:, :] = row_block({0: -FAR}, SEG0).astype(BF)
    s = jnp.dot(k_rows, q_aug[:, :queries], preferred_element_type=F32)
    top = jnp.max(s, axis=0, keepdims=True)
    p = jnp.exp2(s - top).astype(BF)
    o = jnp.dot(v_aug, p, preferred_element_type=F32)
    total = o[E : E + 1]
    high, middle_part, low = pieces_of(top + jnp.log2(total))
    block = row_block({0: high, 1: middle_part, 2: low}, queries)
    result[:, lanes] = jnp.concatenate([o[:E] * (1.0 / total), block], axis=0).astype(BF)


class Names:
    def __init__(self, refs):
        self.refs = list(refs)

    def take(self, count):
        taken, self.refs = self.refs[:count], self.refs[count:]
        return taken

    def one(self):
        return self.take(1)[0]


def group_place(branch):
    stride = 2**branch
    me = lax.axis_index("seq")
    return me // stride * stride, me % stride


def meet(*axes):
    barrier = pltpu.get_barrier_semaphore()
    count = 0
    for axis in axes:
        size = lax.axis_size(axis)
        me = lax.axis_index(axis)

        @pl.loop(1, size)
        def _(step):
            pl.semaphore_signal(
                barrier, inc=1, device_id={axis: (me + step) % size}, device_id_type=pl.DeviceIdType.MESH
            )

        count += size - 1
    pl.semaphore_wait(barrier, count)


class Reduction:
    STEPS = 7

    def __init__(self, order, total, half, quarter, others, send, recv, begun=False):
        self.total, self.begun = total, begun
        self.half, self.quarter, self.others = half, quarter, others
        self.send, self.recv = send, recv
        me = lax.axis_index("seq")
        self.rest = lax.axis_size("seq") // 4
        self.me = me
        bits = (me % 2, me // 2 % 2)
        self.bits = [bits[bit] for bit in order]
        self.partners = [me + (1 - 2 * bits[bit]) * 2**bit for bit in order]
        self.place = me // 4

    def copy(self, source, target, device, sem):
        return pltpu.make_async_remote_copy(
            src_ref=source,
            dst_ref=target,
            send_sem=self.send.at[sem],
            recv_sem=self.recv.at[sem],
            device_id={"seq": device},
            device_id_type=pl.DeviceIdType.MESH,
        )

    def copies(self, number):
        one, two = self.bits
        rest = self.rest
        others = []
        for step in range(1, rest):
            place = (self.place + step) % rest
            others.append((step, place, place * 4 + self.me % 4))
        if number == 0:
            return [self.copy(self.total.at[1 - one], self.half, self.partners[0], 0)]
        if number == 1:
            return [self.copy(self.half.at[1 - two], self.quarter, self.partners[1], 1)]
        if number == 2:
            return [
                self.copy(self.quarter.at[place], self.others.at[step - 1], device, 1 + step)
                for step, place, device in others
            ]
        if number == 3:
            block = self.total.at[one, two, self.place]
            return [self.copy(block, block, device, rest + step) for step, place, device in others]
        if number == 4:
            block = self.total.at[one, two]
            return [self.copy(block, block, self.partners[1], 2 * rest)]
        if number == 5:
            block = self.total.at[one]
            return [self.copy(block, block, self.partners[0], 2 * rest + 1)]
        return []

    def finish_first(self):
        one, rest = self.bits[0], self.rest
        for copy in self.copies(0):
            copy.wait()

        @pl.loop(0, 2 * rest)
        def _(i):
            j, z = i // rest, i % rest
            mine = self.total[one, j, z].astype(F32)
            self.half[j, z] = (mine + self.half[j, z].astype(F32)).astype(BF)

    def step(self, number):
        one, two = self.bits
        rest = self.rest
        if number == 0 and self.begun:
            return
        if number == 1:
            if not self.begun:
                self.finish_first()
        elif number > 0:
            for copy in self.copies(number - 1):
                copy.wait()
        if number == 2:

            @pl.loop(0, rest)
            def _(z):
                mine = self.half[two, z].astype(F32)
                self.quarter[z] = (mine + self.quarter[z].astype(F32)).astype(BF)

        elif number == 3:
            mine = self.quarter[self.place].astype(F32)
            for step in range(1, rest):
                mine = mine + self.others[step - 1].astype(F32)
            self.total[one, two, self.place] = mine.astype(BF)
        for copy in self.copies(number):
            copy.start()

    @staticmethod
    def scratch(size, rows, columns):
        rest = size // 4
        count = 2 * rest + 2
        return [
            pltpu.VMEM((2, rest, rows, columns), BF),
            pltpu.VMEM((rest, rows, columns), BF),
            pltpu.VMEM((rest - 1, rows, columns), BF),
            pltpu.SemaphoreType.DMA((count,)),
            pltpu.SemaphoreType.DMA((count,)),
        ]


def reduction_parts(value, size):
    rows, columns = value.shape
    return value.reshape(2, 2, size // 4, rows // size, columns)


def reduction_whole(value):
    return value.reshape(-1, value.shape[-1])


def make_reductions(orders, totals, scratch):
    out = []
    for order, total in zip(orders, totals):
        out.append(Reduction(order, total, *scratch[:5]))
        scratch = scratch[5:]
    return out


def group_copies(branch, source, target, send_sems, recv_sems, local_sem):
    stride = 2**branch
    base, place = group_place(branch)
    first = stride - branch - 2
    copies = [
        pltpu.make_async_copy(source.at[place], target.at[place], local_sem.at[branch - 1])
    ]
    for step in range(1, stride):
        member = (place + step) % stride
        copies.append(
            pltpu.make_async_remote_copy(
                src_ref=source.at[member],
                dst_ref=target.at[place],
                send_sem=send_sems.at[first + step],
                recv_sem=recv_sems.at[first + step],
                device_id={"seq": base + member},
                device_id_type=pl.DeviceIdType.MESH,
            )
        )
    return copies


def forward_kernel(heads, starts, tokens, cotangent, bits, gain, shift, in_proj, *refs):
    count = BRANCHES - 1
    names = Names(refs)
    far = names.take(4 + count)
    first, backs = names.one(), names.take(count)
    near = names.take(4 + count)
    (x_rows, normed, cot, own), gots = near[:4], near[4:]
    outs, sends = names.take(count), names.take(count)
    x, q_aug, result, in_send, in_recv, in_local, out_send, out_recv, out_local = names.take(9)
    spread_rows, normed_own, cot_own, normed_t, head_sems, far_sem = names.take(6)
    saves = [pltpu.make_async_copy(near[i], far[i], far_sem.at[i]) for i in range(4 + count)]
    me_head = lax.axis_index("head")
    rows, width = tokens.shape
    per_slot = rows // SLOTS

    def fill(source):
        for column in range(width // 128):
            spread_rows[column] = source[:, column * 128 : (column + 1) * 128].astype(F32)

    def picked(slot):
        at = pl.ds(slot_place(slot), per_slot, stride=SLOTS)
        return jnp.concatenate([spread_rows[column, at, :] for column in range(width // 128)], axis=1)

    fill(tokens)

    @over_slots
    def _(slot):
        value = picked(slot)
        x_rows[pl.ds(pl.multiple_of(slot * per_slot, per_slot), per_slot)] = value
        low = (norm_of(value)[0] * gain[...][None] + shift[...][None]).astype(BF)
        normed_own[slot] = low
        normed[slot, me_head] = low

    meet("seq", "head")
    for copy in head_copies(normed_own, normed, head_sems, 0, False):
        copy.start()
    saves[0].start()
    fill(cotangent)

    @over_slots
    def _(slot):
        low = picked(slot).astype(BF)
        cot_own[slot] = low
        cot[slot, me_head] = low

    for copy in head_copies(cot_own, cot, head_sems, 1, False):
        copy.start()
    own[0, :, 3 * E :, :] = jnp.broadcast_to(bits[...][None], (heads,) + bits.shape)
    turned = [in_proj[j].T for j in range(3)]
    for copy in head_copies(normed_own, normed, head_sems, 0, False):
        copy.wait()
    normed_t[...] = normed[...].reshape(SEG0, width).T
    for j in range(3):
        value = jnp.dot(turned[j], normed_t[...], preferred_element_type=F32)
        if j == 0:
            value = value * (E ** (-0.5) * LOG2E)
        own[0, :, j * E : (j + 1) * E, :] = value.astype(BF).reshape(heads, E, SEG0)
    saves[1].start()
    saves[3].start()

    coming = {}
    for branch in range(1, BRANCHES):

        @pl.loop(0, heads)
        def _(head):
            spread_blocks(heads, head, starts, own[0, head].astype(F32), sends, [branch])

        coming[branch] = group_copies(branch, sends[branch - 1], gots[branch - 1], in_send, in_recv, in_local)
        for copy in coming[branch]:
            copy.start()

    @pl.loop(0, heads)
    def _(head):
        x[...] = own[0, head]
        forward_unit(x, q_aug, result, 0, SEG0)
        first[0, head] = result[...]

    for copy in head_copies(cot_own, cot, head_sems, 1, False):
        copy.wait()
    saves[2].start()
    leaving = []
    for branch in range(1, BRANCHES):
        stride, lanes, units, split = branch_shape(branch, heads)
        got, out = gots[branch - 1], outs[branch - 1]
        for copy in coming[branch]:
            copy.wait()
        saves[3 + branch].start()
        queries = SEG0 // split
        base = 0 if split == 1 else lax.axis_index("seq") % split * queries

        @pl.loop(0, units)
        def _(unit):
            load_unit(got, unit, lanes, x)
            forward_unit(x, q_aug, result, base, queries)
            store_unit(out, unit, lanes, result)

        copies = group_copies(branch, out, backs[branch - 1], out_send, out_recv, out_local)
        for copy in copies:
            copy.start()
        leaving += copies
    for copy in leaving + saves:
        copy.wait()


def exchange_scratch():
    copies = 2**BRANCHES - 2 - BRANCHES + 1
    one = [
        pltpu.SemaphoreType.DMA((copies,)),
        pltpu.SemaphoreType.DMA((copies,)),
        pltpu.SemaphoreType.DMA((BRANCHES - 1,)),
    ]
    return one + one


def unit_cost(units, dots):
    return pl.CostEstimate(
        flops=dots * 2 * units * SEG0 * SEG0 * 256,
        transcendentals=units * SEG0 * SEG0,
        bytes_accessed=units * SEG0 * 1000,
    )


def vmem_specs(count):
    return [pl.BlockSpec(memory_space=pltpu.VMEM)] * count


def forward(heads, starts, tokens, cotangent, bits, gain, shift, in_proj):
    head_size = lax.axis_size("head")
    rows, width = tokens.shape
    shard = jax.ShapeDtypeStruct((SLOTS, head_size, rows // SLOTS, width), BF)
    own_rows = pltpu.VMEM((SLOTS, rows // SLOTS, width), BF)
    backs = send_shapes(heads, ROWS_OUT)
    gots = send_shapes(heads, ROWS_IN)
    own = jax.ShapeDtypeStruct((1, heads, ROWS_IN, SEG0), BF)
    far = [jax.ShapeDtypeStruct((rows, width), F32), shard, shard, own] + gots
    results = pl.pallas_call(
        partial(forward_kernel, heads),
        in_specs=[pl.BlockSpec(memory_space=pltpu.SMEM)] + vmem_specs(6),
        out_specs=[pl.BlockSpec(memory_space=pl.ANY)] * len(far) + vmem_specs(1 + len(backs)),
        out_shape=far + [jax.ShapeDtypeStruct((1, heads, ROWS_OUT, SEG0), BF)] + backs,
        scratch_shapes=[pltpu.VMEM(shape.shape, shape.dtype) for shape in far + backs + gots]
        + [
            pltpu.VMEM((ROWS_IN, SEG0), BF),
            pltpu.VMEM((ROWS_OUT, SEG0), BF),
            pltpu.VMEM((ROWS_OUT, SEG0), BF),
        ]
        + exchange_scratch()
        + [
            pltpu.VMEM((width // 128, rows, 128), F32),
            own_rows,
            own_rows,
            pltpu.VMEM((width, SEG0), BF),
            pltpu.SemaphoreType.DMA((2, 2, head_size - 1)),
            pltpu.SemaphoreType.DMA((len(far),)),
        ],
        compiler_params=pltpu.CompilerParams(
            vmem_limit_bytes=60 * 2**20, collective_id=0, has_side_effects=True
        ),
        cost_estimate=unit_cost(2 * heads, 2),
        name="forward",
    )(starts, tokens, cotangent, bits, gain, shift, in_proj)
    return results[:4], results[4 : len(far)], results[len(far)], results[len(far) + 1 :]


def backward_unit(x, g, q_aug, gk, gv, result, base, queries, tile):
    if isinstance(base, int):
        lanes = slice(base, base + queries)
    else:
        lanes = pl.ds(pl.multiple_of(base, 128), queries)
    extra = g[E:, lanes].astype(F32)
    ids = lax.broadcasted_iota(jnp.int32, extra.shape, 0)
    q = x[0:E, lanes]
    q_aug[0:E, :queries] = q
    q_aug[E:, :queries] = jnp.where(ids >= 12, extra, x[3 * E :, lanes].astype(F32) * -FAR).astype(BF)
    bits = x[3 * E :, :].astype(F32)
    k_aug = jnp.concatenate([x[E : 2 * E, :], (1.0 - bits).astype(BF)], axis=0)
    k_rows = k_aug.T
    v_ids = lax.broadcasted_iota(jnp.int32, bits.shape, 0)
    v_bits = jnp.where(v_ids < 3, 1.0, 0.0).astype(BF)
    v_rows = jnp.concatenate([x[2 * E : 3 * E, :], v_bits], axis=0).T
    q_rows = jnp.concatenate([q, jnp.zeros((BIT_ROWS, queries), BF)], axis=0).T
    g_all = g[:, lanes]
    g_rows = g_all.T
    if queries < SEG0:
        result[0:E, :] = jnp.zeros((E, SEG0), BF)
    for step in range(queries // tile):
        column = step * tile
        span = slice(column, column + tile)
        p = jnp.exp2(jnp.dot(k_rows, q_aug[:, span], preferred_element_type=F32))
        gs = p * jnp.dot(v_rows, g_all[:, span], preferred_element_type=F32)
        p, gs = p.astype(BF), gs.astype(BF)
        target = span if isinstance(base, int) else pl.ds(pl.multiple_of(base + column, 128), tile)
        result[0:E, target] = jnp.dot(k_aug, gs, preferred_element_type=F32)[:E].astype(BF)
        new_k = jnp.dot(gs, q_rows[span], preferred_element_type=F32)
        new_v = jnp.dot(p, g_rows[span], preferred_element_type=F32)
        if step == 0:
            gk[...] = new_k
            gv[...] = new_v
        else:
            gk[...] += new_k
            gv[...] += new_v
    result[E : 2 * E, :] = (gk[...].T[:E] * LN2).astype(BF)
    result[2 * E :, :] = gv[...].T[:E].astype(BF)


ORDERS = {
    'u1': (0, 1), 'u2': (0, 1), 'd1': (1, 0), 'd2': (1, 0), 'o': (0, 1), 'i0': (1, 0), 'i1': (1, 0), 'i2': (0,
    1),
}
EARLY = [
    (0, 'd1', 0), (0, 'u1', 0), (0, 'd1', 1), (0, 'u2', 0), (0, 'u1', 1), (2, 'o', 0), (4, 'u2', 1), (5, 'u1',
    2), (7, 'd1', 2), (9, 'u1', 3), (10, 'd2', 0), (12, 'd2', 1), (12, 'o', 1), (12, 'd1', 3), (13, 'u2', 2),
    (14, 'u1', 4),
]
TAIL = [
    'gather', ('d1', 4), 'in1', ('i1', 0), ('d2', 2), 'in2', ('u2', 3), ('i2', 0), 'in0', ('i0', 0), ('d2',
    3), ('i1', 1), ('i2', 1), ('u1', 5), ('u2', 4), ('d2', 4), ('d1', 5), ('o', 2), ('i2', 2), ('i0', 1),
    ('i1', 2), ('i2', 3), 'one', ('d2', 5), ('o', 3), ('i1', 3), ('u1', 6), ('u2', 5), 'norm', ('i2', 4),
    'gain0', ('i0', 2), ('i1', 4), ('i0', 3), 'gain1', ('o', 4), ('i0', 4), ('i2', 5), 'gain2', ('i1', 5),
    ('o', 5), ('i0', 5), 'gain3', ('i0', 6), ('d2', 6), ('u2', 6), 'gain4', ('d1', 6), ('i1', 6), ('i2', 6),
    ('o', 6),
]


def stream_names(streams):
    pairs = streams // 2
    return [kind + str(i + 1) for i in range(pairs) for kind in "ud"] + ["o"]


def backward_kernel(heads, streams, *refs):
    branches = BRANCHES - 1
    names = Names(refs)
    starts, gain, gains_two = names.take(3)
    sends = names.take(branches)
    far = names.take(branches + 6)
    parts = names.take(streams)
    far_totals, gains_out = names.take(5), names.one()
    near_totals, save_sem = names.take(5), names.one()
    up_total, down_total, out_total, in_total, grad_tokens = near_totals
    chunks = (streams - 1) // 2
    totals = []
    for chunk in range(chunks):
        lanes = pl.ds(chunk * (up_total.shape[-1] // chunks), up_total.shape[-1] // chunks)
        totals += [up_total.at[:, :, :, :, lanes], down_total.at[chunk]]
    totals.append(out_total)
    in_totals = [in_total.at[j] for j in range(3)]
    near = names.take(branches + 6)
    (own, own_g), units_in, (normed, in_proj, x_rows, grad_hidden) = near[:2], near[2:-4], near[-4:]
    far_sem = names.one()
    first = names.one()
    backs, gots, outs = names.take(branches), names.take(branches), names.take(branches)
    x, g, q_aug, gk, gv, result = names.take(6)
    total, grads, grads_t, normed_t, spread_rows, head_send, head_recv = names.take(7)
    gain_head, gain_one, gain_two, gain_rest = names.take(4)
    in_send, in_recv, in_local, out_send, out_recv, out_local = names.take(6)
    part_sem, head_sems, gain_sems = names.take(3)
    labels = stream_names(streams) + ["i0", "i1", "i2"]
    reductions = make_reductions(
        [ORDERS[label] for label in labels], list(totals) + list(in_totals), names.take(5 * streams + 15)
    )
    reductions = dict(zip(labels, reductions))
    for label in labels[: streams - 1]:
        reductions[label].begun = True

    shapes = [branch_shape(b, heads) for b in range(BRANCHES)]
    size, head_size = lax.axis_size("seq"), lax.axis_size("head")
    me, me_head = lax.axis_index("seq"), lax.axis_index("head")
    rest = size // 4
    tile = 512
    per_slot = x_rows.shape[0] // SLOTS
    width = x_rows.shape[1]


    def fill(s):
        target = reductions[labels[s]].half if s < streams - 1 else totals[-1]
        return pltpu.make_async_copy(parts[s], target, part_sem.at[s])

    def load(i):
        return pltpu.make_async_copy(far[i], near[i], far_sem.at[i])

    for s in range(streams):
        fill(s).start()
    for i in range(branches + 6):
        load(i).start()
    meet("seq", "head")

    def coming(branch):
        return group_copies(branch, sends[branch - 1], gots[branch - 1], in_send, in_recv, in_local)

    def leaving(branch):
        return group_copies(branch, outs[branch - 1], backs[branch - 1], out_send, out_recv, out_local)

    for branch in range(1, BRANCHES):
        for copy in coming(branch):
            copy.start()
    for i in range(2):
        load(i).wait()

    def advance(label, number):
        if label in labels[:streams] and number == (1 if reductions[label].begun else 0):
            fill(labels.index(label)).wait()
        reductions[label].step(number)

    def split_branch(branch):
        stride, lanes, units, split = shapes[branch]
        queries = SEG0 // split
        load(1 + branch).wait()
        for copy in coming(branch):
            copy.wait()
        load_unit(units_in[branch - 1], 0, lanes, x)
        load_unit(gots[branch - 1], 0, lanes, g)
        backward_unit(x, g, q_aug, gk, gv, result, me % split * queries, queries, min(tile, queries))
        store_unit(outs[branch - 1], 0, lanes, result)

    runs, at = [(0, 0, 0, heads // 2)], heads // 2
    split_at = None
    for branch in range(1, BRANCHES):
        if shapes[branch][3] == 1:
            runs.append((branch, at, 0, shapes[branch][2]))
            at += shapes[branch][2]
    split_at = at
    runs.append((0, at, heads // 2, heads - heads // 2))
    blocks = at + heads - heads // 2
    plan = {}
    for block, stream, step in EARLY:
        if stream in labels:
            plan.setdefault(block * blocks // 15, []).append((stream, step))

    @pl.loop(0, blocks)
    def _(block):
        for after, events in plan.items():

            @pl.when(block == after)
            def _(events=events):
                for stream, step in events:
                    advance(stream, step)

        @pl.when(block == split_at)
        def _():
            for branch in range(1, BRANCHES):
                if shapes[branch][3] > 1:
                    split_branch(branch)
                    for copy in leaving(branch):
                        copy.start()

        for branch, low, unit, count in runs:

            @pl.when((block >= low) & (block < low + count))
            def _(branch=branch, low=low, unit=unit):
                if branch == 0:
                    x[...] = own[0, block - low + unit]
                    g[...] = own_g[0, block - low + unit]
                else:

                    @pl.when(block == low)
                    def _():
                        load(1 + branch).wait()
                        for copy in coming(branch):
                            copy.wait()

                    load_unit(units_in[branch - 1], block - low, shapes[branch][1], x)
                    load_unit(gots[branch - 1], block - low, shapes[branch][1], g)

        backward_unit(x, g, q_aug, gk, gv, result, 0, SEG0, tile)
        for branch, low, unit, count in runs:

            @pl.when((block >= low) & (block < low + count))
            def _(branch=branch, low=low, unit=unit, count=count):
                if branch == 0:
                    first[block - low + unit] = result[...]
                else:
                    store_unit(outs[branch - 1], block - low, shapes[branch][1], result)

                    @pl.when(block == low + count - 1)
                    def _():
                        for copy in leaving(branch):
                            copy.start()

    def saves(index):
        return pltpu.make_async_copy(near_totals[index], far_totals[index], save_sem.at[index])

    def save(index):
        saves(index).start()

    tasks = {}

    def task(work):
        tasks[work.__name__] = work

    @task
    def gather():
        for i in range(4):
            load(branches + 2 + i).wait()
        for branch in range(1, BRANCHES):
            for copy in leaving(branch):
                copy.wait()

        @pl.loop(0, heads)
        def _(head):
            total[...] = first[head].astype(F32)
            for branch in range(1, BRANCHES):
                stride, lanes, per, split = shapes[branch]
                back, start = backs[branch - 1], reversed_bits(starts[branch, head], branch)
                if split == 1:
                    value = back[head // per, head % per].astype(F32)
                else:
                    value = back[head * split, 0].astype(F32)
                    for copy in range(1, split):
                        value = value + back[head * split + copy, 0].astype(F32)
                if lanes < 128:
                    value = unpacked(value, 3 * E, start % 2)
                    start = start // 2
                    lanes = 128
                for block in range(SEG0 // lanes):
                    span = slice(block * lanes, (block + 1) * lanes)
                    total[:, span] += jnp.where(start == block, value, 0.0)
            grads[0, head] = (total[0:E, :] * E ** (-0.5)).astype(BF)
            grads[1, head] = total[E : 2 * E, :].astype(BF)
            grads[2, head] = total[2 * E :, :].astype(BF)

        normed_t[...] = normed[...].reshape(SEG0, width).T

    def in_gradient(j):
        rows_in = in_totals[0].shape[3]
        chunk = width // 2
        grads_t[j] = grads[j].reshape(heads * E, SEG0).T
        for half in range(2):
            value = jnp.dot(
                normed_t[half * chunk : (half + 1) * chunk], grads_t[j], preferred_element_type=F32
            ).astype(BF)
            for part in range(chunk // rows_in):
                index = half * (chunk // rows_in) + part
                in_totals[j][index // (2 * rest), index // rest % 2, index % rest] = value[
                    part * rows_in : (part + 1) * rows_in
                ]

    for j in range(3):
        tasks[f"in{j}"] = partial(in_gradient, j)

    def head_swaps():
        swaps = []
        for step in range(1, head_size):
            device = (me_head + step) % head_size
            swaps.append(
                pltpu.make_async_remote_copy(
                    src_ref=head_send.at[device],
                    dst_ref=head_recv.at[step - 1],
                    send_sem=head_sems.at[0, step - 1],
                    recv_sem=head_sems.at[1, step - 1],
                    device_id={"head": device},
                    device_id_type=pl.DeviceIdType.MESH,
                )
            )
        return swaps

    @task
    def one():
        for half in range(2):
            rows = slice(half * SEG0 // 2, (half + 1) * SEG0 // 2)
            value = jnp.zeros((SEG0 // 2, width), F32)
            for j in range(3):
                value = value + lax.dot_general(
                    grads_t[j, rows], in_proj[j], (((1,), (1,)), ((), ())), preferred_element_type=F32
                )
            value = value.astype(BF)
            for slot in range(SLOTS // 2):
                for device in range(head_size):
                    begin = (slot * head_size + device) * per_slot
                    place = (half * SLOTS // 2 + slot) * per_slot
                    head_send[device, place : place + per_slot] = value[begin : begin + per_slot]
        for swap in head_swaps():
            swap.start()

    @task
    def norm():
        for swap in head_swaps():
            swap.wait()
        gain_head[me_head] = jnp.zeros(gains_out.shape, F32)
        gain_head[me_head, 2:4] = gains_two[...]

        @pl.loop(0, SLOTS)
        def _(slot):
            rows = pl.ds(pl.multiple_of(slot * per_slot, per_slot), per_slot)
            grad = head_send[me_head, rows].astype(F32)
            for step in range(1, head_size):
                grad = grad + head_recv[step - 1, rows].astype(F32)
            values = x_rows[rows]
            centred = values - jnp.mean(values, axis=-1, keepdims=True)
            scale = lax.rsqrt(jnp.mean(centred * centred, axis=-1, keepdims=True) + EPS)
            unit = centred * scale
            scaled = grad * gain[...][None]
            inner = jnp.mean(scaled * unit, axis=-1, keepdims=True)
            out = grad_hidden[rows] + scale * (
                scaled - jnp.mean(scaled, axis=-1, keepdims=True) - unit * inner
            )
            place = slot_place(slot)
            for column in range(width // 128):
                lanes = slice(column * 128, (column + 1) * 128)
                spread_rows[column, pl.ds(place, per_slot, stride=SLOTS), :] = out[:, lanes]
            gain_head[me_head, 0:1] += jnp.sum(grad * unit, axis=0, keepdims=True)
            gain_head[me_head, 1:2] += jnp.sum(grad, axis=0, keepdims=True)

        for column in range(width // 128):
            grad_tokens[:, column * 128 : (column + 1) * 128] = spread_rows[column]
        save(4)

    def gain_copy(source, target, axis, device, sem):
        return pltpu.make_async_remote_copy(
            src_ref=source,
            dst_ref=target,
            send_sem=gain_sems.at[0, sem],
            recv_sem=gain_sems.at[1, sem],
            device_id={axis: device},
            device_id_type=pl.DeviceIdType.MESH,
        )

    def gain_copies(stage):
        if stage == 0:
            mine = gain_head.at[me_head]
            return [
                gain_copy(mine, mine, "head", (me_head + step) % head_size, step - 1)
                for step in range(1, head_size)
            ]
        if stage == 1:
            return [gain_copy(gain_one.at[0], gain_one.at[1], "seq", me + 1 - 2 * (me % 2), head_size)]
        if stage == 2:
            device = me + 2 - 4 * (me // 2 % 2)
            return [gain_copy(gain_two.at[0], gain_two.at[1], "seq", device, head_size + 1)]
        spot = me // 4
        block = gain_rest.at[spot]
        return [
            gain_copy(block, block, "seq", (spot + step) % rest * 4 + me % 4, head_size + 1 + step)
            for step in range(1, rest)
        ]

    def summed(ref, count):
        value = ref[0]
        for index in range(1, count):
            value = value + ref[index]
        return value

    def gain_stage(stage):
        if stage > 0:
            for swap in gain_copies(stage - 1):
                swap.wait()
        if stage == 1:
            gain_one[0] = summed(gain_head, head_size)
        elif stage == 2:
            gain_two[0] = summed(gain_one, 2)
        elif stage == 3:
            gain_rest[me // 4] = summed(gain_two, 2)
        elif stage == 4:
            gains_out[...] = summed(gain_rest, rest)
            return
        for swap in gain_copies(stage):
            swap.start()

    for stage in range(5):
        tasks[f"gain{stage}"] = partial(gain_stage, stage)

    groups = [[], [], ["o"], ["i0", "i1", "i2"]]
    for chunk in range(chunks):
        groups[0].append(labels[2 * chunk])
        groups[1].append(labels[2 * chunk + 1])
    for item in TAIL:
        if isinstance(item, str):
            tasks[item]()
        elif item[0] in labels:
            advance(item[0], item[1])
            if item[1] == Reduction.STEPS - 1:
                for index, group in enumerate(groups):
                    if item[0] in group:
                        group.remove(item[0])
                        if not group:
                            save(index)
    for index in range(5):
        saves(index).wait()


def backward(heads, starts, own, own_g, units, sends, parts, normed, in_proj, x_rows, grad_hidden, gain, gains_two):
    size, head_size = lax.axis_size("seq"), lax.axis_size("head")
    rest = size // 4
    rows, width = x_rows.shape
    in_shape = (2, 2, rest, width // size, heads * E)
    scratch = []
    for part in parts:
        scratch += Reduction.scratch(size, *part.shape[-2:])
    for _ in range(3):
        scratch += Reduction.scratch(size, *in_shape[-2:])
    streams = len(parts)
    chunks = (streams - 1) // 2
    far = [own, own_g] + list(units) + [normed, in_proj, x_rows, grad_hidden]
    totals = [
        jax.ShapeDtypeStruct((2, 2, rest, width // size, chunks * parts[0].shape[-1]), BF),
        jax.ShapeDtypeStruct((chunks, 2, 2, rest) + parts[1].shape[-2:], BF),
        jax.ShapeDtypeStruct(parts[-1].shape, BF),
        jax.ShapeDtypeStruct((3,) + in_shape, BF),
        jax.ShapeDtypeStruct((rows, width), F32),
    ]
    results = pl.pallas_call(
        partial(backward_kernel, heads, streams),
        in_specs=[pl.BlockSpec(memory_space=pltpu.SMEM)]
        + vmem_specs(2)
        + [pl.BlockSpec(memory_space=pl.ANY)] * (len(sends) + len(far) + streams),
        out_specs=[pl.BlockSpec(memory_space=pl.ANY)] * len(totals) + vmem_specs(1),
        out_shape=totals + [jax.ShapeDtypeStruct((8, width), F32)],
        scratch_shapes=[pltpu.VMEM(value.shape, value.dtype) for value in totals]
        + [pltpu.SemaphoreType.DMA((len(totals),))]
        + [pltpu.VMEM(value.shape, value.dtype) for value in far]
        + [pltpu.SemaphoreType.DMA((len(far),)), pltpu.VMEM((heads, 3 * E, SEG0), BF)]
        + [pltpu.VMEM(shape.shape, BF) for shape in send_shapes(heads, 3 * E)]
        + [pltpu.VMEM(shape.shape, BF) for shape in send_shapes(heads, ROWS_OUT)]
        + [pltpu.VMEM(shape.shape, BF) for shape in send_shapes(heads, 3 * E)]
        + [
            pltpu.VMEM((ROWS_IN, SEG0), BF),
            pltpu.VMEM((ROWS_OUT, SEG0), BF),
            pltpu.VMEM((ROWS_OUT, SEG0), BF),
            pltpu.VMEM((SEG0, ROWS_OUT), F32),
            pltpu.VMEM((SEG0, ROWS_OUT), F32),
            pltpu.VMEM((3 * E, SEG0), BF),
            pltpu.VMEM((3 * E, SEG0), F32),
            pltpu.VMEM((3, heads, E, SEG0), BF),
            pltpu.VMEM((3, SEG0, heads * E), BF),
            pltpu.VMEM((width, SEG0), BF),
            pltpu.VMEM((width // 128, rows, 128), F32),
            pltpu.VMEM((head_size, rows, width), BF),
            pltpu.VMEM((head_size - 1, rows, width), BF),
            pltpu.VMEM((head_size, 8, width), F32),
            pltpu.VMEM((2, 8, width), F32),
            pltpu.VMEM((2, 8, width), F32),
            pltpu.VMEM((rest, 8, width), F32),
        ]
        + exchange_scratch()
        + [
            pltpu.SemaphoreType.DMA((streams,)),
            pltpu.SemaphoreType.DMA((2, head_size - 1)),
            pltpu.SemaphoreType.DMA((2, head_size + 1 + rest)),
        ]
        + scratch,
        compiler_params=pltpu.CompilerParams(
            vmem_limit_bytes=60 * 2**20, collective_id=1, has_side_effects=True
        ),
        cost_estimate=unit_cost(2 * heads, 5),
        name="backward",
    )(starts, gain, gains_two, *sends, *far, *parts)
    up_total, down_total, out_total, in_total = results[:4]
    sums = [
        in_total.reshape(3, width, heads * E),
        out_total.reshape(-1, width),
        up_total.reshape(width, -1),
        down_total.reshape(-1, width),
    ]
    return sums, results[4], results[5]


def finish_kernel(gains, *refs):
    count = (len(refs) - 4) // 2
    for source, target in zip(refs[:count], refs[count : 2 * count]):
        target[...] = source[...].astype(target.dtype)
    for index in range(4):
        refs[2 * count + index][...] = gains[index]


def finish(values, types, gains):
    steps = 2
    specs = []
    for value in values:
        shape = list(value.shape)
        shape[-2] //= steps
        if value.ndim == 3:
            specs.append(pl.BlockSpec(tuple(shape), lambda i: (0, i, 0)))
        else:
            specs.append(pl.BlockSpec(tuple(shape), lambda i: (i, 0)))
    return pl.pallas_call(
        finish_kernel,
        grid=(steps,),
        in_specs=[pl.BlockSpec(gains.shape, lambda i: (0, 0))] + specs,
        out_specs=specs + [pl.BlockSpec(gains.shape[1:], lambda i: (0,))] * 4,
        out_shape=[jax.ShapeDtypeStruct(value.shape, kind) for value, kind in zip(values, types)]
        + [jax.ShapeDtypeStruct(gains.shape[1:], F32)] * 4,
        compiler_params=pltpu.CompilerParams(vmem_limit_bytes=61 * 2**20),
        name="finish",
    )(gains, *values)


def middle_kernel(heads, *refs):
    branches = BRANCHES - 1
    names = Names(refs)
    starts, first = names.take(2)
    backs = names.take(branches)
    gain, shift = names.take(2)
    far = names.take(5)
    chunks = max(1, far[3].shape[1] // far[0].shape[1])
    saved = 4 + branches + 2 * chunks
    far_results, gains_two = names.take(saved), names.one()
    near_results, save_sem = names.take(saved), names.one()
    block_out, grad_hidden, own_g, out_total = near_results[:4]
    sends, halves = near_results[4 : 4 + branches], near_results[4 + branches :]
    saves = [pltpu.make_async_copy(near_results[i], far_results[i], save_sem.at[i]) for i in range(saved)]
    merged, lse, mixed, turned, part, got, part_two, got_two = names.take(8)
    hidden_one, normed_own, normed, spread_rows, normed_t = names.take(5)
    down_sum, norm_sum, up_grad, down_grad, totals = names.take(5)
    head_sems, first_sems, far_sem = names.take(3)
    near = names.take(5)
    out_proj, x_rows, cot, up, down = near[2], near[0], near[1], near[3], near[4]
    loads = [pltpu.make_async_copy(far[i], near[i], far_sem.at[i]) for i in range(5)]
    for i in (2, 0, 1, 3, 4):
        loads[i].start()

    head_size, me_head = lax.axis_size("head"), lax.axis_index("head")
    me = lax.axis_index("seq")
    rest = lax.axis_size("seq") // 4
    width = x_rows.shape[1]
    per_slot = x_rows.shape[0] // SLOTS
    tile = 256

    meet("seq", "head")

    @pl.loop(0, heads)
    def _(head):
        own = first[0, head].astype(F32)
        merged[head] = own[:E]
        lse[head] = own[E : E + 1] + own[E + 1 : E + 2] + own[E + 2 : E + 3]
        for branch in range(1, BRANCHES):
            stride, lanes, per, split = branch_shape(branch, heads)
            back, start = backs[branch - 1], reversed_bits(starts[branch, head], branch)
            share = max(1, 128 // lanes)
            for copy in range(split):
                if split == 1:
                    value = back[head // per, head % per].astype(F32)
                else:
                    value = back[head * split + copy, 0].astype(F32)
                if share > 1:
                    value = unpacked(value, ROWS_OUT, start % share)
                new_lse = value[E : E + 1] + value[E + 1 : E + 2] + value[E + 2 : E + 3]
                if share > 1:
                    ids = lax.broadcasted_iota(jnp.int32, new_lse.shape, 1)
                    new_lse = jnp.where(ids // lanes == start % share, new_lse, -FAR)
                span = lanes * share
                for block in range(SEG0 // span):
                    at = slice(block * span, (block + 1) * span)
                    new = jnp.where(start // share == block, new_lse, -FAR)
                    old = lse[head, :, at]
                    top = jnp.maximum(old, new)
                    both = top + jnp.log2(jnp.exp2(old - top) + jnp.exp2(new - top))
                    lse[head, :, at] = both
                    merged[head, :, at] = merged[head, :, at] * jnp.exp2(old - both) + value[:E] * jnp.exp2(
                        new - both
                    )
        mixed[head] = merged[head].astype(BF)

    def rows_of(ref):
        return ref[...].reshape(SEG0, width)

    turned[...] = mixed[...].reshape(heads * E, SEG0).T
    loads[2].wait()
    for step in range(SEG0 // tile):
        at = slice(step * tile // (head_size * per_slot), (step + 1) * tile // (head_size * per_slot))
        value = jnp.dot(turned[step * tile : (step + 1) * tile], out_proj[...], preferred_element_type=F32)
        part[at] = value.astype(BF).reshape(-1, head_size, per_slot, width)
    for copy in head_copies(part, got, head_sems, 0, True):
        copy.start()
    for ref in (down_sum, norm_sum, up_grad, down_grad):
        ref[...] = jnp.zeros_like(ref)
    loads[0].wait()
    for copy in head_copies(part, got, head_sems, 0, True):
        copy.wait()

    def rows_at(slot):
        return pl.ds(pl.multiple_of(slot * per_slot, per_slot), per_slot)

    @over_slots
    def _(slot):
        value = x_rows[rows_at(slot)] + part[slot, me_head].astype(F32)
        for step in range(1, head_size):
            value = value + got[step - 1, slot].astype(F32)
        hidden_one[rows_at(slot)] = value
        unit, scale = norm_of(value)
        low = (unit * gain[...][None] + shift[...][None]).astype(BF)
        normed_own[slot] = low
        normed[slot, me_head] = low

    for copy in head_copies(normed_own, normed, head_sems, 1, False):
        copy.start()
    for copy in head_copies(normed_own, normed, head_sems, 1, False):
        copy.wait()
    normed_t[...] = rows_of(normed).T
    for i in (1, 3, 4):
        loads[i].wait()

    chunk_width = up.shape[1] // chunks
    orders = {0: ORDERS["u1"], 1: ORDERS["d1"]}
    firsts = []
    for chunk in range(chunks):
        for kind in range(2):
            index = 2 * chunk + kind
            firsts.append(
                Reduction(
                    orders[kind], totals.at[index], halves[index], None, None,
                    first_sems.at[0, pl.ds(index, 1)], first_sems.at[1, pl.ds(index, 1)],
                )
            )
    slots = tile // (head_size * per_slot)
    contract_last = (((1,), (1,)), ((), ()))

    for chunk in range(chunks):
        units = slice(chunk * chunk_width, (chunk + 1) * chunk_width)
        if chunk > 0:
            up_grad[...] = jnp.zeros_like(up_grad)
            down_grad[...] = jnp.zeros_like(down_grad)

        @pl.loop(0, SEG0 // tile)
        def _(step):
            rows = pl.ds(pl.multiple_of(step * tile, tile), tile)
            low = normed[pl.ds(step * slots, slots)].reshape(tile, width)
            back = cot[pl.ds(step * slots, slots)].reshape(tile, width)
            pre = jnp.dot(low, up[:, units], preferred_element_type=F32)
            grad = lax.dot_general(back, down[units], contract_last, preferred_element_type=F32)
            share = 0.5 + 0.5 * lax.erf(pre * math.sqrt(0.5))
            density = jnp.exp2(pre * pre * (-0.5 * LOG2E)) * (1.0 / math.sqrt(2.0 * math.pi))
            hidden = (pre * share).astype(BF)
            grad = (grad * (share + pre * density)).astype(BF)
            down_sum[rows] += jnp.dot(hidden, down[units], preferred_element_type=F32)
            norm_sum[rows] += lax.dot_general(grad, up[:, units], contract_last, preferred_element_type=F32)
            up_grad[...] += jnp.dot(normed_t[:, rows], grad, preferred_element_type=F32)
            down_grad[...] += jnp.dot(hidden.T, back, preferred_element_type=F32)

        pieces = totals.shape[3] * 4
        size = totals.shape[4]
        for piece in range(pieces):
            spot = (piece // (2 * rest), piece // rest % 2, piece % rest)
            span = slice(piece * size, (piece + 1) * size)
            totals[(2 * chunk,) + spot] = up_grad[span].astype(BF)
            totals[(2 * chunk + 1,) + spot] = down_grad[span].astype(BF)
        firsts[2 * chunk].step(0)
        firsts[2 * chunk + 1].step(0)

    for ref, value in ((part, down_sum), (part_two, norm_sum)):

        @pl.loop(0, SLOTS)
        def _(slot):
            for device in range(head_size):
                begin = pl.multiple_of((slot * head_size + device) * per_slot, per_slot)
                ref[slot, device] = value[pl.ds(begin, per_slot)].astype(BF)

    for copy in head_copies(part_two, got_two, head_sems, 2, True) + head_copies(part, got, head_sems, 3, True):
        copy.start()
    for copy in head_copies(part_two, got_two, head_sems, 2, True):
        copy.wait()
    gains_two[...] = jnp.zeros_like(gains_two)

    @over_slots
    def _(slot):
        grad = part_two[slot, me_head].astype(F32)
        for step in range(1, head_size):
            grad = grad + got_two[step - 1, slot].astype(F32)
        unit, scale = norm_of(hidden_one[rows_at(slot)])
        scaled = grad * gain[...][None]
        inner = jnp.mean(scaled * unit, axis=-1, keepdims=True)
        out = cot[slot, me_head].astype(F32) + scale * (
            scaled - jnp.mean(scaled, axis=-1, keepdims=True) - unit * inner
        )
        grad_hidden[rows_at(slot)] = out
        normed_own[slot] = out.astype(BF)
        normed[slot, me_head] = out.astype(BF)
        gains_two[0:1] += jnp.sum(grad * unit, axis=0, keepdims=True)
        gains_two[1:2] += jnp.sum(grad, axis=0, keepdims=True)

    for copy in head_copies(normed_own, normed, head_sems, 4, False):
        copy.start()
    saves[1].start()
    for copy in head_copies(part, got, head_sems, 3, True):
        copy.wait()

    @pl.loop(0, SLOTS)
    def _(slot):
        value = hidden_one[rows_at(slot)] + part[slot, me_head].astype(F32)
        for step in range(1, head_size):
            value = value + got[step - 1, slot].astype(F32)
        place = slot_place(slot)
        for column in range(width // 128):
            lanes = slice(column * 128, (column + 1) * 128)
            spread_rows[column, pl.ds(place, per_slot, stride=SLOTS), :] = value[:, lanes]

    for column in range(width // 128):
        block_out[:, column * 128 : (column + 1) * 128] = spread_rows[column].astype(BF)
    saves[0].start()
    for copy in head_copies(normed_own, normed, head_sems, 4, False):
        copy.wait()

    value = jnp.dot(mixed[...].reshape(heads * E, SEG0), rows_of(normed), preferred_element_type=F32)
    size = out_total.shape[3]
    for piece in range(4 * rest):
        spot = (piece // (2 * rest), piece // rest % 2, piece % rest)
        out_total[spot] = value[piece * size : (piece + 1) * size].astype(BF)
    saves[3].start()

    normed_t[...] = rows_of(normed).T
    value = jnp.dot(out_proj[...], normed_t[...], preferred_element_type=F32)
    own_g[0, :, :E, :] = value.astype(BF).reshape(heads, E, SEG0)

    @pl.loop(0, heads)
    def _(head):
        low = own_g[0, head, :E, :]
        dots = jnp.sum(low.astype(F32) * merged[head], axis=0, keepdims=True)
        d = pieces_of(-dots)
        m = pieces_of(-lse[head])
        placed = {0: d[0], 1: d[1], 2: d[2], 12: m[0], 13: m[1], 14: m[2]}
        own_g[0, head, E:, :] = row_block(placed, SEG0).astype(BF)
        own = jnp.concatenate([low.astype(F32), row_block(placed, SEG0)], axis=0)
        spread_blocks(heads, head, starts, own, sends)

    for index in [2] + list(range(4, 4 + branches)):
        saves[index].start()
    for index, reduction in enumerate(firsts):
        reduction.finish_first()
        saves[4 + branches + index].start()
    for copy in saves:
        copy.wait()


def middle(heads, starts, first, backs, x_rows, cot, out_proj, up, down, gain, shift):
    size, head_size = lax.axis_size("seq"), lax.axis_size("head")
    rest = size // 4
    rows, width = x_rows.shape
    per_slot = rows // SLOTS
    chunks = max(1, up.shape[1] // width)
    shard = (SLOTS, head_size, per_slot, width)
    own = (SLOTS, per_slot, width)
    got = (head_size - 1,) + own
    sends = send_shapes(heads, ROWS_OUT)
    piece = (2, rest, width // size, up.shape[1] // chunks)
    out_piece = (2, 2, rest, heads * E // size, width)
    far = [x_rows, cot, out_proj, up, down]
    saved = [
        jax.ShapeDtypeStruct((rows, width), BF),
        jax.ShapeDtypeStruct((rows, width), F32),
        jax.ShapeDtypeStruct((1, heads, ROWS_OUT, SEG0), BF),
        jax.ShapeDtypeStruct(out_piece, BF),
    ]
    saved += sends + [jax.ShapeDtypeStruct(piece, BF)] * (2 * chunks)
    results = pl.pallas_call(
        partial(middle_kernel, heads),
        in_specs=[pl.BlockSpec(memory_space=pltpu.SMEM)]
        + vmem_specs(1 + len(backs) + 2)
        + [pl.BlockSpec(memory_space=pl.ANY)] * 5,
        out_specs=[pl.BlockSpec(memory_space=pl.ANY)] * len(saved) + vmem_specs(1),
        out_shape=saved + [jax.ShapeDtypeStruct((2, width), F32)],
        scratch_shapes=[pltpu.VMEM(value.shape, value.dtype) for value in saved]
        + [pltpu.SemaphoreType.DMA((len(saved),))]
        + [
            pltpu.VMEM((heads, E, SEG0), F32),
            pltpu.VMEM((heads, 1, SEG0), F32),
            pltpu.VMEM((heads, E, SEG0), BF),
            pltpu.VMEM((SEG0, heads * E), BF),
            pltpu.VMEM(shard, BF),
            pltpu.VMEM(got, BF),
            pltpu.VMEM(shard, BF),
            pltpu.VMEM(got, BF),
            pltpu.VMEM((rows, width), F32),
            pltpu.VMEM(own, BF),
            pltpu.VMEM(shard, BF),
            pltpu.VMEM((width // 128, rows, 128), F32),
            pltpu.VMEM((width, SEG0), BF),
            pltpu.VMEM((SEG0, width), F32),
            pltpu.VMEM((SEG0, width), F32),
            pltpu.VMEM((width, up.shape[1] // chunks), F32),
            pltpu.VMEM((up.shape[1] // chunks, width), F32),
            pltpu.VMEM((2 * chunks, 2) + piece, BF),
            pltpu.SemaphoreType.DMA((2, 5, head_size - 1)),
            pltpu.SemaphoreType.DMA((2, 2 * chunks)),
            pltpu.SemaphoreType.DMA((5,)),
        ]
        + [pltpu.VMEM(value.shape, value.dtype) for value in far],
        compiler_params=pltpu.CompilerParams(
            vmem_limit_bytes=60 * 2**20, collective_id=2, has_side_effects=True
        ),
        cost_estimate=pl.CostEstimate(
            flops=14 * SEG0 * width * up.shape[1], transcendentals=0, bytes_accessed=40 * 2**20
        ),
        name="middle",
    )(starts, first, *backs, gain, shift, *far)
    block_out, grad_hidden, own_g, out_total = results[:4]
    sends, halves = results[4 : 4 + len(sends)], results[4 + len(sends) : -1]
    return block_out, grad_hidden, results[-1], own_g, sends, list(halves) + [out_total]


def local(
    tokens,
    documents,
    offsets,
    in_proj,
    out_proj,
    up_proj,
    down_proj,
    first_gain,
    first_shift,
    second_gain,
    second_shift,
    cotangent,
):
    head_count = lax.axis_size("head")
    seq_id = lax.axis_index("seq")
    row_count = tokens.shape[0]
    seq_len = row_count * head_count
    heads = offsets.shape[1]
    per_slot = row_count // SLOTS

    my_docs = lax.dynamic_slice_in_dim(documents, seq_id * seq_len, seq_len)
    my_docs = my_docs.reshape(head_count, per_slot, 2, 2, 2, 2).transpose(5, 4, 3, 2, 0, 1).reshape(seq_len)
    bit_ids = jnp.arange(BIT_ROWS, dtype=jnp.int32)[:, None]
    doc_bit = my_docs[None, :] // 2 ** (bit_ids % DOC_BITS) % 2
    bits = jnp.where(bit_ids < DOC_BITS, doc_bit, jnp.where(bit_ids < 2 * DOC_BITS, 1 - doc_bit, 0))
    bits = bits.astype(BF)

    (x_rows, normed, cot_all, own), units, first_out, outs = forward(
        heads, offsets, tokens, cotangent, bits, first_gain, first_shift, in_proj
    )
    block_out, grad_hidden, gains_two, own_g, sends_g, parts = middle(
        heads, offsets, first_out, outs, x_rows, cot_all, out_proj, up_proj, down_proj, second_gain, second_shift
    )
    sums, grad_tokens, gains = backward(
        heads, offsets, own, own_g, units, sends_g, parts,
        normed, in_proj, x_rows, grad_hidden, first_gain, gains_two,
    )
    return tuple(finish([block_out, grad_tokens] + sums, [BF] + [F32] * 5, gains))


def solution(mesh):
    placed = (
        P(("seq", "head"), None),
        P(),
        P(None, "head"),
        P(None, None, "head"),
        P("head", None),
        P(None, "head"),
        P("head", None),
        P(),
        P(),
        P(),
        P(),
        P(("seq", "head"), None),
    )
    return jax.shard_map(
        local,
        mesh=mesh,
        in_specs=placed,
        out_specs=(
            P(("seq", "head"), None),
            P(("seq", "head"), None),
            P(None, None, "head"),
            P("head", None),
            P(None, "head"),
            P("head", None),
            P(),
            P(),
            P(),
            P(),
        ),
        check_vma=False,
    )
```

```python
import math
from functools import partial

import jax
import jax.numpy as jnp
from jax import lax
from jax.experimental import pallas as pl
from jax.experimental.pallas import tpu as pltpu
from jax.sharding import PartitionSpec as P

E = 48
BRANCHES = 5
SEG0 = 1024
SLOTS = 16
BIT_ROWS = 16
DOC_BITS = 6
ROWS_IN = 3 * E + BIT_ROWS
ROWS_OUT = E + BIT_ROWS
EPS = 1e-05
FAR = 1e30
LOG2E = math.log2(math.e)
LN2 = math.log(2.0)
BF = jnp.bfloat16
F32 = jnp.float32
VMEM_LIMIT = 48 * 2**20


def reversed_bits(value, count):
    out = value % 2
    for bit in range(1, count):
        out = out * 2 + value // 2**bit % 2
    return out


def branch_shape(branch, heads):
    stride = 2**branch
    return (stride, SEG0 // stride, max(1, heads // stride), max(1, stride // heads))


def pieces_of(value):
    high = value.astype(BF).astype(F32)
    rest = value - high
    middle = rest.astype(BF).astype(F32)
    return high, middle, (rest - middle).astype(BF).astype(F32)


def row_block(placed, columns):
    ids = lax.broadcasted_iota(jnp.int32, (BIT_ROWS, columns), 0)
    block = jnp.zeros((BIT_ROWS, columns), F32)
    for row, value in placed.items():
        block = jnp.where(ids == row, value, block)
    return block


def turned_half(block):
    return jnp.concatenate([block[:, 64:], block[:, :64]], axis=1)


def low_half():
    return lax.broadcasted_iota(jnp.int32, (1, 128), 1) < 64


def packed_rows(rows, count):
    return rows if count >= 128 else (rows // 2 + 15) // 16 * 16


def packed(block, half):
    rows = packed_rows(block.shape[0], 64)
    upper, lower = block[:rows], block[block.shape[0] - rows :]
    if isinstance(half, int):
        return jnp.where(low_half(), turned_half(upper) if half else upper, lower if half else turned_half(lower))
    upper = jnp.where(half == 0, upper, turned_half(upper))
    lower = jnp.where(half == 0, turned_half(lower), lower)
    return jnp.where(low_half(), upper, lower)


def unpacked(value, rows, half):
    size = value.shape[0]
    other = turned_half(value)
    upper = jnp.where(half == 0, value, other)
    lower = jnp.where(half == 0, other, value)
    both = jnp.concatenate([upper, lower[2 * size - rows :]], axis=0)
    return jnp.where(low_half() == (half == 0), both, 0.0)


def send_shapes(heads, rows):
    outs = []
    for branch in range(1, BRANCHES):
        stride, count, per, split = branch_shape(branch, heads)
        outs.append(jax.ShapeDtypeStruct((stride, per, packed_rows(rows, count), max(count, 128)), BF))
    return outs


def spread_blocks(heads, head, starts, value, sends, branches=range(1, BRANCHES)):
    for branch in branches:
        stride, lanes, per, split = branch_shape(branch, heads)
        send, start = sends[branch - 1], reversed_bits(starts[branch, head], branch)
        share = max(1, 128 // lanes)
        span = lanes * share
        block = value[:, :span]
        for part in range(1, SEG0 // span):
            block = jnp.where(start // share == part, value[:, part * span : (part + 1) * span], block)
        if share > 1:
            block = packed(block, start % share)
        block = block.astype(BF)
        if split == 1:
            send[head // per, head % per] = block
        else:
            for copy in range(split):
                send[head * split + copy, 0] = block


def norm_of(values):
    centred = values - jnp.mean(values, axis=-1, keepdims=True)
    scale = lax.rsqrt(jnp.mean(centred * centred, axis=-1, keepdims=True) + EPS)
    return centred * scale, scale


def slot_place(slot):
    return slot % 2 * 8 + slot // 2 % 2 * 4 + slot // 4 % 2 * 2 + slot // 8


def over_slots(body, unroll=4):
    @pl.loop(0, SLOTS // unroll)
    def _(step):
        for part in range(unroll):
            body(step * unroll + part)


def head_copies(source, target, sems, index, scatter):
    size, me = lax.axis_size("head"), lax.axis_index("head")
    copies = []
    for step in range(1, size):
        device = (me + step) % size
        copies.append(
            pltpu.make_async_remote_copy(
                src_ref=source.at[:, device] if scatter else source,
                dst_ref=target.at[step - 1] if scatter else target.at[:, me],
                send_sem=sems.at[0, index, step - 1],
                recv_sem=sems.at[1, index, step - 1],
                device_id={"head": device},
                device_id_type=pl.DeviceIdType.MESH,
            )
        )
    return copies


def load_unit(ref, unit, count, x):
    width = ref.shape[-1]
    if count >= 128:
        for block in range(ref.shape[0]):
            x[:, block * width : (block + 1) * width] = ref[block, unit]
        return
    rows, size = x.shape[0], ref.shape[2]
    for block in range(ref.shape[0] // 2):
        lanes = slice(block * 128, (block + 1) * 128)
        left = ref[2 * block, unit].astype(F32)
        right = ref[2 * block + 1, unit].astype(F32)
        x[:size, lanes] = jnp.where(low_half(), left, turned_half(right)).astype(BF)
        x[rows - size :, lanes] = jnp.where(low_half(), turned_half(left), right).astype(BF)


def store_unit(ref, unit, count, result):
    width = ref.shape[-1]
    for block in range(SEG0 // width):
        value = result[:, block * width : (block + 1) * width]
        if count >= 128:
            ref[block, unit] = value
        else:
            value = value.astype(F32)
            ref[2 * block, unit] = packed(value, 0).astype(BF)
            ref[2 * block + 1, unit] = packed(value, 1).astype(BF)


def forward_unit(x, q_aug, result, base, queries):
    if isinstance(base, int):
        lanes = slice(base, base + queries)
    else:
        lanes = pl.ds(pl.multiple_of(base, 128), queries)
    q_aug[0:E, :queries] = x[0:E, lanes]
    q_aug[E:, :queries] = (x[3 * E :, lanes].astype(F32) * -FAR).astype(BF)
    bits = x[3 * E :, :].astype(F32)
    k_rows = jnp.concatenate([x[E : 2 * E, :], (1.0 - bits).astype(BF)], axis=0).T
    v_aug = jnp.concatenate([x[2 * E : 3 * E, :], jnp.ones(bits.shape, BF)], axis=0)
    if queries < SEG0:
        result[0:E, :] = jnp.zeros((E, SEG0), BF)
        result[E:, :] = row_block({0: -FAR}, SEG0).astype(BF)
    s = jnp.dot(k_rows, q_aug[:, :queries], preferred_element_type=F32)
    top = jnp.max(s, axis=0, keepdims=True)
    p = jnp.exp2(s - top).astype(BF)
    o = jnp.dot(v_aug, p, preferred_element_type=F32)
    total = o[E : E + 1]
    high, middle_part, low = pieces_of(top + jnp.log2(total))
    block = row_block({0: high, 1: middle_part, 2: low}, queries)
    result[:, lanes] = jnp.concatenate([o[:E] * (1.0 / total), block], axis=0).astype(BF)


class Names:
    def __init__(self, refs):
        self.refs = list(refs)

    def take(self, count):
        taken, self.refs = self.refs[:count], self.refs[count:]
        return taken

    def one(self):
        return self.take(1)[0]


def group_place(branch):
    stride = 2**branch
    me = lax.axis_index("seq")
    return me // stride * stride, me % stride


def meet(*axes):
    barrier = pltpu.get_barrier_semaphore()
    count = 0
    for axis in axes:
        size = lax.axis_size(axis)
        me = lax.axis_index(axis)

        @pl.loop(1, size)
        def _(step):
            pl.semaphore_signal(
                barrier, inc=1, device_id={axis: (me + step) % size}, device_id_type=pl.DeviceIdType.MESH
            )

        count += size - 1
    pl.semaphore_wait(barrier, count)


class Reduction:
    STEPS = 7

    def __init__(self, order, total, half, quarter, others, send, recv, begun=False):
        self.total, self.begun = total, begun
        self.half, self.quarter, self.others = half, quarter, others
        self.send, self.recv = send, recv
        me = lax.axis_index("seq")
        self.rest = lax.axis_size("seq") // 4
        self.me = me
        bits = (me % 2, me // 2 % 2)
        self.bits = [bits[bit] for bit in order]
        self.partners = [me + (1 - 2 * bits[bit]) * 2**bit for bit in order]
        self.place = me // 4

    def copy(self, source, target, device, sem):
        return pltpu.make_async_remote_copy(
            src_ref=source,
            dst_ref=target,
            send_sem=self.send.at[sem],
            recv_sem=self.recv.at[sem],
            device_id={"seq": device},
            device_id_type=pl.DeviceIdType.MESH,
        )

    def copies(self, number):
        one, two = self.bits
        rest = self.rest
        others = []
        for step in range(1, rest):
            place = (self.place + step) % rest
            others.append((step, place, place * 4 + self.me % 4))
        if number == 0:
            return [self.copy(self.total.at[1 - one], self.half, self.partners[0], 0)]
        if number == 1:
            return [self.copy(self.half.at[1 - two], self.quarter, self.partners[1], 1)]
        if number == 2:
            return [
                self.copy(self.quarter.at[place], self.others.at[step - 1], device, 1 + step)
                for step, place, device in others
            ]
        if number == 3:
            block = self.total.at[one, two, self.place]
            return [self.copy(block, block, device, rest + step) for step, place, device in others]
        if number == 4:
            block = self.total.at[one, two]
            return [self.copy(block, block, self.partners[1], 2 * rest)]
        if number == 5:
            block = self.total.at[one]
            return [self.copy(block, block, self.partners[0], 2 * rest + 1)]
        return []

    def finish_first(self):
        one, rest = self.bits[0], self.rest
        for copy in self.copies(0):
            copy.wait()

        @pl.loop(0, 2 * rest)
        def _(i):
            j, z = i // rest, i % rest
            mine = self.total[one, j, z].astype(F32)
            self.half[j, z] = (mine + self.half[j, z].astype(F32)).astype(BF)

    def step(self, number):
        one, two = self.bits
        rest = self.rest
        if number == 0 and self.begun:
            return
        if number == 1:
            if not self.begun:
                self.finish_first()
        elif number > 0:
            for copy in self.copies(number - 1):
                copy.wait()
        if number == 2:

            @pl.loop(0, rest)
            def _(z):
                mine = self.half[two, z].astype(F32)
                self.quarter[z] = (mine + self.quarter[z].astype(F32)).astype(BF)

        elif number == 3:
            mine = self.quarter[self.place].astype(F32)
            for step in range(1, rest):
                mine = mine + self.others[step - 1].astype(F32)
            self.total[one, two, self.place] = mine.astype(BF)
        for copy in self.copies(number):
            copy.start()

    @staticmethod
    def scratch(size, rows, columns):
        rest = size // 4
        count = 2 * rest + 2
        return [
            pltpu.VMEM((2, rest, rows, columns), BF),
            pltpu.VMEM((rest, rows, columns), BF),
            pltpu.VMEM((rest - 1, rows, columns), BF),
            pltpu.SemaphoreType.DMA((count,)),
            pltpu.SemaphoreType.DMA((count,)),
        ]


def reduction_parts(value, size):
    rows, columns = value.shape
    return value.reshape(2, 2, size // 4, rows // size, columns)


def reduction_whole(value):
    return value.reshape(-1, value.shape[-1])


def make_reductions(orders, totals, scratch):
    out = []
    for order, total in zip(orders, totals):
        out.append(Reduction(order, total, *scratch[:5]))
        scratch = scratch[5:]
    return out


def group_copies(branch, source, target, send_sems, recv_sems, local_sem):
    stride = 2**branch
    base, place = group_place(branch)
    first = stride - branch - 2
    copies = [
        pltpu.make_async_copy(source.at[place], target.at[place], local_sem.at[branch - 1])
    ]
    for step in range(1, stride):
        member = (place + step) % stride
        copies.append(
            pltpu.make_async_remote_copy(
                src_ref=source.at[member],
                dst_ref=target.at[place],
                send_sem=send_sems.at[first + step],
                recv_sem=recv_sems.at[first + step],
                device_id={"seq": base + member},
                device_id_type=pl.DeviceIdType.MESH,
            )
        )
    return copies


def forward_kernel(heads, starts, tokens, cotangent, bits, gain, shift, in_proj, *refs):
    count = BRANCHES - 1
    names = Names(refs)
    far = names.take(4 + count)
    first, backs = names.one(), names.take(count)
    near = names.take(4 + count)
    (x_rows, normed, cot, own), gots = near[:4], near[4:]
    outs, sends = names.take(count), names.take(count)
    x, q_aug, result, in_send, in_recv, in_local, out_send, out_recv, out_local = names.take(9)
    spread_rows, normed_own, cot_own, normed_t, head_sems, far_sem = names.take(6)
    saves = [pltpu.make_async_copy(near[i], far[i], far_sem.at[i]) for i in range(4 + count)]
    me_head = lax.axis_index("head")
    rows, width = tokens.shape
    per_slot = rows // SLOTS

    def fill(source):
        for column in range(width // 128):
            spread_rows[column] = source[:, column * 128 : (column + 1) * 128].astype(F32)

    def picked(slot):
        at = pl.ds(slot_place(slot), per_slot, stride=SLOTS)
        return jnp.concatenate([spread_rows[column, at, :] for column in range(width // 128)], axis=1)

    fill(tokens)

    @over_slots
    def _(slot):
        value = picked(slot)
        x_rows[pl.ds(pl.multiple_of(slot * per_slot, per_slot), per_slot)] = value
        low = (norm_of(value)[0] * gain[...][None] + shift[...][None]).astype(BF)
        normed_own[slot] = low
        normed[slot, me_head] = low

    meet("seq", "head")
    for copy in head_copies(normed_own, normed, head_sems, 0, False):
        copy.start()
    saves[0].start()
    fill(cotangent)

    @over_slots
    def _(slot):
        low = picked(slot).astype(BF)
        cot_own[slot] = low
        cot[slot, me_head] = low

    for copy in head_copies(cot_own, cot, head_sems, 1, False):
        copy.start()
    own[0, :, 3 * E :, :] = jnp.broadcast_to(bits[...][None], (heads,) + bits.shape)
    turned = [in_proj[j].T for j in range(3)]
    for copy in head_copies(normed_own, normed, head_sems, 0, False):
        copy.wait()
    normed_t[...] = normed[...].reshape(SEG0, width).T
    for j in range(3):
        value = jnp.dot(turned[j], normed_t[...], preferred_element_type=F32)
        if j == 0:
            value = value * (E ** (-0.5) * LOG2E)
        own[0, :, j * E : (j + 1) * E, :] = value.astype(BF).reshape(heads, E, SEG0)
    saves[1].start()
    saves[3].start()

    coming = {}
    for branch in range(1, BRANCHES):

        @pl.loop(0, heads)
        def _(head):
            spread_blocks(heads, head, starts, own[0, head].astype(F32), sends, [branch])

        coming[branch] = group_copies(branch, sends[branch - 1], gots[branch - 1], in_send, in_recv, in_local)
        for copy in coming[branch]:
            copy.start()

    @pl.loop(0, heads)
    def _(head):
        x[...] = own[0, head]
        forward_unit(x, q_aug, result, 0, SEG0)
        first[0, head] = result[...]

    for copy in head_copies(cot_own, cot, head_sems, 1, False):
        copy.wait()
    saves[2].start()
    leaving = []
    for branch in range(1, BRANCHES):
        stride, lanes, units, split = branch_shape(branch, heads)
        got, out = gots[branch - 1], outs[branch - 1]
        for copy in coming[branch]:
            copy.wait()
        saves[3 + branch].start()
        queries = SEG0 // split
        base = 0 if split == 1 else lax.axis_index("seq") % split * queries

        @pl.loop(0, units)
        def _(unit):
            load_unit(got, unit, lanes, x)
            forward_unit(x, q_aug, result, base, queries)
            store_unit(out, unit, lanes, result)

        copies = group_copies(branch, out, backs[branch - 1], out_send, out_recv, out_local)
        for copy in copies:
            copy.start()
        leaving += copies
    for copy in leaving + saves:
        copy.wait()


def exchange_scratch():
    copies = 2**BRANCHES - 2 - BRANCHES + 1
    one = [
        pltpu.SemaphoreType.DMA((copies,)),
        pltpu.SemaphoreType.DMA((copies,)),
        pltpu.SemaphoreType.DMA((BRANCHES - 1,)),
    ]
    return one + one


def unit_cost(units, dots):
    return pl.CostEstimate(
        flops=dots * 2 * units * SEG0 * SEG0 * 256,
        transcendentals=units * SEG0 * SEG0,
        bytes_accessed=units * SEG0 * 1000,
    )


def vmem_specs(count):
    return [pl.BlockSpec(memory_space=pltpu.VMEM)] * count


def forward(heads, starts, tokens, cotangent, bits, gain, shift, in_proj):
    head_size = lax.axis_size("head")
    rows, width = tokens.shape
    shard = jax.ShapeDtypeStruct((SLOTS, head_size, rows // SLOTS, width), BF)
    own_rows = pltpu.VMEM((SLOTS, rows // SLOTS, width), BF)
    backs = send_shapes(heads, ROWS_OUT)
    gots = send_shapes(heads, ROWS_IN)
    own = jax.ShapeDtypeStruct((1, heads, ROWS_IN, SEG0), BF)
    far = [jax.ShapeDtypeStruct((rows, width), F32), shard, shard, own] + gots
    results = pl.pallas_call(
        partial(forward_kernel, heads),
        in_specs=[pl.BlockSpec(memory_space=pltpu.SMEM)] + vmem_specs(6),
        out_specs=[pl.BlockSpec(memory_space=pl.ANY)] * len(far) + vmem_specs(1 + len(backs)),
        out_shape=far + [jax.ShapeDtypeStruct((1, heads, ROWS_OUT, SEG0), BF)] + backs,
        scratch_shapes=[pltpu.VMEM(shape.shape, shape.dtype) for shape in far + backs + gots]
        + [
            pltpu.VMEM((ROWS_IN, SEG0), BF),
            pltpu.VMEM((ROWS_OUT, SEG0), BF),
            pltpu.VMEM((ROWS_OUT, SEG0), BF),
        ]
        + exchange_scratch()
        + [
            pltpu.VMEM((width // 128, rows, 128), F32),
            own_rows,
            own_rows,
            pltpu.VMEM((width, SEG0), BF),
            pltpu.SemaphoreType.DMA((2, 2, head_size - 1)),
            pltpu.SemaphoreType.DMA((len(far),)),
        ],
        compiler_params=pltpu.CompilerParams(
            vmem_limit_bytes=60 * 2**20, collective_id=0, has_side_effects=True
        ),
        cost_estimate=unit_cost(2 * heads, 2),
        name="forward",
    )(starts, tokens, cotangent, bits, gain, shift, in_proj)
    return results[:4], results[4 : len(far)], results[len(far)], results[len(far) + 1 :]


def backward_unit(x, g, q_aug, gk, gv, result, base, queries, tile):
    if isinstance(base, int):
        lanes = slice(base, base + queries)
    else:
        lanes = pl.ds(pl.multiple_of(base, 128), queries)
    extra = g[E:, lanes].astype(F32)
    ids = lax.broadcasted_iota(jnp.int32, extra.shape, 0)
    q = x[0:E, lanes]
    q_aug[0:E, :queries] = q
    q_aug[E:, :queries] = jnp.where(ids >= 12, extra, x[3 * E :, lanes].astype(F32) * -FAR).astype(BF)
    bits = x[3 * E :, :].astype(F32)
    k_aug = jnp.concatenate([x[E : 2 * E, :], (1.0 - bits).astype(BF)], axis=0)
    k_rows = k_aug.T
    v_ids = lax.broadcasted_iota(jnp.int32, bits.shape, 0)
    v_bits = jnp.where(v_ids < 3, 1.0, 0.0).astype(BF)
    v_rows = jnp.concatenate([x[2 * E : 3 * E, :], v_bits], axis=0).T
    q_rows = jnp.concatenate([q, jnp.zeros((BIT_ROWS, queries), BF)], axis=0).T
    g_all = g[:, lanes]
    g_rows = g_all.T
    if queries < SEG0:
        result[0:E, :] = jnp.zeros((E, SEG0), BF)
    for step in range(queries // tile):
        column = step * tile
        span = slice(column, column + tile)
        p = jnp.exp2(jnp.dot(k_rows, q_aug[:, span], preferred_element_type=F32))
        gs = p * jnp.dot(v_rows, g_all[:, span], preferred_element_type=F32)
        p, gs = p.astype(BF), gs.astype(BF)
        target = span if isinstance(base, int) else pl.ds(pl.multiple_of(base + column, 128), tile)
        result[0:E, target] = jnp.dot(k_aug, gs, preferred_element_type=F32)[:E].astype(BF)
        new_k = jnp.dot(gs, q_rows[span], preferred_element_type=F32)
        new_v = jnp.dot(p, g_rows[span], preferred_element_type=F32)
        if step == 0:
            gk[...] = new_k
            gv[...] = new_v
        else:
            gk[...] += new_k
            gv[...] += new_v
    result[E : 2 * E, :] = (gk[...].T[:E] * LN2).astype(BF)
    result[2 * E :, :] = gv[...].T[:E].astype(BF)


ORDERS = {
    'u1': (0, 1), 'u2': (0, 1), 'd1': (1, 0), 'd2': (1, 0), 'o': (0, 1), 'i0': (1, 0), 'i1': (0, 1), 'i2': (1,
    0),
}
EARLY = [
    (1, 'd1', 0), (1, 'u1', 0), (2, 'd1', 1), (2, 'u1', 1), (3, 'o', 0), (6, 'u1', 2), (6, 'd2', 0), (6, 'u2',
    0), (8, 'u2', 1), (8, 'd1', 2), (10, 'u1', 3), (12, 'd1', 3), (12, 'd2', 1), (13, 'u2', 2), (13, 'o', 1),
]
TAIL = [
    ('u1', 4), 'gather', ('d1', 4), 'in0', ('i0', 0), ('d2', 2), 'in1', ('u1', 5), 'in2', ('i2', 0), ('i0',
    1), ('d1', 5), ('u2', 3), ('o', 2), ('d2', 3), 'one', ('i2', 1), 'norm', ('i0', 2), ('i1', 0), ('u1', 6),
    ('u2', 4), ('o', 3), ('d2', 4), ('i0', 3), ('i1', 1), 'gain0', ('o', 4), ('i0', 4), ('i2', 2), ('i1', 2),
    ('d2', 5), 'gain1', ('u2', 5), ('i2', 3), ('i1', 3), ('i1', 4), ('i0', 5), 'gain2', ('i2', 4), ('o', 5),
    ('i1', 5), ('i2', 5), ('d2', 6), 'gain3', ('i2', 6), ('u2', 6), 'gain4', ('d1', 6), ('o', 6), ('i1', 6),
    ('i0', 6),
]


def stream_names(streams):
    pairs = streams // 2
    return [kind + str(i + 1) for i in range(pairs) for kind in "ud"] + ["o"]


def backward_kernel(heads, streams, *refs):
    branches = BRANCHES - 1
    names = Names(refs)
    starts, gain, gains_two = names.take(3)
    sends = names.take(branches)
    far = names.take(branches + 6)
    parts = names.take(streams)
    far_totals, gains_out = names.take(5), names.one()
    near_totals, save_sem = names.take(5), names.one()
    up_total, down_total, out_total, in_total, grad_tokens = near_totals
    chunks = (streams - 1) // 2
    totals = []
    for chunk in range(chunks):
        lanes = pl.ds(chunk * (up_total.shape[-1] // chunks), up_total.shape[-1] // chunks)
        totals += [up_total.at[:, :, :, :, lanes], down_total.at[chunk]]
    totals.append(out_total)
    in_totals = [in_total.at[j] for j in range(3)]
    near = names.take(branches + 6)
    (own, own_g), units_in, (normed, in_proj, x_rows, grad_hidden) = near[:2], near[2:-4], near[-4:]
    far_sem = names.one()
    first = names.one()
    backs, gots, outs = names.take(branches), names.take(branches), names.take(branches)
    x, g, q_aug, gk, gv, result = names.take(6)
    total, grads, grads_t, normed_t, spread_rows, head_send, head_recv = names.take(7)
    gain_head, gain_one, gain_two, gain_rest = names.take(4)
    in_send, in_recv, in_local, out_send, out_recv, out_local = names.take(6)
    part_sem, head_sems, gain_sems = names.take(3)
    labels = stream_names(streams) + ["i0", "i1", "i2"]
    reductions = make_reductions(
        [ORDERS[label] for label in labels], list(totals) + list(in_totals), names.take(5 * streams + 15)
    )
    reductions = dict(zip(labels, reductions))
    for label in labels[: streams - 1]:
        reductions[label].begun = True

    shapes = [branch_shape(b, heads) for b in range(BRANCHES)]
    size, head_size = lax.axis_size("seq"), lax.axis_size("head")
    me, me_head = lax.axis_index("seq"), lax.axis_index("head")
    rest = size // 4
    tile = 512
    per_slot = x_rows.shape[0] // SLOTS
    width = x_rows.shape[1]


    def fill(s):
        target = reductions[labels[s]].half if s < streams - 1 else totals[-1]
        return pltpu.make_async_copy(parts[s], target, part_sem.at[s])

    def load(i):
        return pltpu.make_async_copy(far[i], near[i], far_sem.at[i])

    for s in range(streams):
        fill(s).start()
    for i in range(branches + 6):
        load(i).start()
    meet("seq", "head")

    def coming(branch):
        return group_copies(branch, sends[branch - 1], gots[branch - 1], in_send, in_recv, in_local)

    def leaving(branch):
        return group_copies(branch, outs[branch - 1], backs[branch - 1], out_send, out_recv, out_local)

    for branch in range(1, BRANCHES):
        for copy in coming(branch):
            copy.start()
    for i in range(2):
        load(i).wait()

    def advance(label, number):
        if label in labels[:streams] and number == (1 if reductions[label].begun else 0):
            fill(labels.index(label)).wait()
        reductions[label].step(number)

    def split_branch(branch):
        stride, lanes, units, split = shapes[branch]
        queries = SEG0 // split
        load(1 + branch).wait()
        for copy in coming(branch):
            copy.wait()
        load_unit(units_in[branch - 1], 0, lanes, x)
        load_unit(gots[branch - 1], 0, lanes, g)
        backward_unit(x, g, q_aug, gk, gv, result, me % split * queries, queries, min(tile, queries))
        store_unit(outs[branch - 1], 0, lanes, result)

    runs, at = [(0, 0, 0, heads // 2)], heads // 2
    split_at = None
    for branch in range(1, BRANCHES):
        if shapes[branch][3] == 1:
            runs.append((branch, at, 0, shapes[branch][2]))
            at += shapes[branch][2]
    split_at = at
    runs.append((0, at, heads // 2, heads - heads // 2))
    blocks = at + heads - heads // 2
    plan = {}
    for block, stream, step in EARLY:
        if stream in labels:
            plan.setdefault(block * blocks // 15, []).append((stream, step))

    @pl.loop(0, blocks)
    def _(block):
        for after, events in plan.items():

            @pl.when(block == after)
            def _(events=events):
                for stream, step in events:
                    advance(stream, step)

        @pl.when(block == split_at)
        def _():
            for branch in range(1, BRANCHES):
                if shapes[branch][3] > 1:
                    split_branch(branch)
                    for copy in leaving(branch):
                        copy.start()

        for branch, low, unit, count in runs:

            @pl.when((block >= low) & (block < low + count))
            def _(branch=branch, low=low, unit=unit):
                if branch == 0:
                    x[...] = own[0, block - low + unit]
                    g[...] = own_g[0, block - low + unit]
                else:

                    @pl.when(block == low)
                    def _():
                        load(1 + branch).wait()
                        for copy in coming(branch):
                            copy.wait()

                    load_unit(units_in[branch - 1], block - low, shapes[branch][1], x)
                    load_unit(gots[branch - 1], block - low, shapes[branch][1], g)

        backward_unit(x, g, q_aug, gk, gv, result, 0, SEG0, tile)
        for branch, low, unit, count in runs:

            @pl.when((block >= low) & (block < low + count))
            def _(branch=branch, low=low, unit=unit, count=count):
                if branch == 0:
                    first[block - low + unit] = result[...]
                else:
                    store_unit(outs[branch - 1], block - low, shapes[branch][1], result)

                    @pl.when(block == low + count - 1)
                    def _():
                        for copy in leaving(branch):
                            copy.start()

    def saves(index):
        return pltpu.make_async_copy(near_totals[index], far_totals[index], save_sem.at[index])

    def save(index):
        saves(index).start()

    tasks = {}

    def task(work):
        tasks[work.__name__] = work

    @task
    def gather():
        for i in range(4):
            load(branches + 2 + i).wait()
        for branch in range(1, BRANCHES):
            for copy in leaving(branch):
                copy.wait()

        @pl.loop(0, heads)
        def _(head):
            total[...] = first[head].astype(F32)
            for branch in range(1, BRANCHES):
                stride, lanes, per, split = shapes[branch]
                back, start = backs[branch - 1], reversed_bits(starts[branch, head], branch)
                if split == 1:
                    value = back[head // per, head % per].astype(F32)
                else:
                    value = back[head * split, 0].astype(F32)
                    for copy in range(1, split):
                        value = value + back[head * split + copy, 0].astype(F32)
                if lanes < 128:
                    value = unpacked(value, 3 * E, start % 2)
                    start = start // 2
                    lanes = 128
                for block in range(SEG0 // lanes):
                    span = slice(block * lanes, (block + 1) * lanes)
                    total[:, span] += jnp.where(start == block, value, 0.0)
            grads[0, head] = (total[0:E, :] * E ** (-0.5)).astype(BF)
            grads[1, head] = total[E : 2 * E, :].astype(BF)
            grads[2, head] = total[2 * E :, :].astype(BF)

        normed_t[...] = normed[...].reshape(SEG0, width).T

    def in_gradient(j):
        rows_in = in_totals[0].shape[3]
        chunk = width // 2
        grads_t[j] = grads[j].reshape(heads * E, SEG0).T
        for half in range(2):
            value = jnp.dot(
                normed_t[half * chunk : (half + 1) * chunk], grads_t[j], preferred_element_type=F32
            ).astype(BF)
            for part in range(chunk // rows_in):
                index = half * (chunk // rows_in) + part
                in_totals[j][index // (2 * rest), index // rest % 2, index % rest] = value[
                    part * rows_in : (part + 1) * rows_in
                ]

    for j in range(3):
        tasks[f"in{j}"] = partial(in_gradient, j)

    def head_swaps():
        swaps = []
        for step in range(1, head_size):
            device = (me_head + step) % head_size
            swaps.append(
                pltpu.make_async_remote_copy(
                    src_ref=head_send.at[device],
                    dst_ref=head_recv.at[step - 1],
                    send_sem=head_sems.at[0, step - 1],
                    recv_sem=head_sems.at[1, step - 1],
                    device_id={"head": device},
                    device_id_type=pl.DeviceIdType.MESH,
                )
            )
        return swaps

    @task
    def one():
        for half in range(2):
            rows = slice(half * SEG0 // 2, (half + 1) * SEG0 // 2)
            value = jnp.zeros((SEG0 // 2, width), F32)
            for j in range(3):
                value = value + lax.dot_general(
                    grads_t[j, rows], in_proj[j], (((1,), (1,)), ((), ())), preferred_element_type=F32
                )
            value = value.astype(BF)
            for slot in range(SLOTS // 2):
                for device in range(head_size):
                    begin = (slot * head_size + device) * per_slot
                    place = (half * SLOTS // 2 + slot) * per_slot
                    head_send[device, place : place + per_slot] = value[begin : begin + per_slot]
        for swap in head_swaps():
            swap.start()

    @task
    def norm():
        for swap in head_swaps():
            swap.wait()
        gain_head[me_head] = jnp.zeros(gains_out.shape, F32)
        gain_head[me_head, 2:4] = gains_two[...]

        @pl.loop(0, SLOTS)
        def _(slot):
            rows = pl.ds(pl.multiple_of(slot * per_slot, per_slot), per_slot)
            grad = head_send[me_head, rows].astype(F32)
            for step in range(1, head_size):
                grad = grad + head_recv[step - 1, rows].astype(F32)
            values = x_rows[rows]
            centred = values - jnp.mean(values, axis=-1, keepdims=True)
            scale = lax.rsqrt(jnp.mean(centred * centred, axis=-1, keepdims=True) + EPS)
            unit = centred * scale
            scaled = grad * gain[...][None]
            inner = jnp.mean(scaled * unit, axis=-1, keepdims=True)
            out = grad_hidden[rows] + scale * (
                scaled - jnp.mean(scaled, axis=-1, keepdims=True) - unit * inner
            )
            place = slot_place(slot)
            for column in range(width // 128):
                lanes = slice(column * 128, (column + 1) * 128)
                spread_rows[column, pl.ds(place, per_slot, stride=SLOTS), :] = out[:, lanes]
            gain_head[me_head, 0:1] += jnp.sum(grad * unit, axis=0, keepdims=True)
            gain_head[me_head, 1:2] += jnp.sum(grad, axis=0, keepdims=True)

        for column in range(width // 128):
            grad_tokens[:, column * 128 : (column + 1) * 128] = spread_rows[column]
        save(4)

    def gain_copy(source, target, axis, device, sem):
        return pltpu.make_async_remote_copy(
            src_ref=source,
            dst_ref=target,
            send_sem=gain_sems.at[0, sem],
            recv_sem=gain_sems.at[1, sem],
            device_id={axis: device},
            device_id_type=pl.DeviceIdType.MESH,
        )

    def gain_copies(stage):
        if stage == 0:
            mine = gain_head.at[me_head]
            return [
                gain_copy(mine, mine, "head", (me_head + step) % head_size, step - 1)
                for step in range(1, head_size)
            ]
        if stage == 1:
            return [gain_copy(gain_one.at[0], gain_one.at[1], "seq", me + 1 - 2 * (me % 2), head_size)]
        if stage == 2:
            device = me + 2 - 4 * (me // 2 % 2)
            return [gain_copy(gain_two.at[0], gain_two.at[1], "seq", device, head_size + 1)]
        spot = me // 4
        block = gain_rest.at[spot]
        return [
            gain_copy(block, block, "seq", (spot + step) % rest * 4 + me % 4, head_size + 1 + step)
            for step in range(1, rest)
        ]

    def summed(ref, count):
        value = ref[0]
        for index in range(1, count):
            value = value + ref[index]
        return value

    def gain_stage(stage):
        if stage > 0:
            for swap in gain_copies(stage - 1):
                swap.wait()
        if stage == 1:
            gain_one[0] = summed(gain_head, head_size)
        elif stage == 2:
            gain_two[0] = summed(gain_one, 2)
        elif stage == 3:
            gain_rest[me // 4] = summed(gain_two, 2)
        elif stage == 4:
            gains_out[...] = summed(gain_rest, rest)
            return
        for swap in gain_copies(stage):
            swap.start()

    for stage in range(5):
        tasks[f"gain{stage}"] = partial(gain_stage, stage)

    groups = [[], [], ["o"], ["i0", "i1", "i2"]]
    for chunk in range(chunks):
        groups[0].append(labels[2 * chunk])
        groups[1].append(labels[2 * chunk + 1])
    for item in TAIL:
        if isinstance(item, str):
            tasks[item]()
        elif item[0] in labels:
            advance(item[0], item[1])
            if item[1] == Reduction.STEPS - 1:
                for index, group in enumerate(groups):
                    if item[0] in group:
                        group.remove(item[0])
                        if not group:
                            save(index)
    for index in range(5):
        saves(index).wait()


def backward(heads, starts, own, own_g, units, sends, parts, normed, in_proj, x_rows, grad_hidden, gain, gains_two):
    size, head_size = lax.axis_size("seq"), lax.axis_size("head")
    rest = size // 4
    rows, width = x_rows.shape
    in_shape = (2, 2, rest, width // size, heads * E)
    scratch = []
    for part in parts:
        scratch += Reduction.scratch(size, *part.shape[-2:])
    for _ in range(3):
        scratch += Reduction.scratch(size, *in_shape[-2:])
    streams = len(parts)
    chunks = (streams - 1) // 2
    far = [own, own_g] + list(units) + [normed, in_proj, x_rows, grad_hidden]
    totals = [
        jax.ShapeDtypeStruct((2, 2, rest, width // size, chunks * parts[0].shape[-1]), BF),
        jax.ShapeDtypeStruct((chunks, 2, 2, rest) + parts[1].shape[-2:], BF),
        jax.ShapeDtypeStruct(parts[-1].shape, BF),
        jax.ShapeDtypeStruct((3,) + in_shape, BF),
        jax.ShapeDtypeStruct((rows, width), F32),
    ]
    results = pl.pallas_call(
        partial(backward_kernel, heads, streams),
        in_specs=[pl.BlockSpec(memory_space=pltpu.SMEM)]
        + vmem_specs(2)
        + [pl.BlockSpec(memory_space=pl.ANY)] * (len(sends) + len(far) + streams),
        out_specs=[pl.BlockSpec(memory_space=pl.ANY)] * len(totals) + vmem_specs(1),
        out_shape=totals + [jax.ShapeDtypeStruct((8, width), F32)],
        scratch_shapes=[pltpu.VMEM(value.shape, value.dtype) for value in totals]
        + [pltpu.SemaphoreType.DMA((len(totals),))]
        + [pltpu.VMEM(value.shape, value.dtype) for value in far]
        + [pltpu.SemaphoreType.DMA((len(far),)), pltpu.VMEM((heads, 3 * E, SEG0), BF)]
        + [pltpu.VMEM(shape.shape, BF) for shape in send_shapes(heads, 3 * E)]
        + [pltpu.VMEM(shape.shape, BF) for shape in send_shapes(heads, ROWS_OUT)]
        + [pltpu.VMEM(shape.shape, BF) for shape in send_shapes(heads, 3 * E)]
        + [
            pltpu.VMEM((ROWS_IN, SEG0), BF),
            pltpu.VMEM((ROWS_OUT, SEG0), BF),
            pltpu.VMEM((ROWS_OUT, SEG0), BF),
            pltpu.VMEM((SEG0, ROWS_OUT), F32),
            pltpu.VMEM((SEG0, ROWS_OUT), F32),
            pltpu.VMEM((3 * E, SEG0), BF),
            pltpu.VMEM((3 * E, SEG0), F32),
            pltpu.VMEM((3, heads, E, SEG0), BF),
            pltpu.VMEM((3, SEG0, heads * E), BF),
            pltpu.VMEM((width, SEG0), BF),
            pltpu.VMEM((width // 128, rows, 128), F32),
            pltpu.VMEM((head_size, rows, width), BF),
            pltpu.VMEM((head_size - 1, rows, width), BF),
            pltpu.VMEM((head_size, 8, width), F32),
            pltpu.VMEM((2, 8, width), F32),
            pltpu.VMEM((2, 8, width), F32),
            pltpu.VMEM((rest, 8, width), F32),
        ]
        + exchange_scratch()
        + [
            pltpu.SemaphoreType.DMA((streams,)),
            pltpu.SemaphoreType.DMA((2, head_size - 1)),
            pltpu.SemaphoreType.DMA((2, head_size + 1 + rest)),
        ]
        + scratch,
        compiler_params=pltpu.CompilerParams(
            vmem_limit_bytes=60 * 2**20, collective_id=1, has_side_effects=True
        ),
        cost_estimate=unit_cost(2 * heads, 5),
        name="backward",
    )(starts, gain, gains_two, *sends, *far, *parts)
    up_total, down_total, out_total, in_total = results[:4]
    sums = [
        in_total.reshape(3, width, heads * E),
        out_total.reshape(-1, width),
        up_total.reshape(width, -1),
        down_total.reshape(-1, width),
    ]
    return sums, results[4], results[5]


def finish_kernel(gains, *refs):
    count = (len(refs) - 4) // 2
    for source, target in zip(refs[:count], refs[count : 2 * count]):
        target[...] = source[...].astype(target.dtype)
    for index in range(4):
        refs[2 * count + index][...] = gains[index]


def finish(values, types, gains):
    steps = 2
    specs = []
    for value in values:
        shape = list(value.shape)
        shape[-2] //= steps
        if value.ndim == 3:
            specs.append(pl.BlockSpec(tuple(shape), lambda i: (0, i, 0)))
        else:
            specs.append(pl.BlockSpec(tuple(shape), lambda i: (i, 0)))
    return pl.pallas_call(
        finish_kernel,
        grid=(steps,),
        in_specs=[pl.BlockSpec(gains.shape, lambda i: (0, 0))] + specs,
        out_specs=specs + [pl.BlockSpec(gains.shape[1:], lambda i: (0,))] * 4,
        out_shape=[jax.ShapeDtypeStruct(value.shape, kind) for value, kind in zip(values, types)]
        + [jax.ShapeDtypeStruct(gains.shape[1:], F32)] * 4,
        compiler_params=pltpu.CompilerParams(vmem_limit_bytes=61 * 2**20),
        name="finish",
    )(gains, *values)


def middle_kernel(heads, *refs):
    branches = BRANCHES - 1
    names = Names(refs)
    starts, first = names.take(2)
    backs = names.take(branches)
    gain, shift = names.take(2)
    far = names.take(5)
    chunks = max(1, far[3].shape[1] // far[0].shape[1])
    saved = 4 + branches + 2 * chunks
    far_results, gains_two = names.take(saved), names.one()
    near_results, save_sem = names.take(saved), names.one()
    block_out, grad_hidden, own_g, out_total = near_results[:4]
    sends, halves = near_results[4 : 4 + branches], near_results[4 + branches :]
    saves = [pltpu.make_async_copy(near_results[i], far_results[i], save_sem.at[i]) for i in range(saved)]
    merged, lse, mixed, turned, part, got, part_two, got_two = names.take(8)
    hidden_one, normed_own, normed, spread_rows, normed_t = names.take(5)
    down_sum, norm_sum, up_grad, down_grad, totals = names.take(5)
    head_sems, first_sems, far_sem = names.take(3)
    near = names.take(5)
    out_proj, x_rows, cot, up, down = near[2], near[0], near[1], near[3], near[4]
    loads = [pltpu.make_async_copy(far[i], near[i], far_sem.at[i]) for i in range(5)]
    for i in (2, 0, 1, 3, 4):
        loads[i].start()

    head_size, me_head = lax.axis_size("head"), lax.axis_index("head")
    me = lax.axis_index("seq")
    rest = lax.axis_size("seq") // 4
    width = x_rows.shape[1]
    per_slot = x_rows.shape[0] // SLOTS
    tile = 256

    meet("seq", "head")

    @pl.loop(0, heads)
    def _(head):
        own = first[0, head].astype(F32)
        merged[head] = own[:E]
        lse[head] = own[E : E + 1] + own[E + 1 : E + 2] + own[E + 2 : E + 3]
        for branch in range(1, BRANCHES):
            stride, lanes, per, split = branch_shape(branch, heads)
            back, start = backs[branch - 1], reversed_bits(starts[branch, head], branch)
            share = max(1, 128 // lanes)
            for copy in range(split):
                if split == 1:
                    value = back[head // per, head % per].astype(F32)
                else:
                    value = back[head * split + copy, 0].astype(F32)
                if share > 1:
                    value = unpacked(value, ROWS_OUT, start % share)
                new_lse = value[E : E + 1] + value[E + 1 : E + 2] + value[E + 2 : E + 3]
                if share > 1:
                    ids = lax.broadcasted_iota(jnp.int32, new_lse.shape, 1)
                    new_lse = jnp.where(ids // lanes == start % share, new_lse, -FAR)
                span = lanes * share
                for block in range(SEG0 // span):
                    at = slice(block * span, (block + 1) * span)
                    new = jnp.where(start // share == block, new_lse, -FAR)
                    old = lse[head, :, at]
                    top = jnp.maximum(old, new)
                    both = top + jnp.log2(jnp.exp2(old - top) + jnp.exp2(new - top))
                    lse[head, :, at] = both
                    merged[head, :, at] = merged[head, :, at] * jnp.exp2(old - both) + value[:E] * jnp.exp2(
                        new - both
                    )
        mixed[head] = merged[head].astype(BF)

    def rows_of(ref):
        return ref[...].reshape(SEG0, width)

    turned[...] = mixed[...].reshape(heads * E, SEG0).T
    loads[2].wait()
    for step in range(SEG0 // tile):
        at = slice(step * tile // (head_size * per_slot), (step + 1) * tile // (head_size * per_slot))
        value = jnp.dot(turned[step * tile : (step + 1) * tile], out_proj[...], preferred_element_type=F32)
        part[at] = value.astype(BF).reshape(-1, head_size, per_slot, width)
    for copy in head_copies(part, got, head_sems, 0, True):
        copy.start()
    for ref in (down_sum, norm_sum, up_grad, down_grad):
        ref[...] = jnp.zeros_like(ref)
    loads[0].wait()
    for copy in head_copies(part, got, head_sems, 0, True):
        copy.wait()

    def rows_at(slot):
        return pl.ds(pl.multiple_of(slot * per_slot, per_slot), per_slot)

    @over_slots
    def _(slot):
        value = x_rows[rows_at(slot)] + part[slot, me_head].astype(F32)
        for step in range(1, head_size):
            value = value + got[step - 1, slot].astype(F32)
        hidden_one[rows_at(slot)] = value
        unit, scale = norm_of(value)
        low = (unit * gain[...][None] + shift[...][None]).astype(BF)
        normed_own[slot] = low
        normed[slot, me_head] = low

    for copy in head_copies(normed_own, normed, head_sems, 1, False):
        copy.start()
    for copy in head_copies(normed_own, normed, head_sems, 1, False):
        copy.wait()
    normed_t[...] = rows_of(normed).T
    for i in (1, 3, 4):
        loads[i].wait()

    chunk_width = up.shape[1] // chunks
    orders = {0: ORDERS["u1"], 1: ORDERS["d1"]}
    firsts = []
    for chunk in range(chunks):
        for kind in range(2):
            index = 2 * chunk + kind
            firsts.append(
                Reduction(
                    orders[kind], totals.at[index], halves[index], None, None,
                    first_sems.at[0, pl.ds(index, 1)], first_sems.at[1, pl.ds(index, 1)],
                )
            )
    slots = tile // (head_size * per_slot)
    contract_last = (((1,), (1,)), ((), ()))

    for chunk in range(chunks):
        units = slice(chunk * chunk_width, (chunk + 1) * chunk_width)
        if chunk > 0:
            up_grad[...] = jnp.zeros_like(up_grad)
            down_grad[...] = jnp.zeros_like(down_grad)

        @pl.loop(0, SEG0 // tile)
        def _(step):
            rows = pl.ds(pl.multiple_of(step * tile, tile), tile)
            low = normed[pl.ds(step * slots, slots)].reshape(tile, width)
            back = cot[pl.ds(step * slots, slots)].reshape(tile, width)
            pre = jnp.dot(low, up[:, units], preferred_element_type=F32)
            grad = lax.dot_general(back, down[units], contract_last, preferred_element_type=F32)
            share = 0.5 + 0.5 * lax.erf(pre * math.sqrt(0.5))
            density = jnp.exp2(pre * pre * (-0.5 * LOG2E)) * (1.0 / math.sqrt(2.0 * math.pi))
            hidden = (pre * share).astype(BF)
            grad = (grad * (share + pre * density)).astype(BF)
            down_sum[rows] += jnp.dot(hidden, down[units], preferred_element_type=F32)
            norm_sum[rows] += lax.dot_general(grad, up[:, units], contract_last, preferred_element_type=F32)
            up_grad[...] += jnp.dot(normed_t[:, rows], grad, preferred_element_type=F32)
            down_grad[...] += jnp.dot(hidden.T, back, preferred_element_type=F32)

        pieces = totals.shape[3] * 4
        size = totals.shape[4]
        for piece in range(pieces):
            spot = (piece // (2 * rest), piece // rest % 2, piece % rest)
            span = slice(piece * size, (piece + 1) * size)
            totals[(2 * chunk,) + spot] = up_grad[span].astype(BF)
            totals[(2 * chunk + 1,) + spot] = down_grad[span].astype(BF)
        firsts[2 * chunk].step(0)
        firsts[2 * chunk + 1].step(0)

    for ref, value in ((part, down_sum), (part_two, norm_sum)):

        @pl.loop(0, SLOTS)
        def _(slot):
            for device in range(head_size):
                begin = pl.multiple_of((slot * head_size + device) * per_slot, per_slot)
                ref[slot, device] = value[pl.ds(begin, per_slot)].astype(BF)

    for copy in head_copies(part_two, got_two, head_sems, 2, True) + head_copies(part, got, head_sems, 3, True):
        copy.start()
    for copy in head_copies(part_two, got_two, head_sems, 2, True):
        copy.wait()
    gains_two[...] = jnp.zeros_like(gains_two)

    @over_slots
    def _(slot):
        grad = part_two[slot, me_head].astype(F32)
        for step in range(1, head_size):
            grad = grad + got_two[step - 1, slot].astype(F32)
        unit, scale = norm_of(hidden_one[rows_at(slot)])
        scaled = grad * gain[...][None]
        inner = jnp.mean(scaled * unit, axis=-1, keepdims=True)
        out = cot[slot, me_head].astype(F32) + scale * (
            scaled - jnp.mean(scaled, axis=-1, keepdims=True) - unit * inner
        )
        grad_hidden[rows_at(slot)] = out
        normed_own[slot] = out.astype(BF)
        normed[slot, me_head] = out.astype(BF)
        gains_two[0:1] += jnp.sum(grad * unit, axis=0, keepdims=True)
        gains_two[1:2] += jnp.sum(grad, axis=0, keepdims=True)

    for copy in head_copies(normed_own, normed, head_sems, 4, False):
        copy.start()
    saves[1].start()
    for copy in head_copies(part, got, head_sems, 3, True):
        copy.wait()

    @pl.loop(0, SLOTS)
    def _(slot):
        value = hidden_one[rows_at(slot)] + part[slot, me_head].astype(F32)
        for step in range(1, head_size):
            value = value + got[step - 1, slot].astype(F32)
        place = slot_place(slot)
        for column in range(width // 128):
            lanes = slice(column * 128, (column + 1) * 128)
            spread_rows[column, pl.ds(place, per_slot, stride=SLOTS), :] = value[:, lanes]

    for column in range(width // 128):
        block_out[:, column * 128 : (column + 1) * 128] = spread_rows[column].astype(BF)
    saves[0].start()
    for copy in head_copies(normed_own, normed, head_sems, 4, False):
        copy.wait()

    value = jnp.dot(mixed[...].reshape(heads * E, SEG0), rows_of(normed), preferred_element_type=F32)
    size = out_total.shape[3]
    for piece in range(4 * rest):
        spot = (piece // (2 * rest), piece // rest % 2, piece % rest)
        out_total[spot] = value[piece * size : (piece + 1) * size].astype(BF)
    saves[3].start()

    normed_t[...] = rows_of(normed).T
    value = jnp.dot(out_proj[...], normed_t[...], preferred_element_type=F32)
    own_g[0, :, :E, :] = value.astype(BF).reshape(heads, E, SEG0)

    @pl.loop(0, heads)
    def _(head):
        low = own_g[0, head, :E, :]
        dots = jnp.sum(low.astype(F32) * merged[head], axis=0, keepdims=True)
        d = pieces_of(-dots)
        m = pieces_of(-lse[head])
        placed = {0: d[0], 1: d[1], 2: d[2], 12: m[0], 13: m[1], 14: m[2]}
        own_g[0, head, E:, :] = row_block(placed, SEG0).astype(BF)
        own = jnp.concatenate([low.astype(F32), row_block(placed, SEG0)], axis=0)
        spread_blocks(heads, head, starts, own, sends)

    for index in [2] + list(range(4, 4 + branches)):
        saves[index].start()
    for index, reduction in enumerate(firsts):
        reduction.finish_first()
        saves[4 + branches + index].start()
    for copy in saves:
        copy.wait()


def middle(heads, starts, first, backs, x_rows, cot, out_proj, up, down, gain, shift):
    size, head_size = lax.axis_size("seq"), lax.axis_size("head")
    rest = size // 4
    rows, width = x_rows.shape
    per_slot = rows // SLOTS
    chunks = max(1, up.shape[1] // width)
    shard = (SLOTS, head_size, per_slot, width)
    own = (SLOTS, per_slot, width)
    got = (head_size - 1,) + own
    sends = send_shapes(heads, ROWS_OUT)
    piece = (2, rest, width // size, up.shape[1] // chunks)
    out_piece = (2, 2, rest, heads * E // size, width)
    far = [x_rows, cot, out_proj, up, down]
    saved = [
        jax.ShapeDtypeStruct((rows, width), BF),
        jax.ShapeDtypeStruct((rows, width), F32),
        jax.ShapeDtypeStruct((1, heads, ROWS_OUT, SEG0), BF),
        jax.ShapeDtypeStruct(out_piece, BF),
    ]
    saved += sends + [jax.ShapeDtypeStruct(piece, BF)] * (2 * chunks)
    results = pl.pallas_call(
        partial(middle_kernel, heads),
        in_specs=[pl.BlockSpec(memory_space=pltpu.SMEM)]
        + vmem_specs(1 + len(backs) + 2)
        + [pl.BlockSpec(memory_space=pl.ANY)] * 5,
        out_specs=[pl.BlockSpec(memory_space=pl.ANY)] * len(saved) + vmem_specs(1),
        out_shape=saved + [jax.ShapeDtypeStruct((2, width), F32)],
        scratch_shapes=[pltpu.VMEM(value.shape, value.dtype) for value in saved]
        + [pltpu.SemaphoreType.DMA((len(saved),))]
        + [
            pltpu.VMEM((heads, E, SEG0), F32),
            pltpu.VMEM((heads, 1, SEG0), F32),
            pltpu.VMEM((heads, E, SEG0), BF),
            pltpu.VMEM((SEG0, heads * E), BF),
            pltpu.VMEM(shard, BF),
            pltpu.VMEM(got, BF),
            pltpu.VMEM(shard, BF),
            pltpu.VMEM(got, BF),
            pltpu.VMEM((rows, width), F32),
            pltpu.VMEM(own, BF),
            pltpu.VMEM(shard, BF),
            pltpu.VMEM((width // 128, rows, 128), F32),
            pltpu.VMEM((width, SEG0), BF),
            pltpu.VMEM((SEG0, width), F32),
            pltpu.VMEM((SEG0, width), F32),
            pltpu.VMEM((width, up.shape[1] // chunks), F32),
            pltpu.VMEM((up.shape[1] // chunks, width), F32),
            pltpu.VMEM((2 * chunks, 2) + piece, BF),
            pltpu.SemaphoreType.DMA((2, 5, head_size - 1)),
            pltpu.SemaphoreType.DMA((2, 2 * chunks)),
            pltpu.SemaphoreType.DMA((5,)),
        ]
        + [pltpu.VMEM(value.shape, value.dtype) for value in far],
        compiler_params=pltpu.CompilerParams(
            vmem_limit_bytes=60 * 2**20, collective_id=2, has_side_effects=True
        ),
        cost_estimate=pl.CostEstimate(
            flops=14 * SEG0 * width * up.shape[1], transcendentals=0, bytes_accessed=40 * 2**20
        ),
        name="middle",
    )(starts, first, *backs, gain, shift, *far)
    block_out, grad_hidden, own_g, out_total = results[:4]
    sends, halves = results[4 : 4 + len(sends)], results[4 + len(sends) : -1]
    return block_out, grad_hidden, results[-1], own_g, sends, list(halves) + [out_total]


def local(
    tokens,
    documents,
    offsets,
    in_proj,
    out_proj,
    up_proj,
    down_proj,
    first_gain,
    first_shift,
    second_gain,
    second_shift,
    cotangent,
):
    head_count = lax.axis_size("head")
    seq_id = lax.axis_index("seq")
    row_count = tokens.shape[0]
    seq_len = row_count * head_count
    heads = offsets.shape[1]
    per_slot = row_count // SLOTS

    my_docs = lax.dynamic_slice_in_dim(documents, seq_id * seq_len, seq_len)
    my_docs = my_docs.reshape(head_count, per_slot, 2, 2, 2, 2).transpose(5, 4, 3, 2, 0, 1).reshape(seq_len)
    bit_ids = jnp.arange(BIT_ROWS, dtype=jnp.int32)[:, None]
    doc_bit = my_docs[None, :] // 2 ** (bit_ids % DOC_BITS) % 2
    bits = jnp.where(bit_ids < DOC_BITS, doc_bit, jnp.where(bit_ids < 2 * DOC_BITS, 1 - doc_bit, 0))
    bits = bits.astype(BF)

    (x_rows, normed, cot_all, own), units, first_out, outs = forward(
        heads, offsets, tokens, cotangent, bits, first_gain, first_shift, in_proj
    )
    block_out, grad_hidden, gains_two, own_g, sends_g, parts = middle(
        heads, offsets, first_out, outs, x_rows, cot_all, out_proj, up_proj, down_proj, second_gain, second_shift
    )
    sums, grad_tokens, gains = backward(
        heads, offsets, own, own_g, units, sends_g, parts,
        normed, in_proj, x_rows, grad_hidden, first_gain, gains_two,
    )
    return tuple(finish([block_out, grad_tokens] + sums, [BF] + [F32] * 5, gains))


def solution(mesh):
    placed = (
        P(("seq", "head"), None),
        P(),
        P(None, "head"),
        P(None, None, "head"),
        P("head", None),
        P(None, "head"),
        P("head", None),
        P(),
        P(),
        P(),
        P(),
        P(("seq", "head"), None),
    )
    return jax.shard_map(
        local,
        mesh=mesh,
        in_specs=placed,
        out_specs=(
            P(("seq", "head"), None),
            P(("seq", "head"), None),
            P(None, None, "head"),
            P("head", None),
            P(None, "head"),
            P("head", None),
            P(),
            P(),
            P(),
            P(),
        ),
        check_vma=False,
    )
```
